256 devices in a mesh: space: 16 (over z, x_lo), vel: 16 (over y, x_hi, core).
Axes of the slice: x: 4 (x_hi: 2, x_lo: 2; x = x_hi * 2 + x_lo), y: 4, z: 8, core: 2. Of those that a mesh axis runs over, the one named last changes fastest.
Arguments:
- velocity_dist: bfloat16 [32768, 4096], P('vel', 'space'), may hold values from -6 to 6
- macro_state: float32 [13, 4096], P(None, ('space', 'vel')), may hold values from -2 to 2
- collision_rate: float32 [4096], P('space'), may hold values from 0.25 to 2
- wall_flags: int32 [4096], P('space'), may hold values 0 or 1
- diffusivity: float32 [13], replicated, may hold values from 0.5 to 8
- coupling: float32 [13, 13], replicated, may hold values from -0.25 to 4.5, as said below
Outputs:
- dist_out: bfloat16 [32768, 4096], P('vel', 'space')
- macro_out: float32 [13, 4096], P(None, ('space', 'vel'))
The draws below stay inside these ranges and needn't reach their ends.
Inputs may be any that keep to these rules, and one draw needn't show every extreme that they name: `coupling`: symmetric, with each diagonal entry larger than the sum of magnitudes of the other entries of its row.
All inputs are finite; a program needn't handle non-finite values. No bound on the sum of `wall_flags` on one device may be relied on, other than what follows from the above.
Results may differ from the reference program's by a relative error of at most 0.001.
Values sent between devices are 32-bit elements; how exact they have to be, the bound alone decides.
No kernel may reach another device: no remote copies, remote signals or barrier semaphores. Data moves between devices by JAX's collectives and lax.ppermute only.
A program may use at most 64 MiB of HBM per device.

```python
import math
import jax
import jax.numpy as jnp
from jax import lax

NV1 = 32
VEL = 32768
K = 13
ITERS = 3
SWEEPS = 2
NX = 4096
N_VEL = 16


def draw_coupling(key, part):
    spread = 0.15
    perturb = jax.random.uniform(jax.random.fold_in(key, 11), (K, K), jnp.float32, -spread, spread)
    symmetric = 0.5 * (perturb + perturb.T)
    offdiag = symmetric * (1.0 - jnp.eye(K, dtype=jnp.float32))
    margin = jax.random.uniform(jax.random.fold_in(key, 12), (K,), jnp.float32, 0.5, 1.5)
    diagonal = jnp.sum(jnp.abs(offdiag), axis=1) + margin
    return offdiag + jnp.diag(diagonal)


def touch_ends(drawn, own_key, least, high):
    longest = drawn.shape.index(max(drawn.shape))
    spots = []
    for shift in (0, 1):
        where = [jax.random.randint(jax.random.fold_in(own_key, axis), (), 0, length) for axis, length in enumerate(drawn.shape)]
        where[longest] = (where[longest] + shift) % drawn.shape[longest]
        spots.append(tuple(where))
    return drawn.at[spots[0]].set(least).at[spots[1]].set(high)


def steps_of(rng, shape, cuts, smallest, top_value):
    loudness, own = 1.0, jax.random.fold_in(rng, 6)
    for position, shards_of in cuts:
        draws = jnp.exp(jax.random.uniform(jax.random.fold_in(own, position), (shards_of,), jnp.float32, smallest / len(cuts), top_value / len(cuts)))
        loudness = loudness * jnp.repeat(draws, shape[position] // shards_of).reshape([-1 if axis == position else 1 for axis in range(len(shape))])
    return loudness


def scatter_about(key, extent, scale, bound, cuts=(), kind=jnp.bfloat16):
    values = scale * jax.random.normal(key, extent, jnp.float32)
    if cuts:
        values = values * steps_of(key, extent, cuts, -0.22, 0.18)
    return jnp.clip(values, -bound, bound).astype(kind)


def setup_inputs(seed: int = 0) -> dict:
    keys = jax.random.split(jax.random.key(seed), 7)
    return {
        "velocity_dist": scatter_about(keys[0], (VEL, NX), 1.0, 6.0, ((0, 16), (1, 16))),
        "macro_state": scatter_about(keys[1], (K, NX), 0.3, 2.0, ((1, 256),), jnp.float32),
        "collision_rate": jnp.clip(jnp.exp(math.log(2.0) - 2.0794415 * jax.random.uniform(keys[2], (NX,), jnp.float32) ** steps_of(keys[2], (NX,), ((0, 16),), -0.2, 0.2)), 0.25, 2.0),
        "wall_flags": touch_ends((jax.random.randint(keys[3], (NX,), 0, 8) < 1).astype(jnp.int32), jax.random.fold_in(keys[3], 1), 0, 1),
        "diffusivity": jnp.clip(jnp.exp(jax.random.uniform(keys[4], (K,), jnp.float32, math.log(0.5), math.log(8.0))), 0.5, 8.0),
        "coupling": draw_coupling(jax.random.fold_in(keys[6], 71), 0),
    }


highest = lax.Precision.HIGHEST
speed_limit = 4.0
time_step = 0.125
shakhov_weights = (1.0, 1.0, 1.0, 1.0, 1.0, 0.0, 0.0, 0.0, 0.0, 0.0, 1.0 / 3.0, 1.0 / 3.0, 1.0 / 3.0)

def velocity_table(first_row, number):
    indices = first_row + jnp.arange(number, dtype=jnp.int32)
    first_index = indices // (NV1 * NV1)
    second_index = indices // NV1 % NV1
    third_index = indices % NV1
    spacing = 2.0 * speed_limit / NV1
    speed_x = (first_index.astype(jnp.float32) + 0.5) * spacing - speed_limit
    speed_y = (second_index.astype(jnp.float32) + 0.5) * spacing - speed_limit
    speed_z = (third_index.astype(jnp.float32) + 0.5) * spacing - speed_limit
    speed_square = speed_x * speed_x + speed_y * speed_y + speed_z * speed_z
    weight = jnp.exp(-0.5 * speed_square) * (spacing ** 3 / (2.0 * math.pi) ** 1.5)
    return (speed_x, speed_y, speed_z, weight)

def moment_basis(speed_x, speed_y, speed_z):
    speed_square = speed_x * speed_x + speed_y * speed_y + speed_z * speed_z
    entries = [jnp.ones_like(speed_x), speed_x, speed_y, speed_z, (speed_square - 3.0) / math.sqrt(6.0), speed_x * speed_y, speed_x * speed_z, speed_y * speed_z, 0.5 * (speed_x * speed_x - speed_y * speed_y), (speed_x * speed_x + speed_y * speed_y - 2.0 * speed_z * speed_z) / math.sqrt(12.0), speed_x * (speed_square - 5.0) / math.sqrt(10.0), speed_y * (speed_square - 5.0) / math.sqrt(10.0), speed_z * (speed_square - 5.0) / math.sqrt(10.0)]
    return jnp.stack(entries)

def apply_operator(moments, diffusivity, coupling):
    padded = jnp.pad(moments, ((0, 0), (1, 1)))
    second_diff = 2.0 * moments - padded[:, :-2] - padded[:, 2:]
    return jnp.dot(coupling, moments, precision=highest) + diffusivity[:, None] * second_diff

def synthetic(residual, diffusivity, coupling):
    result = jnp.zeros_like(residual)
    for repeat in range(SWEEPS):
        applied = apply_operator(residual, diffusivity, coupling)
        step_size = jnp.sum(residual * residual) / jnp.sum(residual * applied)
        result = result + step_size * residual
        residual = residual - step_size * applied
    return result

def reference(velocity_dist, macro_state, collision_rate, wall_flags, diffusivity, coupling):
    total_rows = velocity_dist.shape[0]
    cell_count = velocity_dist.shape[1]
    blocks = N_VEL
    block_rows = total_rows // blocks
    relax_rate = time_step * collision_rate * (1.0 + wall_flags.astype(jnp.float32))
    shakhov = jnp.array(shakhov_weights, dtype=jnp.float32)
    distribution = velocity_dist.astype(jnp.float32).reshape(blocks, block_rows, cell_count)
    starts = jnp.arange(blocks, dtype=jnp.int32) * block_rows
    current = macro_state
    for iteration in range(ITERS):

        def kinetic(pieces):
            velocity_block, first_row = pieces
            speed_x, speed_y, speed_z, weight = velocity_table(first_row, block_rows)
            basis_rows = moment_basis(speed_x, speed_y, speed_z)
            equilibrium = jnp.dot((basis_rows * shakhov[:, None]).T, current, precision=highest)
            padded = jnp.pad(velocity_block, ((0, 0), (1, 1)))
            gradient = jnp.where((speed_x > 0.0)[:, None], velocity_block - padded[:, :-2], padded[:, 2:] - velocity_block)
            advanced = velocity_block - (time_step * speed_x)[:, None] * gradient + relax_rate[None, :] * (equilibrium - velocity_block)
            partial_value = jnp.dot(basis_rows * weight[None, :], advanced, precision=highest)
            return (advanced, partial_value)
        halves, partials = lax.map(kinetic, (distribution, starts))
        shares = lax.optimization_barrier(jnp.sum(partials, axis=0))
        correction = synthetic(shares - current, diffusivity, coupling)
        current = shares + correction

        def correct(pieces):
            velocity_block, first_row = pieces
            speed_x, speed_y, speed_z, weight = velocity_table(first_row, block_rows)
            basis_rows = moment_basis(speed_x, speed_y, speed_z)
            return velocity_block + jnp.dot(basis_rows.T, correction, precision=highest)
        distribution = lax.map(correct, (halves, starts))
    return (distribution.reshape(total_rows, cell_count).astype(jnp.bfloat16), current)
```

```python
import math

import jax
import jax.numpy as jnp
import numpy as np
from jax import lax
from jax.experimental import pallas as pl
from jax.experimental.pallas import tpu as pltpu
from jax.sharding import PartitionSpec as P

NV1 = 32
K = 13
time_step = 0.125
spacing = 8.0 / NV1
CELLS = 256
WIDE = 384
PEERS = 16
ROWS = 2048
BLOCK = 1024
bf16 = jnp.bfloat16
f32 = jnp.float32


def parts_of(x, number):
    rest = np.asarray(x, np.float64)
    out = []
    for _ in range(number):
        piece = rest.astype(np.float32).astype(bf16)
        out.append(piece)
        rest = rest - piece.astype(np.float64)
    return out


def grid_constants():
    v = (np.arange(NV1) + 0.5) * spacing - 4.0
    w = np.exp(-0.5 * v * v) * spacing / math.sqrt(2.0 * math.pi)
    vy, vz = np.repeat(v, NV1), np.tile(v, NV1)
    wyz = np.repeat(w, NV1) * np.tile(w, NV1)
    one = np.ones_like(vy)
    yz = vy * vy + vz * vz
    phi = np.stack([one, vy, vz, vy * vz, vy * vy, vz * vz, vy * yz, vz * yz])
    cmat = np.zeros((NV1, K, 8))
    for i, x in enumerate(v):
        c = cmat[i]
        c[0, 0] = 1.0
        c[1, 0] = x
        c[2, 1] = 1.0
        c[3, 2] = 1.0
        c[4, 0] = (x * x - 3.0) / math.sqrt(6.0)
        c[4, 4] = c[4, 5] = 1.0 / math.sqrt(6.0)
        c[5, 1] = x
        c[6, 2] = x
        c[7, 3] = 1.0
        c[8, 0] = 0.5 * x * x
        c[8, 4] = -0.5
        c[9, 0] = x * x / math.sqrt(12.0)
        c[9, 4] = 1.0 / math.sqrt(12.0)
        c[9, 5] = -2.0 / math.sqrt(12.0)
        c[10, 0] = x * (x * x - 5.0) / math.sqrt(10.0)
        c[10, 4] = c[10, 5] = x / math.sqrt(10.0)
        c[11, 1] = (x * x - 5.0) / math.sqrt(10.0)
        c[11, 6] = 1.0 / math.sqrt(10.0)
        c[12, 2] = (x * x - 5.0) / math.sqrt(10.0)
        c[12, 7] = 1.0 / math.sqrt(10.0)
    a = time_step * np.abs(v)
    plus = v > 0.0
    proj = phi * wyz
    groups = [np.ones(NV1)]
    for power in (1, 2, 3):
        groups += [a**power * plus, a**power * ~plus]
    big = np.zeros((7 * 16, 8 * NV1))
    for g, factor in enumerate(groups):
        for i in range(NV1):
            big[16 * g : 16 * g + K, 8 * i : 8 * i + 8] = factor[i] * w[i] * cmat[i]
    gram2 = proj @ phi.T
    shakhov = np.array([1.0] * 5 + [0.0] * 5 + [1.0 / 3.0] * 3)

    def between(factor):
        out = np.zeros((16, 16))
        for i in range(NV1):
            out[:K, :K] += factor[i] * w[i] * cmat[i] @ gram2 @ cmat[i].T
        return out

    c16 = np.zeros(16)
    c16[:K] = shakhov
    g, gp, gm, g2p, g2m = (between(groups[k]) for k in (0, 1, 2, 3, 4))
    mats = [g, gp, gm, g * c16, gp * c16, gm * c16, g2p, g2m, g2p * c16, g2m * c16]
    mats = six_terms(np.concatenate(mats, axis=0))
    big3 = np.concatenate(parts_of(big, 3), axis=0)
    p3 = np.concatenate(parts_of(proj, 3) + [np.zeros((8, BLOCK), bf16)], axis=0)
    ph, pm = parts_of(phi.T, 2)
    phi_k = np.concatenate([ph, ph, pm, np.zeros((BLOCK, 104), bf16)], axis=1)
    own = np.zeros((PEERS, 16, 16))
    speed = np.zeros((PEERS, 16, 128), np.float32)
    for j in range(PEERS):
        for u in range(2):
            own[j, 8 * u : 8 * u + 8, :K] = cmat[2 * j + u].T
            speed[j, 8 * u : 8 * u + 8] = a[2 * j + u]
    own = six_terms(own)
    return big3, mats, p3, phi_k, own, speed, shakhov


def six_terms(x):
    h, m, low = parts_of(x, 3)
    return np.concatenate([h, h, h, m, m, low], axis=-1)


BASES = (1, 3, 9)


def pair_table():
    entries = []
    for stage, size in enumerate(BASES):
        for quantity in range(4):
            for i in range(size):
                for j in range(i, size):
                    entries.append((stage, quantity, i, j))
    return entries


PAIRS = pair_table()


def pair_arrays():
    kind = np.full((8, 128), -1, np.int32)
    left = np.zeros((8, 128), np.int32)
    right = np.zeros((8, 128), np.int32)
    twice = np.zeros((8, 128), np.float32)
    for n, (stage, quantity, i, j) in enumerate(PAIRS):
        at = (n // 128, n % 128)
        kind[at] = 4 * stage + quantity
        left[at], right[at] = i, j
        twice[at] = 1.0 if i == j else 2.0
    return kind, left, right, twice


def lanes_of(shape):
    return lax.broadcasted_iota(jnp.int32, shape, len(shape) - 1)


def rows_of(shape):
    return lax.broadcasted_iota(jnp.int32, shape, 0)


def stack6(f):
    h = f.astype(bf16)
    rest = f - h.astype(f32)
    m = rest.astype(bf16)
    low = (rest - m.astype(f32)).astype(bf16)
    return jnp.concatenate([h, m, low, h, m, h], axis=0)


def relax_of(rate, flags):
    return (time_step * rate) * (1.0 + flags.astype(f32))


def shift_up(x):
    return pltpu.roll(x, 1, 1)


def shift_down(x):
    return pltpu.roll(x, x.shape[1] - 1, 1)


def diff_up(x):
    return x - shift_up(x)


def diff_down(x):
    return x - shift_down(x)


def sums_kernel(place, dist, p3, owned, rate, flags, sums, up, down, edge):
    positive = place[1] >= PEERS // 2
    parts = []
    for u in range(2):
        y = jnp.dot(p3[...], dist[pl.ds(u * BLOCK, BLOCK), :], preferred_element_type=f32)
        parts.append(y[0:8] + y[8:16] + y[16:24])
    w = jnp.concatenate(parts, axis=0)
    sums[...] = w
    lane = lanes_of((16, 128))
    row = rows_of((16, 128))
    mine = owned[...]
    relax = relax_of(rate[...], flags[...])
    r_first = jnp.broadcast_to(pltpu.roll(relax[:, 0:128], 48, 1), (16, 128))
    r_last = jnp.broadcast_to(pltpu.roll(relax[:, 128:256], 48, 1), (16, 128))
    zero = jnp.zeros((16, 128), f32)
    up[...] = (
        jnp.where(lane >= 120, w[:, 128:256], zero)
        + pltpu.roll(mine, 16, 1)
        + jnp.where((row == K) & (lane >= 32) & (lane < 48), r_last, zero)
    )
    down[...] = (
        jnp.where(lane < 8, w[:, 0:128], zero)
        + pltpu.roll(mine, 32, 1)
        + jnp.where((row == K) & (lane >= 48) & (lane < 64), r_first, zero)
    )
    e_lane = lanes_of((16, CELLS))
    e_row = rows_of((16, CELLS))
    first = jnp.where(positive, CELLS - 8, 0)
    pick = jnp.where((e_lane == e_row + first) & (e_row < 8), 1.0, 0.0).astype(bf16)
    for u in range(2):
        e = lax.dot_general(
            pick,
            dist[pl.ds(u * BLOCK, BLOCK), :],
            (((1,), (1,)), ((), ())),
            preferred_element_type=f32,
        )
        edge[:, pl.ds(u * BLOCK, BLOCK)] = e[0:8]


def pack_kernel(sums, up, down, owned, out):
    third = up[...] + down[...] + owned[...]
    whole = jnp.concatenate([sums[...], third], axis=1)
    for j in range(PEERS):
        out[j] = whole


N_FIELDS = 28


def fields_kernel(n_space, place, got, rate, flags, big3, mats, diffusivity, fields, relax_out, partial, table):
    slab = place[0]
    lane = lanes_of((1, WIDE))
    right = (lane >= CELLS) & (lane < CELLS + 8)
    left = lane >= WIDE - 8
    own = lane < CELLS
    inside = own | (right & (slab < n_space - 1)) | (left & (slab > 0))
    mask = jnp.where(inside, 1.0, 0.0)

    w = got[...].reshape(PEERS * 16, WIDE)
    w = jnp.where(own | right | left, w, 0.0)
    wh = w.astype(bf16)
    w_rest = w - wh.astype(f32)
    wm = w_rest.astype(bf16)
    wl = (w_rest - wm.astype(f32)).astype(bf16)
    y = jnp.dot(big3[...], wh, preferred_element_type=f32)
    z = jnp.dot(big3[0:224], wm, preferred_element_type=f32)
    t = jnp.dot(big3[0:112], wl, preferred_element_type=f32)
    mu = ((y[224:336] + z[112:224]) + (y[112:224] + z[0:112])) + t + y[0:112]
    mu = [mu[16 * g : 16 * g + 16] for g in range(7)]

    lane1 = lanes_of((16, 128))
    row1 = rows_of((16, 128))
    zero = jnp.zeros((16, 128), f32)
    halves = [zero, zero]
    for j in range(PEERS):
        tile = got[j, :, 2 * 128 : 3 * 128]
        amount = (16 * j - 16) % 128
        moved = pltpu.roll(tile, amount, 1) if amount else tile
        begin = 16 * (j % 8)
        halves[j // 8] = jnp.where((lane1 >= begin) & (lane1 < begin + 16), moved, halves[j // 8])
    from_first = pltpu.roll(got[0, :, 2 * 128 : 3 * 128], 80, 1)
    from_last = pltpu.roll(got[PEERS - 1, :, 2 * 128 : 3 * 128], 80, 1)
    ends = jnp.where(lane1 < 8, from_first, jnp.where(lane1 >= 120, from_last, zero))
    start = jnp.concatenate([halves[0], halves[1], ends], axis=1)
    start = jnp.where(rows_of((16, WIDE)) < K, start, 0.0)
    relax_own = relax_of(rate[...], flags[...])
    relax_ends = jnp.where((lane1 < 8) | (lane1 >= 120), from_first, zero)[K : K + 1]
    relax1 = jnp.concatenate([relax_own, relax_ends], axis=1)
    relax_out[...] = jnp.broadcast_to(relax1, (8, WIDE))
    r = jnp.broadcast_to(relax1, (16, WIDE))
    keep = 1.0 - r
    mask = jnp.broadcast_to(mask, (16, WIDE))
    diffusion = jnp.concatenate([diffusivity[...]] * 3, axis=1)

    def advance(base, ups, downs):
        new = keep * base - diff_up(ups[0]) - diff_down(downs[0])
        new_ups = [keep * ups[n] - diff_up(ups[n + 1]) for n in range(len(ups) - 1)]
        new_downs = [keep * downs[n] - diff_down(downs[n + 1]) for n in range(len(downs) - 1)]
        return new, new_ups, new_downs

    ups, downs = [mu[1], mu[3], mu[5]], [mu[2], mu[4], mu[6]]
    s1, ups, downs = advance(mu[0], ups, downs)
    s2, ups, downs = advance(s1, ups, downs)
    s3, _, _ = advance(s2, ups, downs)

    def times(first, last, inputs):
        stacked = stack6(jnp.concatenate(inputs, axis=1) if len(inputs) > 1 else inputs[0])
        y = jnp.dot(mats[16 * first : 16 * last], stacked, preferred_element_type=f32)
        out = []
        for n in range(len(inputs)):
            cut = y[:, n * WIDE : (n + 1) * WIDE]
            out.append([cut[16 * g : 16 * g + 16] for g in range(last - first)])
        return out

    def applied(f, coupled):
        return mask * (coupled + diffusion * (2.0 * f - shift_up(f) - shift_down(f)))

    def streamed(g, gp, gm):
        return keep * g - diff_up(gp) - diff_down(gm)

    def streamed_twice(k1, gp, gm, g2p, g2m):
        return keep * k1 - diff_up(keep * gp - diff_up(g2p)) - diff_down(keep * gm - diff_down(g2m))

    ((gc, gcp, gcm, _, _, g2cp, g2cm),) = times(4, 11, [start])
    relaxed = r * gc
    shares = mask * (s1 + relaxed)
    res = mask * (shares - start)
    k1_start = streamed(relaxed, r * gcp, r * gcm)
    k2_start = streamed_twice(k1_start, r * gcp, r * gcm, r * g2cp, r * g2cm)

    def parts(f, ys):
        out = [applied(f, ys[0])]
        k1 = streamed(ys[1], ys[2], ys[3])
        rg = r * ys[4]
        held = rg - f
        out += [mask * (k1 + held), held]
        if len(ys) > 5:
            out.append(streamed_twice(k1, ys[2], ys[3], ys[7], ys[8]))
            out.append(streamed(rg, r * ys[5], r * ys[6]) + held)
        return out

    y_shares, y_res = times(0, 9, [shares, res])
    rg = r * y_shares[4]
    held_shares = rg - shares
    n_shares = streamed(rg, r * y_shares[5], r * y_shares[6]) + held_shares
    p0 = mask * (s2 + k1_start + held_shares)
    e, p1, _, k2_res, n_res = parts(res, y_res)

    y_e, y_p0, y_p1 = times(0, 9, [e, p0, p1])
    ee, p2, _, k2_e, n_e = parts(e, y_e)
    ap0, q3, held_p0 = parts(p0, y_p0[:5])
    ap1, q4, held_p1 = parts(p1, y_p1[:5])
    q0 = mask * (s3 + k2_start + n_shares + held_p0)
    q1 = mask * (k2_res + n_res + held_p1)

    y_p2, y_ap0, y_ap1, y_q0, y_q1, y_q3, y_q4 = times(0, 5, [p2, ap0, ap1, q0, q1, q3, q4])
    ap2, q5, held_p2 = parts(p2, y_p2)
    aap0, q6, _ = parts(ap0, y_ap0)
    aap1, q7, _ = parts(ap1, y_ap1)
    q2 = mask * (k2_e + n_e + held_p2)
    aq0, aq1, aq3, aq4 = (applied(f, y[0]) for f, y in ((q0, y_q0), (q1, y_q1), (q3, y_q3), (q4, y_q4)))

    (y_ap2,) = times(0, 5, [ap2])
    aap2, q8, _ = parts(ap2, y_ap2)
    first = [q2, q5, q6, q7, aq0, aq1, aq3, aq4]
    aq2, aq5, aq6, aq7, aaq0, aaq1, aaq3, aaq4 = (applied(f, y[0]) for f, y in zip(first, times(0, 1, first)))
    second = [q8, aq2, aq5, aq6, aq7]
    aq8, aaq2, aaq5, aaq6, aaq7 = (applied(f, y[0]) for f, y in zip(second, times(0, 1, second)))
    ((y_aq8,),) = times(0, 1, [aq8])
    aaq8 = applied(aq8, y_aq8)

    q = [q0, q1, q2, q3, q4, q5, q6, q7, q8]
    aq = [aq0, aq1, aq2, aq3, aq4, aq5, aq6, aq7, aq8]
    aaq = [aaq0, aaq1, aaq2, aaq3, aaq4, aaq5, aaq6, aaq7, aaq8]
    for n, f in enumerate([start, shares, res, e, p0, p1, p2, ap0, ap1, ap2] + q + aq):
        fields[n] = f

    plain = [[res], [p0, p1, p2], q]
    once = [[e], [ap0, ap1, ap2], aq]
    again = [[ee], [aap0, aap1, aap2], aaq]
    table[...] = jnp.zeros((256, 128), f32)
    for n, (stage, quantity, i, j) in enumerate(PAIRS):
        a, b = ((plain, plain), (plain, once), (once, once), (once, again))[quantity]
        product = a[stage][i][:, 0:CELLS] * b[stage][j][:, 0:CELLS]
        folded = (product[0:8, 0:128] + product[0:8, 128:256]) + (product[8:16, 0:128] + product[8:16, 128:256])
        table[n : n + 1, :] = jnp.sum(folded, axis=0, keepdims=True)
    ones = jnp.ones((8, 128), f32)
    tops = [
        lax.dot_general(
            ones,
            table[128 * n : 128 * n + 128, :],
            (((1,), (1,)), ((), ())),
            precision=lax.Precision.HIGHEST,
            preferred_element_type=f32,
        )
        for n in range(2)
    ]
    row8 = rows_of((8, 128))
    line = jnp.where(row8 == 0, tops[0], jnp.where(row8 == 1, tops[1], 0.0))
    for j in range(n_space):
        partial[j] = line


UPDATE_ROWS = 256


def update_kernel(
    n_space,
    place,
    partial,
    fields,
    relax_in,
    kind,
    left,
    right,
    twice,
    coupling,
    diffusivity,
    own6,
    speed,
    shakhov,
    dist,
    phi_k,
    halo,
    out,
    macro,
    bands_h,
    bands_l,
    mixed,
    band_ends,
):
    step = pl.program_id(0)
    positive = place[1] >= PEERS // 2

    @pl.when(step == 0)
    def _():
        total = partial[0]
        for j in range(1, n_space):
            total = total + partial[j]
        total = total * twice[...]
        cpl = coupling[...]
        lane16 = lanes_of((16, 128))
        row16 = rows_of((16, 128))
        size = jnp.sum(jnp.abs(cpl), axis=1, keepdims=True)
        middle = jnp.sum(jnp.where(lane16 == row16, cpl, 0.0), axis=1, keepdims=True)
        real = row16[:, 0:1] < K
        most = jnp.max(jnp.where(real, size + 4.0 * diffusivity[:, 0:1], 0.0), axis=0, keepdims=True)
        least = jnp.min(jnp.where(real, 2.0 * middle - size, 1e30), axis=0, keepdims=True)
        low_step, high_step = 1.0 / most, 1.0 / least

        def summed(weighted, which):
            picked = jnp.where(kind[...] == which, weighted, 0.0)
            return jnp.sum(jnp.sum(picked, axis=0, keepdims=True), axis=1, keepdims=True)

        def clipped(x):
            return jnp.minimum(jnp.maximum(x, low_step), high_step)

        def weights_of(stage, weighted):
            rr, ra, aa, aaa = (summed(weighted, 4 * stage + n) for n in range(4))
            s1 = clipped(rr / ra)
            rr2 = rr - 2.0 * s1 * ra + s1 * s1 * aa
            ra2 = ra - 2.0 * s1 * aa + s1 * s1 * aaa
            s2 = clipped(rr2 / ra2)
            return s1 + s2, -s1 * s2

        li, ri = left[...], right[...]

        def choose(index, zero, one, two):
            return jnp.where(index == 0, zero, jnp.where(index == 1, one, two))

        a1, b1 = weights_of(0, total)
        a2, b2 = weights_of(1, total * choose(li, 1.0, a1, b1) * choose(ri, 1.0, a1, b1))

        def both(index):
            outer = (index >= 3).astype(jnp.int32) + (index >= 6).astype(jnp.int32)
            return choose(outer, 1.0, a2, b2) * choose(index - 3 * outer, 1.0, a1, b1)

        a3, b3 = weights_of(2, total * both(li) * both(ri))

        start, shares, res, e = (fields[n] for n in range(4))
        corr1 = a1 * res + b1 * e
        cur1 = shares + corr1
        res2 = fields[4] + a1 * fields[5] + b1 * fields[6]
        e2 = fields[7] + a1 * fields[8] + b1 * fields[9]
        corr2 = a2 * res2 + b2 * e2
        cur2 = res2 + cur1 + corr2

        def third(at):
            rows = [fields[at + 3 * n] + a1 * fields[at + 3 * n + 1] + b1 * fields[at + 3 * n + 2] for n in range(3)]
            return rows[0] + a2 * rows[1] + b2 * rows[2]

        res3, e3 = third(10), third(19)
        corr3 = a3 * res3 + b3 * e3
        cur3 = res3 + cur2 + corr3
        mine = pltpu.roll(cur3[:, 0:CELLS], lax.rem(CELLS - 16 * place[1], CELLS), 1)
        macro[...] = mine[0:K, 0:16]

        r = jnp.broadcast_to(relax_in[0:1, :], (16, WIDE))
        scaled = shakhov[:, 0:1] * r
        f1 = scaled * start + corr1
        f2 = scaled * cur1 + corr2
        f3 = scaled * cur2 + corr3
        y = jnp.dot(own6[place[1]], stack6(jnp.concatenate([f1, f2, f3], axis=1)), preferred_element_type=f32)
        y1, y2, y3 = (y[:, n * WIDE : (n + 1) * WIDE] for n in range(3))
        a = speed[place[1]][:, 0:1]

        def before(x):
            return jnp.where(positive, shift_up(x), shift_down(x))

        stay = 1.0 - r - a

        def moved(x):
            return stay * x + a * before(x)

        h = (moved(moved(y1) + y2) + y3)[:, 0:CELLS]
        hh = h.astype(bf16).astype(f32)
        hm = (h - hh).astype(bf16).astype(f32)

        once = before(stay)
        two = before(once)
        t0 = stay * stay * stay
        t1 = a * (stay * (stay + once) + once * once)
        t2 = a * a * (stay + once + two)
        t3 = jnp.broadcast_to(a * a * a, (16, WIDE))
        towards = jnp.where(positive, 1, -1)
        at = rows_of((CELLS, CELLS))
        to = lanes_of((CELLS, CELLS))
        at8 = rows_of((8, CELLS))
        to8 = lanes_of((8, CELLS))
        at8 = jnp.where(positive, at8 - 8, at8 + CELLS)
        for u in range(2):
            ts = [x[8 * u : 8 * u + 1, 0:CELLS] for x in (t0, t1, t2, t3)]

            def band(source, target):
                shape = source.shape
                back = (target - source) * towards
                value = jnp.zeros(shape, f32)
                for n, x in enumerate(ts):
                    value = jnp.where(back == n, jnp.broadcast_to(x, shape), value)
                return value

            b = band(at, to)
            bh = b.astype(bf16)
            bands_h[u] = bh
            bands_l[u] = (b - bh.astype(f32)).astype(bf16)
            b8 = band(at8, to8)
            b8h = b8.astype(bf16).astype(f32)
            band_ends[u] = jnp.concatenate([b8h, b8 - b8h], axis=0).astype(bf16)
            hu, mu = hh[8 * u : 8 * u + 8], hm[8 * u : 8 * u + 8]
            mixed[u] = jnp.concatenate([hu, mu, hu, jnp.zeros((104, CELLS), f32)], axis=0).astype(bf16)

    u = step // (BLOCK // UPDATE_ROWS)
    x = dist[...]
    value = jnp.dot(x, bands_h[u], preferred_element_type=f32)
    value += jnp.dot(x, bands_l[u], preferred_element_type=f32)
    value += jnp.dot(phi_k[...], mixed[u], preferred_element_type=f32)
    ends = halo[...]
    ends = jnp.concatenate([ends, ends], axis=0).astype(bf16)
    value += lax.dot_general(ends, band_ends[u], (((0,), (0,)), ((), ())), preferred_element_type=f32)
    out[...] = value.astype(bf16)


def vmem():
    return pl.BlockSpec(memory_space=pltpu.VMEM)


def smem():
    return pl.BlockSpec(memory_space=pltpu.SMEM)


def rounded(x):
    return lax.reduce_precision(x, 8, 7)


def make_per_device(n_space):
    big3, mats, p3, phi_k, own6, speed, shakhov = grid_constants()
    kind, left, right, twice = pair_arrays()
    shakhov16 = np.zeros((16, 128), np.float32)
    shakhov16[:K] = shakhov[:, None]

    def per_device(velocity_dist, macro_state, collision_rate, wall_flags, diffusivity, coupling):
        place = jnp.stack([lax.axis_index("space"), lax.axis_index("vel")]).astype(jnp.int32)
        rate = collision_rate.reshape(1, CELLS)
        flags = wall_flags.reshape(1, CELLS)
        owned = jnp.pad(macro_state, ((0, 3), (16, 96)))
        sums, up, down, edge = pl.pallas_call(
            sums_kernel,
            out_shape=(
                jax.ShapeDtypeStruct((16, CELLS), f32),
                jax.ShapeDtypeStruct((16, 128), f32),
                jax.ShapeDtypeStruct((16, 128), f32),
                jax.ShapeDtypeStruct((8, ROWS), f32),
            ),
            in_specs=[smem()] + [vmem()] * 5,
            out_specs=(vmem(),) * 4,
        )(place, velocity_dist, p3, owned, rate, flags)
        rising = [(i, i + 1) for i in range(n_space - 1)]
        falling = [(j, i) for i, j in rising]
        from_left = lax.ppermute(up, "space", rising)
        from_right = lax.ppermute(down, "space", falling)
        packed = pl.pallas_call(
            pack_kernel,
            out_shape=jax.ShapeDtypeStruct((PEERS, 16, WIDE), f32),
            in_specs=[vmem()] * 4,
            out_specs=vmem(),
        )(sums, from_left, from_right, owned)
        got = lax.all_to_all(packed, "vel", split_axis=0, concat_axis=0, tiled=True)
        half = PEERS // 2
        upwind = [(i * PEERS + n, j * PEERS + n) for i, j in rising for n in range(half, PEERS)]
        upwind += [(j * PEERS + n, i * PEERS + n) for i, j in rising for n in range(half)]
        halo = lax.ppermute(edge, ("space", "vel"), upwind)

        cpl = jnp.pad(coupling, ((0, 3), (0, 3)))
        h = rounded(cpl)
        m = rounded(cpl - h)
        low = rounded(cpl - h - m)
        cpl6 = jnp.concatenate([h, h, h, m, m, low], axis=1).astype(bf16)
        all_mats = jnp.concatenate([cpl6, jnp.asarray(mats)], axis=0)
        spread_diff = jnp.broadcast_to(jnp.pad(diffusivity, (0, 3))[:, None], (16, 128))
        fields, relax, partial = pl.pallas_call(
            lambda *refs: fields_kernel(n_space, *refs),
            out_shape=(
                jax.ShapeDtypeStruct((N_FIELDS, 16, WIDE), f32),
                jax.ShapeDtypeStruct((8, WIDE), f32),
                jax.ShapeDtypeStruct((n_space, 8, 128), f32),
            ),
            in_specs=[smem()] + [vmem()] * 6,
            out_specs=(vmem(),) * 3,
            scratch_shapes=[pltpu.VMEM((256, 128), f32)],
            name="fields",
        )(place, got, rate, flags, big3, all_mats, spread_diff)
        partial = lax.all_to_all(partial, "space", split_axis=0, concat_axis=0, tiled=True)

        blocks = ROWS // UPDATE_ROWS
        per_speed = BLOCK // UPDATE_ROWS
        cpl_wide = jnp.pad(coupling, ((0, 3), (0, 115)))
        return pl.pallas_call(
            lambda *refs: update_kernel(n_space, *refs),
            grid=(blocks,),
            out_shape=(
                jax.ShapeDtypeStruct((ROWS, CELLS), bf16),
                jax.ShapeDtypeStruct((K, 16), f32),
            ),
            in_specs=[smem()]
            + [vmem()] * 12
            + [
                pl.BlockSpec((UPDATE_ROWS, CELLS), lambda i: (i, 0)),
                pl.BlockSpec((UPDATE_ROWS, 128), lambda i: (i % per_speed, 0)),
                pl.BlockSpec((8, UPDATE_ROWS), lambda i: (0, i)),
            ],
            out_specs=(
                pl.BlockSpec((UPDATE_ROWS, CELLS), lambda i: (i, 0)),
                pl.BlockSpec((K, 16), lambda i: (0, 0)),
            ),
            scratch_shapes=[
                pltpu.VMEM((2, CELLS, CELLS), bf16),
                pltpu.VMEM((2, CELLS, CELLS), bf16),
                pltpu.VMEM((2, 128, CELLS), bf16),
                pltpu.VMEM((2, 16, CELLS), bf16),
            ],
            name="update",
        )(
            place,
            partial,
            fields,
            relax,
            kind,
            left,
            right,
            twice,
            cpl_wide,
            spread_diff,
            own6,
            speed,
            shakhov16,
            velocity_dist,
            phi_k,
            halo,
        )

    return per_device


def solution(mesh):
    placed = (P("vel", "space"), P(None, ("space", "vel")), P("space"), P("space"), P(), P())
    return jax.shard_map(
        make_per_device(mesh.shape["space"]),
        mesh=mesh,
        in_specs=placed,
        out_specs=(P("vel", "space"), P(None, ("space", "vel"))),
        check_vma=False,
    )
```

```python
import math

import jax
import jax.numpy as jnp
import numpy as np
from jax import lax
from jax.experimental import pallas as pl
from jax.experimental.pallas import tpu as pltpu
from jax.sharding import PartitionSpec as P

NV1 = 32
K = 13
time_step = 0.125
spacing = 8.0 / NV1
CELLS = 256
WIDE = 384
PEERS = 16
ROWS = 2048
BLOCK = 1024
bf16 = jnp.bfloat16
f32 = jnp.float32


def parts_of(x, number):
    rest = np.asarray(x, np.float64)
    out = []
    for _ in range(number):
        piece = rest.astype(np.float32).astype(bf16)
        out.append(piece)
        rest = rest - piece.astype(np.float64)
    return out


def grid_constants():
    v = (np.arange(NV1) + 0.5) * spacing - 4.0
    w = np.exp(-0.5 * v * v) * spacing / math.sqrt(2.0 * math.pi)
    vy, vz = np.repeat(v, NV1), np.tile(v, NV1)
    wyz = np.repeat(w, NV1) * np.tile(w, NV1)
    one = np.ones_like(vy)
    yz = vy * vy + vz * vz
    phi = np.stack([one, vy, vz, vy * vz, vy * vy, vz * vz, vy * yz, vz * yz])
    cmat = np.zeros((NV1, K, 8))
    for i, x in enumerate(v):
        c = cmat[i]
        c[0, 0] = 1.0
        c[1, 0] = x
        c[2, 1] = 1.0
        c[3, 2] = 1.0
        c[4, 0] = (x * x - 3.0) / math.sqrt(6.0)
        c[4, 4] = c[4, 5] = 1.0 / math.sqrt(6.0)
        c[5, 1] = x
        c[6, 2] = x
        c[7, 3] = 1.0
        c[8, 0] = 0.5 * x * x
        c[8, 4] = -0.5
        c[9, 0] = x * x / math.sqrt(12.0)
        c[9, 4] = 1.0 / math.sqrt(12.0)
        c[9, 5] = -2.0 / math.sqrt(12.0)
        c[10, 0] = x * (x * x - 5.0) / math.sqrt(10.0)
        c[10, 4] = c[10, 5] = x / math.sqrt(10.0)
        c[11, 1] = (x * x - 5.0) / math.sqrt(10.0)
        c[11, 6] = 1.0 / math.sqrt(10.0)
        c[12, 2] = (x * x - 5.0) / math.sqrt(10.0)
        c[12, 7] = 1.0 / math.sqrt(10.0)
    a = time_step * np.abs(v)
    plus = v > 0.0
    proj = phi * wyz
    groups = [np.ones(NV1)]
    for power in (1, 2, 3):
        groups += [a**power * plus, a**power * ~plus]
    big = np.zeros((7 * 16, 8 * NV1))
    for g, factor in enumerate(groups):
        for i in range(NV1):
            big[16 * g : 16 * g + K, 8 * i : 8 * i + 8] = factor[i] * w[i] * cmat[i]
    gram2 = proj @ phi.T
    shakhov = np.array([1.0] * 5 + [0.0] * 5 + [1.0 / 3.0] * 3)

    def between(factor):
        out = np.zeros((16, 16))
        for i in range(NV1):
            out[:K, :K] += factor[i] * w[i] * cmat[i] @ gram2 @ cmat[i].T
        return out

    c16 = np.zeros(16)
    c16[:K] = shakhov
    g, gp, gm, g2p, g2m = (between(groups[k]) for k in (0, 1, 2, 3, 4))
    mats = [g, gp, gm, g * c16, gp * c16, gm * c16, g2p, g2m, g2p * c16, g2m * c16]
    block = np.zeros((BLOCK + 336, 256), bf16)
    block[16:176, 128:224] = six_terms(np.concatenate(mats, axis=0))
    block[BLOCK:] = np.concatenate(parts_of(big, 3), axis=0)
    p3 = np.concatenate(parts_of(proj, 3) + [np.zeros((8, BLOCK), bf16)], axis=0)
    ph, pm = parts_of(phi.T, 2)
    block[0:BLOCK, 0:24] = np.concatenate([ph, ph, pm], axis=1)
    own = np.zeros((PEERS, 16, 16))
    for j in range(PEERS):
        for u in range(2):
            own[j, 8 * u : 8 * u + 8, :K] = cmat[2 * j + u].T
    own = np.concatenate([six_terms(own), np.zeros((PEERS, 16, 32), bf16)], axis=2)
    return block, p3, own


def six_terms(x):
    h, m, low = parts_of(x, 3)
    return np.concatenate([h, h, h, m, m, low], axis=-1)


BASES = (1, 3, 9)


def pair_table():
    entries = []
    for stage, size in enumerate(BASES):
        for quantity in range(4):
            for i in range(size):
                for j in range(i, size):
                    entries.append((stage, quantity, i, j))
    return entries


PAIRS = pair_table()


def pair_arrays():
    kind = np.full((8, 128), -1, np.int32)
    left = np.zeros((8, 128), np.int32)
    right = np.zeros((8, 128), np.int32)
    twice = np.zeros((8, 128), np.int32)
    for n, (stage, quantity, i, j) in enumerate(PAIRS):
        at = (n // 128, n % 128)
        kind[at] = 4 * stage + quantity
        left[at], right[at] = i, j
        twice[at] = 1 if i == j else 2
    return np.concatenate([kind, left, right, twice], axis=0).astype(np.float32)


def lanes_of(shape):
    return lax.broadcasted_iota(jnp.int32, shape, len(shape) - 1)


def rows_of(shape):
    return lax.broadcasted_iota(jnp.int32, shape, 0)


def stack6(f):
    h = f.astype(bf16)
    rest = f - h.astype(f32)
    m = rest.astype(bf16)
    low = (rest - m.astype(f32)).astype(bf16)
    return jnp.concatenate([h, m, low, h, m, h], axis=0)


def relax_of(rate, flags):
    return (time_step * rate) * (1.0 + flags.astype(f32))


def shift_up(x):
    return pltpu.roll(x, 1, 1)


def shift_down(x):
    return pltpu.roll(x, x.shape[1] - 1, 1)


def diff_up(x):
    return x - shift_up(x)


def diff_down(x):
    return x - shift_down(x)


def copies_of(pairs, sems):
    made = [pltpu.make_async_copy(x, y, sems.at[n]) for n, (x, y) in enumerate(pairs)]
    for copy in made:
        copy.start()
    return made


def sums_kernel(
    dist_in,
    p3_in,
    start_in,
    rate_in,
    flags_in,
    sums,
    up,
    down,
    edge,
    owned,
    dist,
    p3,
    start,
    rate,
    flags,
    padded,
    sems,
):
    positive = lax.axis_index("vel") >= PEERS // 2
    halves = [pl.ds(u * BLOCK, BLOCK) for u in range(2)]
    pairs = [(p3_in, p3), (start_in, start), (rate_in, rate), (flags_in, flags)]
    pairs += [(dist_in.at[half, :], dist.at[half, :]) for half in halves]
    waits = copies_of(pairs, sems)
    for copy in waits[:4]:
        copy.wait()
    parts = []
    for u in range(2):
        waits[4 + u].wait()
        y = jnp.dot(p3[...], dist[halves[u], :], preferred_element_type=f32)
        parts.append(y[0:8] + y[8:16] + y[16:24])
    w = jnp.concatenate(parts, axis=0)
    sums[...] = w
    lane = lanes_of((16, 128))
    row = rows_of((16, 128))
    padded[...] = jnp.zeros((16, 128), f32)
    padded[0:K, 0:16] = start[...]
    mine = pltpu.roll(padded[...], 16, 1)
    owned[...] = mine
    relax = relax_of(rate[...], flags[...])
    near_edge = jnp.where(positive, relax[:, 128:256], relax[:, 0:128])
    edge[:, ROWS : ROWS + 128] = jnp.broadcast_to(near_edge, (8, 128))
    r_first = jnp.broadcast_to(pltpu.roll(relax[:, 0:128], 48, 1), (16, 128))
    r_last = jnp.broadcast_to(pltpu.roll(relax[:, 128:256], 48, 1), (16, 128))
    zero = jnp.zeros((16, 128), f32)
    up[...] = (
        jnp.where(lane >= 120, w[:, 128:256], zero)
        + pltpu.roll(mine, 16, 1)
        + jnp.where((row == K) & (lane >= 32) & (lane < 48), r_last, zero)
    )
    down[...] = (
        jnp.where(lane < 8, w[:, 0:128], zero)
        + pltpu.roll(mine, 32, 1)
        + jnp.where((row == K) & (lane >= 48) & (lane < 64), r_first, zero)
    )
    e_lane = lanes_of((16, CELLS))
    e_row = rows_of((16, CELLS))
    first = jnp.where(positive, CELLS - 8, 0)
    pick = jnp.where((e_lane == e_row + first) & (e_row < 8), 1.0, 0.0).astype(bf16)
    for u in range(2):
        e = lax.dot_general(
            pick,
            dist[pl.ds(u * BLOCK, BLOCK), :],
            (((1,), (1,)), ((), ())),
            preferred_element_type=f32,
        )
        edge[:, pl.ds(u * BLOCK, BLOCK)] = e[0:8]


def pack_kernel(sums, up, down, owned, out, whole, sems):
    whole[:, 0:CELLS] = sums[...]
    whole[:, CELLS:WIDE] = up[...] + down[...] + owned[...]
    for copy in copies_of([(whole, out.at[j]) for j in range(PEERS)], sems):
        copy.wait()


N_FIELDS = 28


def fields_kernel(n_space, got, known, block, fields, partial, table, line, sems):
    slab = lax.axis_index("space")
    lane = lanes_of((1, WIDE))
    right = (lane >= CELLS) & (lane < CELLS + 8)
    left = lane >= WIDE - 8
    own = lane < CELLS
    inside = own | (right & (slab < n_space - 1)) | (left & (slab > 0))
    mask = jnp.where(inside, 1.0, 0.0)

    w = got[...].reshape(PEERS * 16, WIDE)
    w = jnp.where(own | right | left, w, 0.0)
    wh = w.astype(bf16)
    w_rest = w - wh.astype(f32)
    wm = w_rest.astype(bf16)
    wl = (w_rest - wm.astype(f32)).astype(bf16)
    y = jnp.dot(block[BLOCK : BLOCK + 336, :], wh, preferred_element_type=f32)
    z = jnp.dot(block[BLOCK : BLOCK + 224, :], wm, preferred_element_type=f32)
    t = jnp.dot(block[BLOCK : BLOCK + 112, :], wl, preferred_element_type=f32)
    mu = ((y[224:336] + z[112:224]) + (y[112:224] + z[0:112])) + t + y[0:112]
    mu = [mu[16 * g : 16 * g + 16] for g in range(7)]

    lane1 = lanes_of((16, 128))
    row1 = rows_of((16, 128))
    zero = jnp.zeros((16, 128), f32)
    halves = [zero, zero]
    for j in range(PEERS):
        tile = got[j, :, 2 * 128 : 3 * 128]
        amount = (16 * j - 16) % 128
        moved = pltpu.roll(tile, amount, 1) if amount else tile
        begin = 16 * (j % 8)
        halves[j // 8] = jnp.where((lane1 >= begin) & (lane1 < begin + 16), moved, halves[j // 8])
    from_first = pltpu.roll(got[0, :, 2 * 128 : 3 * 128], 80, 1)
    from_last = pltpu.roll(got[PEERS - 1, :, 2 * 128 : 3 * 128], 80, 1)
    ends = jnp.where(lane1 < 8, from_first, jnp.where(lane1 >= 120, from_last, zero))
    start = jnp.concatenate([halves[0], halves[1], ends], axis=1)
    start = jnp.where(rows_of((16, WIDE)) < K, start, 0.0)
    relax_ends = jnp.where((lane1 < 8) | (lane1 >= 120), from_first, zero)[K : K + 1]
    relax1 = jnp.concatenate([known[0:1, 0:CELLS], relax_ends], axis=1)
    r = jnp.broadcast_to(relax1, (16, WIDE))
    keep = 1.0 - r
    mask = jnp.broadcast_to(mask, (16, WIDE))
    diffusion = jnp.concatenate([known[8:24, 128:256]] * 3, axis=1)

    def advance(base, ups, downs):
        new = keep * base - diff_up(ups[0]) - diff_down(downs[0])
        new_ups = [keep * ups[n] - diff_up(ups[n + 1]) for n in range(len(ups) - 1)]
        new_downs = [keep * downs[n] - diff_down(downs[n + 1]) for n in range(len(downs) - 1)]
        return new, new_ups, new_downs

    ups, downs = [mu[1], mu[3], mu[5]], [mu[2], mu[4], mu[6]]
    s1, ups, downs = advance(mu[0], ups, downs)
    s2, ups, downs = advance(s1, ups, downs)
    s3, _, _ = advance(s2, ups, downs)

    def times(first, last, inputs):
        stacked = stack6(jnp.concatenate(inputs, axis=1) if len(inputs) > 1 else inputs[0])
        y = jnp.dot(block[16 * first : 16 * last, 128:224], stacked, preferred_element_type=f32)
        out = []
        for n in range(len(inputs)):
            cut = y[:, n * WIDE : (n + 1) * WIDE]
            out.append([cut[16 * g : 16 * g + 16] for g in range(last - first)])
        return out

    def applied(f, coupled):
        return mask * (coupled + diffusion * (2.0 * f - shift_up(f) - shift_down(f)))

    def streamed(g, gp, gm):
        return keep * g - diff_up(gp) - diff_down(gm)

    def streamed_twice(k1, gp, gm, g2p, g2m):
        return keep * k1 - diff_up(keep * gp - diff_up(g2p)) - diff_down(keep * gm - diff_down(g2m))

    ((gc, gcp, gcm, _, _, g2cp, g2cm),) = times(4, 11, [start])
    relaxed = r * gc
    shares = mask * (s1 + relaxed)
    res = mask * (shares - start)
    k1_start = streamed(relaxed, r * gcp, r * gcm)
    k2_start = streamed_twice(k1_start, r * gcp, r * gcm, r * g2cp, r * g2cm)

    def parts(f, ys):
        out = [applied(f, ys[0])]
        k1 = streamed(ys[1], ys[2], ys[3])
        rg = r * ys[4]
        held = rg - f
        out += [mask * (k1 + held), held]
        if len(ys) > 5:
            out.append(streamed_twice(k1, ys[2], ys[3], ys[7], ys[8]))
            out.append(streamed(rg, r * ys[5], r * ys[6]) + held)
        return out

    y_shares, y_res = times(0, 9, [shares, res])
    rg = r * y_shares[4]
    held_shares = rg - shares
    n_shares = streamed(rg, r * y_shares[5], r * y_shares[6]) + held_shares
    p0 = mask * (s2 + k1_start + held_shares)
    e, p1, _, k2_res, n_res = parts(res, y_res)

    y_e, y_p0, y_p1 = times(0, 9, [e, p0, p1])
    ee, p2, _, k2_e, n_e = parts(e, y_e)
    ap0, q3, held_p0 = parts(p0, y_p0[:5])
    ap1, q4, held_p1 = parts(p1, y_p1[:5])
    q0 = mask * (s3 + k2_start + n_shares + held_p0)
    q1 = mask * (k2_res + n_res + held_p1)

    y_p2, y_ap0, y_ap1, y_q0, y_q1, y_q3, y_q4 = times(0, 5, [p2, ap0, ap1, q0, q1, q3, q4])
    ap2, q5, held_p2 = parts(p2, y_p2)
    aap0, q6, _ = parts(ap0, y_ap0)
    aap1, q7, _ = parts(ap1, y_ap1)
    q2 = mask * (k2_e + n_e + held_p2)
    aq0, aq1, aq3, aq4 = (applied(f, y[0]) for f, y in ((q0, y_q0), (q1, y_q1), (q3, y_q3), (q4, y_q4)))

    (y_ap2,) = times(0, 5, [ap2])
    aap2, q8, _ = parts(ap2, y_ap2)
    first = [q2, q5, q6, q7, aq0, aq1, aq3, aq4]
    aq2, aq5, aq6, aq7, aaq0, aaq1, aaq3, aaq4 = (applied(f, y[0]) for f, y in zip(first, times(0, 1, first)))
    second = [q8, aq2, aq5, aq6, aq7]
    aq8, aaq2, aaq5, aaq6, aaq7 = (applied(f, y[0]) for f, y in zip(second, times(0, 1, second)))
    ((y_aq8,),) = times(0, 1, [aq8])
    aaq8 = applied(aq8, y_aq8)

    q = [q0, q1, q2, q3, q4, q5, q6, q7, q8]
    aq = [aq0, aq1, aq2, aq3, aq4, aq5, aq6, aq7, aq8]
    aaq = [aaq0, aaq1, aaq2, aaq3, aaq4, aaq5, aaq6, aaq7, aaq8]
    for n, f in enumerate([start, shares, res, e, p0, p1, p2, ap0, ap1, ap2] + q + aq):
        fields[n] = f

    plain = [[res], [p0, p1, p2], q]
    once = [[e], [ap0, ap1, ap2], aq]
    again = [[ee], [aap0, aap1, aap2], aaq]
    table[...] = jnp.zeros((256, 128), f32)
    for n, (stage, quantity, i, j) in enumerate(PAIRS):
        a, b = ((plain, plain), (plain, once), (once, once), (once, again))[quantity]
        product = a[stage][i][:, 0:CELLS] * b[stage][j][:, 0:CELLS]
        folded = (product[0:8, 0:128] + product[0:8, 128:256]) + (product[8:16, 0:128] + product[8:16, 128:256])
        table[n : n + 1, :] = jnp.sum(folded, axis=0, keepdims=True)
    ones = jnp.ones((8, 128), f32)
    tops = [
        lax.dot_general(
            ones,
            table[128 * n : 128 * n + 128, :],
            (((1,), (1,)), ((), ())),
            precision=lax.Precision.HIGHEST,
            preferred_element_type=f32,
        )
        for n in range(2)
    ]
    row8 = rows_of((8, 128))
    line[...] = jnp.where(row8 == 0, tops[0], jnp.where(row8 == 1, tops[1], 0.0))
    for copy in copies_of([(line, partial.at[j]) for j in range(n_space)], sems):
        copy.wait()


def speeds_of(shape):
    number = 2 * lax.axis_index("vel") + jnp.where(rows_of(shape) >= 8, 1, 0)
    return time_step * jnp.abs((number.astype(f32) + 0.5) * spacing - 4.0)


def stream_kernel(
    halo,
    dist_in,
    block_in,
    pairs_in,
    own_in,
    coupling_in,
    diff_in,
    rate_in,
    flags_in,
    out,
    table,
    block,
    dist,
    own6,
    coupling_raw,
    diff_raw,
    rate,
    flags,
    sems,
):
    vel = lax.axis_index("vel")
    positive = vel >= PEERS // 2
    moves = [(rate_in, rate), (flags_in, flags), (dist_in, dist), (coupling_in, coupling_raw), (diff_in, diff_raw)]
    moves += [(own_in.at[vel], own6), (pairs_in, table.at[24:56, 0:128]), (block_in, block)]
    waits = copies_of(moves, sems)
    waits[0].wait()
    waits[1].wait()
    towards = jnp.where(positive, 1, -1)
    lane = lanes_of((1, 128))
    low = jnp.where(positive, 120, 0)
    ends = jnp.where((lane >= low) & (lane < low + 8), halo[0:1, ROWS : ROWS + 128], 0.0)
    r = jnp.concatenate([relax_of(rate[...], flags[...]), ends], axis=1)
    table[0:8, :] = jnp.broadcast_to(r, (8, WIDE))
    a = speeds_of((16, WIDE))
    stay = 1.0 - jnp.broadcast_to(r, (16, WIDE)) - a

    def before(x):
        return jnp.where(positive, shift_up(x), shift_down(x))

    once = before(stay)
    two = before(once)
    t0 = stay * stay * stay
    t1 = a * (stay * (stay + once) + once * once)
    t2 = a * a * (stay + once + two)
    t3 = a * a * a
    waits[2].wait()
    back = (lanes_of((CELLS, CELLS)) - rows_of((CELLS, CELLS))) * towards
    at8 = rows_of((8, CELLS))
    at8 = jnp.where(positive, at8 - 8, at8 + CELLS)
    back8 = (lanes_of((8, CELLS)) - at8) * towards
    for u in range(2):
        ts = [x[8 * u : 8 * u + 1, 0:CELLS] for x in (t0, t1, t2, t3)]

        def band(distance):
            value = jnp.zeros(distance.shape, f32)
            for n, x in enumerate(ts):
                value = jnp.where(distance == n, jnp.broadcast_to(x, distance.shape), value)
            return value

        b = band(back)
        bh = b.astype(bf16)
        bl = (b - bh.astype(f32)).astype(bf16)
        b8 = band(back8)
        b8h = b8.astype(bf16).astype(f32)
        b8 = jnp.concatenate([b8h, b8 - b8h], axis=0).astype(bf16)
        rows = pl.ds(u * BLOCK, BLOCK)
        x = dist[rows, :]
        value = jnp.dot(x, bh, preferred_element_type=f32)
        value += jnp.dot(x, bl, preferred_element_type=f32)
        h = halo[:, rows]
        h = jnp.concatenate([h, h], axis=0).astype(bf16)
        value += lax.dot_general(h, b8, (((0,), (0,)), ((), ())), preferred_element_type=f32)
        out[rows, :] = value

    for copy in waits[3:]:
        copy.wait()
    table[8:24, 0:128] = jnp.zeros((16, 128), f32)
    table[8 : 8 + K, 0:K] = coupling_raw[...]
    c = table[8:24, 0:128]
    ch = c.astype(bf16).astype(f32)
    cm = (c - ch).astype(bf16).astype(f32)
    pieces = [ch, ch, ch, cm, cm, c - ch - cm]
    six = pieces[0]
    for n in range(1, 6):
        six = six + pltpu.roll(pieces[n], 16 * n, 1)
    block[0:16, 128:256] = six.astype(bf16)
    block[176:192, 128:256] = own6[...]
    shape = (16, K)
    chosen = jnp.where(lanes_of(shape) == rows_of(shape), jnp.broadcast_to(diff_raw[...], shape), 0.0)
    table[8:24, 128:256] = jnp.broadcast_to(jnp.sum(chosen, axis=1, keepdims=True), (16, 128))


UPDATE_ROWS = 512


def update_kernel(
    n_space,
    partial,
    fields,
    known,
    block,
    base,
    out,
    macro,
    done,
    macro_part,
    sems,
):
    place = lax.axis_index("vel")
    positive = place >= PEERS // 2
    total = partial[0]
    for j in range(1, n_space):
        total = total + partial[j]
    total = total * known[48:56, 0:128]
    cpl = known[8:24, 0:128]
    lane16 = lanes_of((16, 128))
    row16 = rows_of((16, 128))
    size = jnp.sum(jnp.abs(cpl), axis=1, keepdims=True)
    middle = jnp.sum(jnp.where(lane16 == row16, cpl, 0.0), axis=1, keepdims=True)
    real = row16[:, 0:1] < K
    most = jnp.max(jnp.where(real, size + 4.0 * known[8:24, 128:129], 0.0), axis=0, keepdims=True)
    least = jnp.min(jnp.where(real, 2.0 * middle - size, 1e30), axis=0, keepdims=True)
    low_step, high_step = 1.0 / most, 1.0 / least

    def summed(weighted, which):
        picked = jnp.where(known[24:32, 0:128] == which, weighted, 0.0)
        return jnp.sum(jnp.sum(picked, axis=0, keepdims=True), axis=1, keepdims=True)

    def clipped(x):
        return jnp.minimum(jnp.maximum(x, low_step), high_step)

    def weights_of(stage, weighted):
        rr, ra, aa, aaa = (summed(weighted, 4 * stage + n) for n in range(4))
        s1 = clipped(rr / ra)
        rr2 = rr - 2.0 * s1 * ra + s1 * s1 * aa
        ra2 = ra - 2.0 * s1 * aa + s1 * s1 * aaa
        s2 = clipped(rr2 / ra2)
        return s1 + s2, -s1 * s2

    li, ri = (known[n : n + 8, 0:128].astype(jnp.int32) for n in (32, 40))

    def choose(index, zero, one, two):
        return jnp.where(index == 0, zero, jnp.where(index == 1, one, two))

    a1, b1 = weights_of(0, total)
    a2, b2 = weights_of(1, total * choose(li, 1.0, a1, b1) * choose(ri, 1.0, a1, b1))

    def both(index):
        outer = (index >= 3).astype(jnp.int32) + (index >= 6).astype(jnp.int32)
        return choose(outer, 1.0, a2, b2) * choose(index - 3 * outer, 1.0, a1, b1)

    a3, b3 = weights_of(2, total * both(li) * both(ri))

    start, shares, res, e = (fields[n] for n in range(4))
    corr1 = a1 * res + b1 * e
    cur1 = shares + corr1
    res2 = fields[4] + a1 * fields[5] + b1 * fields[6]
    e2 = fields[7] + a1 * fields[8] + b1 * fields[9]
    corr2 = a2 * res2 + b2 * e2
    cur2 = res2 + cur1 + corr2

    def third(at):
        rows = [fields[at + 3 * n] + a1 * fields[at + 3 * n + 1] + b1 * fields[at + 3 * n + 2] for n in range(3)]
        return rows[0] + a2 * rows[1] + b2 * rows[2]

    res3, e3 = third(10), third(19)
    corr3 = a3 * res3 + b3 * e3
    cur3 = res3 + cur2 + corr3
    mine = pltpu.roll(cur3[:, 0:CELLS], lax.rem(CELLS - 16 * place, CELLS), 1)
    macro_part[...] = mine[0:K, 0:16]
    macro_copy = pltpu.make_async_copy(macro_part, macro, sems.at[ROWS // UPDATE_ROWS])
    macro_copy.start()

    r = jnp.broadcast_to(known[0:1, :], (16, WIDE))
    row = rows_of((16, WIDE))
    scaled = r * jnp.where(row < 5, 1.0, jnp.where(row < 10, 0.0, 1.0 / 3.0))
    f1 = scaled * start + corr1
    f2 = scaled * cur1 + corr2
    f3 = scaled * cur2 + corr3
    y = jnp.dot(block[176:192, 128:224], stack6(jnp.concatenate([f1, f2, f3], axis=1)), preferred_element_type=f32)
    y1, y2, y3 = (y[:, n * WIDE : (n + 1) * WIDE] for n in range(3))
    a = speeds_of((16, WIDE))

    def before(x):
        return jnp.where(positive, shift_up(x), shift_down(x))

    stay = 1.0 - r - a

    def moved(x):
        return stay * x + a * before(x)

    h = (moved(moved(y1) + y2) + y3)[:, 0:CELLS]
    hh = h.astype(bf16).astype(f32)
    hm = (h - hh).astype(bf16).astype(f32)

    sends = [macro_copy]
    for u in range(2):
        hu, mu = hh[8 * u : 8 * u + 8], hm[8 * u : 8 * u + 8]
        mixed = jnp.concatenate([hu, mu, hu, jnp.zeros((104, CELLS), f32)], axis=0).astype(bf16)
        for n in range(BLOCK // UPDATE_ROWS):
            part = u * (BLOCK // UPDATE_ROWS) + n
            rows = pl.ds(part * UPDATE_ROWS, UPDATE_ROWS)
            value = jnp.dot(block[pl.ds(n * UPDATE_ROWS, UPDATE_ROWS), 0:128], mixed, preferred_element_type=f32)
            done[rows, :] = (base[rows, :] + value).astype(bf16)
            copy = pltpu.make_async_copy(done.at[rows, :], out.at[rows, :], sems.at[part])
            copy.start()
            sends.append(copy)
    for copy in sends:
        copy.wait()


def vmem():
    return pl.BlockSpec(memory_space=pltpu.VMEM)


def hbm():
    return pl.BlockSpec(memory_space=pltpu.HBM)


def shaped(shape, dtype=f32):
    return pltpu.VMEM(shape, dtype)


def stored(shape, dtype=f32):
    return pltpu.HBM(shape, dtype)


def placed_at(space, arrays):
    return [pltpu.with_memory_space_constraint(x, space) for x in arrays]


def near(*arrays):
    return placed_at(pltpu.VMEM, arrays)


def far(*arrays):
    return placed_at(pltpu.HBM, arrays)


def limit(mib):
    return pltpu.CompilerParams(vmem_limit_bytes=mib * 2**20)


def make_per_device(n_space):
    block, p3, own6 = grid_constants()
    pairs = pair_arrays()

    def per_device(velocity_dist, macro_state, collision_rate, wall_flags, diffusivity, coupling):
        rate = collision_rate.reshape(1, CELLS)
        flags = wall_flags.reshape(1, CELLS)
        sums, up, down, edge, owned = pl.pallas_call(
            sums_kernel,
            out_shape=(
                shaped((16, CELLS)),
                shaped((16, 128)),
                shaped((16, 128)),
                shaped((8, ROWS + 128)),
                shaped((16, 128)),
            ),
            in_specs=[hbm()] * 5,
            out_specs=(vmem(),) * 5,
            scratch_shapes=[
                pltpu.VMEM((ROWS, CELLS), bf16),
                pltpu.VMEM((32, BLOCK), bf16),
                pltpu.VMEM((K, 16), f32),
                pltpu.VMEM((1, CELLS), f32),
                pltpu.VMEM((1, CELLS), jnp.int32),
                pltpu.VMEM((16, 128), f32),
                pltpu.SemaphoreType.DMA((6,)),
            ],
            compiler_params=limit(8),
            name="sums",
        )(*far(velocity_dist, jnp.asarray(p3), macro_state, rate, flags))
        rising = [(i, i + 1) for i in range(n_space - 1)]
        falling = [(j, i) for i, j in rising]
        from_left = lax.ppermute(up, "space", rising)
        from_right = lax.ppermute(down, "space", falling)
        packed = pl.pallas_call(
            pack_kernel,
            out_shape=stored((PEERS, 16, WIDE)),
            in_specs=[vmem()] * 4,
            out_specs=hbm(),
            scratch_shapes=[pltpu.VMEM((16, WIDE), f32), pltpu.SemaphoreType.DMA((PEERS,))],
            compiler_params=limit(4),
            name="pack",
        )(*near(sums, from_left, from_right, owned))
        got = lax.all_to_all(packed, "vel", split_axis=0, concat_axis=0, tiled=True)
        half = PEERS // 2
        upwind = [(i * PEERS + n, j * PEERS + n) for i, j in rising for n in range(half, PEERS)]
        upwind += [(j * PEERS + n, i * PEERS + n) for i, j in rising for n in range(half)]
        halo = lax.ppermute(edge, ("space", "vel"), upwind)
        base, known, constants = pl.pallas_call(
            stream_kernel,
            out_shape=(shaped((ROWS, CELLS)), shaped((56, WIDE)), shaped(block.shape, bf16)),
            in_specs=[vmem()] + [hbm()] * 8,
            out_specs=(vmem(),) * 3,
            scratch_shapes=[
                pltpu.VMEM((ROWS, CELLS), bf16),
                pltpu.VMEM((16, 128), bf16),
                pltpu.VMEM((K, K), f32),
                pltpu.VMEM((1, K), f32),
                pltpu.VMEM((1, CELLS), f32),
                pltpu.VMEM((1, CELLS), jnp.int32),
                pltpu.SemaphoreType.DMA((8,)),
            ],
            compiler_params=limit(16),
            name="stream",
        )(
            *near(halo),
            *far(velocity_dist, *(jnp.asarray(x) for x in (block, pairs, own6)), coupling, diffusivity.reshape(1, K), rate, flags),
        )
        got, base = lax.optimization_barrier((got, base))
        fields, partial = pl.pallas_call(
            lambda *refs: fields_kernel(n_space, *refs),
            out_shape=(shaped((N_FIELDS, 16, WIDE)), stored((n_space, 8, 128))),
            in_specs=[vmem()] * 3,
            out_specs=(vmem(), hbm()),
            scratch_shapes=[
                pltpu.VMEM((256, 128), f32),
                pltpu.VMEM((8, 128), f32),
                pltpu.SemaphoreType.DMA((n_space,)),
            ],
            compiler_params=limit(12),
            name="fields",
        )(*near(got, known, constants))
        partial = lax.all_to_all(partial, "space", split_axis=0, concat_axis=0, tiled=True)
        return pl.pallas_call(
            lambda *refs: update_kernel(n_space, *refs),
            out_shape=(stored((ROWS, CELLS), bf16), stored((K, 16))),
            in_specs=[vmem()] * 5,
            out_specs=(hbm(), hbm()),
            scratch_shapes=[
                pltpu.VMEM((ROWS, CELLS), bf16),
                pltpu.VMEM((K, 16), f32),
                pltpu.SemaphoreType.DMA((ROWS // UPDATE_ROWS + 1,)),
            ],
            compiler_params=limit(12),
            name="update",
        )(*near(partial, fields, known, constants, base))

    return per_device


def solution(mesh):
    placed = (P("vel", "space"), P(None, ("space", "vel")), P("space"), P("space"), P(), P())
    return jax.shard_map(
        make_per_device(mesh.shape["space"]),
        mesh=mesh,
        in_specs=placed,
        out_specs=(P("vel", "space"), P(None, ("space", "vel"))),
        check_vma=False,
    )
```

```python
import math

import jax
import jax.numpy as jnp
import numpy as np
from jax import lax
from jax.experimental import pallas as pl
from jax.experimental.pallas import tpu as pltpu
from jax.sharding import PartitionSpec as P

NV1 = 32
K = 13
time_step = 0.125
spacing = 8.0 / NV1
CELLS = 256
WIDE = 384
PEERS = 16
ROWS = 2048
BLOCK = 1024
bf16 = jnp.bfloat16
f32 = jnp.float32


def parts_of(x, number):
    rest = np.asarray(x, np.float64)
    out = []
    for _ in range(number):
        piece = rest.astype(np.float32).astype(bf16)
        out.append(piece)
        rest = rest - piece.astype(np.float64)
    return out


def grid_constants():
    v = (np.arange(NV1) + 0.5) * spacing - 4.0
    w = np.exp(-0.5 * v * v) * spacing / math.sqrt(2.0 * math.pi)
    vy, vz = np.repeat(v, NV1), np.tile(v, NV1)
    wyz = np.repeat(w, NV1) * np.tile(w, NV1)
    one = np.ones_like(vy)
    yz = vy * vy + vz * vz
    phi = np.stack([one, vy, vz, vy * vz, vy * vy, vz * vz, vy * yz, vz * yz])
    cmat = np.zeros((NV1, K, 8))
    for i, x in enumerate(v):
        c = cmat[i]
        c[0, 0] = 1.0
        c[1, 0] = x
        c[2, 1] = 1.0
        c[3, 2] = 1.0
        c[4, 0] = (x * x - 3.0) / math.sqrt(6.0)
        c[4, 4] = c[4, 5] = 1.0 / math.sqrt(6.0)
        c[5, 1] = x
        c[6, 2] = x
        c[7, 3] = 1.0
        c[8, 0] = 0.5 * x * x
        c[8, 4] = -0.5
        c[9, 0] = x * x / math.sqrt(12.0)
        c[9, 4] = 1.0 / math.sqrt(12.0)
        c[9, 5] = -2.0 / math.sqrt(12.0)
        c[10, 0] = x * (x * x - 5.0) / math.sqrt(10.0)
        c[10, 4] = c[10, 5] = x / math.sqrt(10.0)
        c[11, 1] = (x * x - 5.0) / math.sqrt(10.0)
        c[11, 6] = 1.0 / math.sqrt(10.0)
        c[12, 2] = (x * x - 5.0) / math.sqrt(10.0)
        c[12, 7] = 1.0 / math.sqrt(10.0)
    a = time_step * np.abs(v)
    plus = v > 0.0
    proj = phi * wyz
    groups = [np.ones(NV1)]
    for power in (1, 2, 3):
        groups += [a**power * plus, a**power * ~plus]
    big = np.zeros((7 * 16, 8 * NV1))
    for g, factor in enumerate(groups):
        for i in range(NV1):
            big[16 * g : 16 * g + K, 8 * i : 8 * i + 8] = factor[i] * w[i] * cmat[i]
    gram2 = proj @ phi.T
    shakhov = np.array([1.0] * 5 + [0.0] * 5 + [1.0 / 3.0] * 3)

    def between(factor):
        out = np.zeros((16, 16))
        for i in range(NV1):
            out[:K, :K] += factor[i] * w[i] * cmat[i] @ gram2 @ cmat[i].T
        return out

    c16 = np.zeros(16)
    c16[:K] = shakhov
    g, gp, gm, g2p, g2m = (between(groups[k]) for k in (0, 1, 2, 3, 4))
    mats = [g, gp, gm, g * c16, gp * c16, gm * c16, g2p, g2m, g2p * c16, g2m * c16]
    block = np.zeros((BLOCK + 336, 256), bf16)
    block[16:176, 128:224] = six_terms(np.concatenate(mats, axis=0))
    block[BLOCK:] = np.concatenate(parts_of(big, 3), axis=0)
    p3 = np.concatenate(parts_of(proj, 3) + [np.zeros((8, BLOCK), bf16)], axis=0)
    ph, pm = parts_of(phi.T, 2)
    block[0:BLOCK, 0:24] = np.concatenate([ph, ph, pm], axis=1)
    own = np.zeros((PEERS, 16, 16))
    for j in range(PEERS):
        for u in range(2):
            own[j, 8 * u : 8 * u + 8, :K] = cmat[2 * j + u].T
    own = np.concatenate([six_terms(own), np.zeros((PEERS, 16, 32), bf16)], axis=2)
    return block, p3, own


def six_terms(x):
    h, m, low = parts_of(x, 3)
    return np.concatenate([h, h, h, m, m, low], axis=-1)


BASES = (1, 3, 9)


def pair_table():
    entries = []
    for stage, size in enumerate(BASES):
        for quantity in range(4):
            for i in range(size):
                for j in range(i, size):
                    entries.append((stage, quantity, i, j))
    return entries


PAIRS = pair_table()


def pair_arrays():
    kind = np.full((8, 128), -1, np.int32)
    left = np.zeros((8, 128), np.int32)
    right = np.zeros((8, 128), np.int32)
    twice = np.zeros((8, 128), np.int32)
    for n, (stage, quantity, i, j) in enumerate(PAIRS):
        at = (n // 128, n % 128)
        kind[at] = 4 * stage + quantity
        left[at], right[at] = i, j
        twice[at] = 1 if i == j else 2
    return np.concatenate([kind, left, right, twice], axis=0).astype(np.float32)


def lanes_of(shape):
    return lax.broadcasted_iota(jnp.int32, shape, len(shape) - 1)


def rows_of(shape):
    return lax.broadcasted_iota(jnp.int32, shape, 0)


def stack6(f):
    h = f.astype(bf16)
    rest = f - h.astype(f32)
    m = rest.astype(bf16)
    low = (rest - m.astype(f32)).astype(bf16)
    return jnp.concatenate([h, m, low, h, m, h], axis=0)


def relax_of(rate, flags):
    return (time_step * rate) * (1.0 + flags.astype(f32))


def shift_up(x):
    return pltpu.roll(x, 1, 1)


def shift_down(x):
    return pltpu.roll(x, x.shape[1] - 1, 1)


def diff_up(x):
    return x - shift_up(x)


def diff_down(x):
    return x - shift_down(x)


def copies_of(pairs, sems):
    made = [pltpu.make_async_copy(x, y, sems.at[n]) for n, (x, y) in enumerate(pairs)]
    for copy in made:
        copy.start()
    return made


def sums_kernel(
    dist_in,
    p3_in,
    start_in,
    rate_in,
    flags_in,
    sums,
    ahead,
    back,
    owned,
    dist,
    p3,
    start,
    rate,
    flags,
    padded,
    sems,
):
    positive = lax.axis_index("vel") >= PEERS // 2
    halves = [pl.ds(u * BLOCK, BLOCK) for u in range(2)]
    pairs = [(p3_in, p3), (start_in, start), (rate_in, rate), (flags_in, flags)]
    pairs += [(dist_in.at[half, :], dist.at[half, :]) for half in halves]
    waits = copies_of(pairs, sems)
    for copy in waits[:4]:
        copy.wait()
    parts = []
    for u in range(2):
        waits[4 + u].wait()
        y = jnp.dot(p3[...], dist[halves[u], :], preferred_element_type=f32)
        parts.append(y[0:8] + y[8:16] + y[16:24])
    w = jnp.concatenate(parts, axis=0)
    sums[...] = w
    lane = lanes_of((16, 128))
    row = rows_of((16, 128))
    padded[...] = jnp.zeros((16, 128), f32)
    padded[0:K, 0:16] = start[...]
    mine = pltpu.roll(padded[...], 16, 1)
    owned[...] = mine
    relax = relax_of(rate[...], flags[...])
    r_first = jnp.broadcast_to(pltpu.roll(relax[:, 0:128], 48, 1), (16, 128))
    r_last = jnp.broadcast_to(pltpu.roll(relax[:, 128:256], 48, 1), (16, 128))
    zero = jnp.zeros((16, 128), f32)
    up = (
        jnp.where(lane >= 120, w[:, 128:256], zero)
        + pltpu.roll(mine, 16, 1)
        + jnp.where((row == K) & (lane >= 32) & (lane < 48), r_last, zero)
    )
    down = (
        jnp.where(lane < 8, w[:, 0:128], zero)
        + pltpu.roll(mine, 32, 1)
        + jnp.where((row == K) & (lane >= 48) & (lane < 64), r_first, zero)
    )
    ahead[0:16, :] = jnp.where(positive, up, down)
    back[...] = jnp.where(positive, down, up)
    e_lane = lanes_of((16, CELLS))
    e_row = rows_of((16, CELLS))
    cell = jnp.where(positive, CELLS - 1 - e_row, e_row)
    pick = jnp.where((e_lane == cell) & (e_row < 3), 1.0, 0.0).astype(bf16)
    for u in range(2):
        e = lax.dot_general(pick, dist[halves[u], :], (((1,), (1,)), ((), ())), preferred_element_type=f32)
        for n in range(3):
            for k in range(8):
                at = 16 + 16 * n + 8 * u + k
                ahead[at : at + 1, :] = e[n : n + 1, 128 * k : 128 * k + 128]


def pack_kernel(sums, ahead, back, owned, out, edges, whole, sems):
    whole[:, 0:CELLS] = sums[...]
    whole[:, CELLS:WIDE] = ahead[0:16, :] + back[...] + owned[...]
    for copy in copies_of([(whole, out.at[j]) for j in range(PEERS)] + [(ahead.at[16:64, :], edges)], sems):
        copy.wait()


N_FIELDS = 28


def fields_kernel(n_space, got, known, block, fields, partial, table, line, sems):
    slab = lax.axis_index("space")
    lane = lanes_of((1, WIDE))
    right = (lane >= CELLS) & (lane < CELLS + 8)
    left = lane >= WIDE - 8
    own = lane < CELLS
    inside = own | (right & (slab < n_space - 1)) | (left & (slab > 0))
    mask = jnp.where(inside, 1.0, 0.0)

    w = got[...].reshape(PEERS * 16, WIDE)
    w = jnp.where(own | right | left, w, 0.0)
    wh = w.astype(bf16)
    w_rest = w - wh.astype(f32)
    wm = w_rest.astype(bf16)
    wl = (w_rest - wm.astype(f32)).astype(bf16)
    y = jnp.dot(block[BLOCK : BLOCK + 336, :], wh, preferred_element_type=f32)
    z = jnp.dot(block[BLOCK : BLOCK + 224, :], wm, preferred_element_type=f32)
    t = jnp.dot(block[BLOCK : BLOCK + 112, :], wl, preferred_element_type=f32)
    mu = ((y[224:336] + z[112:224]) + (y[112:224] + z[0:112])) + t + y[0:112]
    mu = [mu[16 * g : 16 * g + 16] for g in range(7)]

    lane1 = lanes_of((16, 128))
    row1 = rows_of((16, 128))
    zero = jnp.zeros((16, 128), f32)
    halves = [zero, zero]
    for j in range(PEERS):
        tile = got[j, :, 2 * 128 : 3 * 128]
        amount = (16 * j - 16) % 128
        moved = pltpu.roll(tile, amount, 1) if amount else tile
        begin = 16 * (j % 8)
        halves[j // 8] = jnp.where((lane1 >= begin) & (lane1 < begin + 16), moved, halves[j // 8])
    from_first = pltpu.roll(got[0, :, 2 * 128 : 3 * 128], 80, 1)
    from_last = pltpu.roll(got[PEERS - 1, :, 2 * 128 : 3 * 128], 80, 1)
    ends = jnp.where(lane1 < 8, from_first, jnp.where(lane1 >= 120, from_last, zero))
    start = jnp.concatenate([halves[0], halves[1], ends], axis=1)
    start = jnp.where(rows_of((16, WIDE)) < K, start, 0.0)
    relax_ends = jnp.where((lane1 < 8) | (lane1 >= 120), from_first, zero)[K : K + 1]
    relax1 = jnp.concatenate([known[16:17, 0:CELLS], relax_ends], axis=1)
    r = jnp.broadcast_to(relax1, (16, WIDE))
    fields[N_FIELDS] = r
    for n in range(3):
        fields[N_FIELDS + 1 + n] = known[16 * n : 16 * n + 16, :]
    fields[N_FIELDS + 4, 0:8] = known[48:56, :]
    keep = 1.0 - r
    mask = jnp.broadcast_to(mask, (16, WIDE))
    diffusion = jnp.concatenate([known[0:16, 128:256]] * 3, axis=1)

    def advance(base, ups, downs):
        new = keep * base - diff_up(ups[0]) - diff_down(downs[0])
        new_ups = [keep * ups[n] - diff_up(ups[n + 1]) for n in range(len(ups) - 1)]
        new_downs = [keep * downs[n] - diff_down(downs[n + 1]) for n in range(len(downs) - 1)]
        return new, new_ups, new_downs

    ups, downs = [mu[1], mu[3], mu[5]], [mu[2], mu[4], mu[6]]
    s1, ups, downs = advance(mu[0], ups, downs)
    s2, ups, downs = advance(s1, ups, downs)
    s3, _, _ = advance(s2, ups, downs)

    def times(first, last, inputs):
        stacked = stack6(jnp.concatenate(inputs, axis=1) if len(inputs) > 1 else inputs[0])
        y = jnp.dot(block[16 * first : 16 * last, 128:224], stacked, preferred_element_type=f32)
        out = []
        for n in range(len(inputs)):
            cut = y[:, n * WIDE : (n + 1) * WIDE]
            out.append([cut[16 * g : 16 * g + 16] for g in range(last - first)])
        return out

    def applied(f, coupled):
        return mask * (coupled + diffusion * (2.0 * f - shift_up(f) - shift_down(f)))

    def streamed(g, gp, gm):
        return keep * g - diff_up(gp) - diff_down(gm)

    def streamed_twice(k1, gp, gm, g2p, g2m):
        return keep * k1 - diff_up(keep * gp - diff_up(g2p)) - diff_down(keep * gm - diff_down(g2m))

    ((gc, gcp, gcm, _, _, g2cp, g2cm),) = times(4, 11, [start])
    relaxed = r * gc
    shares = mask * (s1 + relaxed)
    res = mask * (shares - start)
    k1_start = streamed(relaxed, r * gcp, r * gcm)
    k2_start = streamed_twice(k1_start, r * gcp, r * gcm, r * g2cp, r * g2cm)

    def parts(f, ys):
        out = [applied(f, ys[0])]
        k1 = streamed(ys[1], ys[2], ys[3])
        rg = r * ys[4]
        held = rg - f
        out += [mask * (k1 + held), held]
        if len(ys) > 5:
            out.append(streamed_twice(k1, ys[2], ys[3], ys[7], ys[8]))
            out.append(streamed(rg, r * ys[5], r * ys[6]) + held)
        return out

    y_shares, y_res = times(0, 9, [shares, res])
    rg = r * y_shares[4]
    held_shares = rg - shares
    n_shares = streamed(rg, r * y_shares[5], r * y_shares[6]) + held_shares
    p0 = mask * (s2 + k1_start + held_shares)
    e, p1, _, k2_res, n_res = parts(res, y_res)

    y_e, y_p0, y_p1 = times(0, 9, [e, p0, p1])
    ee, p2, _, k2_e, n_e = parts(e, y_e)
    ap0, q3, held_p0 = parts(p0, y_p0[:5])
    ap1, q4, held_p1 = parts(p1, y_p1[:5])
    q0 = mask * (s3 + k2_start + n_shares + held_p0)
    q1 = mask * (k2_res + n_res + held_p1)

    y_p2, y_ap0, y_ap1, y_q0, y_q1, y_q3, y_q4 = times(0, 5, [p2, ap0, ap1, q0, q1, q3, q4])
    ap2, q5, held_p2 = parts(p2, y_p2)
    aap0, q6, _ = parts(ap0, y_ap0)
    aap1, q7, _ = parts(ap1, y_ap1)
    q2 = mask * (k2_e + n_e + held_p2)
    aq0, aq1, aq3, aq4 = (applied(f, y[0]) for f, y in ((q0, y_q0), (q1, y_q1), (q3, y_q3), (q4, y_q4)))

    (y_ap2,) = times(0, 5, [ap2])
    aap2, q8, _ = parts(ap2, y_ap2)
    first = [q2, q5, q6, q7, aq0, aq1, aq3, aq4]
    aq2, aq5, aq6, aq7, aaq0, aaq1, aaq3, aaq4 = (applied(f, y[0]) for f, y in zip(first, times(0, 1, first)))
    second = [q8, aq2, aq5, aq6, aq7]
    aq8, aaq2, aaq5, aaq6, aaq7 = (applied(f, y[0]) for f, y in zip(second, times(0, 1, second)))
    ((y_aq8,),) = times(0, 1, [aq8])
    aaq8 = applied(aq8, y_aq8)

    q = [q0, q1, q2, q3, q4, q5, q6, q7, q8]
    aq = [aq0, aq1, aq2, aq3, aq4, aq5, aq6, aq7, aq8]
    aaq = [aaq0, aaq1, aaq2, aaq3, aaq4, aaq5, aaq6, aaq7, aaq8]
    for n, f in enumerate([start, shares, res, e, p0, p1, p2, ap0, ap1, ap2] + q + aq):
        fields[n] = f

    plain = [[res], [p0, p1, p2], q]
    once = [[e], [ap0, ap1, ap2], aq]
    again = [[ee], [aap0, aap1, aap2], aaq]
    table[...] = jnp.zeros((256, 128), f32)
    for n, (stage, quantity, i, j) in enumerate(PAIRS):
        a, b = ((plain, plain), (plain, once), (once, once), (once, again))[quantity]
        product = a[stage][i][:, 0:CELLS] * b[stage][j][:, 0:CELLS]
        folded = (product[0:8, 0:128] + product[0:8, 128:256]) + (product[8:16, 0:128] + product[8:16, 128:256])
        table[n : n + 1, :] = jnp.sum(folded, axis=0, keepdims=True)
    ones = jnp.ones((8, 128), f32)
    tops = [
        lax.dot_general(
            ones,
            table[128 * n : 128 * n + 128, :],
            (((1,), (1,)), ((), ())),
            precision=lax.Precision.HIGHEST,
            preferred_element_type=f32,
        )
        for n in range(2)
    ]
    row8 = rows_of((8, 128))
    line[...] = jnp.where(row8 == 0, tops[0], jnp.where(row8 == 1, tops[1], 0.0))
    for copy in copies_of([(line, partial.at[j]) for j in range(n_space)], sems):
        copy.wait()


def speeds_of(shape):
    number = 2 * lax.axis_index("vel") + jnp.where(rows_of(shape) >= 8, 1, 0)
    return time_step * jnp.abs((number.astype(f32) + 0.5) * spacing - 4.0)


def prep_kernel(
    block_in,
    pairs_in,
    own_in,
    coupling_in,
    diff_in,
    rate_in,
    flags_in,
    table,
    block,
    own6,
    coupling_raw,
    diff_raw,
    rate,
    flags,
    sems,
):
    vel = lax.axis_index("vel")
    moves = [(rate_in, rate), (flags_in, flags), (coupling_in, coupling_raw), (diff_in, diff_raw)]
    moves += [(own_in.at[vel], own6), (pairs_in, table.at[24:56, 0:128]), (block_in, block)]
    waits = copies_of(moves, sems)
    waits[0].wait()
    waits[1].wait()
    table[16:24, 0:CELLS] = jnp.broadcast_to(relax_of(rate[...], flags[...]), (8, CELLS))
    for copy in waits[2:]:
        copy.wait()
    table[0:16, 0:128] = jnp.zeros((16, 128), f32)
    table[0:K, 0:K] = coupling_raw[...]
    c = table[0:16, 0:128]
    ch = c.astype(bf16).astype(f32)
    cm = (c - ch).astype(bf16).astype(f32)
    pieces = [ch, ch, ch, cm, cm, c - ch - cm]
    six = pieces[0]
    for n in range(1, 6):
        six = six + pltpu.roll(pieces[n], 16 * n, 1)
    block[0:16, 128:256] = six.astype(bf16)
    block[176:192, 128:256] = own6[...]
    shape = (16, K)
    chosen = jnp.where(lanes_of(shape) == rows_of(shape), jnp.broadcast_to(diff_raw[...], shape), 0.0)
    table[0:16, 128:256] = jnp.broadcast_to(jnp.sum(chosen, axis=1, keepdims=True), (16, 128))


def stream_kernel(fields, _, edges_in, dist_in, out, dist, edges, ends, sems):
    waits = copies_of([(edges_in, edges), (dist_in, dist)], sems)
    positive = lax.axis_index("vel") >= PEERS // 2
    towards = jnp.where(positive, 1, -1)
    ends[...] = jnp.zeros((16, ROWS), f32)
    waits[0].wait()
    for n in range(3):
        for k in range(16):
            row = edges[16 * n + k : 16 * n + k + 1, :]
            ends[n : n + 1, 128 * k : 128 * k + 128] = row
            ends[8 + n : 9 + n, 128 * k : 128 * k + 128] = row
    r = fields[N_FIELDS, 0:1, :]
    a = speeds_of((16, WIDE))
    stay = 1.0 - jnp.broadcast_to(r, (16, WIDE)) - a

    def before(x):
        return jnp.where(positive, shift_up(x), shift_down(x))

    once = before(stay)
    two = before(once)
    t0 = stay * stay * stay
    t1 = a * (stay * (stay + once) + once * once)
    t2 = a * a * (stay + once + two)
    t3 = a * a * a
    waits[1].wait()
    back = (lanes_of((CELLS, CELLS)) - rows_of((CELLS, CELLS))) * towards
    at8 = rows_of((8, CELLS))
    at8 = jnp.where(positive, -1 - at8, at8 + CELLS)
    back8 = (lanes_of((8, CELLS)) - at8) * towards
    for u in range(2):
        ts = [x[8 * u : 8 * u + 1, 0:CELLS] for x in (t0, t1, t2, t3)]

        def band(distance):
            value = jnp.zeros(distance.shape, f32)
            for n, x in enumerate(ts):
                value = jnp.where(distance == n, jnp.broadcast_to(x, distance.shape), value)
            return value

        b = band(back)
        bh = b.astype(bf16)
        bl = (b - bh.astype(f32)).astype(bf16)
        b8 = band(back8)
        b8h = b8.astype(bf16).astype(f32)
        b8 = jnp.concatenate([b8h, b8 - b8h], axis=0).astype(bf16)
        rows = pl.ds(u * BLOCK, BLOCK)
        x = dist[rows, :]
        value = jnp.dot(x, bh, preferred_element_type=f32)
        value += jnp.dot(x, bl, preferred_element_type=f32)
        h = ends[:, rows].astype(bf16)
        value += lax.dot_general(h, b8, (((0,), (0,)), ((), ())), preferred_element_type=f32)
        out[rows, :] = value


UPDATE_ROWS = 512


def update_kernel(
    n_space,
    partial,
    fields,
    block,
    base,
    out,
    macro,
    done,
    macro_part,
    sems,
):
    place = lax.axis_index("vel")
    positive = place >= PEERS // 2

    def known(at):
        return fields[N_FIELDS + 1 + at // 16, at % 16 : at % 16 + 8, 0:128]

    total = partial[0]
    for j in range(1, n_space):
        total = total + partial[j]
    total = total * known(48)
    cpl = fields[N_FIELDS + 1, :, 0:128]
    lane16 = lanes_of((16, 128))
    row16 = rows_of((16, 128))
    size = jnp.sum(jnp.abs(cpl), axis=1, keepdims=True)
    middle = jnp.sum(jnp.where(lane16 == row16, cpl, 0.0), axis=1, keepdims=True)
    real = row16[:, 0:1] < K
    most = jnp.max(jnp.where(real, size + 4.0 * fields[N_FIELDS + 1, :, 128:129], 0.0), axis=0, keepdims=True)
    least = jnp.min(jnp.where(real, 2.0 * middle - size, 1e30), axis=0, keepdims=True)
    low_step, high_step = 1.0 / most, 1.0 / least

    def summed(weighted, which):
        picked = jnp.where(known(24) == which, weighted, 0.0)
        return jnp.sum(jnp.sum(picked, axis=0, keepdims=True), axis=1, keepdims=True)

    def clipped(x):
        return jnp.minimum(jnp.maximum(x, low_step), high_step)

    def weights_of(stage, weighted):
        rr, ra, aa, aaa = (summed(weighted, 4 * stage + n) for n in range(4))
        s1 = clipped(rr / ra)
        rr2 = rr - 2.0 * s1 * ra + s1 * s1 * aa
        ra2 = ra - 2.0 * s1 * aa + s1 * s1 * aaa
        s2 = clipped(rr2 / ra2)
        return s1 + s2, -s1 * s2

    li, ri = (known(n).astype(jnp.int32) for n in (32, 40))

    def choose(index, zero, one, two):
        return jnp.where(index == 0, zero, jnp.where(index == 1, one, two))

    a1, b1 = weights_of(0, total)
    a2, b2 = weights_of(1, total * choose(li, 1.0, a1, b1) * choose(ri, 1.0, a1, b1))

    def both(index):
        outer = (index >= 3).astype(jnp.int32) + (index >= 6).astype(jnp.int32)
        return choose(outer, 1.0, a2, b2) * choose(index - 3 * outer, 1.0, a1, b1)

    a3, b3 = weights_of(2, total * both(li) * both(ri))

    start, shares, res, e = (fields[n] for n in range(4))
    corr1 = a1 * res + b1 * e
    cur1 = shares + corr1
    res2 = fields[4] + a1 * fields[5] + b1 * fields[6]
    e2 = fields[7] + a1 * fields[8] + b1 * fields[9]
    corr2 = a2 * res2 + b2 * e2
    cur2 = res2 + cur1 + corr2

    def third(at):
        rows = [fields[at + 3 * n] + a1 * fields[at + 3 * n + 1] + b1 * fields[at + 3 * n + 2] for n in range(3)]
        return rows[0] + a2 * rows[1] + b2 * rows[2]

    res3, e3 = third(10), third(19)
    corr3 = a3 * res3 + b3 * e3
    cur3 = res3 + cur2 + corr3
    mine = pltpu.roll(cur3[:, 0:CELLS], lax.rem(CELLS - 16 * place, CELLS), 1)
    macro_part[...] = mine[0:K, 0:16]
    macro_copy = pltpu.make_async_copy(macro_part, macro, sems.at[ROWS // UPDATE_ROWS])
    macro_copy.start()

    r = fields[N_FIELDS]
    row = rows_of((16, WIDE))
    scaled = r * jnp.where(row < 5, 1.0, jnp.where(row < 10, 0.0, 1.0 / 3.0))
    f1 = scaled * start + corr1
    f2 = scaled * cur1 + corr2
    f3 = scaled * cur2 + corr3
    y = jnp.dot(block[176:192, 128:224], stack6(jnp.concatenate([f1, f2, f3], axis=1)), preferred_element_type=f32)
    y1, y2, y3 = (y[:, n * WIDE : (n + 1) * WIDE] for n in range(3))
    a = speeds_of((16, WIDE))

    def before(x):
        return jnp.where(positive, shift_up(x), shift_down(x))

    stay = 1.0 - r - a

    def moved(x):
        return stay * x + a * before(x)

    h = (moved(moved(y1) + y2) + y3)[:, 0:CELLS]
    hh = h.astype(bf16).astype(f32)
    hm = (h - hh).astype(bf16).astype(f32)

    sends = [macro_copy]
    for u in range(2):
        hu, mu = hh[8 * u : 8 * u + 8], hm[8 * u : 8 * u + 8]
        mixed = jnp.concatenate([hu, mu, hu, jnp.zeros((104, CELLS), f32)], axis=0).astype(bf16)
        for n in range(BLOCK // UPDATE_ROWS):
            part = u * (BLOCK // UPDATE_ROWS) + n
            rows = pl.ds(part * UPDATE_ROWS, UPDATE_ROWS)
            value = jnp.dot(block[pl.ds(n * UPDATE_ROWS, UPDATE_ROWS), 0:128], mixed, preferred_element_type=f32)
            done[rows, :] = (base[rows, :] + value).astype(bf16)
            copy = pltpu.make_async_copy(done.at[rows, :], out.at[rows, :], sems.at[part])
            copy.start()
            sends.append(copy)
    for copy in sends:
        copy.wait()


def vmem():
    return pl.BlockSpec(memory_space=pltpu.VMEM)


def hbm():
    return pl.BlockSpec(memory_space=pltpu.HBM)


def shaped(shape, dtype=f32):
    return pltpu.VMEM(shape, dtype)


def stored(shape, dtype=f32):
    return pltpu.HBM(shape, dtype)


def placed_at(space, arrays):
    return [pltpu.with_memory_space_constraint(x, space) for x in arrays]


def near(*arrays):
    return placed_at(pltpu.VMEM, arrays)


def far(*arrays):
    return placed_at(pltpu.HBM, arrays)


def limit(mib):
    return pltpu.CompilerParams(vmem_limit_bytes=mib * 2**20)


def make_per_device(n_space):
    block, p3, own6 = grid_constants()
    pairs = pair_arrays()

    def per_device(velocity_dist, macro_state, collision_rate, wall_flags, diffusivity, coupling):
        rate = collision_rate.reshape(1, CELLS)
        flags = wall_flags.reshape(1, CELLS)
        sums, ahead, back, owned = pl.pallas_call(
            sums_kernel,
            out_shape=(
                shaped((16, CELLS)),
                shaped((64, 128)),
                shaped((16, 128)),
                shaped((16, 128)),
            ),
            in_specs=[hbm()] * 5,
            out_specs=(vmem(),) * 4,
            scratch_shapes=[
                pltpu.VMEM((ROWS, CELLS), bf16),
                pltpu.VMEM((32, BLOCK), bf16),
                pltpu.VMEM((K, 16), f32),
                pltpu.VMEM((1, CELLS), f32),
                pltpu.VMEM((1, CELLS), jnp.int32),
                pltpu.VMEM((16, 128), f32),
                pltpu.SemaphoreType.DMA((6,)),
            ],
            compiler_params=limit(8),
            name="sums",
        )(*far(velocity_dist, jnp.asarray(p3), macro_state, rate, flags))
        rising = [(i, i + 1) for i in range(n_space - 1)]
        half = PEERS // 2
        downwind = [(i * PEERS + n, j * PEERS + n) for i, j in rising for n in range(half, PEERS)]
        downwind += [(j * PEERS + n, i * PEERS + n) for i, j in rising for n in range(half)]
        upwind = [(j, i) for i, j in downwind]
        ahead = lax.ppermute(ahead, ("space", "vel"), downwind)
        back = lax.ppermute(back, ("space", "vel"), upwind)
        packed, edges = pl.pallas_call(
            pack_kernel,
            out_shape=(stored((PEERS, 16, WIDE)), stored((48, 128))),
            in_specs=[vmem()] * 4,
            out_specs=(hbm(),) * 2,
            scratch_shapes=[pltpu.VMEM((16, WIDE), f32), pltpu.SemaphoreType.DMA((PEERS + 1,))],
            compiler_params=limit(4),
            name="pack",
        )(*near(sums, ahead, back, owned))
        got = lax.all_to_all(packed, "vel", split_axis=0, concat_axis=0, tiled=True)
        known, constants = pl.pallas_call(
            prep_kernel,
            out_shape=(shaped((56, WIDE)), shaped(block.shape, bf16)),
            in_specs=[hbm()] * 7,
            out_specs=(vmem(),) * 2,
            scratch_shapes=[
                pltpu.VMEM((16, 128), bf16),
                pltpu.VMEM((K, K), f32),
                pltpu.VMEM((1, K), f32),
                pltpu.VMEM((1, CELLS), f32),
                pltpu.VMEM((1, CELLS), jnp.int32),
                pltpu.SemaphoreType.DMA((7,)),
            ],
            compiler_params=limit(4),
            name="prep",
        )(*far(*(jnp.asarray(x) for x in (block, pairs, own6)), coupling, diffusivity.reshape(1, K), rate, flags))
        fields, partial = pl.pallas_call(
            lambda *refs: fields_kernel(n_space, *refs),
            out_shape=(shaped((N_FIELDS + 5, 16, WIDE)), stored((n_space, 8, 128))),
            in_specs=[vmem()] * 3,
            out_specs=(vmem(), hbm()),
            scratch_shapes=[
                pltpu.VMEM((256, 128), f32),
                pltpu.VMEM((8, 128), f32),
                pltpu.SemaphoreType.DMA((n_space,)),
            ],
            compiler_params=limit(12),
            name="fields",
        )(*near(got, known, constants))
        base = pl.pallas_call(
            stream_kernel,
            out_shape=shaped((ROWS, CELLS)),
            in_specs=[vmem()] * 2 + [hbm()] * 2,
            out_specs=vmem(),
            scratch_shapes=[
                pltpu.VMEM((ROWS, CELLS), bf16),
                pltpu.VMEM((48, 128), f32),
                pltpu.VMEM((16, ROWS), f32),
                pltpu.SemaphoreType.DMA((2,)),
            ],
            compiler_params=limit(16),
            name="stream",
        )(*near(fields, constants), *far(edges, velocity_dist))
        partial = lax.all_to_all(partial, "space", split_axis=0, concat_axis=0, tiled=True)
        return pl.pallas_call(
            lambda *refs: update_kernel(n_space, *refs),
            out_shape=(stored((ROWS, CELLS), bf16), stored((K, 16))),
            in_specs=[vmem()] * 4,
            out_specs=(hbm(), hbm()),
            scratch_shapes=[
                pltpu.VMEM((ROWS, CELLS), bf16),
                pltpu.VMEM((K, 16), f32),
                pltpu.SemaphoreType.DMA((ROWS // UPDATE_ROWS + 1,)),
            ],
            compiler_params=limit(12),
            name="update",
        )(*near(partial, fields, constants, base))

    return per_device


def solution(mesh):
    placed = (P("vel", "space"), P(None, ("space", "vel")), P("space"), P("space"), P(), P())
    return jax.shard_map(
        make_per_device(mesh.shape["space"]),
        mesh=mesh,
        in_specs=placed,
        out_specs=(P("vel", "space"), P(None, ("space", "vel"))),
        check_vma=False,
    )
```

```python
import math

import jax
import jax.numpy as jnp
import numpy as np
from jax import lax
from jax.experimental import pallas as pl
from jax.experimental.pallas import tpu as pltpu
from jax.sharding import PartitionSpec as P

NV1 = 32
K = 13
time_step = 0.125
spacing = 8.0 / NV1
CELLS = 256
WIDE = 384
PEERS = 16
ROWS = 2048
BLOCK = 1024
bf16 = jnp.bfloat16
f32 = jnp.float32


def parts_of(x, number):
    rest = np.asarray(x, np.float64)
    out = []
    for _ in range(number):
        piece = rest.astype(np.float32).astype(bf16)
        out.append(piece)
        rest = rest - piece.astype(np.float64)
    return out


def grid_constants():
    v = (np.arange(NV1) + 0.5) * spacing - 4.0
    w = np.exp(-0.5 * v * v) * spacing / math.sqrt(2.0 * math.pi)
    vy, vz = np.repeat(v, NV1), np.tile(v, NV1)
    wyz = np.repeat(w, NV1) * np.tile(w, NV1)
    one = np.ones_like(vy)
    yz = vy * vy + vz * vz
    phi = np.stack([one, vy, vz, vy * vz, vy * vy, vz * vz, vy * yz, vz * yz])
    cmat = np.zeros((NV1, K, 8))
    for i, x in enumerate(v):
        c = cmat[i]
        c[0, 0] = 1.0
        c[1, 0] = x
        c[2, 1] = 1.0
        c[3, 2] = 1.0
        c[4, 0] = (x * x - 3.0) / math.sqrt(6.0)
        c[4, 4] = c[4, 5] = 1.0 / math.sqrt(6.0)
        c[5, 1] = x
        c[6, 2] = x
        c[7, 3] = 1.0
        c[8, 0] = 0.5 * x * x
        c[8, 4] = -0.5
        c[9, 0] = x * x / math.sqrt(12.0)
        c[9, 4] = 1.0 / math.sqrt(12.0)
        c[9, 5] = -2.0 / math.sqrt(12.0)
        c[10, 0] = x * (x * x - 5.0) / math.sqrt(10.0)
        c[10, 4] = c[10, 5] = x / math.sqrt(10.0)
        c[11, 1] = (x * x - 5.0) / math.sqrt(10.0)
        c[11, 6] = 1.0 / math.sqrt(10.0)
        c[12, 2] = (x * x - 5.0) / math.sqrt(10.0)
        c[12, 7] = 1.0 / math.sqrt(10.0)
    a = time_step * np.abs(v)
    plus = v > 0.0
    proj = phi * wyz
    groups = [np.ones(NV1)]
    for power in (1, 2, 3):
        groups += [a**power * plus, a**power * ~plus]
    big = np.zeros((7 * 16, 8 * NV1))
    for g, factor in enumerate(groups):
        for i in range(NV1):
            big[16 * g : 16 * g + K, 8 * i : 8 * i + 8] = factor[i] * w[i] * cmat[i]
    gram2 = proj @ phi.T
    shakhov = np.array([1.0] * 5 + [0.0] * 5 + [1.0 / 3.0] * 3)

    def between(factor):
        out = np.zeros((16, 16))
        for i in range(NV1):
            out[:K, :K] += factor[i] * w[i] * cmat[i] @ gram2 @ cmat[i].T
        return out

    c16 = np.zeros(16)
    c16[:K] = shakhov
    g, gp, gm, g2p, g2m = (between(groups[k]) for k in (0, 1, 2, 3, 4))
    mats = [g, gp, gm, g * c16, gp * c16, gm * c16, g2p, g2m, g2p * c16, g2m * c16]
    block = np.zeros((BLOCK + 336, 256), bf16)
    block[16:176, 128:224] = six_terms(np.concatenate(mats, axis=0))
    block[BLOCK:] = np.concatenate(parts_of(big, 3), axis=0)
    p3 = np.concatenate(parts_of(proj, 3) + [np.zeros((8, BLOCK), bf16)], axis=0)
    ph, pm = parts_of(phi.T, 2)
    block[0:BLOCK, 0:24] = np.concatenate([ph, ph, pm], axis=1)
    own = np.zeros((PEERS, 16, 16))
    for j in range(PEERS):
        for u in range(2):
            own[j, 8 * u : 8 * u + 8, :K] = cmat[2 * j + u].T
    own = np.concatenate([six_terms(own), np.zeros((PEERS, 16, 32), bf16)], axis=2)
    return block, p3, own


def six_terms(x):
    h, m, low = parts_of(x, 3)
    return np.concatenate([h, h, h, m, m, low], axis=-1)


BASES = (1, 3, 9)


def pair_table():
    entries = []
    for stage, size in enumerate(BASES):
        for quantity in range(4):
            for i in range(size):
                for j in range(i, size):
                    entries.append((stage, quantity, i, j))
    return entries


PAIRS = pair_table()


def pair_arrays():
    kind = np.full((8, 128), -1, np.int32)
    left = np.zeros((8, 128), np.int32)
    right = np.zeros((8, 128), np.int32)
    twice = np.zeros((8, 128), np.int32)
    for n, (stage, quantity, i, j) in enumerate(PAIRS):
        at = (n // 128, n % 128)
        kind[at] = 4 * stage + quantity
        left[at], right[at] = i, j
        twice[at] = 1 if i == j else 2
    return np.concatenate([kind, left, right, twice], axis=0).astype(np.float32)


def lanes_of(shape):
    return lax.broadcasted_iota(jnp.int32, shape, len(shape) - 1)


def rows_of(shape):
    return lax.broadcasted_iota(jnp.int32, shape, 0)


def stack6(f):
    h = f.astype(bf16)
    rest = f - h.astype(f32)
    m = rest.astype(bf16)
    low = (rest - m.astype(f32)).astype(bf16)
    return jnp.concatenate([h, m, low, h, m, h], axis=0)


def relax_of(rate, flags):
    return (time_step * rate) * (1.0 + flags.astype(f32))


def shift_up(x):
    return pltpu.roll(x, 1, 1)


def shift_down(x):
    return pltpu.roll(x, x.shape[1] - 1, 1)


def diff_up(x):
    return x - shift_up(x)


def diff_down(x):
    return x - shift_down(x)


def copies_of(pairs, sems):
    made = [pltpu.make_async_copy(x, y, sems.at[n]) for n, (x, y) in enumerate(pairs)]
    for copy in made:
        copy.start()
    return made


def sums_kernel(
    dist_in,
    p3_in,
    start_in,
    rate_in,
    flags_in,
    sums,
    ahead,
    back,
    owned,
    dist,
    p3,
    start,
    rate,
    flags,
    padded,
    sems,
):
    positive = lax.axis_index("vel") >= PEERS // 2
    halves = [pl.ds(u * BLOCK, BLOCK) for u in range(2)]
    pairs = [(p3_in, p3), (start_in, start), (rate_in, rate), (flags_in, flags)]
    pairs += [(dist_in.at[half, :], dist.at[half, :]) for half in halves]
    waits = copies_of(pairs, sems)
    for copy in waits[:4]:
        copy.wait()
    parts = []
    for u in range(2):
        waits[4 + u].wait()
        y = jnp.dot(p3[...], dist[halves[u], :], preferred_element_type=f32)
        parts.append(y[0:8] + y[8:16] + y[16:24])
    w = jnp.concatenate(parts, axis=0)
    sums[...] = w
    lane = lanes_of((16, 128))
    row = rows_of((16, 128))
    padded[...] = jnp.zeros((16, 128), f32)
    padded[0:K, 0:16] = start[...]
    mine = pltpu.roll(padded[...], 16, 1)
    owned[...] = mine
    relax = relax_of(rate[...], flags[...])
    r_first = jnp.broadcast_to(pltpu.roll(relax[:, 0:128], 48, 1), (16, 128))
    r_last = jnp.broadcast_to(pltpu.roll(relax[:, 128:256], 48, 1), (16, 128))
    zero = jnp.zeros((16, 128), f32)
    up = (
        jnp.where(lane >= 120, w[:, 128:256], zero)
        + pltpu.roll(mine, 16, 1)
        + jnp.where((row == K) & (lane >= 32) & (lane < 48), r_last, zero)
    )
    down = (
        jnp.where(lane < 8, w[:, 0:128], zero)
        + pltpu.roll(mine, 32, 1)
        + jnp.where((row == K) & (lane >= 48) & (lane < 64), r_first, zero)
    )
    ahead[0:16, :] = jnp.where(positive, up, down)
    back[...] = jnp.where(positive, down, up)
    e_lane = lanes_of((16, CELLS))
    e_row = rows_of((16, CELLS))
    cell = jnp.where(positive, CELLS - 1 - e_row, e_row)
    pick = jnp.where((e_lane == cell) & (e_row < 3), 1.0, 0.0).astype(bf16)
    for u in range(2):
        e = lax.dot_general(pick, dist[halves[u], :], (((1,), (1,)), ((), ())), preferred_element_type=f32)
        for n in range(3):
            for k in range(8):
                at = 16 + 16 * n + 8 * u + k
                ahead[at : at + 1, :] = e[n : n + 1, 128 * k : 128 * k + 128]


def pack_kernel(sums, ahead, back, owned, out, edges, whole, sems):
    whole[:, 0:CELLS] = sums[...]
    whole[:, CELLS:WIDE] = ahead[0:16, :] + back[...] + owned[...]
    for copy in copies_of([(whole, out.at[j]) for j in range(PEERS)] + [(ahead, edges)], sems):
        copy.wait()


N_FIELDS = 28


def fields_kernel(n_space, got, known, block, fields, partial, table, line, sems):
    slab = lax.axis_index("space")
    lane = lanes_of((1, WIDE))
    right = (lane >= CELLS) & (lane < CELLS + 8)
    left = lane >= WIDE - 8
    own = lane < CELLS
    inside = own | (right & (slab < n_space - 1)) | (left & (slab > 0))
    mask = jnp.where(inside, 1.0, 0.0)

    w = got[...].reshape(PEERS * 16, WIDE)
    w = jnp.where(own | right | left, w, 0.0)
    wh = w.astype(bf16)
    w_rest = w - wh.astype(f32)
    wm = w_rest.astype(bf16)
    wl = (w_rest - wm.astype(f32)).astype(bf16)
    y = jnp.dot(block[BLOCK : BLOCK + 336, :], wh, preferred_element_type=f32)
    z = jnp.dot(block[BLOCK : BLOCK + 224, :], wm, preferred_element_type=f32)
    t = jnp.dot(block[BLOCK : BLOCK + 112, :], wl, preferred_element_type=f32)
    mu = ((y[224:336] + z[112:224]) + (y[112:224] + z[0:112])) + t + y[0:112]
    mu = [mu[16 * g : 16 * g + 16] for g in range(7)]

    lane1 = lanes_of((16, 128))
    row1 = rows_of((16, 128))
    zero = jnp.zeros((16, 128), f32)
    halves = [zero, zero]
    for j in range(PEERS):
        tile = got[j, :, 2 * 128 : 3 * 128]
        amount = (16 * j - 16) % 128
        moved = pltpu.roll(tile, amount, 1) if amount else tile
        begin = 16 * (j % 8)
        halves[j // 8] = jnp.where((lane1 >= begin) & (lane1 < begin + 16), moved, halves[j // 8])
    from_first = pltpu.roll(got[0, :, 2 * 128 : 3 * 128], 80, 1)
    from_last = pltpu.roll(got[PEERS - 1, :, 2 * 128 : 3 * 128], 80, 1)
    ends = jnp.where(lane1 < 8, from_first, jnp.where(lane1 >= 120, from_last, zero))
    start = jnp.concatenate([halves[0], halves[1], ends], axis=1)
    start = jnp.where(rows_of((16, WIDE)) < K, start, 0.0)
    relax_ends = jnp.where((lane1 < 8) | (lane1 >= 120), from_first, zero)[K : K + 1]
    relax1 = jnp.concatenate([known[16:17, 0:CELLS], relax_ends], axis=1)
    r = jnp.broadcast_to(relax1, (16, WIDE))
    fields[N_FIELDS] = r
    keep = 1.0 - r
    mask = jnp.broadcast_to(mask, (16, WIDE))
    diffusion = jnp.concatenate([known[0:16, 128:256]] * 3, axis=1)

    def advance(base, ups, downs):
        new = keep * base - diff_up(ups[0]) - diff_down(downs[0])
        new_ups = [keep * ups[n] - diff_up(ups[n + 1]) for n in range(len(ups) - 1)]
        new_downs = [keep * downs[n] - diff_down(downs[n + 1]) for n in range(len(downs) - 1)]
        return new, new_ups, new_downs

    ups, downs = [mu[1], mu[3], mu[5]], [mu[2], mu[4], mu[6]]
    s1, ups, downs = advance(mu[0], ups, downs)
    s2, ups, downs = advance(s1, ups, downs)
    s3, _, _ = advance(s2, ups, downs)

    def times(first, last, inputs):
        stacked = stack6(jnp.concatenate(inputs, axis=1) if len(inputs) > 1 else inputs[0])
        y = jnp.dot(block[16 * first : 16 * last, 128:224], stacked, preferred_element_type=f32)
        out = []
        for n in range(len(inputs)):
            cut = y[:, n * WIDE : (n + 1) * WIDE]
            out.append([cut[16 * g : 16 * g + 16] for g in range(last - first)])
        return out

    def applied(f, coupled):
        return mask * (coupled + diffusion * (2.0 * f - shift_up(f) - shift_down(f)))

    def streamed(g, gp, gm):
        return keep * g - diff_up(gp) - diff_down(gm)

    def streamed_twice(k1, gp, gm, g2p, g2m):
        return keep * k1 - diff_up(keep * gp - diff_up(g2p)) - diff_down(keep * gm - diff_down(g2m))

    ((gc, gcp, gcm, _, _, g2cp, g2cm),) = times(4, 11, [start])
    relaxed = r * gc
    shares = mask * (s1 + relaxed)
    res = mask * (shares - start)
    k1_start = streamed(relaxed, r * gcp, r * gcm)
    k2_start = streamed_twice(k1_start, r * gcp, r * gcm, r * g2cp, r * g2cm)

    def parts(f, ys):
        out = [applied(f, ys[0])]
        k1 = streamed(ys[1], ys[2], ys[3])
        rg = r * ys[4]
        held = rg - f
        out += [mask * (k1 + held), held]
        if len(ys) > 5:
            out.append(streamed_twice(k1, ys[2], ys[3], ys[7], ys[8]))
            out.append(streamed(rg, r * ys[5], r * ys[6]) + held)
        return out

    y_shares, y_res = times(0, 9, [shares, res])
    rg = r * y_shares[4]
    held_shares = rg - shares
    n_shares = streamed(rg, r * y_shares[5], r * y_shares[6]) + held_shares
    p0 = mask * (s2 + k1_start + held_shares)
    e, p1, _, k2_res, n_res = parts(res, y_res)

    y_e, y_p0, y_p1 = times(0, 9, [e, p0, p1])
    ee, p2, _, k2_e, n_e = parts(e, y_e)
    ap0, q3, held_p0 = parts(p0, y_p0[:5])
    ap1, q4, held_p1 = parts(p1, y_p1[:5])
    q0 = mask * (s3 + k2_start + n_shares + held_p0)
    q1 = mask * (k2_res + n_res + held_p1)

    y_p2, y_ap0, y_ap1, y_q0, y_q1, y_q3, y_q4 = times(0, 5, [p2, ap0, ap1, q0, q1, q3, q4])
    ap2, q5, held_p2 = parts(p2, y_p2)
    aap0, q6, _ = parts(ap0, y_ap0)
    aap1, q7, _ = parts(ap1, y_ap1)
    q2 = mask * (k2_e + n_e + held_p2)
    aq0, aq1, aq3, aq4 = (applied(f, y[0]) for f, y in ((q0, y_q0), (q1, y_q1), (q3, y_q3), (q4, y_q4)))

    (y_ap2,) = times(0, 5, [ap2])
    aap2, q8, _ = parts(ap2, y_ap2)
    first = [q2, q5, q6, q7, aq0, aq1, aq3, aq4]
    aq2, aq5, aq6, aq7, aaq0, aaq1, aaq3, aaq4 = (applied(f, y[0]) for f, y in zip(first, times(0, 1, first)))
    second = [q8, aq2, aq5, aq6, aq7]
    aq8, aaq2, aaq5, aaq6, aaq7 = (applied(f, y[0]) for f, y in zip(second, times(0, 1, second)))
    ((y_aq8,),) = times(0, 1, [aq8])
    aaq8 = applied(aq8, y_aq8)

    q = [q0, q1, q2, q3, q4, q5, q6, q7, q8]
    aq = [aq0, aq1, aq2, aq3, aq4, aq5, aq6, aq7, aq8]
    aaq = [aaq0, aaq1, aaq2, aaq3, aaq4, aaq5, aaq6, aaq7, aaq8]
    for n, f in enumerate([start, shares, res, e, p0, p1, p2, ap0, ap1, ap2] + q + aq):
        fields[n] = f

    plain = [[res], [p0, p1, p2], q]
    once = [[e], [ap0, ap1, ap2], aq]
    again = [[ee], [aap0, aap1, aap2], aaq]
    table[...] = jnp.zeros((256, 128), f32)
    for n, (stage, quantity, i, j) in enumerate(PAIRS):
        a, b = ((plain, plain), (plain, once), (once, once), (once, again))[quantity]
        product = a[stage][i][:, 0:CELLS] * b[stage][j][:, 0:CELLS]
        folded = (product[0:8, 0:128] + product[0:8, 128:256]) + (product[8:16, 0:128] + product[8:16, 128:256])
        table[n : n + 1, :] = jnp.sum(folded, axis=0, keepdims=True)
    ones = jnp.ones((8, 128), f32)
    tops = [
        lax.dot_general(
            ones,
            table[128 * n : 128 * n + 128, :],
            (((1,), (1,)), ((), ())),
            precision=lax.Precision.HIGHEST,
            preferred_element_type=f32,
        )
        for n in range(2)
    ]
    row8 = rows_of((8, 128))
    line[...] = jnp.where(row8 == 0, tops[0], jnp.where(row8 == 1, tops[1], 0.0))
    for copy in copies_of([(line, partial.at[j]) for j in range(n_space)], sems):
        copy.wait()


def speeds_of(shape):
    number = 2 * lax.axis_index("vel") + jnp.where(rows_of(shape) >= 8, 1, 0)
    return time_step * jnp.abs((number.astype(f32) + 0.5) * spacing - 4.0)


def stream_kernel(
    edges_in,
    dist_in,
    block_in,
    pairs_in,
    own_in,
    coupling_in,
    diff_in,
    rate_in,
    flags_in,
    out,
    table,
    block,
    dist,
    edges,
    ends,
    own6,
    coupling_raw,
    diff_raw,
    rate,
    flags,
    sems,
):
    vel = lax.axis_index("vel")
    moves = [(edges_in, edges), (rate_in, rate), (flags_in, flags), (dist_in, dist)]
    moves += [(coupling_in, coupling_raw), (diff_in, diff_raw), (own_in.at[vel], own6)]
    moves += [(pairs_in, table.at[24:56, 0:128]), (block_in, block)]
    waits = copies_of(moves, sems)
    positive = vel >= PEERS // 2
    towards = jnp.where(positive, 1, -1)
    ends[...] = jnp.zeros((16, ROWS), f32)
    waits[0].wait()
    for n in range(3):
        for k in range(16):
            row = edges[16 + 16 * n + k : 17 + 16 * n + k, :]
            ends[n : n + 1, 128 * k : 128 * k + 128] = row
            ends[8 + n : 9 + n, 128 * k : 128 * k + 128] = row
    waits[1].wait()
    waits[2].wait()
    lane = lanes_of((1, 128))
    low = jnp.where(positive, 120, 0)
    near_edge = pltpu.roll(edges[0:16, :], 80, 1)[K : K + 1]
    near_edge = jnp.where((lane >= low) & (lane < low + 8), near_edge, 0.0)
    r = jnp.concatenate([relax_of(rate[...], flags[...]), near_edge], axis=1)
    table[16:24, :] = jnp.broadcast_to(r, (8, WIDE))
    a = speeds_of((16, WIDE))
    stay = 1.0 - jnp.broadcast_to(r, (16, WIDE)) - a

    def before(x):
        return jnp.where(positive, shift_up(x), shift_down(x))

    once = before(stay)
    two = before(once)
    t0 = stay * stay * stay
    t1 = a * (stay * (stay + once) + once * once)
    t2 = a * a * (stay + once + two)
    t3 = a * a * a
    waits[3].wait()
    back = (lanes_of((CELLS, CELLS)) - rows_of((CELLS, CELLS))) * towards
    at8 = rows_of((8, CELLS))
    at8 = jnp.where(positive, -1 - at8, at8 + CELLS)
    back8 = (lanes_of((8, CELLS)) - at8) * towards
    for u in range(2):
        ts = [x[8 * u : 8 * u + 1, 0:CELLS] for x in (t0, t1, t2, t3)]

        def band(distance):
            value = jnp.zeros(distance.shape, f32)
            for n, x in enumerate(ts):
                value = jnp.where(distance == n, jnp.broadcast_to(x, distance.shape), value)
            return value

        b = band(back)
        bh = b.astype(bf16)
        bl = (b - bh.astype(f32)).astype(bf16)
        b8 = band(back8)
        b8h = b8.astype(bf16).astype(f32)
        b8 = jnp.concatenate([b8h, b8 - b8h], axis=0).astype(bf16)
        rows = pl.ds(u * BLOCK, BLOCK)
        x = dist[rows, :]
        value = jnp.dot(x, bh, preferred_element_type=f32)
        value += jnp.dot(x, bl, preferred_element_type=f32)
        h = ends[:, rows].astype(bf16)
        value += lax.dot_general(h, b8, (((0,), (0,)), ((), ())), preferred_element_type=f32)
        out[rows, :] = value

    for copy in waits[4:]:
        copy.wait()
    table[0:16, 0:128] = jnp.zeros((16, 128), f32)
    table[0:K, 0:K] = coupling_raw[...]
    c = table[0:16, 0:128]
    ch = c.astype(bf16).astype(f32)
    cm = (c - ch).astype(bf16).astype(f32)
    pieces = [ch, ch, ch, cm, cm, c - ch - cm]
    six = pieces[0]
    for n in range(1, 6):
        six = six + pltpu.roll(pieces[n], 16 * n, 1)
    block[0:16, 128:256] = six.astype(bf16)
    block[176:192, 128:256] = own6[...]
    shape = (16, K)
    chosen = jnp.where(lanes_of(shape) == rows_of(shape), jnp.broadcast_to(diff_raw[...], shape), 0.0)
    table[0:16, 128:256] = jnp.broadcast_to(jnp.sum(chosen, axis=1, keepdims=True), (16, 128))


UPDATE_ROWS = 512


def update_kernel(
    n_space,
    partial,
    fields,
    table,
    block,
    base,
    out,
    macro,
    done,
    macro_part,
    sems,
):
    place = lax.axis_index("vel")
    positive = place >= PEERS // 2

    def known(at):
        return table[at : at + 8, 0:128]

    total = partial[0]
    for j in range(1, n_space):
        total = total + partial[j]
    total = total * known(48)
    cpl = table[0:16, 0:128]
    lane16 = lanes_of((16, 128))
    row16 = rows_of((16, 128))
    size = jnp.sum(jnp.abs(cpl), axis=1, keepdims=True)
    middle = jnp.sum(jnp.where(lane16 == row16, cpl, 0.0), axis=1, keepdims=True)
    real = row16[:, 0:1] < K
    most = jnp.max(jnp.where(real, size + 4.0 * table[0:16, 128:129], 0.0), axis=0, keepdims=True)
    least = jnp.min(jnp.where(real, 2.0 * middle - size, 1e30), axis=0, keepdims=True)
    low_step, high_step = 1.0 / most, 1.0 / least

    def summed(weighted, which):
        picked = jnp.where(known(24) == which, weighted, 0.0)
        return jnp.sum(jnp.sum(picked, axis=0, keepdims=True), axis=1, keepdims=True)

    def clipped(x):
        return jnp.minimum(jnp.maximum(x, low_step), high_step)

    def weights_of(stage, weighted):
        rr, ra, aa, aaa = (summed(weighted, 4 * stage + n) for n in range(4))
        s1 = clipped(rr / ra)
        rr2 = rr - 2.0 * s1 * ra + s1 * s1 * aa
        ra2 = ra - 2.0 * s1 * aa + s1 * s1 * aaa
        s2 = clipped(rr2 / ra2)
        return s1 + s2, -s1 * s2

    li, ri = (known(n).astype(jnp.int32) for n in (32, 40))

    def choose(index, zero, one, two):
        return jnp.where(index == 0, zero, jnp.where(index == 1, one, two))

    a1, b1 = weights_of(0, total)
    a2, b2 = weights_of(1, total * choose(li, 1.0, a1, b1) * choose(ri, 1.0, a1, b1))

    def both(index):
        outer = (index >= 3).astype(jnp.int32) + (index >= 6).astype(jnp.int32)
        return choose(outer, 1.0, a2, b2) * choose(index - 3 * outer, 1.0, a1, b1)

    a3, b3 = weights_of(2, total * both(li) * both(ri))

    start, shares, res, e = (fields[n] for n in range(4))
    corr1 = a1 * res + b1 * e
    cur1 = shares + corr1
    res2 = fields[4] + a1 * fields[5] + b1 * fields[6]
    e2 = fields[7] + a1 * fields[8] + b1 * fields[9]
    corr2 = a2 * res2 + b2 * e2
    cur2 = res2 + cur1 + corr2

    def third(at):
        rows = [fields[at + 3 * n] + a1 * fields[at + 3 * n + 1] + b1 * fields[at + 3 * n + 2] for n in range(3)]
        return rows[0] + a2 * rows[1] + b2 * rows[2]

    res3, e3 = third(10), third(19)
    corr3 = a3 * res3 + b3 * e3
    cur3 = res3 + cur2 + corr3
    mine = pltpu.roll(cur3[:, 0:CELLS], lax.rem(CELLS - 16 * place, CELLS), 1)
    macro_part[...] = mine[0:K, 0:16]
    macro_copy = pltpu.make_async_copy(macro_part, macro, sems.at[ROWS // UPDATE_ROWS])
    macro_copy.start()

    r = fields[N_FIELDS]
    row = rows_of((16, WIDE))
    scaled = r * jnp.where(row < 5, 1.0, jnp.where(row < 10, 0.0, 1.0 / 3.0))
    f1 = scaled * start + corr1
    f2 = scaled * cur1 + corr2
    f3 = scaled * cur2 + corr3
    y = jnp.dot(block[176:192, 128:224], stack6(jnp.concatenate([f1, f2, f3], axis=1)), preferred_element_type=f32)
    y1, y2, y3 = (y[:, n * WIDE : (n + 1) * WIDE] for n in range(3))
    a = speeds_of((16, WIDE))

    def before(x):
        return jnp.where(positive, shift_up(x), shift_down(x))

    stay = 1.0 - r - a

    def moved(x):
        return stay * x + a * before(x)

    h = (moved(moved(y1) + y2) + y3)[:, 0:CELLS]
    hh = h.astype(bf16).astype(f32)
    hm = (h - hh).astype(bf16).astype(f32)

    sends = [macro_copy]
    for u in range(2):
        hu, mu = hh[8 * u : 8 * u + 8], hm[8 * u : 8 * u + 8]
        mixed = jnp.concatenate([hu, mu, hu, jnp.zeros((104, CELLS), f32)], axis=0).astype(bf16)
        for n in range(BLOCK // UPDATE_ROWS):
            part = u * (BLOCK // UPDATE_ROWS) + n
            rows = pl.ds(part * UPDATE_ROWS, UPDATE_ROWS)
            value = jnp.dot(block[pl.ds(n * UPDATE_ROWS, UPDATE_ROWS), 0:128], mixed, preferred_element_type=f32)
            done[rows, :] = (base[rows, :] + value).astype(bf16)
            copy = pltpu.make_async_copy(done.at[rows, :], out.at[rows, :], sems.at[part])
            copy.start()
            sends.append(copy)
    for copy in sends:
        copy.wait()


def vmem():
    return pl.BlockSpec(memory_space=pltpu.VMEM)


def hbm():
    return pl.BlockSpec(memory_space=pltpu.HBM)


def shaped(shape, dtype=f32):
    return pltpu.VMEM(shape, dtype)


def stored(shape, dtype=f32):
    return pltpu.HBM(shape, dtype)


def placed_at(space, arrays):
    return [pltpu.with_memory_space_constraint(x, space) for x in arrays]


def near(*arrays):
    return placed_at(pltpu.VMEM, arrays)


def far(*arrays):
    return placed_at(pltpu.HBM, arrays)


def limit(mib):
    return pltpu.CompilerParams(vmem_limit_bytes=mib * 2**20)


def make_per_device(n_space):
    block, p3, own6 = grid_constants()
    pairs = pair_arrays()

    def per_device(velocity_dist, macro_state, collision_rate, wall_flags, diffusivity, coupling):
        rate = collision_rate.reshape(1, CELLS)
        flags = wall_flags.reshape(1, CELLS)
        sums, ahead, back, owned = pl.pallas_call(
            sums_kernel,
            out_shape=(
                shaped((16, CELLS)),
                shaped((64, 128)),
                shaped((16, 128)),
                shaped((16, 128)),
            ),
            in_specs=[hbm()] * 5,
            out_specs=(vmem(),) * 4,
            scratch_shapes=[
                pltpu.VMEM((ROWS, CELLS), bf16),
                pltpu.VMEM((32, BLOCK), bf16),
                pltpu.VMEM((K, 16), f32),
                pltpu.VMEM((1, CELLS), f32),
                pltpu.VMEM((1, CELLS), jnp.int32),
                pltpu.VMEM((16, 128), f32),
                pltpu.SemaphoreType.DMA((6,)),
            ],
            compiler_params=limit(8),
            name="sums",
        )(*far(velocity_dist, jnp.asarray(p3), macro_state, rate, flags))
        rising = [(i, i + 1) for i in range(n_space - 1)]
        half = PEERS // 2
        downwind = [(i * PEERS + n, j * PEERS + n) for i, j in rising for n in range(half, PEERS)]
        downwind += [(j * PEERS + n, i * PEERS + n) for i, j in rising for n in range(half)]
        upwind = [(j, i) for i, j in downwind]
        ahead = lax.ppermute(ahead, ("space", "vel"), downwind)
        back = lax.ppermute(back, ("space", "vel"), upwind)
        packed, edges = pl.pallas_call(
            pack_kernel,
            out_shape=(stored((PEERS, 16, WIDE)), stored((64, 128))),
            in_specs=[vmem()] * 4,
            out_specs=(hbm(),) * 2,
            scratch_shapes=[pltpu.VMEM((16, WIDE), f32), pltpu.SemaphoreType.DMA((PEERS + 1,))],
            compiler_params=limit(4),
            name="pack",
        )(*near(sums, ahead, back, owned))
        got = lax.all_to_all(packed, "vel", split_axis=0, concat_axis=0, tiled=True)
        base, known, constants = pl.pallas_call(
            stream_kernel,
            out_shape=(shaped((ROWS, CELLS)), shaped((56, WIDE)), shaped(block.shape, bf16)),
            in_specs=[hbm()] * 9,
            out_specs=(vmem(),) * 3,
            scratch_shapes=[
                pltpu.VMEM((ROWS, CELLS), bf16),
                pltpu.VMEM((64, 128), f32),
                pltpu.VMEM((16, ROWS), f32),
                pltpu.VMEM((16, 128), bf16),
                pltpu.VMEM((K, K), f32),
                pltpu.VMEM((1, K), f32),
                pltpu.VMEM((1, CELLS), f32),
                pltpu.VMEM((1, CELLS), jnp.int32),
                pltpu.SemaphoreType.DMA((9,)),
            ],
            compiler_params=limit(16),
            name="stream",
        )(
            *far(edges, velocity_dist, *(jnp.asarray(x) for x in (block, pairs, own6))),
            *far(coupling, diffusivity.reshape(1, K), rate, flags),
        )
        got, base = lax.optimization_barrier((got, base))
        fields, partial = pl.pallas_call(
            lambda *refs: fields_kernel(n_space, *refs),
            out_shape=(shaped((N_FIELDS + 1, 16, WIDE)), stored((n_space, 8, 128))),
            in_specs=[vmem()] * 3,
            out_specs=(vmem(), hbm()),
            scratch_shapes=[
                pltpu.VMEM((256, 128), f32),
                pltpu.VMEM((8, 128), f32),
                pltpu.SemaphoreType.DMA((n_space,)),
            ],
            compiler_params=limit(12),
            name="fields",
        )(*near(got, known, constants))
        partial = lax.all_to_all(partial, "space", split_axis=0, concat_axis=0, tiled=True)
        return pl.pallas_call(
            lambda *refs: update_kernel(n_space, *refs),
            out_shape=(stored((ROWS, CELLS), bf16), stored((K, 16))),
            in_specs=[vmem()] * 5,
            out_specs=(hbm(), hbm()),
            scratch_shapes=[
                pltpu.VMEM((ROWS, CELLS), bf16),
                pltpu.VMEM((K, 16), f32),
                pltpu.SemaphoreType.DMA((ROWS // UPDATE_ROWS + 1,)),
            ],
            compiler_params=limit(12),
            name="update",
        )(*near(partial, fields, known, constants, base))

    return per_device


def solution(mesh):
    placed = (P("vel", "space"), P(None, ("space", "vel")), P("space"), P("space"), P(), P())
    return jax.shard_map(
        make_per_device(mesh.shape["space"]),
        mesh=mesh,
        in_specs=placed,
        out_specs=(P("vel", "space"), P(None, ("space", "vel"))),
        check_vma=False,
    )
```

```python
import math

import jax
import jax.numpy as jnp
import numpy as np
from jax import lax
from jax.experimental import pallas as pl
from jax.experimental.pallas import tpu as pltpu
from jax.sharding import PartitionSpec as P

NV1 = 32
K = 13
time_step = 0.125
spacing = 8.0 / NV1
CELLS = 256
WIDE = 384
PEERS = 16
ROWS = 2048
BLOCK = 1024
bf16 = jnp.bfloat16
f32 = jnp.float32


def parts_of(x, number):
    rest = np.asarray(x, np.float64)
    out = []
    for _ in range(number):
        piece = rest.astype(np.float32).astype(bf16)
        out.append(piece)
        rest = rest - piece.astype(np.float64)
    return out


def grid_constants():
    v = (np.arange(NV1) + 0.5) * spacing - 4.0
    w = np.exp(-0.5 * v * v) * spacing / math.sqrt(2.0 * math.pi)
    vy, vz = np.repeat(v, NV1), np.tile(v, NV1)
    wyz = np.repeat(w, NV1) * np.tile(w, NV1)
    one = np.ones_like(vy)
    yz = vy * vy + vz * vz
    phi = np.stack([one, vy, vz, vy * vz, vy * vy, vz * vz, vy * yz, vz * yz])
    cmat = np.zeros((NV1, K, 8))
    for i, x in enumerate(v):
        c = cmat[i]
        c[0, 0] = 1.0
        c[1, 0] = x
        c[2, 1] = 1.0
        c[3, 2] = 1.0
        c[4, 0] = (x * x - 3.0) / math.sqrt(6.0)
        c[4, 4] = c[4, 5] = 1.0 / math.sqrt(6.0)
        c[5, 1] = x
        c[6, 2] = x
        c[7, 3] = 1.0
        c[8, 0] = 0.5 * x * x
        c[8, 4] = -0.5
        c[9, 0] = x * x / math.sqrt(12.0)
        c[9, 4] = 1.0 / math.sqrt(12.0)
        c[9, 5] = -2.0 / math.sqrt(12.0)
        c[10, 0] = x * (x * x - 5.0) / math.sqrt(10.0)
        c[10, 4] = c[10, 5] = x / math.sqrt(10.0)
        c[11, 1] = (x * x - 5.0) / math.sqrt(10.0)
        c[11, 6] = 1.0 / math.sqrt(10.0)
        c[12, 2] = (x * x - 5.0) / math.sqrt(10.0)
        c[12, 7] = 1.0 / math.sqrt(10.0)
    a = time_step * np.abs(v)
    plus = v > 0.0
    proj = phi * wyz
    groups = [np.ones(NV1)]
    for power in (1, 2, 3):
        groups += [a**power * plus, a**power * ~plus]
    big = np.zeros((7 * 16, 8 * NV1))
    for g, factor in enumerate(groups):
        for i in range(NV1):
            big[16 * g : 16 * g + K, 8 * i : 8 * i + 8] = factor[i] * w[i] * cmat[i]
    gram2 = proj @ phi.T
    shakhov = np.array([1.0] * 5 + [0.0] * 5 + [1.0 / 3.0] * 3)

    def between(factor):
        out = np.zeros((16, 16))
        for i in range(NV1):
            out[:K, :K] += factor[i] * w[i] * cmat[i] @ gram2 @ cmat[i].T
        return out

    c16 = np.zeros(16)
    c16[:K] = shakhov
    g, gp, gm, g2p, g2m = (between(groups[k]) for k in (0, 1, 2, 3, 4))
    mats = [g, gp, gm, g * c16, gp * c16, gm * c16, g2p, g2m, g2p * c16, g2m * c16]
    block = np.zeros((BLOCK + 336, 256), bf16)
    block[16:176, 128:224] = six_terms(np.concatenate(mats, axis=0))
    block[BLOCK:] = np.concatenate(parts_of(big, 3), axis=0)
    p3 = np.concatenate(parts_of(proj, 3) + [np.zeros((8, BLOCK), bf16)], axis=0)
    ph, pm = parts_of(phi.T, 2)
    block[0:BLOCK, 0:24] = np.concatenate([ph, ph, pm], axis=1)
    own = np.zeros((PEERS, 16, 16))
    for j in range(PEERS):
        for u in range(2):
            own[j, 8 * u : 8 * u + 8, :K] = cmat[2 * j + u].T
    own = np.concatenate([six_terms(own), np.zeros((PEERS, 16, 32), bf16)], axis=2)
    return block, p3, own


def six_terms(x):
    h, m, low = parts_of(x, 3)
    return np.concatenate([h, h, h, m, m, low], axis=-1)


BASES = (1, 3, 9)


def pair_table():
    entries = []
    for stage, size in enumerate(BASES):
        for quantity in range(4):
            for i in range(size):
                for j in range(i, size):
                    entries.append((stage, quantity, i, j))
    return entries


PAIRS = pair_table()


def pair_arrays():
    kind = np.full((8, 128), -1, np.int32)
    left = np.zeros((8, 128), np.int32)
    right = np.zeros((8, 128), np.int32)
    twice = np.zeros((8, 128), np.int32)
    for n, (stage, quantity, i, j) in enumerate(PAIRS):
        at = (n // 128, n % 128)
        kind[at] = 4 * stage + quantity
        left[at], right[at] = i, j
        twice[at] = 1 if i == j else 2
    return np.concatenate([kind, left, right, twice], axis=0).astype(np.float32)


def lanes_of(shape):
    return lax.broadcasted_iota(jnp.int32, shape, len(shape) - 1)


def rows_of(shape):
    return lax.broadcasted_iota(jnp.int32, shape, 0)


def stack6(f):
    h = f.astype(bf16)
    rest = f - h.astype(f32)
    m = rest.astype(bf16)
    low = (rest - m.astype(f32)).astype(bf16)
    return jnp.concatenate([h, m, low, h, m, h], axis=0)


def relax_of(rate, flags):
    return (time_step * rate) * (1.0 + flags.astype(f32))


def shift_up(x):
    return pltpu.roll(x, 1, 1)


def shift_down(x):
    return pltpu.roll(x, x.shape[1] - 1, 1)


def diff_up(x):
    return x - shift_up(x)


def diff_down(x):
    return x - shift_down(x)


def copies_of(pairs, sems):
    made = [pltpu.make_async_copy(x, y, sems.at[n]) for n, (x, y) in enumerate(pairs)]
    for copy in made:
        copy.start()
    return made


def sums_kernel(dist_in, p3_in, start_in, packed, edges, dist, p3, start, whole, padded, sems, sends):
    positive = lax.axis_index("vel") >= PEERS // 2
    halves = [pl.ds(u * BLOCK, BLOCK) for u in range(2)]
    pairs = [(p3_in, p3), (start_in, start)]
    pairs += [(dist_in.at[half, :], dist.at[half, :]) for half in halves]
    waits = copies_of(pairs, sems)
    waits[0].wait()
    waits[1].wait()
    padded[...] = jnp.zeros((16, 128), f32)
    padded[0:K, 0:16] = start[...]
    whole[32:40, :] = padded[0:8, :] + pltpu.roll(padded[8:16, :], 16, 1)
    for u in range(2):
        waits[2 + u].wait()
        y = jnp.dot(p3[...], dist[halves[u], :], preferred_element_type=f32)
        w = y[0:8] + y[8:16] + y[16:24]
        whole[8 * u : 8 * u + 8, :] = w[:, 0:128]
        whole[16 + 8 * u : 24 + 8 * u, :] = w[:, 128:256]
    going = copies_of([(whole, packed.at[j]) for j in range(PEERS)], sends)
    e_lane = lanes_of((16, CELLS))
    e_row = rows_of((16, CELLS))
    cell = jnp.where(positive, CELLS - 1 - e_row, e_row)
    pick = jnp.where((e_lane == cell) & (e_row < 3), 1.0, 0.0).astype(bf16)
    for u in range(2):
        e = lax.dot_general(pick, dist[halves[u], :], (((1,), (1,)), ((), ())), preferred_element_type=f32)
        for n in range(3):
            for k in range(8):
                at = 16 * n + 8 * u + k
                edges[at : at + 1, :] = e[n : n + 1, 128 * k : 128 * k + 128]
    for copy in going:
        copy.wait()


N_FIELDS = 28
RIM = 7
SIDE = 13
STRIPS = 512


def own_shifts():
    lane = lanes_of((16, CELLS))

    def up(x):
        return jnp.where(lane == 0, 0.0, pltpu.roll(x, 1, 1))

    def down(x):
        return jnp.where(lane == CELLS - 1, 0.0, pltpu.roll(x, CELLS - 1, 1))

    return up, down


def advance_three(keep, base, ups, downs, up, down):
    out = []
    for _ in range(3):
        base = keep * base
        if ups:
            base = base - (ups[0] - up(ups[0]))
        if downs:
            base = base - (downs[0] - down(downs[0]))
        ups = [keep * x - (y - up(y)) for x, y in zip(ups[:-1], ups[1:])]
        downs = [keep * x - (y - down(y)) for x, y in zip(downs[:-1], downs[1:])]
        out.append(base)
    return out


def fields_of(s1, s2, s3, start, r, mask, diffusion, block, up, down):
    width = r.shape[1]
    keep = 1.0 - r

    def up_diff(x):
        return x - up(x)

    def down_diff(x):
        return x - down(x)

    def times(first, last, inputs):
        stacked = stack6(jnp.concatenate(inputs, axis=1) if len(inputs) > 1 else inputs[0])
        y = jnp.dot(block[16 * first : 16 * last, 128:224], stacked, preferred_element_type=f32)
        out = []
        for n in range(len(inputs)):
            cut = y[:, n * width : (n + 1) * width]
            out.append([cut[16 * g : 16 * g + 16] for g in range(last - first)])
        return out

    def applied(f, coupled):
        return mask * (coupled + diffusion * (2.0 * f - up(f) - down(f)))

    def streamed(g, gp, gm):
        return keep * g - up_diff(gp) - down_diff(gm)

    def streamed_twice(k1, gp, gm, g2p, g2m):
        return keep * k1 - up_diff(keep * gp - up_diff(g2p)) - down_diff(keep * gm - down_diff(g2m))

    ((gc, gcp, gcm, _, _, g2cp, g2cm),) = times(4, 11, [start])
    relaxed = r * gc
    shares = mask * (s1 + relaxed)
    res = mask * (shares - start)
    k1_start = streamed(relaxed, r * gcp, r * gcm)
    k2_start = streamed_twice(k1_start, r * gcp, r * gcm, r * g2cp, r * g2cm)

    def parts(f, ys):
        out = [applied(f, ys[0])]
        k1 = streamed(ys[1], ys[2], ys[3])
        rg = r * ys[4]
        held = rg - f
        out += [mask * (k1 + held), held]
        if len(ys) > 5:
            out.append(streamed_twice(k1, ys[2], ys[3], ys[7], ys[8]))
            out.append(streamed(rg, r * ys[5], r * ys[6]) + held)
        return out

    y_shares, y_res = times(0, 9, [shares, res])
    rg = r * y_shares[4]
    held_shares = rg - shares
    n_shares = streamed(rg, r * y_shares[5], r * y_shares[6]) + held_shares
    p0 = mask * (s2 + k1_start + held_shares)
    e, p1, _, k2_res, n_res = parts(res, y_res)

    y_e, y_p0, y_p1 = times(0, 9, [e, p0, p1])
    ee, p2, _, k2_e, n_e = parts(e, y_e)
    ap0, q3, held_p0 = parts(p0, y_p0[:5])
    ap1, q4, held_p1 = parts(p1, y_p1[:5])
    q0 = mask * (s3 + k2_start + n_shares + held_p0)
    q1 = mask * (k2_res + n_res + held_p1)

    y_p2, y_ap0, y_ap1, y_q0, y_q1, y_q3, y_q4 = times(0, 5, [p2, ap0, ap1, q0, q1, q3, q4])
    ap2, q5, held_p2 = parts(p2, y_p2)
    aap0, q6, _ = parts(ap0, y_ap0)
    aap1, q7, _ = parts(ap1, y_ap1)
    q2 = mask * (k2_e + n_e + held_p2)
    aq0, aq1, aq3, aq4 = (applied(f, y[0]) for f, y in ((q0, y_q0), (q1, y_q1), (q3, y_q3), (q4, y_q4)))

    (y_ap2,) = times(0, 5, [ap2])
    aap2, q8, _ = parts(ap2, y_ap2)
    first = [q2, q5, q6, q7, aq0, aq1, aq3, aq4]
    aq2, aq5, aq6, aq7, aaq0, aaq1, aaq3, aaq4 = (applied(f, y[0]) for f, y in zip(first, times(0, 1, first)))
    second = [q8, aq2, aq5, aq6, aq7]
    aq8, aaq2, aaq5, aaq6, aaq7 = (applied(f, y[0]) for f, y in zip(second, times(0, 1, second)))
    ((y_aq8,),) = times(0, 1, [aq8])
    aaq8 = applied(aq8, y_aq8)

    q = [q0, q1, q2, q3, q4, q5, q6, q7, q8]
    aq = [aq0, aq1, aq2, aq3, aq4, aq5, aq6, aq7, aq8]
    aaq = [aaq0, aaq1, aaq2, aaq3, aaq4, aaq5, aaq6, aaq7, aaq8]
    fields = [start, shares, res, e, p0, p1, p2, ap0, ap1, ap2] + q + aq
    plain = [[res], [p0, p1, p2], q]
    once = [[e], [ap0, ap1, ap2], aq]
    again = [[ee], [aap0, aap1, aap2], aaq]
    return fields, plain, once, again


def inner_products(plain, once, again, counted, table):
    kept_plain = [[counted * x for x in xs] for xs in plain]
    kept_once = [[counted * x for x in xs] for xs in once]
    tiles = counted.shape[1] // 128
    table[208:256, :] = jnp.zeros((48, 128), f32)
    for n, (stage, quantity, i, j) in enumerate(PAIRS):
        a, b = ((kept_plain, plain), (kept_plain, once), (kept_once, once), (kept_once, again))[quantity]
        product = a[stage][i] * b[stage][j]
        folded = product[:, 0:128]
        for t in range(1, tiles):
            folded = folded + product[:, 128 * t : 128 * t + 128]
        table[n : n + 1, :] = jnp.sum(folded[0:8] + folded[8:16], axis=0, keepdims=True)
    ones = jnp.ones((8, 128), f32)
    return [
        lax.dot_general(
            ones,
            table[128 * n : 128 * n + 128, :],
            (((1,), (1,)), ((), ())),
            precision=lax.Precision.HIGHEST,
            preferred_element_type=f32,
        )
        for n in range(2)
    ]


def fields_kernel(n_space, got, known, block, fields, sent, table, line, sems):
    slab = lax.axis_index("space")
    wide = (16, CELLS)
    w = jnp.concatenate([got[:, 16 * t : 16 * t + 16, :].reshape(PEERS * 16, 128) for t in range(2)], axis=1)
    wh = w.astype(bf16)
    w_rest = w - wh.astype(f32)
    wm = w_rest.astype(bf16)
    wl = (w_rest - wm.astype(f32)).astype(bf16)
    y = jnp.dot(block[BLOCK : BLOCK + 336, :], wh, preferred_element_type=f32)
    z = jnp.dot(block[BLOCK : BLOCK + 224, :], wm, preferred_element_type=f32)
    t = jnp.dot(block[BLOCK : BLOCK + 112, :], wl, preferred_element_type=f32)
    mu = ((y[224:336] + z[112:224]) + (y[112:224] + z[0:112])) + t + y[0:112]
    mu = [mu[16 * g : 16 * g + 16] for g in range(7)]

    lane8 = lanes_of((8, 128))
    parts = [[jnp.zeros((8, 128), f32)] * 2 for _ in range(2)]
    for j in range(PEERS):
        tile = got[j, 32:40, :]
        here = lane8 // 16 == j % 8
        for half in range(2):
            amount = (16 * j - 16 * half) % 128
            moved = pltpu.roll(tile, amount, 1) if amount else tile
            parts[half][j // 8] = jnp.where(here, moved, parts[half][j // 8])
    start = jnp.concatenate([jnp.concatenate(x, axis=1) for x in parts], axis=0)

    r = jnp.broadcast_to(known[16:17, 0:CELLS], wide)
    diffusion = jnp.concatenate([known[0:16, 128:256]] * 2, axis=1)
    up, down = own_shifts()
    s1, s2, s3 = advance_three(1.0 - r, mu[0], [mu[1], mu[3], mu[5]], [mu[2], mu[4], mu[6]], up, down)
    out, plain, once, again = fields_of(s1, s2, s3, start, r, 1.0, diffusion, block, up, down)
    for n, f in enumerate(out):
        fields[n] = f
    lane = lanes_of(wide)
    low = jnp.where(slab > 0, RIM, 0)
    high = jnp.where(slab < n_space - 1, CELLS - RIM, CELLS)
    counted = jnp.where((lane >= low) & (lane < high), 1.0, 0.0)
    tops = inner_products(plain, once, again, counted, table)

    lane1 = lanes_of((16, 128))
    row1 = rows_of((16, 128))
    start_relax = jnp.where(rows_of(wide) == K, r, start)
    tile = jnp.zeros((16, 128), f32)
    for n, f in enumerate([s1, s2, s3, start_relax]):
        at = lane1 - 32 * n
        begin = pltpu.roll(f[:, 0:128], 32 * n, 1) if n else f[:, 0:128]
        tile = jnp.where((at >= 0) & (at < SIDE), begin, tile)
        end = pltpu.roll(f[:, 128:256], (32 * n + 16 + SIDE) % 128, 1)
        tile = jnp.where((at >= 16) & (at < 16 + SIDE), end, tile)
        if n < 3:
            begin = pltpu.roll(mu[2 + 2 * n][:, 0:128], 32 * n + SIDE, 1)
            tile = jnp.where((at >= SIDE) & (at < 16), begin, tile)
            end = pltpu.roll(mu[1 + 2 * n][:, 128:256], (32 * n + 32) % 128, 1)
            tile = jnp.where((at >= 16 + SIDE) & (at < 32), end, tile)
    row_a = jnp.broadcast_to(tops[0][0:1], (16, 128))
    row_b = jnp.broadcast_to(tops[1][0:1], (16, 128))
    line[...] = jnp.where(row1 == 14, row_a, jnp.where(row1 == 15, row_b, tile))
    for copy in copies_of([(line, sent.at[j]) for j in range(n_space)], sems):
        copy.wait()


def speeds_of(shape):
    number = 2 * lax.axis_index("vel") + jnp.where(rows_of(shape) >= 8, 1, 0)
    return time_step * jnp.abs((number.astype(f32) + 0.5) * spacing - 4.0)


def bands_of(r, positive):
    a = speeds_of(r.shape)
    stay = 1.0 - r - a

    def before(x):
        return jnp.where(positive, shift_up(x), shift_down(x))

    once = before(stay)
    two = before(once)
    t0 = stay * stay * stay
    t1 = a * (stay * (stay + once) + once * once)
    t2 = a * a * (stay + once + two)
    return t0, t1, t2, a * a * a


def banded(weights, u, distance):
    value = jnp.zeros(distance.shape, f32)
    for n, x in enumerate(weights):
        row = jnp.broadcast_to(x[8 * u : 8 * u + 1, 0:CELLS], distance.shape)
        value = jnp.where(distance == n, row, value)
    return value


def stream_kernel(
    dist_in,
    block_in,
    pairs_in,
    own_in,
    coupling_in,
    diff_in,
    rate_in,
    flags_in,
    out,
    table,
    block,
    dist,
    own6,
    coupling_raw,
    diff_raw,
    rate,
    flags,
    sems,
):
    vel = lax.axis_index("vel")
    positive = vel >= PEERS // 2
    moves = [(rate_in, rate), (flags_in, flags), (dist_in, dist)]
    moves += [(coupling_in, coupling_raw), (diff_in, diff_raw), (own_in.at[vel], own6)]
    moves += [(pairs_in, table.at[24:56, 0:128]), (block_in, block)]
    waits = copies_of(moves, sems)
    waits[0].wait()
    waits[1].wait()
    relax = relax_of(rate[...], flags[...])
    table[16:24, 0:CELLS] = jnp.broadcast_to(relax, (8, CELLS))
    weights = bands_of(jnp.broadcast_to(relax, (16, CELLS)), positive)
    towards = jnp.where(positive, 1, -1)
    distance = (lanes_of((CELLS, CELLS)) - rows_of((CELLS, CELLS))) * towards
    waits[2].wait()
    for u in range(2):
        b = banded(weights, u, distance)
        bh = b.astype(bf16)
        bl = (b - bh.astype(f32)).astype(bf16)
        rows = pl.ds(u * BLOCK, BLOCK)
        x = dist[rows, :]
        value = jnp.dot(x, bh, preferred_element_type=f32)
        value += jnp.dot(x, bl, preferred_element_type=f32)
        out[rows, :] = value

    for copy in waits[3:]:
        copy.wait()
    table[0:16, 0:128] = jnp.zeros((16, 128), f32)
    table[0:K, 0:K] = coupling_raw[...]
    c = table[0:16, 0:128]
    ch = c.astype(bf16).astype(f32)
    cm = (c - ch).astype(bf16).astype(f32)
    pieces = [ch, ch, ch, cm, cm, c - ch - cm]
    six = pieces[0]
    for n in range(1, 6):
        six = six + pltpu.roll(pieces[n], 16 * n, 1)
    block[0:16, 128:256] = six.astype(bf16)
    block[176:192, 128:256] = own6[...]
    shape = (16, K)
    chosen = jnp.where(lanes_of(shape) == rows_of(shape), jnp.broadcast_to(diff_raw[...], shape), 0.0)
    table[0:16, 128:256] = jnp.broadcast_to(jnp.sum(chosen, axis=1, keepdims=True), (16, 128))


UPDATE_ROWS = 512


def strips_of(n_space, sent):
    quarter = lanes_of((16, 128)) // 32
    raw = []
    for n in range(4):
        tiles = []
        for t in range(4):
            tile = jnp.zeros((16, 128), f32)
            for k in range(4):
                j = 4 * t + k
                if j < n_space:
                    amount = 32 * (k - n) % 128
                    moved = pltpu.roll(sent[j], amount, 1) if amount else sent[j]
                    tile = jnp.where(quarter == k, moved, tile)
            tiles.append(tile)
        raw.append(jnp.concatenate(tiles, axis=1))
    shape = (16, STRIPS)
    lane = lanes_of(shape)
    row = rows_of(shape)
    at = (lane + 16) % 32
    valid = (lane >= 16) & (lane < 16 + 32 * (n_space - 1)) & (at < 2 * SIDE)
    mask = jnp.where(valid, 1.0, 0.0)
    moments = jnp.where(row < K, mask, 0.0)
    closer = [pltpu.roll(x, STRIPS - 3, 1) for x in raw]
    arrays = [jnp.where(at < SIDE, x, y) for x, y in zip(raw, closer)]
    r = mask * jnp.broadcast_to(arrays[3][K : K + 1], shape)
    s1, s2, s3, start = (moments * x for x in arrays)
    ups = [jnp.where((at >= SIDE - 3) & (at < SIDE), moments * x, 0.0) for x in closer[:3]]
    downs = [pltpu.roll(x, STRIPS - 16, 1) for x in raw[:3]]
    downs = [jnp.where((at >= SIDE) & (at < SIDE + 3), moments * x, 0.0) for x in downs]
    zero = jnp.zeros(shape, f32)
    over_up = advance_three(1.0 - r, zero, ups, [], shift_up, shift_down)
    over_down = advance_three(1.0 - r, zero, [], downs, shift_up, shift_down)
    s = [x + jnp.where(at < SIDE, y, z) for x, y, z in zip((s1, s2, s3), over_down, over_up)]
    s = [mask * x for x in s]
    counted = jnp.where((at >= SIDE - RIM) & (at < SIDE + RIM), mask, 0.0)
    return s, start, r, mask, counted


def update_kernel(
    n_space,
    sent,
    fields,
    table,
    block,
    base,
    edges_in,
    out,
    macro,
    done,
    macro_part,
    products,
    edges,
    ends,
    sems,
):
    place = lax.axis_index("vel")
    slab = lax.axis_index("space")
    positive = place >= PEERS // 2
    (edge_copy,) = copies_of([(edges_in, edges)], sems.at[pl.ds(ROWS // UPDATE_ROWS + 1, 1)])

    def known(at):
        return table[at : at + 8, 0:128]

    (s1, s2, s3), strip_start, strip_r, strip_mask, counted = strips_of(n_space, sent)
    diffusion = jnp.concatenate([table[0:16, 128:256]] * 4, axis=1)
    strip_fields, plain, once, again = fields_of(
        s1, s2, s3, strip_start, strip_r, strip_mask, diffusion, block, shift_up, shift_down
    )
    tops = inner_products(plain, once, again, counted, products)
    gathered = sent[0, 8:16, :]
    for j in range(1, n_space):
        gathered = gathered + sent[j, 8:16, :]
    row8 = rows_of((8, 128))
    line_a = gathered[6:7] + tops[0][0:1]
    line_b = gathered[7:8] + tops[1][0:1]
    total = jnp.where(row8 == 0, line_a, jnp.where(row8 == 1, line_b, 0.0))
    total = total * known(48)
    cpl = table[0:16, 0:128]
    lane16 = lanes_of((16, 128))
    row16 = rows_of((16, 128))
    size = jnp.sum(jnp.abs(cpl), axis=1, keepdims=True)
    middle = jnp.sum(jnp.where(lane16 == row16, cpl, 0.0), axis=1, keepdims=True)
    real = row16[:, 0:1] < K
    most = jnp.max(jnp.where(real, size + 4.0 * table[0:16, 128:129], 0.0), axis=0, keepdims=True)
    least = jnp.min(jnp.where(real, 2.0 * middle - size, 1e30), axis=0, keepdims=True)
    low_step, high_step = 1.0 / most, 1.0 / least

    def summed(weighted, which):
        picked = jnp.where(known(24) == which, weighted, 0.0)
        return jnp.sum(jnp.sum(picked, axis=0, keepdims=True), axis=1, keepdims=True)

    def clipped(x):
        return jnp.minimum(jnp.maximum(x, low_step), high_step)

    def weights_of(stage, weighted):
        rr, ra, aa, aaa = (summed(weighted, 4 * stage + n) for n in range(4))
        s1 = clipped(rr / ra)
        rr2 = rr - 2.0 * s1 * ra + s1 * s1 * aa
        ra2 = ra - 2.0 * s1 * aa + s1 * s1 * aaa
        s2 = clipped(rr2 / ra2)
        return s1 + s2, -s1 * s2

    li, ri = (known(n).astype(jnp.int32) for n in (32, 40))

    def choose(index, zero, one, two):
        return jnp.where(index == 0, zero, jnp.where(index == 1, one, two))

    a1, b1 = weights_of(0, total)
    a2, b2 = weights_of(1, total * choose(li, 1.0, a1, b1) * choose(ri, 1.0, a1, b1))

    def both(index):
        outer = (index >= 3).astype(jnp.int32) + (index >= 6).astype(jnp.int32)
        return choose(outer, 1.0, a2, b2) * choose(index - 3 * outer, 1.0, a1, b1)

    a3, b3 = weights_of(2, total * both(li) * both(ri))

    def last_fields(at, r):
        start, shares, res, e = (at(n) for n in range(4))
        corr1 = a1 * res + b1 * e
        cur1 = shares + corr1
        res2 = at(4) + a1 * at(5) + b1 * at(6)
        e2 = at(7) + a1 * at(8) + b1 * at(9)
        corr2 = a2 * res2 + b2 * e2
        cur2 = res2 + cur1 + corr2

        def third(first):
            rows = [at(first + 3 * n) + a1 * at(first + 3 * n + 1) + b1 * at(first + 3 * n + 2) for n in range(3)]
            return rows[0] + a2 * rows[1] + b2 * rows[2]

        res3, e3 = third(10), third(19)
        corr3 = a3 * res3 + b3 * e3
        row = rows_of(r.shape)
        scaled = r * jnp.where(row < 5, 1.0, jnp.where(row < 10, 0.0, 1.0 / 3.0))
        f1 = scaled * start + corr1
        f2 = scaled * cur1 + corr2
        f3 = scaled * cur2 + corr3
        return f1, f2, f3, res3 + cur2 + corr3, r

    own = last_fields(lambda n: fields[n], jnp.broadcast_to(table[16:17, 0:CELLS], (16, CELLS)))
    strips = last_fields(lambda n: strip_fields[n], strip_r)
    lane1 = lanes_of((16, 128))
    has_left, has_right = jnp.where(slab > 0, 1, 0), jnp.where(slab < n_space - 1, 1, 0)
    near_left = (lane1 < RIM * has_left)
    near_right = (lane1 >= 128 - RIM * has_right)
    far_left = (lane1 >= 128 - 2 * has_left)
    far_right = (lane1 < 2 * has_right)
    wide = []
    for x, y in zip(own, strips):
        y = pltpu.roll(y, lax.rem(STRIPS + 16 - 32 * slab, STRIPS), 1)[:, 0:128]
        from_left = pltpu.roll(y, 128 - SIDE, 1)
        from_right = pltpu.roll(y, 96 - SIDE, 1)
        tiles = [
            jnp.where(near_left, from_left, x[:, 0:128]),
            jnp.where(near_right, from_right, x[:, 128:256]),
            jnp.where(far_left, from_left, jnp.where(far_right, from_right, 0.0)),
        ]
        wide.append(jnp.concatenate(tiles, axis=1))
    f1, f2, f3, cur3, r = wide
    mine = pltpu.roll(cur3[:, 0:CELLS], lax.rem(CELLS - 16 * place, CELLS), 1)
    macro_part[...] = mine[0:K, 0:16]
    macro_copy = pltpu.make_async_copy(macro_part, macro, sems.at[ROWS // UPDATE_ROWS])
    macro_copy.start()
    y = jnp.dot(
        block[176:192, 128:224], stack6(jnp.concatenate([f1, f2, f3], axis=1)), preferred_element_type=f32
    )
    y1, y2, y3 = (y[:, n * WIDE : (n + 1) * WIDE] for n in range(3))
    a = speeds_of((16, WIDE))
    stay = 1.0 - r - a

    def moved(x):
        return stay * x + a * jnp.where(positive, shift_up(x), shift_down(x))

    h = (moved(moved(y1) + y2) + y3)[:, 0:CELLS]
    hh = h.astype(bf16).astype(f32)
    hm = (h - hh).astype(bf16).astype(f32)

    weights = bands_of(r, positive)
    towards = jnp.where(positive, 1, -1)
    at8 = rows_of((8, CELLS))
    at8 = jnp.where(positive, -1 - at8, at8 + CELLS)
    distance = (lanes_of((8, CELLS)) - at8) * towards
    ends[...] = jnp.zeros((16, ROWS), f32)
    edge_copy.wait()
    for n in range(3):
        for k in range(16):
            row = edges[16 * n + k : 16 * n + k + 1, :]
            ends[n : n + 1, 128 * k : 128 * k + 128] = row
            ends[8 + n : 9 + n, 128 * k : 128 * k + 128] = row

    sends = [macro_copy]
    for u in range(2):
        hu, mu = hh[8 * u : 8 * u + 8], hm[8 * u : 8 * u + 8]
        mixed = jnp.concatenate([hu, mu, hu, jnp.zeros((104, CELLS), f32)], axis=0).astype(bf16)
        b = banded(weights, u, distance)
        bh = b.astype(bf16).astype(f32)
        b = jnp.concatenate([bh, b - bh], axis=0).astype(bf16)
        for n in range(BLOCK // UPDATE_ROWS):
            part = u * (BLOCK // UPDATE_ROWS) + n
            rows = pl.ds(part * UPDATE_ROWS, UPDATE_ROWS)
            value = jnp.dot(block[pl.ds(n * UPDATE_ROWS, UPDATE_ROWS), 0:128], mixed, preferred_element_type=f32)
            value += lax.dot_general(
                ends[:, rows].astype(bf16), b, (((0,), (0,)), ((), ())), preferred_element_type=f32
            )
            done[rows, :] = (base[rows, :] + value).astype(bf16)
            copy = pltpu.make_async_copy(done.at[rows, :], out.at[rows, :], sems.at[part])
            copy.start()
            sends.append(copy)
    for copy in sends:
        copy.wait()


def vmem():
    return pl.BlockSpec(memory_space=pltpu.VMEM)


def hbm():
    return pl.BlockSpec(memory_space=pltpu.HBM)


def shaped(shape, dtype=f32):
    return pltpu.VMEM(shape, dtype)


def stored(shape, dtype=f32):
    return pltpu.HBM(shape, dtype)


def placed_at(space, arrays):
    return [pltpu.with_memory_space_constraint(x, space) for x in arrays]


def near(*arrays):
    return placed_at(pltpu.VMEM, arrays)


def far(*arrays):
    return placed_at(pltpu.HBM, arrays)


def limit(mib):
    return pltpu.CompilerParams(vmem_limit_bytes=mib * 2**20)


def make_per_device(n_space):
    block, p3, own6 = grid_constants()
    pairs = pair_arrays()

    def per_device(velocity_dist, macro_state, collision_rate, wall_flags, diffusivity, coupling):
        rate = collision_rate.reshape(1, CELLS)
        flags = wall_flags.reshape(1, CELLS)
        packed, edges = pl.pallas_call(
            sums_kernel,
            out_shape=(stored((PEERS, 40, 128)), stored((48, 128))),
            in_specs=[hbm()] * 3,
            out_specs=(hbm(), vmem()),
            scratch_shapes=[
                pltpu.VMEM((ROWS, CELLS), bf16),
                pltpu.VMEM((32, BLOCK), bf16),
                pltpu.VMEM((K, 16), f32),
                pltpu.VMEM((40, 128), f32),
                pltpu.VMEM((16, 128), f32),
                pltpu.SemaphoreType.DMA((4,)),
                pltpu.SemaphoreType.DMA((PEERS,)),
            ],
            compiler_params=limit(8),
            name="sums",
        )(*far(velocity_dist, jnp.asarray(p3), macro_state))
        got = lax.all_to_all(packed, "vel", split_axis=0, concat_axis=0, tiled=True)
        rising = [(i, i + 1) for i in range(n_space - 1)]
        half = PEERS // 2
        downwind = [(i * PEERS + n, j * PEERS + n) for i, j in rising for n in range(half, PEERS)]
        downwind += [(j * PEERS + n, i * PEERS + n) for i, j in rising for n in range(half)]
        edges = lax.ppermute(edges, ("space", "vel"), downwind)
        base, known, constants = pl.pallas_call(
            stream_kernel,
            out_shape=(shaped((ROWS, CELLS)), shaped((56, WIDE)), shaped(block.shape, bf16)),
            in_specs=[hbm()] * 8,
            out_specs=(vmem(),) * 3,
            scratch_shapes=[
                pltpu.VMEM((ROWS, CELLS), bf16),
                pltpu.VMEM((16, 128), bf16),
                pltpu.VMEM((K, K), f32),
                pltpu.VMEM((1, K), f32),
                pltpu.VMEM((1, CELLS), f32),
                pltpu.VMEM((1, CELLS), jnp.int32),
                pltpu.SemaphoreType.DMA((8,)),
            ],
            compiler_params=limit(16),
            cost_estimate=pl.CostEstimate(flops=600_000_000, bytes_accessed=4_000_000, transcendentals=0),
            name="stream",
        )(
            *far(velocity_dist, *(jnp.asarray(x) for x in (block, pairs, own6))),
            *far(coupling, diffusivity.reshape(1, K), rate, flags),
        )
        got, base, edges = lax.optimization_barrier((got, base, edges))
        fields, sent = pl.pallas_call(
            lambda *refs: fields_kernel(n_space, *refs),
            out_shape=(shaped((N_FIELDS, 16, CELLS)), stored((n_space, 16, 128))),
            in_specs=[vmem()] * 3,
            out_specs=(vmem(), hbm()),
            scratch_shapes=[
                pltpu.VMEM((256, 128), f32),
                pltpu.VMEM((16, 128), f32),
                pltpu.SemaphoreType.DMA((n_space,)),
            ],
            compiler_params=limit(12),
            name="fields",
        )(*near(got, known, constants))
        sent = lax.all_to_all(sent, "space", split_axis=0, concat_axis=0, tiled=True)
        return pl.pallas_call(
            lambda *refs: update_kernel(n_space, *refs),
            out_shape=(stored((ROWS, CELLS), bf16), stored((K, 16))),
            in_specs=[vmem()] * 5 + [hbm()],
            out_specs=(hbm(), hbm()),
            scratch_shapes=[
                pltpu.VMEM((ROWS, CELLS), bf16),
                pltpu.VMEM((K, 16), f32),
                pltpu.VMEM((256, 128), f32),
                pltpu.VMEM((48, 128), f32),
                pltpu.VMEM((16, ROWS), f32),
                pltpu.SemaphoreType.DMA((ROWS // UPDATE_ROWS + 2,)),
            ],
            compiler_params=limit(12),
            name="update",
        )(*near(sent, fields, known, constants, base), *far(edges))

    return per_device


def solution(mesh):
    placed = (P("vel", "space"), P(None, ("space", "vel")), P("space"), P("space"), P(), P())
    return jax.shard_map(
        make_per_device(mesh.shape["space"]),
        mesh=mesh,
        in_specs=placed,
        out_specs=(P("vel", "space"), P(None, ("space", "vel"))),
        check_vma=False,
    )
```

```python
import math

import jax
import jax.numpy as jnp
import numpy as np
from jax import lax
from jax.experimental import pallas as pl
from jax.experimental.pallas import tpu as pltpu
from jax.sharding import PartitionSpec as P

NV1 = 32
K = 13
time_step = 0.125
spacing = 8.0 / NV1
CELLS = 256
WIDE = 384
PEERS = 16
ROWS = 2048
BLOCK = 1024
bf16 = jnp.bfloat16
f32 = jnp.float32


def parts_of(x, number):
    rest = np.asarray(x, np.float64)
    out = []
    for _ in range(number):
        piece = rest.astype(np.float32).astype(bf16)
        out.append(piece)
        rest = rest - piece.astype(np.float64)
    return out


def grid_constants():
    v = (np.arange(NV1) + 0.5) * spacing - 4.0
    w = np.exp(-0.5 * v * v) * spacing / math.sqrt(2.0 * math.pi)
    vy, vz = np.repeat(v, NV1), np.tile(v, NV1)
    wyz = np.repeat(w, NV1) * np.tile(w, NV1)
    one = np.ones_like(vy)
    yz = vy * vy + vz * vz
    phi = np.stack([one, vy, vz, vy * vz, vy * vy, vz * vz, vy * yz, vz * yz])
    cmat = np.zeros((NV1, K, 8))
    for i, x in enumerate(v):
        c = cmat[i]
        c[0, 0] = 1.0
        c[1, 0] = x
        c[2, 1] = 1.0
        c[3, 2] = 1.0
        c[4, 0] = (x * x - 3.0) / math.sqrt(6.0)
        c[4, 4] = c[4, 5] = 1.0 / math.sqrt(6.0)
        c[5, 1] = x
        c[6, 2] = x
        c[7, 3] = 1.0
        c[8, 0] = 0.5 * x * x
        c[8, 4] = -0.5
        c[9, 0] = x * x / math.sqrt(12.0)
        c[9, 4] = 1.0 / math.sqrt(12.0)
        c[9, 5] = -2.0 / math.sqrt(12.0)
        c[10, 0] = x * (x * x - 5.0) / math.sqrt(10.0)
        c[10, 4] = c[10, 5] = x / math.sqrt(10.0)
        c[11, 1] = (x * x - 5.0) / math.sqrt(10.0)
        c[11, 6] = 1.0 / math.sqrt(10.0)
        c[12, 2] = (x * x - 5.0) / math.sqrt(10.0)
        c[12, 7] = 1.0 / math.sqrt(10.0)
    a = time_step * np.abs(v)
    plus = v > 0.0
    proj = phi * wyz
    groups = [np.ones(NV1)]
    for power in (1, 2, 3):
        groups += [a**power * plus, a**power * ~plus]
    big = np.zeros((7 * 16, 8 * NV1))
    for g, factor in enumerate(groups):
        for i in range(NV1):
            big[16 * g : 16 * g + K, 8 * i : 8 * i + 8] = factor[i] * w[i] * cmat[i]
    gram2 = proj @ phi.T
    shakhov = np.array([1.0] * 5 + [0.0] * 5 + [1.0 / 3.0] * 3)

    def between(factor):
        out = np.zeros((16, 16))
        for i in range(NV1):
            out[:K, :K] += factor[i] * w[i] * cmat[i] @ gram2 @ cmat[i].T
        return out

    c16 = np.zeros(16)
    c16[:K] = shakhov
    g, gp, gm, g2p, g2m = (between(groups[k]) for k in (0, 1, 2, 3, 4))
    mats = [g, gp, gm, g * c16, gp * c16, gm * c16, g2p, g2m, g2p * c16, g2m * c16]
    block = np.zeros((BLOCK + 336, 256), bf16)
    block[16:176, 128:224] = six_terms(np.concatenate(mats, axis=0))
    block[BLOCK:] = np.concatenate(parts_of(big, 3), axis=0)
    p3 = np.concatenate(parts_of(proj, 3) + [np.zeros((8, BLOCK), bf16)], axis=0)
    ph, pm = parts_of(phi.T, 2)
    block[0:BLOCK, 0:24] = np.concatenate([ph, ph, pm], axis=1)
    own = np.zeros((PEERS, 16, 16))
    for j in range(PEERS):
        for u in range(2):
            own[j, 8 * u : 8 * u + 8, :K] = cmat[2 * j + u].T
    own = np.concatenate([six_terms(own), np.zeros((PEERS, 16, 32), bf16)], axis=2)
    return block, p3, own


def six_terms(x):
    h, m, low = parts_of(x, 3)
    return np.concatenate([h, h, h, m, m, low], axis=-1)


BASES = (1, 3, 9)


def pair_table():
    entries = []
    for stage, size in enumerate(BASES):
        for quantity in range(4):
            for i in range(size):
                for j in range(i, size):
                    entries.append((stage, quantity, i, j))
    return entries


PAIRS = pair_table()


def pair_arrays():
    kind = np.full((8, 128), -1, np.int32)
    left = np.zeros((8, 128), np.int32)
    right = np.zeros((8, 128), np.int32)
    twice = np.zeros((8, 128), np.int32)
    for n, (stage, quantity, i, j) in enumerate(PAIRS):
        at = (n // 128, n % 128)
        kind[at] = 4 * stage + quantity
        left[at], right[at] = i, j
        twice[at] = 1 if i == j else 2
    return np.concatenate([kind, left, right, twice], axis=0).astype(np.float32)


def lanes_of(shape):
    return lax.broadcasted_iota(jnp.int32, shape, len(shape) - 1)


def rows_of(shape):
    return lax.broadcasted_iota(jnp.int32, shape, 0)


def stack6(f):
    h = f.astype(bf16)
    rest = f - h.astype(f32)
    m = rest.astype(bf16)
    low = (rest - m.astype(f32)).astype(bf16)
    return jnp.concatenate([h, m, low, h, m, h], axis=0)


def relax_of(rate, flags):
    return (time_step * rate) * (1.0 + flags.astype(f32))


def shift_up(x):
    return pltpu.roll(x, 1, 1)


def shift_down(x):
    return pltpu.roll(x, x.shape[1] - 1, 1)


def diff_up(x):
    return x - shift_up(x)


def diff_down(x):
    return x - shift_down(x)


def copies_of(pairs, sems):
    made = [pltpu.make_async_copy(x, y, sems.at[n]) for n, (x, y) in enumerate(pairs)]
    for copy in made:
        copy.start()
    return made


def sums_kernel(dist_in, p3_in, start_in, packed, edges, dist, p3, start, padded, sems):
    positive = lax.axis_index("vel") >= PEERS // 2
    halves = [pl.ds(u * BLOCK, BLOCK) for u in range(2)]
    pairs = [(p3_in, p3), (start_in, start)]
    pairs += [(dist_in.at[half, :], dist.at[half, :]) for half in halves]
    waits = copies_of(pairs, sems)
    waits[0].wait()
    waits[1].wait()
    padded[...] = jnp.zeros((16, 128), f32)
    padded[0:K, 0:16] = start[...]
    owned = padded[0:8, :] + pltpu.roll(padded[8:16, :], 16, 1)
    for j in range(PEERS):
        packed[j, 32:40, :] = owned
    for u in range(2):
        waits[2 + u].wait()
        y = jnp.dot(p3[...], dist[halves[u], :], preferred_element_type=f32)
        w = y[0:8] + y[8:16] + y[16:24]
        for j in range(PEERS):
            packed[j, 8 * u : 8 * u + 8, :] = w[:, 0:128]
            packed[j, 16 + 8 * u : 24 + 8 * u, :] = w[:, 128:256]
    e_lane = lanes_of((16, CELLS))
    e_row = rows_of((16, CELLS))
    cell = jnp.where(positive, CELLS - 1 - e_row, e_row)
    pick = jnp.where((e_lane == cell) & (e_row < 3), 1.0, 0.0).astype(bf16)
    for u in range(2):
        e = lax.dot_general(pick, dist[halves[u], :], (((1,), (1,)), ((), ())), preferred_element_type=f32)
        for n in range(3):
            for k in range(8):
                at = 16 * n + 8 * u + k
                edges[at : at + 1, :] = e[n : n + 1, 128 * k : 128 * k + 128]


N_FIELDS = 28
RIM = 7
SIDE = 13
STRIPS = 512


def tiles_of(x):
    return [x[:, 128 * t : 128 * t + 128] for t in range(x.shape[1] // 128)]


def own_shifts():
    lane = lanes_of((16, 128))
    zero = jnp.zeros((16, 128), f32)

    def up(x):
        first, second = (pltpu.roll(t, 1, 1) for t in tiles_of(x))
        return jnp.concatenate([jnp.where(lane == 0, zero, first), jnp.where(lane == 0, first, second)], axis=1)

    def down(x):
        first, second = (pltpu.roll(t, 127, 1) for t in tiles_of(x))
        return jnp.concatenate([jnp.where(lane == 127, second, first), jnp.where(lane == 127, zero, second)], axis=1)

    return up, down


def strip_up(x):
    return jnp.concatenate([pltpu.roll(t, 1, 1) for t in tiles_of(x)], axis=1)


def strip_down(x):
    return jnp.concatenate([pltpu.roll(t, 127, 1) for t in tiles_of(x)], axis=1)


def advance_three(keep, base, ups, downs, up, down):
    out = []
    for _ in range(3):
        base = keep * base
        if ups:
            base = base - (ups[0] - up(ups[0]))
        if downs:
            base = base - (downs[0] - down(downs[0]))
        ups = [keep * x - (y - up(y)) for x, y in zip(ups[:-1], ups[1:])]
        downs = [keep * x - (y - down(y)) for x, y in zip(downs[:-1], downs[1:])]
        out.append(base)
    return out


def fields_of(s1, s2, s3, start, r, mask, diffusion, block, up, down):
    width = r.shape[1]
    keep = 1.0 - r

    def up_diff(x):
        return x - up(x)

    def down_diff(x):
        return x - down(x)

    def times(first, last, inputs):
        stacked = stack6(jnp.concatenate(inputs, axis=1) if len(inputs) > 1 else inputs[0])
        y = jnp.dot(block[16 * first : 16 * last, 128:224], stacked, preferred_element_type=f32)
        out = []
        for n in range(len(inputs)):
            cut = y[:, n * width : (n + 1) * width]
            out.append([cut[16 * g : 16 * g + 16] for g in range(last - first)])
        return out

    def applied(f, coupled):
        return mask * (coupled + diffusion * (2.0 * f - up(f) - down(f)))

    def streamed(g, gp, gm):
        return keep * g - up_diff(gp) - down_diff(gm)

    def streamed_twice(k1, gp, gm, g2p, g2m):
        return keep * k1 - up_diff(keep * gp - up_diff(g2p)) - down_diff(keep * gm - down_diff(g2m))

    ((gc, gcp, gcm, _, _, g2cp, g2cm),) = times(4, 11, [start])
    relaxed = r * gc
    shares = mask * (s1 + relaxed)
    res = mask * (shares - start)
    k1_start = streamed(relaxed, r * gcp, r * gcm)
    k2_start = streamed_twice(k1_start, r * gcp, r * gcm, r * g2cp, r * g2cm)

    def parts(f, ys):
        out = [applied(f, ys[0])]
        k1 = streamed(ys[1], ys[2], ys[3])
        rg = r * ys[4]
        held = rg - f
        out += [mask * (k1 + held), held]
        if len(ys) > 5:
            out.append(streamed_twice(k1, ys[2], ys[3], ys[7], ys[8]))
            out.append(streamed(rg, r * ys[5], r * ys[6]) + held)
        return out

    y_shares, y_res = times(0, 9, [shares, res])
    rg = r * y_shares[4]
    held_shares = rg - shares
    n_shares = streamed(rg, r * y_shares[5], r * y_shares[6]) + held_shares
    p0 = mask * (s2 + k1_start + held_shares)
    e, p1, _, k2_res, n_res = parts(res, y_res)

    y_e, y_p0, y_p1 = times(0, 9, [e, p0, p1])
    ee, p2, _, k2_e, n_e = parts(e, y_e)
    ap0, q3, held_p0 = parts(p0, y_p0[:5])
    ap1, q4, held_p1 = parts(p1, y_p1[:5])
    q0 = mask * (s3 + k2_start + n_shares + held_p0)
    q1 = mask * (k2_res + n_res + held_p1)

    y_p2, y_ap0, y_ap1, y_q0, y_q1, y_q3, y_q4 = times(0, 5, [p2, ap0, ap1, q0, q1, q3, q4])
    ap2, q5, held_p2 = parts(p2, y_p2)
    aap0, q6, _ = parts(ap0, y_ap0)
    aap1, q7, _ = parts(ap1, y_ap1)
    q2 = mask * (k2_e + n_e + held_p2)
    aq0, aq1, aq3, aq4 = (applied(f, y[0]) for f, y in ((q0, y_q0), (q1, y_q1), (q3, y_q3), (q4, y_q4)))

    (y_ap2,) = times(0, 5, [ap2])
    aap2, q8, _ = parts(ap2, y_ap2)
    first = [q2, q5, q6, q7, aq0, aq1, aq3, aq4]
    aq2, aq5, aq6, aq7, aaq0, aaq1, aaq3, aaq4 = (applied(f, y[0]) for f, y in zip(first, times(0, 1, first)))
    second = [q8, aq2, aq5, aq6, aq7]
    aq8, aaq2, aaq5, aaq6, aaq7 = (applied(f, y[0]) for f, y in zip(second, times(0, 1, second)))
    ((y_aq8,),) = times(0, 1, [aq8])
    aaq8 = applied(aq8, y_aq8)

    q = [q0, q1, q2, q3, q4, q5, q6, q7, q8]
    aq = [aq0, aq1, aq2, aq3, aq4, aq5, aq6, aq7, aq8]
    aaq = [aaq0, aaq1, aaq2, aaq3, aaq4, aaq5, aaq6, aaq7, aaq8]
    fields = [start, shares, res, e, p0, p1, p2, ap0, ap1, ap2] + q + aq
    plain = [[res], [p0, p1, p2], q]
    once = [[e], [ap0, ap1, ap2], aq]
    again = [[ee], [aap0, aap1, aap2], aaq]
    return fields, plain, once, again


EARLY = 4 * 1 + 4 * 6


def inner_products(plain, once, again, counted, table):
    lefts = [[[counted * x for x in xs] for xs in xss] for xss in (plain, once)]
    rights = [plain, once, again]
    if counted.shape[1] == STRIPS:
        def folded(x):
            halves = [x[:, 0:256], x[:, 256:512]]
            moved = [pltpu.roll(t, 16, 1) for t in tiles_of(halves[1])]
            return halves[0] + jnp.concatenate(moved, axis=1)

        lefts = [[[folded(x) for x in xs] for xs in xss] for xss in lefts]
        rights = lefts + [[[folded(counted * x) for x in xs] for xs in again]]
    table[EARLY:256, :] = jnp.zeros((256 - EARLY, 128), f32)
    table[256 : 256 + EARLY, :] = jnp.zeros((EARLY, 128), f32)
    table[len(PAIRS) + 128 : 384, :] = jnp.zeros((256 - len(PAIRS), 128), f32)
    ones = jnp.ones((8, 128), f32)
    tops = []
    for n, (stage, quantity, i, j) in enumerate(PAIRS):
        x, y = ((0, 0), (0, 1), (1, 1), (1, 2))[quantity]
        product = lefts[x][stage][i] * rights[y][stage][j]
        half = product[:, 0:128] + product[:, 128:256]
        at = n if n < EARLY else n + 128
        table[at : at + 1, :] = jnp.sum(half[0:8] + half[8:16], axis=0, keepdims=True)
    for n in range(3):
        tops.append(
            lax.dot_general(
                ones,
                table[128 * n : 128 * n + 128, :],
                (((1,), (1,)), ((), ())),
                precision=lax.Precision.HIGHEST,
                preferred_element_type=f32,
            )
        )
    return tops


def fields_kernel(n_space, got, known, block, fields, sent, table):
    slab = lax.axis_index("space")
    wide = (16, CELLS)
    w = jnp.concatenate([got[:, 16 * t : 16 * t + 16, :].reshape(PEERS * 16, 128) for t in range(2)], axis=1)
    wh = w.astype(bf16)
    w_rest = w - wh.astype(f32)
    wm = w_rest.astype(bf16)
    wl = (w_rest - wm.astype(f32)).astype(bf16)
    y = jnp.dot(block[BLOCK : BLOCK + 336, :], wh, preferred_element_type=f32)
    z = jnp.dot(block[BLOCK : BLOCK + 224, :], wm, preferred_element_type=f32)
    t = jnp.dot(block[BLOCK : BLOCK + 112, :], wl, preferred_element_type=f32)
    mu = ((y[224:336] + z[112:224]) + (y[112:224] + z[0:112])) + t + y[0:112]
    mu = [mu[16 * g : 16 * g + 16] for g in range(7)]

    lane8 = lanes_of((8, 128))
    parts = [[jnp.zeros((8, 128), f32)] * 2 for _ in range(2)]
    for j in range(PEERS):
        tile = got[j, 32:40, :]
        here = lane8 // 16 == j % 8
        for half in range(2):
            amount = (16 * j - 16 * half) % 128
            moved = pltpu.roll(tile, amount, 1) if amount else tile
            parts[half][j // 8] = jnp.where(here, moved, parts[half][j // 8])
    start = jnp.concatenate([jnp.concatenate(x, axis=1) for x in parts], axis=0)

    r = jnp.broadcast_to(known[16:17, 0:CELLS], wide)
    diffusion = jnp.concatenate([known[0:16, 128:256]] * 2, axis=1)
    up, down = own_shifts()
    s1, s2, s3 = advance_three(1.0 - r, mu[0], [mu[1], mu[3], mu[5]], [mu[2], mu[4], mu[6]], up, down)
    out, plain, once, again = fields_of(s1, s2, s3, start, r, 1.0, diffusion, block, up, down)
    for n, f in enumerate(out):
        fields[n] = f
    lane = lanes_of(wide)
    low = jnp.where(slab > 0, RIM, 0)
    high = jnp.where(slab < n_space - 1, CELLS - RIM, CELLS)
    counted = jnp.where((lane >= low) & (lane < high), 1.0, 0.0)
    tops = inner_products(plain, once, again, counted, table)

    lane1 = lanes_of((16, 128))
    row1 = rows_of((16, 128))
    start_relax = jnp.where(rows_of(wide) == K, r, start)
    tile = jnp.zeros((16, 128), f32)
    for n, f in enumerate([s1, s2, s3, start_relax]):
        at = lane1 - 32 * n
        begin = pltpu.roll(f[:, 0:128], 32 * n, 1) if n else f[:, 0:128]
        tile = jnp.where((at >= 0) & (at < SIDE), begin, tile)
        end = pltpu.roll(f[:, 128:256], (32 * n + 16 + SIDE) % 128, 1)
        tile = jnp.where((at >= 16) & (at < 16 + SIDE), end, tile)
        if n < 3:
            begin = pltpu.roll(mu[2 + 2 * n][:, 0:128], 32 * n + SIDE, 1)
            tile = jnp.where((at >= SIDE) & (at < 16), begin, tile)
            end = pltpu.roll(mu[1 + 2 * n][:, 128:256], (32 * n + 32) % 128, 1)
            tile = jnp.where((at >= 16 + SIDE) & (at < 32), end, tile)
    row_a = jnp.broadcast_to(tops[0][0:1] + tops[1][0:1], (16, 128))
    row_b = jnp.broadcast_to(tops[2][0:1], (16, 128))
    tile = jnp.where(row1 == 14, row_a, jnp.where(row1 == 15, row_b, tile))
    for j in range(n_space):
        sent[j] = tile


def speeds_of(shape):
    number = 2 * lax.axis_index("vel") + jnp.where(rows_of(shape) >= 8, 1, 0)
    return time_step * jnp.abs((number.astype(f32) + 0.5) * spacing - 4.0)


def bands_of(r, positive):
    a = speeds_of(r.shape)
    stay = 1.0 - r - a

    def before(x):
        return jnp.where(positive, shift_up(x), shift_down(x))

    once = before(stay)
    two = before(once)
    t0 = stay * stay * stay
    t1 = a * (stay * (stay + once) + once * once)
    t2 = a * a * (stay + once + two)
    return t0, t1, t2, a * a * a


def banded(weights, u, distance):
    value = jnp.zeros(distance.shape, f32)
    for n, x in enumerate(weights):
        row = jnp.broadcast_to(x[8 * u : 8 * u + 1, 0 : distance.shape[1]], distance.shape)
        value = jnp.where(distance == n, row, value)
    return value


def stream_kernel(
    dist_in,
    block_in,
    pairs_in,
    own_in,
    coupling_in,
    diff_in,
    rate_in,
    flags_in,
    out,
    table,
    block,
    dist,
    own6,
    coupling_raw,
    diff_raw,
    rate,
    flags,
    sems,
):
    vel = lax.axis_index("vel")
    positive = vel >= PEERS // 2
    moves = [(rate_in, rate), (flags_in, flags), (dist_in, dist)]
    moves += [(coupling_in, coupling_raw), (diff_in, diff_raw), (own_in.at[vel], own6)]
    moves += [(pairs_in, table.at[24:56, 0:128]), (block_in, block)]
    waits = copies_of(moves, sems)
    waits[0].wait()
    waits[1].wait()
    relax = relax_of(rate[...], flags[...])
    table[16:24, 0:CELLS] = jnp.broadcast_to(relax, (8, CELLS))
    weights = bands_of(jnp.broadcast_to(relax, (16, CELLS)), positive)
    towards = jnp.where(positive, 1, -1)
    distance = (lanes_of((CELLS, CELLS)) - rows_of((CELLS, CELLS))) * towards
    waits[2].wait()
    for u in range(2):
        b = banded(weights, u, distance)
        bh = b.astype(bf16)
        bl = (b - bh.astype(f32)).astype(bf16)
        rows = pl.ds(u * BLOCK, BLOCK)
        x = dist[rows, :]
        value = jnp.dot(x, bh, preferred_element_type=f32)
        value += jnp.dot(x, bl, preferred_element_type=f32)
        out[rows, :] = value

    for copy in waits[3:]:
        copy.wait()
    table[0:16, 0:128] = jnp.zeros((16, 128), f32)
    table[0:K, 0:K] = coupling_raw[...]
    c = table[0:16, 0:128]
    ch = c.astype(bf16).astype(f32)
    cm = (c - ch).astype(bf16).astype(f32)
    pieces = [ch, ch, ch, cm, cm, c - ch - cm]
    six = pieces[0]
    for n in range(1, 6):
        six = six + pltpu.roll(pieces[n], 16 * n, 1)
    block[0:16, 128:256] = six.astype(bf16)
    block[176:192, 128:256] = own6[...]
    shape = (16, K)
    chosen = jnp.where(lanes_of(shape) == rows_of(shape), jnp.broadcast_to(diff_raw[...], shape), 0.0)
    table[0:16, 128:256] = jnp.broadcast_to(jnp.sum(chosen, axis=1, keepdims=True), (16, 128))


UPDATE_ROWS = 512


def strips_of(n_space, sent):
    quarter = lanes_of((16, 128)) // 32
    raw = []
    for n in range(4):
        tiles = []
        for t in range(4):
            tile = jnp.zeros((16, 128), f32)
            for k in range(4):
                j = 4 * t + k
                if j < n_space:
                    amount = 32 * (k - n) % 128
                    moved = pltpu.roll(sent[j], amount, 1) if amount else sent[j]
                    tile = jnp.where(quarter == k, moved, tile)
            tiles.append(tile)
        raw.append(jnp.concatenate(tiles, axis=1))
    shape = (16, STRIPS)
    lane = lanes_of(shape)
    row = rows_of(shape)
    at = lane % 32
    valid = (lane < 32 * (n_space - 1)) & (at < 2 * SIDE)
    mask = jnp.where(valid, 1.0, 0.0)
    moments = jnp.where(row < K, mask, 0.0)
    raw = [pltpu.roll(x, STRIPS - 16, 1) for x in raw]
    closer = [pltpu.roll(x, STRIPS - 3, 1) for x in raw]
    arrays = [jnp.where(at < SIDE, x, y) for x, y in zip(raw, closer)]
    r = mask * jnp.broadcast_to(arrays[3][K : K + 1], shape)
    s1, s2, s3, start = (moments * x for x in arrays)
    ups = [jnp.where((at >= SIDE - 3) & (at < SIDE), moments * x, 0.0) for x in closer[:3]]
    downs = [pltpu.roll(x, STRIPS - 16, 1) for x in raw[:3]]
    downs = [jnp.where((at >= SIDE) & (at < SIDE + 3), moments * x, 0.0) for x in downs]
    zero = jnp.zeros(shape, f32)
    over_up = advance_three(1.0 - r, zero, ups, [], strip_up, strip_down)
    over_down = advance_three(1.0 - r, zero, [], downs, strip_up, strip_down)
    s = [x + jnp.where(at < SIDE, y, z) for x, y, z in zip((s1, s2, s3), over_down, over_up)]
    s = [mask * x for x in s]
    counted = jnp.where((at >= SIDE - RIM) & (at < SIDE + RIM), mask, 0.0)
    return s, start, r, mask, counted


def update_kernel(
    n_space,
    sent,
    fields,
    table,
    block,
    base,
    edges_in,
    out,
    macro,
    done,
    macro_part,
    products,
    edges,
    ends,
    sems,
):
    place = lax.axis_index("vel")
    slab = lax.axis_index("space")
    positive = place >= PEERS // 2
    (edge_copy,) = copies_of([(edges_in, edges)], sems.at[pl.ds(ROWS // UPDATE_ROWS + 1, 1)])

    def known(at):
        return table[at : at + 8, 0:128]

    (s1, s2, s3), strip_start, strip_r, strip_mask, counted = strips_of(n_space, sent)
    diffusion = jnp.concatenate([table[0:16, 128:256]] * 4, axis=1)
    strip_fields, plain, once, again = fields_of(
        s1, s2, s3, strip_start, strip_r, strip_mask, diffusion, block, strip_up, strip_down
    )
    tops = inner_products(plain, once, again, counted, products)
    gathered = sent[0, 8:16, :]
    for j in range(1, n_space):
        gathered = gathered + sent[j, 8:16, :]
    row8 = rows_of((8, 128))
    early = jnp.where(row8 == 0, gathered[6:7] + tops[0][0:1], 0.0) * known(48)
    line_a = gathered[6:7] + tops[1][0:1]
    line_b = gathered[7:8] + tops[2][0:1]
    total = jnp.where(row8 == 0, line_a, jnp.where(row8 == 1, line_b, 0.0))
    total = total * known(48)
    cpl = table[0:16, 0:128]
    lane16 = lanes_of((16, 128))
    row16 = rows_of((16, 128))
    size = jnp.sum(jnp.abs(cpl), axis=1, keepdims=True)
    middle = jnp.sum(jnp.where(lane16 == row16, cpl, 0.0), axis=1, keepdims=True)
    real = row16[:, 0:1] < K
    most = jnp.max(jnp.where(real, size + 4.0 * table[0:16, 128:129], 0.0), axis=0, keepdims=True)
    least = jnp.min(jnp.where(real, 2.0 * middle - size, 1e30), axis=0, keepdims=True)
    low_step, high_step = 1.0 / most, 1.0 / least

    def summed(weighted, which):
        picked = jnp.where(known(24) == which, weighted, 0.0)
        return jnp.sum(jnp.sum(picked, axis=0, keepdims=True), axis=1, keepdims=True)

    def clipped(x):
        return jnp.minimum(jnp.maximum(x, low_step), high_step)

    def weights_of(stage, weighted):
        rr, ra, aa, aaa = (summed(weighted, 4 * stage + n) for n in range(4))
        s1 = clipped(rr / ra)
        rr2 = rr - 2.0 * s1 * ra + s1 * s1 * aa
        ra2 = ra - 2.0 * s1 * aa + s1 * s1 * aaa
        s2 = clipped(rr2 / ra2)
        return s1 + s2, -s1 * s2

    li, ri = (known(n).astype(jnp.int32) for n in (32, 40))

    def choose(index, zero, one, two):
        return jnp.where(index == 0, zero, jnp.where(index == 1, one, two))

    a1, b1 = weights_of(0, early)
    a2, b2 = weights_of(1, early * choose(li, 1.0, a1, b1) * choose(ri, 1.0, a1, b1))

    def both(index):
        outer = (index >= 3).astype(jnp.int32) + (index >= 6).astype(jnp.int32)
        return choose(outer, 1.0, a2, b2) * choose(index - 3 * outer, 1.0, a1, b1)

    a3, b3 = weights_of(2, total * both(li) * both(ri))

    def last_fields(at, r):
        start, shares, res, e = (at(n) for n in range(4))
        corr1 = a1 * res + b1 * e
        cur1 = shares + corr1
        res2 = at(4) + a1 * at(5) + b1 * at(6)
        e2 = at(7) + a1 * at(8) + b1 * at(9)
        corr2 = a2 * res2 + b2 * e2
        cur2 = res2 + cur1 + corr2

        def third(first):
            rows = [at(first + 3 * n) + a1 * at(first + 3 * n + 1) + b1 * at(first + 3 * n + 2) for n in range(3)]
            return rows[0] + a2 * rows[1] + b2 * rows[2]

        res3, e3 = third(10), third(19)
        corr3 = a3 * res3 + b3 * e3
        row = rows_of(r.shape)
        scaled = r * jnp.where(row < 5, 1.0, jnp.where(row < 10, 0.0, 1.0 / 3.0))
        f1 = scaled * start + corr1
        f2 = scaled * cur1 + corr2
        f3 = scaled * cur2 + corr3
        return f1, f2, f3, res3 + cur2 + corr3, r

    own = last_fields(lambda n: fields[n], jnp.broadcast_to(table[16:17, 0:CELLS], (16, CELLS)))
    strips = last_fields(lambda n: strip_fields[n], strip_r)
    lane1 = lanes_of((16, 128))
    has_left, has_right = jnp.where(slab > 0, 1, 0), jnp.where(slab < n_space - 1, 1, 0)
    near_left = (lane1 < RIM * has_left)
    near_right = (lane1 >= 128 - RIM * has_right)
    far_left = (lane1 >= 128 - 2 * has_left)
    far_right = (lane1 < 2 * has_right)
    wide = []
    for x, y in zip(own, strips):
        y = pltpu.roll(y, lax.rem(STRIPS + 32 - 32 * slab, STRIPS), 1)[:, 0:128]
        from_left = pltpu.roll(y, 128 - SIDE, 1)
        from_right = pltpu.roll(y, 96 - SIDE, 1)
        tiles = [
            jnp.where(near_left, from_left, x[:, 0:128]),
            jnp.where(near_right, from_right, x[:, 128:256]),
            jnp.where(far_left, from_left, jnp.where(far_right, from_right, 0.0)),
        ]
        wide.append(jnp.concatenate(tiles, axis=1))
    f1, f2, f3, cur3, r = wide
    mine = pltpu.roll(cur3[:, 0:CELLS], lax.rem(CELLS - 16 * place, CELLS), 1)
    macro_part[...] = mine[0:K, 0:16]
    macro_copy = pltpu.make_async_copy(macro_part, macro, sems.at[ROWS // UPDATE_ROWS])
    macro_copy.start()
    y = jnp.dot(
        block[176:192, 128:224], stack6(jnp.concatenate([f1, f2, f3], axis=1)), preferred_element_type=f32
    )
    y1, y2, y3 = (y[:, n * WIDE : (n + 1) * WIDE] for n in range(3))
    a = speeds_of((16, WIDE))
    stay = 1.0 - r - a

    def moved(x):
        return stay * x + a * jnp.where(positive, shift_up(x), shift_down(x))

    h = (moved(moved(y1) + y2) + y3)[:, 0:CELLS]
    hh = h.astype(bf16).astype(f32)
    hm = (h - hh).astype(bf16).astype(f32)

    weights = bands_of(r, positive)
    towards = jnp.where(positive, 1, -1)
    at8 = rows_of((8, 128))
    at8 = jnp.where(positive, -1 - at8, at8 + CELLS)
    low = jnp.where(positive, 0, CELLS - 128)
    distance = (lanes_of((8, 128)) + low - at8) * towards
    weights = [jnp.where(positive, x[:, 0:128], x[:, 128:256]) for x in weights]
    ends[...] = jnp.zeros((16, ROWS), f32)
    edge_copy.wait()
    for n in range(3):
        for k in range(16):
            row = edges[16 * n + k : 16 * n + k + 1, :]
            ends[n : n + 1, 128 * k : 128 * k + 128] = row
            ends[8 + n : 9 + n, 128 * k : 128 * k + 128] = row

    sends = [macro_copy]
    for u in range(2):
        hu, mu = hh[8 * u : 8 * u + 8], hm[8 * u : 8 * u + 8]
        mixed = jnp.concatenate([hu, mu, hu, jnp.zeros((104, CELLS), f32)], axis=0).astype(bf16)
        b = banded(weights, u, distance)
        bh = b.astype(bf16).astype(f32)
        b = jnp.concatenate([bh, b - bh], axis=0).astype(bf16)
        for n in range(BLOCK // UPDATE_ROWS):
            part = u * (BLOCK // UPDATE_ROWS) + n
            rows = pl.ds(part * UPDATE_ROWS, UPDATE_ROWS)
            value = jnp.dot(block[pl.ds(n * UPDATE_ROWS, UPDATE_ROWS), 0:128], mixed, preferred_element_type=f32)
            near = lax.dot_general(ends[:, rows].astype(bf16), b, (((0,), (0,)), ((), ())), preferred_element_type=f32)
            value += base[rows, :]
            done[rows, 0:128] = (value[:, 0:128] + jnp.where(positive, near, 0.0)).astype(bf16)
            done[rows, 128:256] = (value[:, 128:256] + jnp.where(positive, 0.0, near)).astype(bf16)
            copy = pltpu.make_async_copy(done.at[rows, :], out.at[rows, :], sems.at[part])
            copy.start()
            sends.append(copy)
    for copy in sends:
        copy.wait()


def vmem():
    return pl.BlockSpec(memory_space=pltpu.VMEM)


def hbm():
    return pl.BlockSpec(memory_space=pltpu.HBM)


def shaped(shape, dtype=f32):
    return pltpu.VMEM(shape, dtype)


def stored(shape, dtype=f32):
    return pltpu.HBM(shape, dtype)


def placed_at(space, arrays):
    return [pltpu.with_memory_space_constraint(x, space) for x in arrays]


def near(*arrays):
    return placed_at(pltpu.VMEM, arrays)


def far(*arrays):
    return placed_at(pltpu.HBM, arrays)


def limit(mib):
    return pltpu.CompilerParams(vmem_limit_bytes=mib * 2**20)


def make_per_device(n_space):
    block, p3, own6 = grid_constants()
    pairs = pair_arrays()

    def per_device(velocity_dist, macro_state, collision_rate, wall_flags, diffusivity, coupling):
        rate = collision_rate.reshape(1, CELLS)
        flags = wall_flags.reshape(1, CELLS)
        packed, edges = pl.pallas_call(
            sums_kernel,
            out_shape=(shaped((PEERS, 40, 128)), shaped((48, 128))),
            in_specs=[hbm()] * 3,
            out_specs=(vmem(), vmem()),
            scratch_shapes=[
                pltpu.VMEM((ROWS, CELLS), bf16),
                pltpu.VMEM((32, BLOCK), bf16),
                pltpu.VMEM((K, 16), f32),
                pltpu.VMEM((16, 128), f32),
                pltpu.SemaphoreType.DMA((4,)),
            ],
            compiler_params=limit(8),
            name="sums",
        )(*far(velocity_dist, jnp.asarray(p3), macro_state))
        got = lax.all_to_all(packed, "vel", split_axis=0, concat_axis=0, tiled=True)
        rising = [(i, i + 1) for i in range(n_space - 1)]
        half = PEERS // 2
        downwind = [(i * PEERS + n, j * PEERS + n) for i, j in rising for n in range(half, PEERS)]
        downwind += [(j * PEERS + n, i * PEERS + n) for i, j in rising for n in range(half)]
        edges = lax.ppermute(edges, ("space", "vel"), downwind)
        base, known, constants = pl.pallas_call(
            stream_kernel,
            out_shape=(shaped((ROWS, CELLS)), shaped((56, WIDE)), shaped(block.shape, bf16)),
            in_specs=[hbm()] * 8,
            out_specs=(vmem(),) * 3,
            scratch_shapes=[
                pltpu.VMEM((ROWS, CELLS), bf16),
                pltpu.VMEM((16, 128), bf16),
                pltpu.VMEM((K, K), f32),
                pltpu.VMEM((1, K), f32),
                pltpu.VMEM((1, CELLS), f32),
                pltpu.VMEM((1, CELLS), jnp.int32),
                pltpu.SemaphoreType.DMA((8,)),
            ],
            compiler_params=limit(16),
            cost_estimate=pl.CostEstimate(flops=600_000_000, bytes_accessed=4_000_000, transcendentals=0),
            name="stream",
        )(
            *far(velocity_dist, *(jnp.asarray(x) for x in (block, pairs, own6))),
            *far(coupling, diffusivity.reshape(1, K), rate, flags),
        )
        got, base, edges = lax.optimization_barrier((got, base, edges))
        fields, sent = pl.pallas_call(
            lambda *refs: fields_kernel(n_space, *refs),
            out_shape=(shaped((N_FIELDS, 16, CELLS)), shaped((n_space, 16, 128))),
            in_specs=[vmem()] * 3,
            out_specs=(vmem(), vmem()),
            scratch_shapes=[pltpu.VMEM((384, 128), f32)],
            compiler_params=limit(12),
            name="fields",
        )(*near(got, known, constants))
        sent = lax.all_to_all(sent, "space", split_axis=0, concat_axis=0, tiled=True)
        return pl.pallas_call(
            lambda *refs: update_kernel(n_space, *refs),
            out_shape=(stored((ROWS, CELLS), bf16), stored((K, 16))),
            in_specs=[vmem()] * 5 + [hbm()],
            out_specs=(hbm(), hbm()),
            scratch_shapes=[
                pltpu.VMEM((ROWS, CELLS), bf16),
                pltpu.VMEM((K, 16), f32),
                pltpu.VMEM((384, 128), f32),
                pltpu.VMEM((48, 128), f32),
                pltpu.VMEM((16, ROWS), f32),
                pltpu.SemaphoreType.DMA((ROWS // UPDATE_ROWS + 2,)),
            ],
            compiler_params=limit(12),
            name="update",
        )(*near(sent, fields, known, constants, base), *far(edges))

    return per_device


def solution(mesh):
    placed = (P("vel", "space"), P(None, ("space", "vel")), P("space"), P("space"), P(), P())
    return jax.shard_map(
        make_per_device(mesh.shape["space"]),
        mesh=mesh,
        in_specs=placed,
        out_specs=(P("vel", "space"), P(None, ("space", "vel"))),
        check_vma=False,
    )
```

```python
import math

import jax
import jax.numpy as jnp
import numpy as np
from jax import lax
from jax.experimental import pallas as pl
from jax.experimental.pallas import tpu as pltpu
from jax.sharding import PartitionSpec as P

NV1 = 32
K = 13
time_step = 0.125
spacing = 8.0 / NV1
CELLS = 256
WIDE = 384
PEERS = 16
ROWS = 2048
BLOCK = 1024
bf16 = jnp.bfloat16
f32 = jnp.float32


def parts_of(x, number):
    rest = np.asarray(x, np.float64)
    out = []
    for _ in range(number):
        piece = rest.astype(np.float32).astype(bf16)
        out.append(piece)
        rest = rest - piece.astype(np.float64)
    return out


def grid_constants():
    v = (np.arange(NV1) + 0.5) * spacing - 4.0
    w = np.exp(-0.5 * v * v) * spacing / math.sqrt(2.0 * math.pi)
    vy, vz = np.repeat(v, NV1), np.tile(v, NV1)
    wyz = np.repeat(w, NV1) * np.tile(w, NV1)
    one = np.ones_like(vy)
    yz = vy * vy + vz * vz
    phi = np.stack([one, vy, vz, vy * vz, vy * vy, vz * vz, vy * yz, vz * yz])
    cmat = np.zeros((NV1, K, 8))
    for i, x in enumerate(v):
        c = cmat[i]
        c[0, 0] = 1.0
        c[1, 0] = x
        c[2, 1] = 1.0
        c[3, 2] = 1.0
        c[4, 0] = (x * x - 3.0) / math.sqrt(6.0)
        c[4, 4] = c[4, 5] = 1.0 / math.sqrt(6.0)
        c[5, 1] = x
        c[6, 2] = x
        c[7, 3] = 1.0
        c[8, 0] = 0.5 * x * x
        c[8, 4] = -0.5
        c[9, 0] = x * x / math.sqrt(12.0)
        c[9, 4] = 1.0 / math.sqrt(12.0)
        c[9, 5] = -2.0 / math.sqrt(12.0)
        c[10, 0] = x * (x * x - 5.0) / math.sqrt(10.0)
        c[10, 4] = c[10, 5] = x / math.sqrt(10.0)
        c[11, 1] = (x * x - 5.0) / math.sqrt(10.0)
        c[11, 6] = 1.0 / math.sqrt(10.0)
        c[12, 2] = (x * x - 5.0) / math.sqrt(10.0)
        c[12, 7] = 1.0 / math.sqrt(10.0)
    a = time_step * np.abs(v)
    plus = v > 0.0
    proj = phi * wyz
    groups = [np.ones(NV1)]
    for power in (1, 2, 3):
        groups += [a**power * plus, a**power * ~plus]
    big = np.zeros((7 * 16, 8 * NV1))
    for g, factor in enumerate(groups):
        for i in range(NV1):
            big[16 * g : 16 * g + K, 8 * i : 8 * i + 8] = factor[i] * w[i] * cmat[i]
    gram2 = proj @ phi.T
    shakhov = np.array([1.0] * 5 + [0.0] * 5 + [1.0 / 3.0] * 3)

    def between(factor):
        out = np.zeros((16, 16))
        for i in range(NV1):
            out[:K, :K] += factor[i] * w[i] * cmat[i] @ gram2 @ cmat[i].T
        return out

    c16 = np.zeros(16)
    c16[:K] = shakhov
    g, gp, gm, g2p, g2m = (between(groups[k]) for k in (0, 1, 2, 3, 4))
    mats = [g, gp, gm, g * c16, gp * c16, gm * c16, g2p, g2m, g2p * c16, g2m * c16]
    block = np.zeros((BLOCK + 224, 256), bf16)
    block[16:176, 128:176] = three_terms(np.concatenate(mats, axis=0))
    block[BLOCK:] = np.concatenate(parts_of(big, 2), axis=0)
    p3 = np.concatenate(parts_of(proj, 2), axis=0)
    ph, pm = parts_of(phi.T, 2)
    block[0:BLOCK, 0:24] = np.concatenate([ph, ph, pm], axis=1)
    own = np.zeros((PEERS, 16, 16))
    for j in range(PEERS):
        for u in range(2):
            own[j, 8 * u : 8 * u + 8, :K] = cmat[2 * j + u].T
    own = np.concatenate([three_terms(own), np.zeros((PEERS, 16, 80), bf16)], axis=2)
    return block, p3, own


def three_terms(x):
    h, m = parts_of(x, 2)
    return np.concatenate([h, h, m], axis=-1)


BASES = (1, 3, 9)


def pair_table():
    entries = []
    for stage, size in enumerate(BASES):
        for quantity in range(4):
            for i in range(size):
                for j in range(i, size):
                    entries.append((stage, quantity, i, j))
    return entries


PAIRS = pair_table()


def pair_arrays():
    kind = np.full((8, 128), -1, np.int32)
    left = np.zeros((8, 128), np.int32)
    right = np.zeros((8, 128), np.int32)
    twice = np.zeros((8, 128), np.int32)
    for n, (stage, quantity, i, j) in enumerate(PAIRS):
        at = (n // 128, n % 128)
        kind[at] = 4 * stage + quantity
        left[at], right[at] = i, j
        twice[at] = 1 if i == j else 2
    return np.concatenate([kind, left, right, twice], axis=0).astype(np.float32)


def lanes_of(shape):
    return lax.broadcasted_iota(jnp.int32, shape, len(shape) - 1)


def rows_of(shape):
    return lax.broadcasted_iota(jnp.int32, shape, 0)


def split3(f):
    h = f.astype(bf16)
    m = (f - h.astype(f32)).astype(bf16)
    return jnp.concatenate([h, m, h], axis=0)


def relax_of(rate, flags):
    return (time_step * rate) * (1.0 + flags.astype(f32))


def shift_up(x):
    return pltpu.roll(x, 1, 1)


def shift_down(x):
    return pltpu.roll(x, x.shape[1] - 1, 1)


def diff_up(x):
    return x - shift_up(x)


def diff_down(x):
    return x - shift_down(x)


def copies_of(pairs, sems):
    made = [pltpu.make_async_copy(x, y, sems.at[n]) for n, (x, y) in enumerate(pairs)]
    for copy in made:
        copy.start()
    return made


CHUNKS = 8


def chunks_of(source, target):
    rows = [pl.ds(n * (ROWS // CHUNKS), ROWS // CHUNKS) for n in range(CHUNKS)]
    return [(source.at[row, :], target.at[row, :]) for row in rows]


def sums_kernel(dist_in, p3_in, start_in, packed, edges, dist, p3, start, padded, sems):
    positive = lax.axis_index("vel") >= PEERS // 2
    halves = [pl.ds(u * BLOCK, BLOCK) for u in range(2)]
    pairs = [(p3_in, p3), (start_in, start)] + chunks_of(dist_in, dist)
    waits = copies_of(pairs, sems)
    waits[0].wait()
    waits[1].wait()
    padded[...] = jnp.zeros((16, 128), f32)
    padded[0:K, 0:16] = start[...]
    owned = padded[0:8, :] + pltpu.roll(padded[8:16, :], 16, 1)
    for j in range(PEERS):
        packed[j, 32:40, :] = owned
    for u in range(2):
        for n in range(CHUNKS // 2):
            waits[2 + u * (CHUNKS // 2) + n].wait()
        y = jnp.dot(p3[...], dist[halves[u], :], preferred_element_type=f32)
        w = y[0:8] + y[8:16]
        for j in range(PEERS):
            packed[j, 8 * u : 8 * u + 8, :] = w[:, 0:128]
            packed[j, 16 + 8 * u : 24 + 8 * u, :] = w[:, 128:256]
    e_lane = lanes_of((16, CELLS))
    e_row = rows_of((16, CELLS))
    cell = jnp.where(positive, CELLS - 1 - e_row, e_row)
    pick = jnp.where((e_lane == cell) & (e_row < 3), 1.0, 0.0).astype(bf16)
    for u in range(2):
        e = lax.dot_general(pick, dist[halves[u], :], (((1,), (1,)), ((), ())), preferred_element_type=f32)
        for n in range(3):
            for k in range(8):
                at = 16 * n + 8 * u + k
                edges[at : at + 1, :] = e[n : n + 1, 128 * k : 128 * k + 128]


N_FIELDS = 28
RIM = 7
SIDE = 13
STRIPS = 512


def tiles_of(x):
    return [x[:, 128 * t : 128 * t + 128] for t in range(x.shape[1] // 128)]


def own_shifts():
    lane = lanes_of((16, 128))
    zero = jnp.zeros((16, 128), f32)

    def up(x):
        first, second = (pltpu.roll(t, 1, 1) for t in tiles_of(x))
        return jnp.concatenate([jnp.where(lane == 0, zero, first), jnp.where(lane == 0, first, second)], axis=1)

    def down(x):
        first, second = (pltpu.roll(t, 127, 1) for t in tiles_of(x))
        return jnp.concatenate([jnp.where(lane == 127, second, first), jnp.where(lane == 127, zero, second)], axis=1)

    return up, down


def strip_up(x):
    return jnp.concatenate([pltpu.roll(t, 1, 1) for t in tiles_of(x)], axis=1)


def strip_down(x):
    return jnp.concatenate([pltpu.roll(t, 127, 1) for t in tiles_of(x)], axis=1)


def advance_three(keep, base, ups, downs, up, down):
    out = []
    for _ in range(3):
        base = keep * base
        if ups:
            base = base - (ups[0] - up(ups[0]))
        if downs:
            base = base - (downs[0] - down(downs[0]))
        ups = [keep * x - (y - up(y)) for x, y in zip(ups[:-1], ups[1:])]
        downs = [keep * x - (y - down(y)) for x, y in zip(downs[:-1], downs[1:])]
        out.append(base)
    return out


def fields_of(s1, s2, s3, start, r, mask, diffusion, block, up, down):
    width = r.shape[1]
    keep = 1.0 - r

    def up_diff(x):
        return x - up(x)

    def down_diff(x):
        return x - down(x)

    def times(first, last, inputs):
        stacked = split3(jnp.concatenate(inputs, axis=1) if len(inputs) > 1 else inputs[0])
        y = jnp.dot(block[16 * first : 16 * last, 128:176], stacked, preferred_element_type=f32)
        out = []
        for n in range(len(inputs)):
            cut = y[:, n * width : (n + 1) * width]
            out.append([cut[16 * g : 16 * g + 16] for g in range(last - first)])
        return out

    def applied(f, coupled):
        return mask * (coupled + diffusion * (2.0 * f - up(f) - down(f)))

    def streamed(g, gp, gm):
        return keep * g - up_diff(gp) - down_diff(gm)

    def streamed_twice(k1, gp, gm, g2p, g2m):
        return keep * k1 - up_diff(keep * gp - up_diff(g2p)) - down_diff(keep * gm - down_diff(g2m))

    ((gc, gcp, gcm, _, _, g2cp, g2cm),) = times(4, 11, [start])
    relaxed = r * gc
    shares = mask * (s1 + relaxed)
    res = mask * (shares - start)
    k1_start = streamed(relaxed, r * gcp, r * gcm)
    k2_start = streamed_twice(k1_start, r * gcp, r * gcm, r * g2cp, r * g2cm)

    def parts(f, ys):
        out = [applied(f, ys[0])]
        k1 = streamed(ys[1], ys[2], ys[3])
        rg = r * ys[4]
        held = rg - f
        out += [mask * (k1 + held), held]
        if len(ys) > 5:
            out.append(streamed_twice(k1, ys[2], ys[3], ys[7], ys[8]))
            out.append(streamed(rg, r * ys[5], r * ys[6]) + held)
        return out

    y_shares, y_res = times(0, 9, [shares, res])
    rg = r * y_shares[4]
    held_shares = rg - shares
    n_shares = streamed(rg, r * y_shares[5], r * y_shares[6]) + held_shares
    p0 = mask * (s2 + k1_start + held_shares)
    e, p1, _, k2_res, n_res = parts(res, y_res)

    y_e, y_p0, y_p1 = times(0, 9, [e, p0, p1])
    ee, p2, _, k2_e, n_e = parts(e, y_e)
    ap0, q3, held_p0 = parts(p0, y_p0[:5])
    ap1, q4, held_p1 = parts(p1, y_p1[:5])
    q0 = mask * (s3 + k2_start + n_shares + held_p0)
    q1 = mask * (k2_res + n_res + held_p1)

    y_p2, y_ap0, y_ap1, y_q0, y_q1, y_q3, y_q4 = times(0, 5, [p2, ap0, ap1, q0, q1, q3, q4])
    ap2, q5, held_p2 = parts(p2, y_p2)
    aap0, q6, _ = parts(ap0, y_ap0)
    aap1, q7, _ = parts(ap1, y_ap1)
    q2 = mask * (k2_e + n_e + held_p2)
    aq0, aq1, aq3, aq4 = (applied(f, y[0]) for f, y in ((q0, y_q0), (q1, y_q1), (q3, y_q3), (q4, y_q4)))

    (y_ap2,) = times(0, 5, [ap2])
    aap2, q8, _ = parts(ap2, y_ap2)
    first = [q2, q5, q6, q7, aq0, aq1, aq3, aq4]
    aq2, aq5, aq6, aq7, aaq0, aaq1, aaq3, aaq4 = (applied(f, y[0]) for f, y in zip(first, times(0, 1, first)))
    second = [q8, aq2, aq5, aq6, aq7]
    aq8, aaq2, aaq5, aaq6, aaq7 = (applied(f, y[0]) for f, y in zip(second, times(0, 1, second)))
    ((y_aq8,),) = times(0, 1, [aq8])
    aaq8 = applied(aq8, y_aq8)

    q = [q0, q1, q2, q3, q4, q5, q6, q7, q8]
    aq = [aq0, aq1, aq2, aq3, aq4, aq5, aq6, aq7, aq8]
    aaq = [aaq0, aaq1, aaq2, aaq3, aaq4, aaq5, aaq6, aaq7, aaq8]
    fields = [start, shares, res, e, p0, p1, p2, ap0, ap1, ap2] + q + aq
    plain = [[res], [p0, p1, p2], q]
    once = [[e], [ap0, ap1, ap2], aq]
    again = [[ee], [aap0, aap1, aap2], aaq]
    return fields, plain, once, again


EARLY = 4 * 1 + 4 * 6


def inner_products(plain, once, again, counted, table):
    lefts = [[[counted * x for x in xs] for xs in xss] for xss in (plain, once)]
    rights = [plain, once, again]
    if counted.shape[1] == STRIPS:
        def folded(x):
            halves = [x[:, 0:256], x[:, 256:512]]
            moved = [pltpu.roll(t, 16, 1) for t in tiles_of(halves[1])]
            return halves[0] + jnp.concatenate(moved, axis=1)

        lefts = [[[folded(x) for x in xs] for xs in xss] for xss in lefts]
        rights = lefts + [[[folded(counted * x) for x in xs] for xs in again]]
    table[EARLY:256, :] = jnp.zeros((256 - EARLY, 128), f32)
    table[256 : 256 + EARLY, :] = jnp.zeros((EARLY, 128), f32)
    table[len(PAIRS) + 128 : 384, :] = jnp.zeros((256 - len(PAIRS), 128), f32)
    ones = jnp.ones((8, 128), f32)
    tops = []
    for n, (stage, quantity, i, j) in enumerate(PAIRS):
        x, y = ((0, 0), (0, 1), (1, 1), (1, 2))[quantity]
        product = lefts[x][stage][i] * rights[y][stage][j]
        half = product[:, 0:128] + product[:, 128:256]
        at = n if n < EARLY else n + 128
        table[at : at + 1, :] = jnp.sum(half[0:8] + half[8:16], axis=0, keepdims=True)
    for n in range(3):
        tops.append(
            lax.dot_general(
                ones,
                table[128 * n : 128 * n + 128, :],
                (((1,), (1,)), ((), ())),
                precision=lax.Precision.HIGHEST,
                preferred_element_type=f32,
            )
        )
    return tops


def fields_kernel(n_space, got, known, block, fields, sent, table):
    slab = lax.axis_index("space")
    wide = (16, CELLS)
    w = jnp.concatenate([got[:, 16 * t : 16 * t + 16, :].reshape(PEERS * 16, 128) for t in range(2)], axis=1)
    wh = w.astype(bf16)
    wm = (w - wh.astype(f32)).astype(bf16)
    y = jnp.dot(block[BLOCK : BLOCK + 224, :], wh, preferred_element_type=f32)
    z = jnp.dot(block[BLOCK : BLOCK + 112, :], wm, preferred_element_type=f32)
    mu = (y[112:224] + z) + y[0:112]
    mu = [mu[16 * g : 16 * g + 16] for g in range(7)]

    lane8 = lanes_of((8, 128))
    parts = [[jnp.zeros((8, 128), f32)] * 2 for _ in range(2)]
    for j in range(PEERS):
        tile = got[j, 32:40, :]
        here = lane8 // 16 == j % 8
        for half in range(2):
            amount = (16 * j - 16 * half) % 128
            moved = pltpu.roll(tile, amount, 1) if amount else tile
            parts[half][j // 8] = jnp.where(here, moved, parts[half][j // 8])
    start = jnp.concatenate([jnp.concatenate(x, axis=1) for x in parts], axis=0)

    r = jnp.broadcast_to(known[16:17, 0:CELLS], wide)
    diffusion = jnp.concatenate([known[0:16, 128:256]] * 2, axis=1)
    up, down = own_shifts()
    s1, s2, s3 = advance_three(1.0 - r, mu[0], [mu[1], mu[3], mu[5]], [mu[2], mu[4], mu[6]], up, down)
    out, plain, once, again = fields_of(s1, s2, s3, start, r, 1.0, diffusion, block, up, down)
    for n, f in enumerate(out):
        fields[n] = f
    lane = lanes_of(wide)
    low = jnp.where(slab > 0, RIM, 0)
    high = jnp.where(slab < n_space - 1, CELLS - RIM, CELLS)
    counted = jnp.where((lane >= low) & (lane < high), 1.0, 0.0)
    tops = inner_products(plain, once, again, counted, table)

    lane1 = lanes_of((16, 128))
    row1 = rows_of((16, 128))
    start_relax = jnp.where(rows_of(wide) == K, r, start)
    tile = jnp.zeros((16, 128), f32)
    for n, f in enumerate([s1, s2, s3, start_relax]):
        at = lane1 - 32 * n
        begin = pltpu.roll(f[:, 0:128], 32 * n, 1) if n else f[:, 0:128]
        tile = jnp.where((at >= 0) & (at < SIDE), begin, tile)
        end = pltpu.roll(f[:, 128:256], (32 * n + 16 + SIDE) % 128, 1)
        tile = jnp.where((at >= 16) & (at < 16 + SIDE), end, tile)
        if n < 3:
            begin = pltpu.roll(mu[2 + 2 * n][:, 0:128], 32 * n + SIDE, 1)
            tile = jnp.where((at >= SIDE) & (at < 16), begin, tile)
            end = pltpu.roll(mu[1 + 2 * n][:, 128:256], (32 * n + 32) % 128, 1)
            tile = jnp.where((at >= 16 + SIDE) & (at < 32), end, tile)
    row_a = jnp.broadcast_to(tops[0][0:1] + tops[1][0:1], (16, 128))
    row_b = jnp.broadcast_to(tops[2][0:1], (16, 128))
    tile = jnp.where(row1 == 14, row_a, jnp.where(row1 == 15, row_b, tile))
    for j in range(n_space):
        sent[j] = tile


def speeds_of(shape):
    number = 2 * lax.axis_index("vel") + jnp.where(rows_of(shape) >= 8, 1, 0)
    return time_step * jnp.abs((number.astype(f32) + 0.5) * spacing - 4.0)


def bands_of(r, positive):
    a = speeds_of(r.shape)
    stay = 1.0 - r - a

    def before(x):
        return jnp.where(positive, shift_up(x), shift_down(x))

    once = before(stay)
    two = before(once)
    t0 = stay * stay * stay
    t1 = a * (stay * (stay + once) + once * once)
    t2 = a * a * (stay + once + two)
    return t0, t1, t2, a * a * a


def banded(weights, u, distance):
    value = jnp.zeros(distance.shape, f32)
    for n, x in enumerate(weights):
        row = jnp.broadcast_to(x[8 * u : 8 * u + 1, 0 : distance.shape[1]], distance.shape)
        value = jnp.where(distance == n, row, value)
    return value


def stream_kernel(
    dist_in,
    block_in,
    pairs_in,
    own_in,
    coupling_in,
    diff_in,
    rate_in,
    flags_in,
    out,
    table,
    block,
    dist,
    own6,
    coupling_raw,
    diff_raw,
    rate,
    flags,
    sems,
):
    vel = lax.axis_index("vel")
    positive = vel >= PEERS // 2
    moves = [(rate_in, rate), (flags_in, flags), (dist_in, dist)]
    moves += [(coupling_in, coupling_raw), (diff_in, diff_raw), (own_in.at[vel], own6)]
    moves += [(pairs_in, table.at[24:56, 0:128]), (block_in, block)]
    waits = copies_of(moves, sems)
    waits[0].wait()
    waits[1].wait()
    relax = relax_of(rate[...], flags[...])
    table[16:24, 0:CELLS] = jnp.broadcast_to(relax, (8, CELLS))
    weights = bands_of(jnp.broadcast_to(relax, (16, CELLS)), positive)
    towards = jnp.where(positive, 1, -1)
    distance = (lanes_of((CELLS, CELLS)) - rows_of((CELLS, CELLS))) * towards
    waits[2].wait()
    for u in range(2):
        b = banded(weights, u, distance)
        bh = b.astype(bf16)
        bl = (b - bh.astype(f32)).astype(bf16)
        rows = pl.ds(u * BLOCK, BLOCK)
        x = dist[rows, :]
        value = jnp.dot(x, bh, preferred_element_type=f32)
        value += jnp.dot(x, bl, preferred_element_type=f32)
        out[rows, :] = value

    for copy in waits[3:]:
        copy.wait()
    table[0:16, 0:128] = jnp.zeros((16, 128), f32)
    table[0:K, 0:K] = coupling_raw[...]
    c = table[0:16, 0:128]
    ch = c.astype(bf16).astype(f32)
    pieces = [ch, ch, c - ch]
    terms = pieces[0]
    for n in range(1, 3):
        terms = terms + pltpu.roll(pieces[n], 16 * n, 1)
    block[0:16, 128:256] = terms.astype(bf16)
    block[176:192, 128:256] = own6[...]
    shape = (16, K)
    chosen = jnp.where(lanes_of(shape) == rows_of(shape), jnp.broadcast_to(diff_raw[...], shape), 0.0)
    table[0:16, 128:256] = jnp.broadcast_to(jnp.sum(chosen, axis=1, keepdims=True), (16, 128))


UPDATE_ROWS = 256


def strips_of(n_space, sent):
    quarter = lanes_of((16, 128)) // 32
    raw = []
    for n in range(4):
        tiles = []
        for t in range(4):
            tile = jnp.zeros((16, 128), f32)
            for k in range(4):
                j = 4 * t + k
                if j < n_space:
                    amount = 32 * (k - n) % 128
                    moved = pltpu.roll(sent[j], amount, 1) if amount else sent[j]
                    tile = jnp.where(quarter == k, moved, tile)
            tiles.append(tile)
        raw.append(jnp.concatenate(tiles, axis=1))
    shape = (16, STRIPS)
    lane = lanes_of(shape)
    row = rows_of(shape)
    at = lane % 32
    valid = (lane < 32 * (n_space - 1)) & (at < 2 * SIDE)
    mask = jnp.where(valid, 1.0, 0.0)
    moments = jnp.where(row < K, mask, 0.0)
    raw = [pltpu.roll(x, STRIPS - 16, 1) for x in raw]
    closer = [pltpu.roll(x, STRIPS - 3, 1) for x in raw]
    arrays = [jnp.where(at < SIDE, x, y) for x, y in zip(raw, closer)]
    r = mask * jnp.broadcast_to(arrays[3][K : K + 1], shape)
    s1, s2, s3, start = (moments * x for x in arrays)
    ups = [jnp.where((at >= SIDE - 3) & (at < SIDE), moments * x, 0.0) for x in closer[:3]]
    downs = [pltpu.roll(x, STRIPS - 16, 1) for x in raw[:3]]
    downs = [jnp.where((at >= SIDE) & (at < SIDE + 3), moments * x, 0.0) for x in downs]
    zero = jnp.zeros(shape, f32)
    over_up = advance_three(1.0 - r, zero, ups, [], strip_up, strip_down)
    over_down = advance_three(1.0 - r, zero, [], downs, strip_up, strip_down)
    s = [x + jnp.where(at < SIDE, y, z) for x, y, z in zip((s1, s2, s3), over_down, over_up)]
    s = [mask * x for x in s]
    counted = jnp.where((at >= SIDE - RIM) & (at < SIDE + RIM), mask, 0.0)
    return s, start, r, mask, counted


def update_kernel(
    n_space,
    sent,
    fields,
    table,
    block,
    base,
    edges_in,
    out,
    macro,
    done,
    macro_part,
    products,
    edges,
    ends,
    sems,
):
    place = lax.axis_index("vel")
    slab = lax.axis_index("space")
    positive = place >= PEERS // 2
    (edge_copy,) = copies_of([(edges_in, edges)], sems.at[pl.ds(ROWS // UPDATE_ROWS + 1, 1)])

    def known(at):
        return table[at : at + 8, 0:128]

    (s1, s2, s3), strip_start, strip_r, strip_mask, counted = strips_of(n_space, sent)
    diffusion = jnp.concatenate([table[0:16, 128:256]] * 4, axis=1)
    strip_fields, plain, once, again = fields_of(
        s1, s2, s3, strip_start, strip_r, strip_mask, diffusion, block, strip_up, strip_down
    )
    tops = inner_products(plain, once, again, counted, products)
    gathered = sent[0, 8:16, :]
    for j in range(1, n_space):
        gathered = gathered + sent[j, 8:16, :]
    row8 = rows_of((8, 128))
    early = jnp.where(row8 == 0, gathered[6:7] + tops[0][0:1], 0.0) * known(48)
    line_a = gathered[6:7] + tops[1][0:1]
    line_b = gathered[7:8] + tops[2][0:1]
    total = jnp.where(row8 == 0, line_a, jnp.where(row8 == 1, line_b, 0.0))
    total = total * known(48)
    cpl = table[0:16, 0:128]
    lane16 = lanes_of((16, 128))
    row16 = rows_of((16, 128))
    size = jnp.sum(jnp.abs(cpl), axis=1, keepdims=True)
    middle = jnp.sum(jnp.where(lane16 == row16, cpl, 0.0), axis=1, keepdims=True)
    real = row16[:, 0:1] < K
    most = jnp.max(jnp.where(real, size + 4.0 * table[0:16, 128:129], 0.0), axis=0, keepdims=True)
    least = jnp.min(jnp.where(real, 2.0 * middle - size, 1e30), axis=0, keepdims=True)
    low_step, high_step = 1.0 / most, 1.0 / least

    def summed(weighted, which):
        picked = jnp.where(known(24) == which, weighted, 0.0)
        return jnp.sum(jnp.sum(picked, axis=0, keepdims=True), axis=1, keepdims=True)

    def clipped(x):
        return jnp.minimum(jnp.maximum(x, low_step), high_step)

    def weights_of(stage, weighted):
        rr, ra, aa, aaa = (summed(weighted, 4 * stage + n) for n in range(4))
        s1 = clipped(rr / ra)
        rr2 = rr - 2.0 * s1 * ra + s1 * s1 * aa
        ra2 = ra - 2.0 * s1 * aa + s1 * s1 * aaa
        s2 = clipped(rr2 / ra2)
        return s1 + s2, -s1 * s2

    li, ri = (known(n).astype(jnp.int32) for n in (32, 40))

    def choose(index, zero, one, two):
        return jnp.where(index == 0, zero, jnp.where(index == 1, one, two))

    a1, b1 = weights_of(0, early)
    a2, b2 = weights_of(1, early * choose(li, 1.0, a1, b1) * choose(ri, 1.0, a1, b1))

    def both(index):
        outer = (index >= 3).astype(jnp.int32) + (index >= 6).astype(jnp.int32)
        return choose(outer, 1.0, a2, b2) * choose(index - 3 * outer, 1.0, a1, b1)

    a3, b3 = weights_of(2, total * both(li) * both(ri))

    def last_fields(at, r):
        start, shares, res, e = (at(n) for n in range(4))
        corr1 = a1 * res + b1 * e
        cur1 = shares + corr1
        res2 = at(4) + a1 * at(5) + b1 * at(6)
        e2 = at(7) + a1 * at(8) + b1 * at(9)
        corr2 = a2 * res2 + b2 * e2
        cur2 = res2 + cur1 + corr2

        def third(first):
            rows = [at(first + 3 * n) + a1 * at(first + 3 * n + 1) + b1 * at(first + 3 * n + 2) for n in range(3)]
            return rows[0] + a2 * rows[1] + b2 * rows[2]

        res3, e3 = third(10), third(19)
        corr3 = a3 * res3 + b3 * e3
        row = rows_of(r.shape)
        scaled = r * jnp.where(row < 5, 1.0, jnp.where(row < 10, 0.0, 1.0 / 3.0))
        f1 = scaled * start + corr1
        f2 = scaled * cur1 + corr2
        f3 = scaled * cur2 + corr3
        return f1, f2, f3, res3 + cur2 + corr3, r

    own = last_fields(lambda n: fields[n], jnp.broadcast_to(table[16:17, 0:CELLS], (16, CELLS)))
    strips = last_fields(lambda n: strip_fields[n], strip_r)
    lane1 = lanes_of((16, 128))
    has_left, has_right = jnp.where(slab > 0, 1, 0), jnp.where(slab < n_space - 1, 1, 0)
    near_left = (lane1 < RIM * has_left)
    near_right = (lane1 >= 128 - RIM * has_right)
    far_left = (lane1 >= 128 - 2 * has_left)
    far_right = (lane1 < 2 * has_right)
    wide = []
    for x, y in zip(own, strips):
        y = pltpu.roll(y, lax.rem(STRIPS + 32 - 32 * slab, STRIPS), 1)[:, 0:128]
        from_left = pltpu.roll(y, 128 - SIDE, 1)
        from_right = pltpu.roll(y, 96 - SIDE, 1)
        tiles = [
            jnp.where(near_left, from_left, x[:, 0:128]),
            jnp.where(near_right, from_right, x[:, 128:256]),
            jnp.where(far_left, from_left, jnp.where(far_right, from_right, 0.0)),
        ]
        wide.append(jnp.concatenate(tiles, axis=1))
    f1, f2, f3, cur3, r = wide
    mine = pltpu.roll(cur3[:, 0:CELLS], lax.rem(CELLS - 16 * place, CELLS), 1)
    macro_part[...] = mine[0:K, 0:16]
    macro_copy = pltpu.make_async_copy(macro_part, macro, sems.at[ROWS // UPDATE_ROWS])
    macro_copy.start()
    y = jnp.dot(
        block[176:192, 128:176], split3(jnp.concatenate([f1, f2, f3], axis=1)), preferred_element_type=f32
    )
    y1, y2, y3 = (y[:, n * WIDE : (n + 1) * WIDE] for n in range(3))
    a = speeds_of((16, WIDE))
    stay = 1.0 - r - a

    def moved(x):
        return stay * x + a * jnp.where(positive, shift_up(x), shift_down(x))

    h = (moved(moved(y1) + y2) + y3)[:, 0:CELLS]
    hh = h.astype(bf16).astype(f32)
    hm = (h - hh).astype(bf16).astype(f32)

    weights = bands_of(r, positive)
    towards = jnp.where(positive, 1, -1)
    at8 = rows_of((8, 128))
    at8 = jnp.where(positive, -1 - at8, at8 + CELLS)
    low = jnp.where(positive, 0, CELLS - 128)
    distance = (lanes_of((8, 128)) + low - at8) * towards
    weights = [jnp.where(positive, x[:, 0:128], x[:, 128:256]) for x in weights]
    ends[...] = jnp.zeros((16, ROWS), f32)
    edge_copy.wait()
    for n in range(3):
        for k in range(16):
            row = edges[16 * n + k : 16 * n + k + 1, :]
            ends[n : n + 1, 128 * k : 128 * k + 128] = row
            ends[8 + n : 9 + n, 128 * k : 128 * k + 128] = row

    sends = [macro_copy]
    for u in range(2):
        hu, mu = hh[8 * u : 8 * u + 8], hm[8 * u : 8 * u + 8]
        mixed = jnp.concatenate([hu, mu, hu, jnp.zeros((104, CELLS), f32)], axis=0).astype(bf16)
        b = banded(weights, u, distance)
        bh = b.astype(bf16).astype(f32)
        b = jnp.concatenate([bh, b - bh], axis=0).astype(bf16)
        for n in range(BLOCK // UPDATE_ROWS):
            part = u * (BLOCK // UPDATE_ROWS) + n
            rows = pl.ds(part * UPDATE_ROWS, UPDATE_ROWS)
            value = jnp.dot(block[pl.ds(n * UPDATE_ROWS, UPDATE_ROWS), 0:128], mixed, preferred_element_type=f32)
            near = lax.dot_general(ends[:, rows].astype(bf16), b, (((0,), (0,)), ((), ())), preferred_element_type=f32)
            value += base[rows, :]
            done[rows, 0:128] = (value[:, 0:128] + jnp.where(positive, near, 0.0)).astype(bf16)
            done[rows, 128:256] = (value[:, 128:256] + jnp.where(positive, 0.0, near)).astype(bf16)
            copy = pltpu.make_async_copy(done.at[rows, :], out.at[rows, :], sems.at[part])
            copy.start()
            sends.append(copy)
    for copy in sends:
        copy.wait()


def vmem():
    return pl.BlockSpec(memory_space=pltpu.VMEM)


def hbm():
    return pl.BlockSpec(memory_space=pltpu.HBM)


def shaped(shape, dtype=f32):
    return pltpu.VMEM(shape, dtype)


def stored(shape, dtype=f32):
    return pltpu.HBM(shape, dtype)


def placed_at(space, arrays):
    return [pltpu.with_memory_space_constraint(x, space) for x in arrays]


def near(*arrays):
    return placed_at(pltpu.VMEM, arrays)


def far(*arrays):
    return placed_at(pltpu.HBM, arrays)


def limit(mib):
    return pltpu.CompilerParams(vmem_limit_bytes=mib * 2**20)


def make_per_device(n_space):
    block, p3, own6 = grid_constants()
    pairs = pair_arrays()

    def per_device(velocity_dist, macro_state, collision_rate, wall_flags, diffusivity, coupling):
        rate = collision_rate.reshape(1, CELLS)
        flags = wall_flags.reshape(1, CELLS)
        packed, edges = pl.pallas_call(
            sums_kernel,
            out_shape=(shaped((PEERS, 40, 128)), shaped((48, 128))),
            in_specs=[hbm()] * 3,
            out_specs=(vmem(), vmem()),
            scratch_shapes=[
                pltpu.VMEM((ROWS, CELLS), bf16),
                pltpu.VMEM((16, BLOCK), bf16),
                pltpu.VMEM((K, 16), f32),
                pltpu.VMEM((16, 128), f32),
                pltpu.SemaphoreType.DMA((2 + CHUNKS,)),
            ],
            compiler_params=limit(8),
            name="sums",
        )(*far(velocity_dist, jnp.asarray(p3), macro_state))
        got = lax.all_to_all(packed, "vel", split_axis=0, concat_axis=0, tiled=True)
        rising = [(i, i + 1) for i in range(n_space - 1)]
        half = PEERS // 2
        downwind = [(i * PEERS + n, j * PEERS + n) for i, j in rising for n in range(half, PEERS)]
        downwind += [(j * PEERS + n, i * PEERS + n) for i, j in rising for n in range(half)]
        edges = lax.ppermute(edges, ("space", "vel"), downwind)
        base, known, constants = pl.pallas_call(
            stream_kernel,
            out_shape=(shaped((ROWS, CELLS)), shaped((56, WIDE)), shaped(block.shape, bf16)),
            in_specs=[hbm()] * 8,
            out_specs=(vmem(),) * 3,
            scratch_shapes=[
                pltpu.VMEM((ROWS, CELLS), bf16),
                pltpu.VMEM((16, 128), bf16),
                pltpu.VMEM((K, K), f32),
                pltpu.VMEM((1, K), f32),
                pltpu.VMEM((1, CELLS), f32),
                pltpu.VMEM((1, CELLS), jnp.int32),
                pltpu.SemaphoreType.DMA((8,)),
            ],
            compiler_params=limit(16),
            cost_estimate=pl.CostEstimate(flops=600_000_000, bytes_accessed=4_000_000, transcendentals=0),
            name="stream",
        )(
            *far(velocity_dist, *(jnp.asarray(x) for x in (block, pairs, own6))),
            *far(coupling, diffusivity.reshape(1, K), rate, flags),
        )
        got, base, edges = lax.optimization_barrier((got, base, edges))
        fields, sent = pl.pallas_call(
            lambda *refs: fields_kernel(n_space, *refs),
            out_shape=(shaped((N_FIELDS, 16, CELLS)), shaped((n_space, 16, 128))),
            in_specs=[vmem()] * 3,
            out_specs=(vmem(), vmem()),
            scratch_shapes=[pltpu.VMEM((384, 128), f32)],
            compiler_params=limit(12),
            name="fields",
        )(*near(got, known, constants))
        sent = lax.all_to_all(sent, "space", split_axis=0, concat_axis=0, tiled=True)
        return pl.pallas_call(
            lambda *refs: update_kernel(n_space, *refs),
            out_shape=(stored((ROWS, CELLS), bf16), stored((K, 16))),
            in_specs=[vmem()] * 5 + [hbm()],
            out_specs=(hbm(), hbm()),
            scratch_shapes=[
                pltpu.VMEM((ROWS, CELLS), bf16),
                pltpu.VMEM((K, 16), f32),
                pltpu.VMEM((384, 128), f32),
                pltpu.VMEM((48, 128), f32),
                pltpu.VMEM((16, ROWS), f32),
                pltpu.SemaphoreType.DMA((ROWS // UPDATE_ROWS + 2,)),
            ],
            compiler_params=limit(12),
            name="update",
        )(*near(sent, fields, known, constants, base), *far(edges))

    return per_device


def solution(mesh):
    placed = (P("vel", "space"), P(None, ("space", "vel")), P("space"), P("space"), P(), P())
    return jax.shard_map(
        make_per_device(mesh.shape["space"]),
        mesh=mesh,
        in_specs=placed,
        out_specs=(P("vel", "space"), P(None, ("space", "vel"))),
        check_vma=False,
    )
```

```python
import math

import jax
import jax.numpy as jnp
import numpy as np
from jax import lax
from jax.experimental import pallas as pl
from jax.experimental.pallas import tpu as pltpu
from jax.sharding import PartitionSpec as P

NV1 = 32
K = 13
time_step = 0.125
spacing = 8.0 / NV1
CELLS = 256
WIDE = 384
PEERS = 16
ROWS = 2048
BLOCK = 1024
bf16 = jnp.bfloat16
f32 = jnp.float32


def parts_of(x, number):
    rest = np.asarray(x, np.float64)
    out = []
    for _ in range(number):
        piece = rest.astype(np.float32).astype(bf16)
        out.append(piece)
        rest = rest - piece.astype(np.float64)
    return out


def grid_constants():
    v = (np.arange(NV1) + 0.5) * spacing - 4.0
    w = np.exp(-0.5 * v * v) * spacing / math.sqrt(2.0 * math.pi)
    vy, vz = np.repeat(v, NV1), np.tile(v, NV1)
    wyz = np.repeat(w, NV1) * np.tile(w, NV1)
    one = np.ones_like(vy)
    yz = vy * vy + vz * vz
    phi = np.stack([one, vy, vz, vy * vz, vy * vy, vz * vz, vy * yz, vz * yz])
    cmat = np.zeros((NV1, K, 8))
    for i, x in enumerate(v):
        c = cmat[i]
        c[0, 0] = 1.0
        c[1, 0] = x
        c[2, 1] = 1.0
        c[3, 2] = 1.0
        c[4, 0] = (x * x - 3.0) / math.sqrt(6.0)
        c[4, 4] = c[4, 5] = 1.0 / math.sqrt(6.0)
        c[5, 1] = x
        c[6, 2] = x
        c[7, 3] = 1.0
        c[8, 0] = 0.5 * x * x
        c[8, 4] = -0.5
        c[9, 0] = x * x / math.sqrt(12.0)
        c[9, 4] = 1.0 / math.sqrt(12.0)
        c[9, 5] = -2.0 / math.sqrt(12.0)
        c[10, 0] = x * (x * x - 5.0) / math.sqrt(10.0)
        c[10, 4] = c[10, 5] = x / math.sqrt(10.0)
        c[11, 1] = (x * x - 5.0) / math.sqrt(10.0)
        c[11, 6] = 1.0 / math.sqrt(10.0)
        c[12, 2] = (x * x - 5.0) / math.sqrt(10.0)
        c[12, 7] = 1.0 / math.sqrt(10.0)
    a = time_step * np.abs(v)
    plus = v > 0.0
    proj = phi * wyz
    groups = [np.ones(NV1)]
    for power in (1, 2, 3):
        groups += [a**power * plus, a**power * ~plus]
    big = np.zeros((7 * 16, 8 * NV1))
    for g, factor in enumerate(groups):
        for i in range(NV1):
            big[16 * g : 16 * g + K, 8 * i : 8 * i + 8] = factor[i] * w[i] * cmat[i]
    gram2 = proj @ phi.T
    shakhov = np.array([1.0] * 5 + [0.0] * 5 + [1.0 / 3.0] * 3)

    def between(factor):
        out = np.zeros((16, 16))
        for i in range(NV1):
            out[:K, :K] += factor[i] * w[i] * cmat[i] @ gram2 @ cmat[i].T
        return out

    c16 = np.zeros(16)
    c16[:K] = shakhov
    g, gp, gm, g2p, g2m = (between(groups[k]) for k in (0, 1, 2, 3, 4))
    mats = [g, gp, gm, g * c16, gp * c16, gm * c16, g2p, g2m, g2p * c16, g2m * c16]
    block = np.zeros((BLOCK + 224, 256), bf16)
    block[16:176, 128:176] = three_terms(np.concatenate(mats, axis=0))
    block[BLOCK:] = np.concatenate(parts_of(big, 2), axis=0)
    p3 = np.concatenate(parts_of(proj, 2), axis=0)
    ph, pm = parts_of(phi.T, 2)
    block[0:BLOCK, 0:24] = np.concatenate([ph, ph, pm], axis=1)
    own = np.zeros((PEERS, 16, 16))
    for j in range(PEERS):
        for u in range(2):
            own[j, 8 * u : 8 * u + 8, :K] = cmat[2 * j + u].T
    own = np.concatenate([three_terms(own), np.zeros((PEERS, 16, 80), bf16)], axis=2)
    return block, p3, own


def three_terms(x):
    h, m = parts_of(x, 2)
    return np.concatenate([h, h, m], axis=-1)


BASES = (1, 3, 9)


def pair_table():
    entries = []
    for stage, size in enumerate(BASES):
        for quantity in range(4):
            for i in range(size):
                for j in range(i, size):
                    entries.append((stage, quantity, i, j))
    return entries


PAIRS = pair_table()


def pair_arrays():
    kind = np.full((8, 128), -1, np.int32)
    left = np.zeros((8, 128), np.int32)
    right = np.zeros((8, 128), np.int32)
    twice = np.zeros((8, 128), np.int32)
    for n, (stage, quantity, i, j) in enumerate(PAIRS):
        at = (n // 128, n % 128)
        kind[at] = 4 * stage + quantity
        left[at], right[at] = i, j
        twice[at] = 1 if i == j else 2
    return np.concatenate([kind, left, right, twice], axis=0).astype(np.float32)


def lanes_of(shape):
    return lax.broadcasted_iota(jnp.int32, shape, len(shape) - 1)


def rows_of(shape):
    return lax.broadcasted_iota(jnp.int32, shape, 0)


def split3(f):
    h = f.astype(bf16)
    m = (f - h.astype(f32)).astype(bf16)
    return jnp.concatenate([h, m, h], axis=0)


def relax_of(rate, flags):
    return (time_step * rate) * (1.0 + flags.astype(f32))


def shift_up(x):
    return pltpu.roll(x, 1, 1)


def shift_down(x):
    return pltpu.roll(x, x.shape[1] - 1, 1)


def diff_up(x):
    return x - shift_up(x)


def diff_down(x):
    return x - shift_down(x)


def copies_of(pairs, sems):
    made = [pltpu.make_async_copy(x, y, sems.at[n]) for n, (x, y) in enumerate(pairs)]
    for copy in made:
        copy.start()
    return made


CHUNKS = 8


def chunks_of(source, target):
    rows = [pl.ds(n * (ROWS // CHUNKS), ROWS // CHUNKS) for n in range(CHUNKS)]
    return [(source.at[row, :], target.at[row, :]) for row in rows]


def sums_kernel(dist_in, p3_in, start_in, packed, edges, dist, p3, start, padded, sems):
    positive = lax.axis_index("vel") >= PEERS // 2
    halves = [pl.ds(u * BLOCK, BLOCK) for u in range(2)]
    pairs = [(p3_in, p3), (start_in, start)] + chunks_of(dist_in, dist)
    waits = copies_of(pairs, sems)
    waits[0].wait()
    waits[1].wait()
    padded[...] = jnp.zeros((16, 128), f32)
    padded[0:K, 0:16] = start[...]
    owned = padded[0:8, :] + pltpu.roll(padded[8:16, :], 16, 1)
    for j in range(PEERS):
        packed[j, 32:40, :] = owned
    e_lane = lanes_of((16, 128))
    e_row = rows_of((16, 128))
    cell = jnp.where(positive, 127 - e_row, e_row)
    pick = jnp.where((e_lane == cell) & (e_row < 3), 1.0, 0.0).astype(bf16)
    side = pl.multiple_of(jnp.where(positive, 128, 0), 128)
    for u in range(2):
        for n in range(CHUNKS // 2):
            waits[2 + u * (CHUNKS // 2) + n].wait()
        y = jnp.dot(p3[...], dist[halves[u], :], preferred_element_type=f32)
        w = y[0:8] + y[8:16]
        for j in range(PEERS):
            packed[j, 8 * u : 8 * u + 8, :] = w[:, 0:128]
            packed[j, 16 + 8 * u : 24 + 8 * u, :] = w[:, 128:256]
        near = dist[halves[u], pl.ds(side, 128)]
        e = lax.dot_general(pick, near, (((1,), (1,)), ((), ())), preferred_element_type=f32)
        for n in range(3):
            for k in range(8):
                at = 16 * n + 8 * u + k
                edges[at : at + 1, :] = e[n : n + 1, 128 * k : 128 * k + 128]


N_FIELDS = 28
RIM = 7
SIDE = 13
STRIPS = 512


def tiles_of(x):
    return [x[:, 128 * t : 128 * t + 128] for t in range(x.shape[1] // 128)]


def own_shifts():
    lane = lanes_of((16, 128))
    zero = jnp.zeros((16, 128), f32)

    def up(x):
        first, second = (pltpu.roll(t, 1, 1) for t in tiles_of(x))
        return jnp.concatenate([jnp.where(lane == 0, zero, first), jnp.where(lane == 0, first, second)], axis=1)

    def down(x):
        first, second = (pltpu.roll(t, 127, 1) for t in tiles_of(x))
        return jnp.concatenate([jnp.where(lane == 127, second, first), jnp.where(lane == 127, zero, second)], axis=1)

    return up, down


STEP = (0, 0, 16, 16)


def tile_roll(x, amount):
    return jnp.concatenate([pltpu.roll(t, amount, 1) for t in tiles_of(x)], axis=1)


def strip_up(x):
    return tile_roll(x, 1)


def strip_down(x):
    return tile_roll(x, 127)


def advance_three(keep, base, ups, downs, up, down):
    out = []
    for _ in range(3):
        base = keep * base
        if ups:
            base = base - (ups[0] - up(ups[0]))
        if downs:
            base = base - (downs[0] - down(downs[0]))
        ups = [keep * x - (y - up(y)) for x, y in zip(ups[:-1], ups[1:])]
        downs = [keep * x - (y - down(y)) for x, y in zip(downs[:-1], downs[1:])]
        out.append(base)
    return out


def fields_of(s1, s2, s3, start, r, mask, diffusion, block, up, down):
    width = r.shape[1]
    keep = 1.0 - r

    def up_diff(x):
        return x - up(x)

    def down_diff(x):
        return x - down(x)

    def times(first, last, inputs):
        stacked = split3(jnp.concatenate(inputs, axis=1) if len(inputs) > 1 else inputs[0])
        y = jnp.dot(block[16 * first : 16 * last, 128:176], stacked, preferred_element_type=f32)
        out = []
        for n in range(len(inputs)):
            cut = y[:, n * width : (n + 1) * width]
            out.append([cut[16 * g : 16 * g + 16] for g in range(last - first)])
        return out

    def applied(f, coupled):
        return mask * (coupled + diffusion * (2.0 * f - up(f) - down(f)))

    def streamed(g, gp, gm):
        return keep * g - up_diff(gp) - down_diff(gm)

    def streamed_twice(k1, gp, gm, g2p, g2m):
        return keep * k1 - up_diff(keep * gp - up_diff(g2p)) - down_diff(keep * gm - down_diff(g2m))

    ((gc, gcp, gcm, _, _, g2cp, g2cm),) = times(4, 11, [start])
    relaxed = r * gc
    shares = mask * (s1 + relaxed)
    res = mask * (shares - start)
    k1_start = streamed(relaxed, r * gcp, r * gcm)
    k2_start = streamed_twice(k1_start, r * gcp, r * gcm, r * g2cp, r * g2cm)

    def parts(f, ys):
        out = [applied(f, ys[0])]
        k1 = streamed(ys[1], ys[2], ys[3])
        rg = r * ys[4]
        held = rg - f
        out += [mask * (k1 + held), held]
        if len(ys) > 5:
            out.append(streamed_twice(k1, ys[2], ys[3], ys[7], ys[8]))
            out.append(streamed(rg, r * ys[5], r * ys[6]) + held)
        return out

    y_shares, y_res = times(0, 9, [shares, res])
    rg = r * y_shares[4]
    held_shares = rg - shares
    n_shares = streamed(rg, r * y_shares[5], r * y_shares[6]) + held_shares
    p0 = mask * (s2 + k1_start + held_shares)
    e, p1, _, k2_res, n_res = parts(res, y_res)

    y_e, y_p0, y_p1 = times(0, 9, [e, p0, p1])
    ee, p2, _, k2_e, n_e = parts(e, y_e)
    ap0, q3, held_p0 = parts(p0, y_p0[:5])
    ap1, q4, held_p1 = parts(p1, y_p1[:5])
    q0 = mask * (s3 + k2_start + n_shares + held_p0)
    q1 = mask * (k2_res + n_res + held_p1)

    y_p2, y_ap0, y_ap1, y_q0, y_q1, y_q3, y_q4 = times(0, 5, [p2, ap0, ap1, q0, q1, q3, q4])
    ap2, q5, held_p2 = parts(p2, y_p2)
    aap0, q6, _ = parts(ap0, y_ap0)
    aap1, q7, _ = parts(ap1, y_ap1)
    q2 = mask * (k2_e + n_e + held_p2)
    aq0, aq1, aq3, aq4 = (applied(f, y[0]) for f, y in ((q0, y_q0), (q1, y_q1), (q3, y_q3), (q4, y_q4)))

    (y_ap2,) = times(0, 5, [ap2])
    aap2, q8, _ = parts(ap2, y_ap2)
    first = [q2, q5, q6, q7, aq0, aq1, aq3, aq4]
    aq2, aq5, aq6, aq7, aaq0, aaq1, aaq3, aaq4 = (applied(f, y[0]) for f, y in zip(first, times(0, 1, first)))
    second = [q8, aq2, aq5, aq6, aq7]
    aq8, aaq2, aaq5, aaq6, aaq7 = (applied(f, y[0]) for f, y in zip(second, times(0, 1, second)))
    ((y_aq8,),) = times(0, 1, [aq8])
    aaq8 = applied(aq8, y_aq8)

    q = [q0, q1, q2, q3, q4, q5, q6, q7, q8]
    aq = [aq0, aq1, aq2, aq3, aq4, aq5, aq6, aq7, aq8]
    aaq = [aaq0, aaq1, aaq2, aaq3, aaq4, aaq5, aaq6, aaq7, aaq8]
    fields = [start, shares, res, e, p0, p1, p2, ap0, ap1, ap2] + q + aq
    plain = [[res], [p0, p1, p2], q]
    once = [[e], [ap0, ap1, ap2], aq]
    again = [[ee], [aap0, aap1, aap2], aaq]
    return fields, plain, once, again


EARLY = 4 * 1 + 4 * 6


def inner_products(plain, once, again, counted, table):
    lefts = [[[counted * x for x in xs] for xs in xss] for xss in (plain, once)]
    rights = [plain, once, again]
    if counted.shape[1] == STRIPS:
        def folded(x):
            return x[:, 0:256] + x[:, 256:512]

        lefts = [[[folded(x) for x in xs] for xs in xss] for xss in lefts]
        rights = lefts + [[[folded(counted * x) for x in xs] for xs in again]]
    table[EARLY:256, :] = jnp.zeros((256 - EARLY, 128), f32)
    table[256 : 256 + EARLY, :] = jnp.zeros((EARLY, 128), f32)
    table[len(PAIRS) + 128 : 384, :] = jnp.zeros((256 - len(PAIRS), 128), f32)
    ones = jnp.ones((8, 128), f32)
    tops = []
    for n, (stage, quantity, i, j) in enumerate(PAIRS):
        x, y = ((0, 0), (0, 1), (1, 1), (1, 2))[quantity]
        product = lefts[x][stage][i] * rights[y][stage][j]
        half = product[:, 0:128] + product[:, 128:256]
        at = n if n < EARLY else n + 128
        table[at : at + 1, :] = jnp.sum(half[0:8] + half[8:16], axis=0, keepdims=True)
    for n in range(3):
        tops.append(
            lax.dot_general(
                ones,
                table[128 * n : 128 * n + 128, :],
                (((1,), (1,)), ((), ())),
                precision=lax.Precision.HIGHEST,
                preferred_element_type=f32,
            )
        )
    return tops


def fields_kernel(n_space, got, known, block, fields, sent, table):
    slab = lax.axis_index("space")
    wide = (16, CELLS)
    w = jnp.concatenate([got[:, 16 * t : 16 * t + 16, :].reshape(PEERS * 16, 128) for t in range(2)], axis=1)
    wh = w.astype(bf16)
    wm = (w - wh.astype(f32)).astype(bf16)
    y = jnp.dot(block[BLOCK : BLOCK + 224, :], wh, preferred_element_type=f32)
    z = jnp.dot(block[BLOCK : BLOCK + 112, :], wm, preferred_element_type=f32)
    mu = (y[112:224] + z) + y[0:112]
    mu = [mu[16 * g : 16 * g + 16] for g in range(7)]

    lane8 = lanes_of((8, 128))
    parts = [[jnp.zeros((8, 128), f32)] * 2 for _ in range(2)]
    for j in range(PEERS):
        tile = got[j, 32:40, :]
        here = lane8 // 16 == j % 8
        for half in range(2):
            amount = (16 * j - 16 * half) % 128
            moved = pltpu.roll(tile, amount, 1) if amount else tile
            parts[half][j // 8] = jnp.where(here, moved, parts[half][j // 8])
    start = jnp.concatenate([jnp.concatenate(x, axis=1) for x in parts], axis=0)

    r = jnp.broadcast_to(known[16:17, 0:CELLS], wide)
    diffusion = jnp.concatenate([known[0:16, 128:256]] * 2, axis=1)
    up, down = own_shifts()
    s1, s2, s3 = advance_three(1.0 - r, mu[0], [mu[1], mu[3], mu[5]], [mu[2], mu[4], mu[6]], up, down)
    out, plain, once, again = fields_of(s1, s2, s3, start, r, 1.0, diffusion, block, up, down)
    for n, f in enumerate(out):
        fields[n] = f
    lane = lanes_of(wide)
    low = jnp.where(slab > 0, RIM, 0)
    high = jnp.where(slab < n_space - 1, CELLS - RIM, CELLS)
    counted = jnp.where((lane >= low) & (lane < high), 1.0, 0.0)
    tops = inner_products(plain, once, again, counted, table)

    lane1 = lanes_of((16, 128))
    row1 = rows_of((16, 128))
    start_relax = jnp.where(rows_of(wide) == K, r, start)
    tile = jnp.zeros((16, 128), f32)
    for n, f in enumerate([s1, s2, s3, start_relax]):
        at = lane1 - 32 * n
        begin = pltpu.roll(f[:, 0:128], 32 * n, 1) if n else f[:, 0:128]
        tile = jnp.where((at >= 0) & (at < SIDE), begin, tile)
        end = pltpu.roll(f[:, 128:256], (32 * n + 16 + SIDE) % 128, 1)
        tile = jnp.where((at >= 16) & (at < 16 + SIDE), end, tile)
        if n < 3:
            begin = pltpu.roll(mu[2 + 2 * n][:, 0:128], 32 * n + SIDE, 1)
            tile = jnp.where((at >= SIDE) & (at < 16), begin, tile)
            end = pltpu.roll(mu[1 + 2 * n][:, 128:256], (32 * n + 32) % 128, 1)
            tile = jnp.where((at >= 16 + SIDE) & (at < 32), end, tile)
    tile = pltpu.roll(tile, lax.rem(32 * lax.rem(slab, 4) + 112, 128), 1)
    row_a = jnp.broadcast_to(tops[0][0:1] + tops[1][0:1], (16, 128))
    row_b = jnp.broadcast_to(tops[2][0:1], (16, 128))
    tile = jnp.where(row1 == 14, row_a, jnp.where(row1 == 15, row_b, tile))
    for j in range(n_space):
        sent[j] = tile


def speeds_of(shape):
    number = 2 * lax.axis_index("vel") + jnp.where(rows_of(shape) >= 8, 1, 0)
    return time_step * jnp.abs((number.astype(f32) + 0.5) * spacing - 4.0)


def bands_of(r, positive):
    a = speeds_of(r.shape)
    stay = 1.0 - r - a

    def before(x):
        return jnp.where(positive, shift_up(x), shift_down(x))

    once = before(stay)
    two = before(once)
    t0 = stay * stay * stay
    t1 = a * (stay * (stay + once) + once * once)
    t2 = a * a * (stay + once + two)
    return t0, t1, t2, a * a * a


def banded(weights, u, distance):
    value = jnp.zeros(distance.shape, f32)
    for n, x in enumerate(weights):
        row = jnp.broadcast_to(x[8 * u : 8 * u + 1, 0 : distance.shape[1]], distance.shape)
        value = jnp.where(distance == n, row, value)
    return value


def stream_kernel(
    dist_in,
    block_in,
    pairs_in,
    own_in,
    coupling_in,
    diff_in,
    rate_in,
    flags_in,
    out,
    table,
    block,
    dist,
    own6,
    coupling_raw,
    diff_raw,
    rate,
    flags,
    sems,
):
    vel = lax.axis_index("vel")
    positive = vel >= PEERS // 2
    moves = [(rate_in, rate), (flags_in, flags), (dist_in, dist)]
    moves += [(coupling_in, coupling_raw), (diff_in, diff_raw), (own_in.at[vel], own6)]
    moves += [(pairs_in, table.at[24:56, 0:128]), (block_in, block)]
    waits = copies_of(moves, sems)
    waits[0].wait()
    waits[1].wait()
    relax = relax_of(rate[...], flags[...])
    table[16:24, 0:CELLS] = jnp.broadcast_to(relax, (8, CELLS))
    weights = bands_of(jnp.broadcast_to(relax, (16, CELLS)), positive)
    towards = jnp.where(positive, 1, -1)
    distance = (lanes_of((CELLS, CELLS)) - rows_of((CELLS, CELLS))) * towards
    waits[2].wait()
    for u in range(2):
        b = banded(weights, u, distance)
        bh = b.astype(bf16)
        bl = (b - bh.astype(f32)).astype(bf16)
        rows = pl.ds(u * BLOCK, BLOCK)
        x = dist[rows, :]
        value = jnp.dot(x, bh, preferred_element_type=f32)
        value += jnp.dot(x, bl, preferred_element_type=f32)
        out[rows, :] = value

    for copy in waits[3:]:
        copy.wait()
    table[0:16, 0:128] = jnp.zeros((16, 128), f32)
    table[0:K, 0:K] = coupling_raw[...]
    c = table[0:16, 0:128]
    ch = c.astype(bf16).astype(f32)
    pieces = [ch, ch, c - ch]
    terms = pieces[0]
    for n in range(1, 3):
        terms = terms + pltpu.roll(pieces[n], 16 * n, 1)
    block[0:16, 128:256] = terms.astype(bf16)
    block[176:192, 128:256] = own6[...]
    shape = (16, K)
    chosen = jnp.where(lanes_of(shape) == rows_of(shape), jnp.broadcast_to(diff_raw[...], shape), 0.0)
    table[0:16, 128:256] = jnp.broadcast_to(jnp.sum(chosen, axis=1, keepdims=True), (16, 128))


UPDATE_ROWS = 256


def strips_of(n_space, sent):
    raw = []
    lane1 = lanes_of((16, 128))
    for n in range(4):
        which = ((lane1 + 128 - 32 * n) % 128 // 16 + 1) // 2
        tiles = []
        for t in range(4):
            tile = jnp.zeros((16, 128), f32)
            for k in range(5):
                if 4 * t + k < n_space:
                    tile = jnp.where(which == k, sent[4 * t + k], tile)
            amount = (STEP[t] - 32 * n) % 128
            tiles.append(pltpu.roll(tile, amount, 1) if amount else tile)
        raw.append(jnp.concatenate(tiles, axis=1))
    shape = (16, STRIPS)
    row = rows_of(shape)
    turned = jnp.concatenate([(lane1 + 128 - STEP[t]) % 128 + 128 * t for t in range(4)], axis=1)
    at = turned % 32
    valid = (turned < 32 * (n_space - 1)) & (at < 2 * SIDE)
    mask = jnp.where(valid, 1.0, 0.0)
    moments = jnp.where(row < K, mask, 0.0)
    closer = [tile_roll(x, 128 - 3) for x in raw]
    arrays = [jnp.where(at < SIDE, x, y) for x, y in zip(raw, closer)]
    r = mask * jnp.broadcast_to(arrays[3][K : K + 1], shape)
    s1, s2, s3, start = (moments * x for x in arrays)
    ups = [jnp.where((at >= SIDE - 3) & (at < SIDE), moments * x, 0.0) for x in closer[:3]]
    downs = [tile_roll(x, 128 - 16) for x in raw[:3]]
    downs = [jnp.where((at >= SIDE) & (at < SIDE + 3), moments * x, 0.0) for x in downs]
    zero = jnp.zeros(shape, f32)
    over_up = advance_three(1.0 - r, zero, ups, [], strip_up, strip_down)
    over_down = advance_three(1.0 - r, zero, [], downs, strip_up, strip_down)
    s = [x + jnp.where(at < SIDE, y, z) for x, y, z in zip((s1, s2, s3), over_down, over_up)]
    s = [mask * x for x in s]
    counted = jnp.where((at >= SIDE - RIM) & (at < SIDE + RIM), mask, 0.0)
    return s, start, r, mask, counted


def update_kernel(
    n_space,
    sent,
    fields,
    table,
    block,
    base,
    edges_in,
    out,
    macro,
    done,
    macro_part,
    products,
    edges,
    ends,
    sems,
):
    place = lax.axis_index("vel")
    slab = lax.axis_index("space")
    positive = place >= PEERS // 2
    (edge_copy,) = copies_of([(edges_in, edges)], sems.at[pl.ds(ROWS // UPDATE_ROWS + 1, 1)])

    def known(at):
        return table[at : at + 8, 0:128]

    (s1, s2, s3), strip_start, strip_r, strip_mask, counted = strips_of(n_space, sent)
    diffusion = jnp.concatenate([table[0:16, 128:256]] * 4, axis=1)
    strip_fields, plain, once, again = fields_of(
        s1, s2, s3, strip_start, strip_r, strip_mask, diffusion, block, strip_up, strip_down
    )
    tops = inner_products(plain, once, again, counted, products)
    gathered = sent[0, 8:16, :]
    for j in range(1, n_space):
        gathered = gathered + sent[j, 8:16, :]
    row8 = rows_of((8, 128))
    early = jnp.where(row8 == 0, gathered[6:7] + tops[0][0:1], 0.0) * known(48)
    line_a = gathered[6:7] + tops[1][0:1]
    line_b = gathered[7:8] + tops[2][0:1]
    total = jnp.where(row8 == 0, line_a, jnp.where(row8 == 1, line_b, 0.0))
    total = total * known(48)
    cpl = table[0:16, 0:128]
    lane16 = lanes_of((16, 128))
    row16 = rows_of((16, 128))
    size = jnp.sum(jnp.abs(cpl), axis=1, keepdims=True)
    middle = jnp.sum(jnp.where(lane16 == row16, cpl, 0.0), axis=1, keepdims=True)
    real = row16[:, 0:1] < K
    most = jnp.max(jnp.where(real, size + 4.0 * table[0:16, 128:129], 0.0), axis=0, keepdims=True)
    least = jnp.min(jnp.where(real, 2.0 * middle - size, 1e30), axis=0, keepdims=True)
    low_step, high_step = 1.0 / most, 1.0 / least

    def summed(weighted, which):
        picked = jnp.where(known(24) == which, weighted, 0.0)
        return jnp.sum(jnp.sum(picked, axis=0, keepdims=True), axis=1, keepdims=True)

    def clipped(x):
        return jnp.minimum(jnp.maximum(x, low_step), high_step)

    def weights_of(stage, weighted):
        rr, ra, aa, aaa = (summed(weighted, 4 * stage + n) for n in range(4))
        s1 = clipped(rr / ra)
        rr2 = rr - 2.0 * s1 * ra + s1 * s1 * aa
        ra2 = ra - 2.0 * s1 * aa + s1 * s1 * aaa
        s2 = clipped(rr2 / ra2)
        return s1 + s2, -s1 * s2

    li, ri = (known(n).astype(jnp.int32) for n in (32, 40))

    def choose(index, zero, one, two):
        return jnp.where(index == 0, zero, jnp.where(index == 1, one, two))

    a1, b1 = weights_of(0, early)
    a2, b2 = weights_of(1, early * choose(li, 1.0, a1, b1) * choose(ri, 1.0, a1, b1))

    def both(index):
        outer = (index >= 3).astype(jnp.int32) + (index >= 6).astype(jnp.int32)
        return choose(outer, 1.0, a2, b2) * choose(index - 3 * outer, 1.0, a1, b1)

    a3, b3 = weights_of(2, total * both(li) * both(ri))

    def last_fields(at, r):
        start, shares, res, e = (at(n) for n in range(4))
        corr1 = a1 * res + b1 * e
        cur1 = shares + corr1
        res2 = at(4) + a1 * at(5) + b1 * at(6)
        e2 = at(7) + a1 * at(8) + b1 * at(9)
        corr2 = a2 * res2 + b2 * e2
        cur2 = res2 + cur1 + corr2

        def third(first):
            rows = [at(first + 3 * n) + a1 * at(first + 3 * n + 1) + b1 * at(first + 3 * n + 2) for n in range(3)]
            return rows[0] + a2 * rows[1] + b2 * rows[2]

        res3, e3 = third(10), third(19)
        corr3 = a3 * res3 + b3 * e3
        row = rows_of(r.shape)
        scaled = r * jnp.where(row < 5, 1.0, jnp.where(row < 10, 0.0, 1.0 / 3.0))
        f1 = scaled * start + corr1
        f2 = scaled * cur1 + corr2
        f3 = scaled * cur2 + corr3
        return f1, f2, f3, res3 + cur2 + corr3, r

    own = last_fields(lambda n: fields[n], jnp.broadcast_to(table[16:17, 0:CELLS], (16, CELLS)))
    strips = last_fields(lambda n: strip_fields[n], strip_r)
    lane1 = lanes_of((16, 128))
    has_left, has_right = jnp.where(slab > 0, 1, 0), jnp.where(slab < n_space - 1, 1, 0)
    near_left = (lane1 < RIM * has_left)
    near_right = (lane1 >= 128 - RIM * has_right)
    far_left = (lane1 >= 128 - 2 * has_left)
    far_right = (lane1 < 2 * has_right)
    wide = []
    for x, y in zip(own, strips):
        y = jnp.concatenate([y[:, 0:256], tile_roll(y[:, 256:512], 112)], axis=1)
        y = pltpu.roll(y, lax.rem(STRIPS + 32 - 32 * slab, STRIPS), 1)[:, 0:128]
        from_left = pltpu.roll(y, 128 - SIDE, 1)
        from_right = pltpu.roll(y, 96 - SIDE, 1)
        tiles = [
            jnp.where(near_left, from_left, x[:, 0:128]),
            jnp.where(near_right, from_right, x[:, 128:256]),
            jnp.where(far_left, from_left, jnp.where(far_right, from_right, 0.0)),
        ]
        wide.append(jnp.concatenate(tiles, axis=1))
    f1, f2, f3, cur3, r = wide
    mine = pltpu.roll(cur3[:, 0:CELLS], lax.rem(CELLS - 16 * place, CELLS), 1)
    macro_part[...] = mine[0:K, 0:16]
    macro_copy = pltpu.make_async_copy(macro_part, macro, sems.at[ROWS // UPDATE_ROWS])
    macro_copy.start()
    y = jnp.dot(
        block[176:192, 128:176], split3(jnp.concatenate([f1, f2, f3], axis=1)), preferred_element_type=f32
    )
    y1, y2, y3 = (y[:, n * WIDE : (n + 1) * WIDE] for n in range(3))
    a = speeds_of((16, WIDE))
    stay = 1.0 - r - a

    def moved(x):
        return stay * x + a * jnp.where(positive, shift_up(x), shift_down(x))

    h = (moved(moved(y1) + y2) + y3)[:, 0:CELLS]
    hh = h.astype(bf16).astype(f32)
    hm = (h - hh).astype(bf16).astype(f32)

    weights = bands_of(r, positive)
    towards = jnp.where(positive, 1, -1)
    at8 = rows_of((8, 128))
    at8 = jnp.where(positive, -1 - at8, at8 + CELLS)
    low = jnp.where(positive, 0, CELLS - 128)
    distance = (lanes_of((8, 128)) + low - at8) * towards
    weights = [jnp.where(positive, x[:, 0:128], x[:, 128:256]) for x in weights]
    ends[...] = jnp.zeros((16, ROWS), f32)
    edge_copy.wait()
    for n in range(3):
        for k in range(16):
            row = edges[16 * n + k : 16 * n + k + 1, :]
            ends[n : n + 1, 128 * k : 128 * k + 128] = row
            ends[8 + n : 9 + n, 128 * k : 128 * k + 128] = row

    sends = [macro_copy]
    for u in range(2):
        hu, mu = hh[8 * u : 8 * u + 8], hm[8 * u : 8 * u + 8]
        mixed = jnp.concatenate([hu, mu, hu, jnp.zeros((104, CELLS), f32)], axis=0).astype(bf16)
        b = banded(weights, u, distance)
        bh = b.astype(bf16).astype(f32)
        b = jnp.concatenate([bh, b - bh], axis=0).astype(bf16)
        for n in range(BLOCK // UPDATE_ROWS):
            part = u * (BLOCK // UPDATE_ROWS) + n
            rows = pl.ds(part * UPDATE_ROWS, UPDATE_ROWS)
            value = jnp.dot(block[pl.ds(n * UPDATE_ROWS, UPDATE_ROWS), 0:128], mixed, preferred_element_type=f32)
            near = lax.dot_general(ends[:, rows].astype(bf16), b, (((0,), (0,)), ((), ())), preferred_element_type=f32)
            value += base[rows, :]
            done[rows, 0:128] = (value[:, 0:128] + jnp.where(positive, near, 0.0)).astype(bf16)
            done[rows, 128:256] = (value[:, 128:256] + jnp.where(positive, 0.0, near)).astype(bf16)
            copy = pltpu.make_async_copy(done.at[rows, :], out.at[rows, :], sems.at[part])
            copy.start()
            sends.append(copy)
    for copy in sends:
        copy.wait()


def vmem():
    return pl.BlockSpec(memory_space=pltpu.VMEM)


def hbm():
    return pl.BlockSpec(memory_space=pltpu.HBM)


def shaped(shape, dtype=f32):
    return pltpu.VMEM(shape, dtype)


def stored(shape, dtype=f32):
    return pltpu.HBM(shape, dtype)


def placed_at(space, arrays):
    return [pltpu.with_memory_space_constraint(x, space) for x in arrays]


def near(*arrays):
    return placed_at(pltpu.VMEM, arrays)


def far(*arrays):
    return placed_at(pltpu.HBM, arrays)


def limit(mib):
    return pltpu.CompilerParams(vmem_limit_bytes=mib * 2**20)


def make_per_device(n_space):
    block, p3, own6 = grid_constants()
    pairs = pair_arrays()

    def per_device(velocity_dist, macro_state, collision_rate, wall_flags, diffusivity, coupling):
        rate = collision_rate.reshape(1, CELLS)
        flags = wall_flags.reshape(1, CELLS)
        packed, edges = pl.pallas_call(
            sums_kernel,
            out_shape=(shaped((PEERS, 40, 128)), shaped((48, 128))),
            in_specs=[hbm()] * 3,
            out_specs=(vmem(), vmem()),
            scratch_shapes=[
                pltpu.VMEM((ROWS, CELLS), bf16),
                pltpu.VMEM((16, BLOCK), bf16),
                pltpu.VMEM((K, 16), f32),
                pltpu.VMEM((16, 128), f32),
                pltpu.SemaphoreType.DMA((2 + CHUNKS,)),
            ],
            compiler_params=limit(8),
            name="sums",
        )(*far(velocity_dist, jnp.asarray(p3), macro_state))
        got = lax.all_to_all(packed, "vel", split_axis=0, concat_axis=0, tiled=True)
        rising = [(i, i + 1) for i in range(n_space - 1)]
        half = PEERS // 2
        downwind = [(i * PEERS + n, j * PEERS + n) for i, j in rising for n in range(half, PEERS)]
        downwind += [(j * PEERS + n, i * PEERS + n) for i, j in rising for n in range(half)]
        edges = lax.ppermute(edges, ("space", "vel"), downwind)
        base, known, constants = pl.pallas_call(
            stream_kernel,
            out_shape=(shaped((ROWS, CELLS)), shaped((56, WIDE)), shaped(block.shape, bf16)),
            in_specs=[hbm()] * 8,
            out_specs=(vmem(),) * 3,
            scratch_shapes=[
                pltpu.VMEM((ROWS, CELLS), bf16),
                pltpu.VMEM((16, 128), bf16),
                pltpu.VMEM((K, K), f32),
                pltpu.VMEM((1, K), f32),
                pltpu.VMEM((1, CELLS), f32),
                pltpu.VMEM((1, CELLS), jnp.int32),
                pltpu.SemaphoreType.DMA((8,)),
            ],
            compiler_params=limit(16),
            cost_estimate=pl.CostEstimate(flops=600_000_000, bytes_accessed=4_000_000, transcendentals=0),
            name="stream",
        )(
            *far(velocity_dist, *(jnp.asarray(x) for x in (block, pairs, own6))),
            *far(coupling, diffusivity.reshape(1, K), rate, flags),
        )
        got, base, edges = lax.optimization_barrier((got, base, edges))
        fields, sent = pl.pallas_call(
            lambda *refs: fields_kernel(n_space, *refs),
            out_shape=(shaped((N_FIELDS, 16, CELLS)), shaped((n_space, 16, 128))),
            in_specs=[vmem()] * 3,
            out_specs=(vmem(), vmem()),
            scratch_shapes=[pltpu.VMEM((384, 128), f32)],
            compiler_params=limit(12),
            name="fields",
        )(*near(got, known, constants))
        sent = lax.all_to_all(sent, "space", split_axis=0, concat_axis=0, tiled=True)
        return pl.pallas_call(
            lambda *refs: update_kernel(n_space, *refs),
            out_shape=(stored((ROWS, CELLS), bf16), stored((K, 16))),
            in_specs=[vmem()] * 5 + [hbm()],
            out_specs=(hbm(), hbm()),
            scratch_shapes=[
                pltpu.VMEM((ROWS, CELLS), bf16),
                pltpu.VMEM((K, 16), f32),
                pltpu.VMEM((384, 128), f32),
                pltpu.VMEM((48, 128), f32),
                pltpu.VMEM((16, ROWS), f32),
                pltpu.SemaphoreType.DMA((ROWS // UPDATE_ROWS + 2,)),
            ],
            compiler_params=limit(12),
            name="update",
        )(*near(sent, fields, known, constants, base), *far(edges))

    return per_device


def solution(mesh):
    placed = (P("vel", "space"), P(None, ("space", "vel")), P("space"), P("space"), P(), P())
    return jax.shard_map(
        make_per_device(mesh.shape["space"]),
        mesh=mesh,
        in_specs=placed,
        out_specs=(P("vel", "space"), P(None, ("space", "vel"))),
        check_vma=False,
    )
```

```python
import math

import jax
import jax.numpy as jnp
import numpy as np
from jax import lax
from jax.experimental import pallas as pl
from jax.experimental.pallas import tpu as pltpu
from jax.sharding import PartitionSpec as P

NV1 = 32
K = 13
time_step = 0.125
spacing = 8.0 / NV1
CELLS = 256
WIDE = 384
PEERS = 16
ROWS = 2048
BLOCK = 1024
bf16 = jnp.bfloat16
f32 = jnp.float32


def parts_of(x, number):
    rest = np.asarray(x, np.float64)
    out = []
    for _ in range(number):
        piece = rest.astype(np.float32).astype(bf16)
        out.append(piece)
        rest = rest - piece.astype(np.float64)
    return out


def grid_constants():
    v = (np.arange(NV1) + 0.5) * spacing - 4.0
    w = np.exp(-0.5 * v * v) * spacing / math.sqrt(2.0 * math.pi)
    vy, vz = np.repeat(v, NV1), np.tile(v, NV1)
    wyz = np.repeat(w, NV1) * np.tile(w, NV1)
    one = np.ones_like(vy)
    yz = vy * vy + vz * vz
    phi = np.stack([one, vy, vz, vy * vz, vy * vy, vz * vz, vy * yz, vz * yz])
    cmat = np.zeros((NV1, K, 8))
    for i, x in enumerate(v):
        c = cmat[i]
        c[0, 0] = 1.0
        c[1, 0] = x
        c[2, 1] = 1.0
        c[3, 2] = 1.0
        c[4, 0] = (x * x - 3.0) / math.sqrt(6.0)
        c[4, 4] = c[4, 5] = 1.0 / math.sqrt(6.0)
        c[5, 1] = x
        c[6, 2] = x
        c[7, 3] = 1.0
        c[8, 0] = 0.5 * x * x
        c[8, 4] = -0.5
        c[9, 0] = x * x / math.sqrt(12.0)
        c[9, 4] = 1.0 / math.sqrt(12.0)
        c[9, 5] = -2.0 / math.sqrt(12.0)
        c[10, 0] = x * (x * x - 5.0) / math.sqrt(10.0)
        c[10, 4] = c[10, 5] = x / math.sqrt(10.0)
        c[11, 1] = (x * x - 5.0) / math.sqrt(10.0)
        c[11, 6] = 1.0 / math.sqrt(10.0)
        c[12, 2] = (x * x - 5.0) / math.sqrt(10.0)
        c[12, 7] = 1.0 / math.sqrt(10.0)
    a = time_step * np.abs(v)
    plus = v > 0.0
    proj = phi * wyz
    groups = [np.ones(NV1)]
    for power in (1, 2, 3):
        groups += [a**power * plus, a**power * ~plus]
    big = np.zeros((7 * 16, 8 * NV1))
    for g, factor in enumerate(groups):
        for i in range(NV1):
            big[16 * g : 16 * g + K, 8 * i : 8 * i + 8] = factor[i] * w[i] * cmat[i]
    gram2 = proj @ phi.T
    shakhov = np.array([1.0] * 5 + [0.0] * 5 + [1.0 / 3.0] * 3)

    def between(factor):
        out = np.zeros((16, 16))
        for i in range(NV1):
            out[:K, :K] += factor[i] * w[i] * cmat[i] @ gram2 @ cmat[i].T
        return out

    c16 = np.zeros(16)
    c16[:K] = shakhov
    g, gp, gm, g2p, g2m = (between(groups[k]) for k in (0, 1, 2, 3, 4))
    mats = [g, gp, gm, g * c16, gp * c16, gm * c16, g2p, g2m, g2p * c16, g2m * c16]
    block = np.zeros((BLOCK + 224, 256), bf16)
    block[16:176, 128:176] = three_terms(np.concatenate(mats, axis=0))
    block[BLOCK:] = np.concatenate(parts_of(big, 2), axis=0)
    p3 = np.concatenate(parts_of(proj, 2), axis=0)
    ph, pm = parts_of(phi.T, 2)
    block[0:BLOCK, 0:24] = np.concatenate([ph, ph, pm], axis=1)
    own = np.zeros((PEERS, 16, 16))
    for j in range(PEERS):
        for u in range(2):
            own[j, 8 * u : 8 * u + 8, :K] = cmat[2 * j + u].T
    own = np.concatenate([three_terms(own), np.zeros((PEERS, 16, 80), bf16)], axis=2)
    return block, p3, own


def three_terms(x):
    h, m = parts_of(x, 2)
    return np.concatenate([h, h, m], axis=-1)


BASES = (1, 3, 9)


def pair_table():
    entries = []
    for stage, size in enumerate(BASES):
        for quantity in range(4):
            for i in range(size):
                for j in range(i, size):
                    entries.append((stage, quantity, i, j))
    return entries


PAIRS = pair_table()


def pair_arrays():
    kind = np.full((8, 128), -1, np.int32)
    left = np.zeros((8, 128), np.int32)
    right = np.zeros((8, 128), np.int32)
    twice = np.zeros((8, 128), np.int32)
    for n, (stage, quantity, i, j) in enumerate(PAIRS):
        at = (n // 128, n % 128)
        kind[at] = 4 * stage + quantity
        left[at], right[at] = i, j
        twice[at] = 1 if i == j else 2
    return np.concatenate([kind, left, right, twice], axis=0).astype(np.float32)


def lanes_of(shape):
    return lax.broadcasted_iota(jnp.int32, shape, len(shape) - 1)


def rows_of(shape):
    return lax.broadcasted_iota(jnp.int32, shape, 0)


def split3(f):
    h = f.astype(bf16)
    m = (f - h.astype(f32)).astype(bf16)
    return jnp.concatenate([h, m, h], axis=0)


def relax_of(rate, flags):
    return (time_step * rate) * (1.0 + flags.astype(f32))


def shift_up(x):
    return pltpu.roll(x, 1, 1)


def shift_down(x):
    return pltpu.roll(x, x.shape[1] - 1, 1)


def diff_up(x):
    return x - shift_up(x)


def diff_down(x):
    return x - shift_down(x)


def copies_of(pairs, sems):
    made = [pltpu.make_async_copy(x, y, sems.at[n]) for n, (x, y) in enumerate(pairs)]
    for copy in made:
        copy.start()
    return made


CHUNKS = 8


def chunks_of(source, target):
    rows = [pl.ds(n * (ROWS // CHUNKS), ROWS // CHUNKS) for n in range(CHUNKS)]
    return [(source.at[row, :], target.at[row, :]) for row in rows]


def sums_kernel(dist_in, p3_in, start_in, packed, edges, dist, p3, start, padded, sems):
    positive = lax.axis_index("vel") >= PEERS // 2
    halves = [pl.ds(u * BLOCK, BLOCK) for u in range(2)]
    pairs = [(p3_in, p3), (start_in, start)] + chunks_of(dist_in, dist)
    waits = copies_of(pairs, sems)
    waits[0].wait()
    waits[1].wait()
    padded[...] = jnp.zeros((16, 128), f32)
    padded[0:K, 0:16] = start[...]
    owned = padded[0:8, :] + pltpu.roll(padded[8:16, :], 16, 1)
    for j in range(PEERS):
        packed[j, 32:40, :] = owned
    e_lane = lanes_of((16, 128))
    e_row = rows_of((16, 128))
    cell = jnp.where(positive, 127 - e_row, e_row)
    pick = jnp.where((e_lane == cell) & (e_row < 3), 1.0, 0.0).astype(bf16)
    side = pl.multiple_of(jnp.where(positive, 128, 0), 128)
    for u in range(2):
        for n in range(CHUNKS // 2):
            waits[2 + u * (CHUNKS // 2) + n].wait()
        y = jnp.dot(p3[...], dist[halves[u], :], preferred_element_type=f32)
        w = y[0:8] + y[8:16]
        for j in range(PEERS):
            packed[j, 8 * u : 8 * u + 8, :] = w[:, 0:128]
            packed[j, 16 + 8 * u : 24 + 8 * u, :] = w[:, 128:256]
        near = dist[halves[u], pl.ds(side, 128)]
        e = lax.dot_general(pick, near, (((1,), (1,)), ((), ())), preferred_element_type=f32)
        for n in range(3):
            for k in range(8):
                at = 16 * n + 8 * u + k
                edges[at : at + 1, :] = e[n : n + 1, 128 * k : 128 * k + 128]


N_FIELDS = 28
RIM = 7
SIDE = 13
STRIPS = 512


def tiles_of(x):
    return [x[:, 128 * t : 128 * t + 128] for t in range(x.shape[1] // 128)]


def own_shifts():
    lane = lanes_of((16, 128))
    zero = jnp.zeros((16, 128), f32)

    def up(x):
        first, second = (pltpu.roll(t, 1, 1) for t in tiles_of(x))
        return jnp.concatenate([jnp.where(lane == 0, zero, first), jnp.where(lane == 0, first, second)], axis=1)

    def down(x):
        first, second = (pltpu.roll(t, 127, 1) for t in tiles_of(x))
        return jnp.concatenate([jnp.where(lane == 127, second, first), jnp.where(lane == 127, zero, second)], axis=1)

    return up, down


STEP = (0, 0, 16, 16)


def tile_roll(x, amount):
    return jnp.concatenate([pltpu.roll(t, amount, 1) for t in tiles_of(x)], axis=1)


def strip_up(x):
    return tile_roll(x, 1)


def strip_down(x):
    return tile_roll(x, 127)


def advance_three(keep, base, ups, downs, up, down):
    out = []
    for _ in range(3):
        base = keep * base
        if ups:
            base = base - (ups[0] - up(ups[0]))
        if downs:
            base = base - (downs[0] - down(downs[0]))
        ups = [keep * x - (y - up(y)) for x, y in zip(ups[:-1], ups[1:])]
        downs = [keep * x - (y - down(y)) for x, y in zip(downs[:-1], downs[1:])]
        out.append(base)
    return out


def fields_of(s1, s2, s3, start, r, mask, diffusion, block, up, down):
    width = r.shape[1]
    keep = 1.0 - r

    def up_diff(x):
        return x - up(x)

    def down_diff(x):
        return x - down(x)

    def times(first, last, inputs):
        stacked = split3(jnp.concatenate(inputs, axis=1) if len(inputs) > 1 else inputs[0])
        y = jnp.dot(block[16 * first : 16 * last, 128:176], stacked, preferred_element_type=f32)
        out = []
        for n in range(len(inputs)):
            cut = y[:, n * width : (n + 1) * width]
            out.append([cut[16 * g : 16 * g + 16] for g in range(last - first)])
        return out

    def applied(f, coupled):
        return mask * (coupled + diffusion * (2.0 * f - up(f) - down(f)))

    def streamed(g, gp, gm):
        return keep * g - up_diff(gp) - down_diff(gm)

    def streamed_twice(k1, gp, gm, g2p, g2m):
        return keep * k1 - up_diff(keep * gp - up_diff(g2p)) - down_diff(keep * gm - down_diff(g2m))

    ((gc, gcp, gcm, _, _, g2cp, g2cm),) = times(4, 11, [start])
    relaxed = r * gc
    shares = mask * (s1 + relaxed)
    res = mask * (shares - start)
    k1_start = streamed(relaxed, r * gcp, r * gcm)
    k2_start = streamed_twice(k1_start, r * gcp, r * gcm, r * g2cp, r * g2cm)

    def parts(f, ys):
        out = [applied(f, ys[0])]
        k1 = streamed(ys[1], ys[2], ys[3])
        rg = r * ys[4]
        held = rg - f
        out += [mask * (k1 + held), held]
        if len(ys) > 5:
            out.append(streamed_twice(k1, ys[2], ys[3], ys[7], ys[8]))
            out.append(streamed(rg, r * ys[5], r * ys[6]) + held)
        return out

    y_shares, y_res = times(0, 9, [shares, res])
    rg = r * y_shares[4]
    held_shares = rg - shares
    n_shares = streamed(rg, r * y_shares[5], r * y_shares[6]) + held_shares
    p0 = mask * (s2 + k1_start + held_shares)
    e, p1, _, k2_res, n_res = parts(res, y_res)

    y_e, y_p0, y_p1 = times(0, 9, [e, p0, p1])
    ee, p2, _, k2_e, n_e = parts(e, y_e)
    ap0, q3, held_p0 = parts(p0, y_p0[:5])
    ap1, q4, held_p1 = parts(p1, y_p1[:5])
    q0 = mask * (s3 + k2_start + n_shares + held_p0)
    q1 = mask * (k2_res + n_res + held_p1)

    y_p2, y_ap0, y_ap1, y_q0, y_q1, y_q3, y_q4 = times(0, 5, [p2, ap0, ap1, q0, q1, q3, q4])
    ap2, q5, held_p2 = parts(p2, y_p2)
    aap0, q6, _ = parts(ap0, y_ap0)
    aap1, q7, _ = parts(ap1, y_ap1)
    q2 = mask * (k2_e + n_e + held_p2)
    aq0, aq1, aq3, aq4 = (applied(f, y[0]) for f, y in ((q0, y_q0), (q1, y_q1), (q3, y_q3), (q4, y_q4)))

    (y_ap2,) = times(0, 5, [ap2])
    aap2, q8, _ = parts(ap2, y_ap2)
    first = [q2, q5, q6, q7, aq0, aq1, aq3, aq4]
    aq2, aq5, aq6, aq7, aaq0, aaq1, aaq3, aaq4 = (applied(f, y[0]) for f, y in zip(first, times(0, 1, first)))
    second = [q8, aq2, aq5, aq6, aq7]
    aq8, aaq2, aaq5, aaq6, aaq7 = (applied(f, y[0]) for f, y in zip(second, times(0, 1, second)))
    ((y_aq8,),) = times(0, 1, [aq8])
    aaq8 = applied(aq8, y_aq8)

    q = [q0, q1, q2, q3, q4, q5, q6, q7, q8]
    aq = [aq0, aq1, aq2, aq3, aq4, aq5, aq6, aq7, aq8]
    aaq = [aaq0, aaq1, aaq2, aaq3, aaq4, aaq5, aaq6, aaq7, aaq8]
    fields = [start, shares, res, e, p0, p1, p2, ap0, ap1, ap2] + q + aq
    plain = [[res], [p0, p1, p2], q]
    once = [[e], [ap0, ap1, ap2], aq]
    again = [[ee], [aap0, aap1, aap2], aaq]
    return fields, plain, once, again


EARLY = 4 * 1 + 4 * 6
LATE_FROM = EARLY // 8 * 8
EARLY_SHEETS = (EARLY + 7) // 8 * 64 + 8
SHEETS = EARLY_SHEETS + 8 * (len(PAIRS) - LATE_FROM) + 8


def product_operands(plain, once, again, counted):
    lefts = [[[counted * x for x in xs] for xs in xss] for xss in (plain, once)]
    rights = [plain, once, again]
    if counted.shape[1] == STRIPS:
        def folded(x):
            return x[:, 0:256] + x[:, 256:512]

        lefts = [[[folded(x) for x in xs] for xs in xss] for xss in lefts]
        rights = lefts + [[[folded(counted * x) for x in xs] for xs in again]]
    return lefts, rights


def inner_products(operands, entries, first, sheets, table):
    lefts, rights = operands
    start = first // 8 * 8
    stop = entries.stop
    zero = jnp.zeros((8, 128), f32)
    end = (stop + 7) // 8 * 8
    for n in range(start, end):
        if n not in entries:
            sheets[8 * (n - start) : 8 * (n - start) + 8, :] = zero
            continue
        stage, quantity, i, j = PAIRS[n]
        x, y = ((0, 0), (0, 1), (1, 1), (1, 2))[quantity]
        product = lefts[x][stage][i] * rights[y][stage][j]
        half = product[:, 0:128] + product[:, 128:256]
        sheets[8 * (n - start) : 8 * (n - start) + 8, :] = half[0:8] + half[8:16]
    lines = (end + 127) // 128
    if start:
        table[0:start, :] = jnp.zeros((start, 128), f32)
    if end < 128 * lines:
        table[end : 128 * lines, :] = jnp.zeros((128 * lines - end, 128), f32)
    for n in range(start, end, 8):
        rows = [sheets[pl.ds(8 * (n - start) + k, 8, stride=8), :] for k in range(8)]
        while len(rows) > 1:
            rows = [p + q for p, q in zip(rows[0::2], rows[1::2])]
        table[n : n + 8, :] = rows[0]
    ones = jnp.ones((8, 128), f32)
    return [
        lax.dot_general(
            ones,
            table[128 * n : 128 * n + 128, :],
            (((1,), (1,)), ((), ())),
            precision=lax.Precision.HIGHEST,
            preferred_element_type=f32,
        )
        for n in range(lines)
    ]


def early_products(operands, sheets, table):
    return inner_products(operands, range(EARLY), 0, sheets.at[0:EARLY_SHEETS, :], table.at[0:128, :])


def late_products(operands, sheets, table):
    return inner_products(operands, range(EARLY, len(PAIRS)), EARLY, sheets.at[EARLY_SHEETS:SHEETS, :], table.at[128:384, :])


def fields_kernel(n_space, got, known, block, fields, sent, table, sheets):
    slab = lax.axis_index("space")
    wide = (16, CELLS)
    w = jnp.concatenate([got[:, 16 * t : 16 * t + 16, :].reshape(PEERS * 16, 128) for t in range(2)], axis=1)
    wh = w.astype(bf16)
    wm = (w - wh.astype(f32)).astype(bf16)
    y = jnp.dot(block[BLOCK : BLOCK + 224, :], wh, preferred_element_type=f32)
    z = jnp.dot(block[BLOCK : BLOCK + 112, :], wm, preferred_element_type=f32)
    mu = (y[112:224] + z) + y[0:112]
    mu = [mu[16 * g : 16 * g + 16] for g in range(7)]

    lane8 = lanes_of((8, 128))
    parts = [[jnp.zeros((8, 128), f32)] * 2 for _ in range(2)]
    for j in range(PEERS):
        tile = got[j, 32:40, :]
        here = lane8 // 16 == j % 8
        for half in range(2):
            amount = (16 * j - 16 * half) % 128
            moved = pltpu.roll(tile, amount, 1) if amount else tile
            parts[half][j // 8] = jnp.where(here, moved, parts[half][j // 8])
    start = jnp.concatenate([jnp.concatenate(x, axis=1) for x in parts], axis=0)

    r = jnp.broadcast_to(known[16:17, 0:CELLS], wide)
    diffusion = jnp.concatenate([known[0:16, 128:256]] * 2, axis=1)
    up, down = own_shifts()
    s1, s2, s3 = advance_three(1.0 - r, mu[0], [mu[1], mu[3], mu[5]], [mu[2], mu[4], mu[6]], up, down)
    out, plain, once, again = fields_of(s1, s2, s3, start, r, 1.0, diffusion, block, up, down)
    for n, f in enumerate(out):
        fields[n] = f
    lane = lanes_of(wide)
    low = jnp.where(slab > 0, RIM, 0)
    high = jnp.where(slab < n_space - 1, CELLS - RIM, CELLS)
    counted = jnp.where((lane >= low) & (lane < high), 1.0, 0.0)
    operands = product_operands(plain, once, again, counted)
    tops = early_products(operands, sheets, table) + late_products(operands, sheets, table)

    lane1 = lanes_of((16, 128))
    row1 = rows_of((16, 128))
    start_relax = jnp.where(rows_of(wide) == K, r, start)
    tile = jnp.zeros((16, 128), f32)
    for n, f in enumerate([s1, s2, s3, start_relax]):
        at = lane1 - 32 * n
        begin = pltpu.roll(f[:, 0:128], 32 * n, 1) if n else f[:, 0:128]
        tile = jnp.where((at >= 0) & (at < SIDE), begin, tile)
        end = pltpu.roll(f[:, 128:256], (32 * n + 16 + SIDE) % 128, 1)
        tile = jnp.where((at >= 16) & (at < 16 + SIDE), end, tile)
        if n < 3:
            begin = pltpu.roll(mu[2 + 2 * n][:, 0:128], 32 * n + SIDE, 1)
            tile = jnp.where((at >= SIDE) & (at < 16), begin, tile)
            end = pltpu.roll(mu[1 + 2 * n][:, 128:256], (32 * n + 32) % 128, 1)
            tile = jnp.where((at >= 16 + SIDE) & (at < 32), end, tile)
    tile = pltpu.roll(tile, lax.rem(32 * lax.rem(slab, 4) + 112, 128), 1)
    row_a = jnp.broadcast_to(tops[0][0:1] + tops[1][0:1], (16, 128))
    row_b = jnp.broadcast_to(tops[2][0:1], (16, 128))
    tile = jnp.where(row1 == 14, row_a, jnp.where(row1 == 15, row_b, tile))
    for j in range(n_space):
        sent[j] = tile


def speeds_of(shape):
    number = 2 * lax.axis_index("vel") + jnp.where(rows_of(shape) >= 8, 1, 0)
    return time_step * jnp.abs((number.astype(f32) + 0.5) * spacing - 4.0)


def bands_of(r, positive):
    a = speeds_of(r.shape)
    stay = 1.0 - r - a

    def before(x):
        return jnp.where(positive, shift_up(x), shift_down(x))

    once = before(stay)
    two = before(once)
    t0 = stay * stay * stay
    t1 = a * (stay * (stay + once) + once * once)
    t2 = a * a * (stay + once + two)
    return t0, t1, t2, a * a * a


def banded(weights, u, distance):
    value = jnp.zeros(distance.shape, f32)
    for n, x in enumerate(weights):
        row = jnp.broadcast_to(x[8 * u : 8 * u + 1, 0 : distance.shape[1]], distance.shape)
        value = jnp.where(distance == n, row, value)
    return value


def stream_kernel(
    dist_in,
    block_in,
    pairs_in,
    own_in,
    coupling_in,
    diff_in,
    rate_in,
    flags_in,
    out,
    table,
    block,
    dist,
    own6,
    coupling_raw,
    diff_raw,
    rate,
    flags,
    sems,
):
    vel = lax.axis_index("vel")
    positive = vel >= PEERS // 2
    moves = [(rate_in, rate), (flags_in, flags), (dist_in, dist)]
    moves += [(coupling_in, coupling_raw), (diff_in, diff_raw), (own_in.at[vel], own6)]
    moves += [(pairs_in, table.at[24:56, 0:128]), (block_in, block)]
    waits = copies_of(moves, sems)
    waits[0].wait()
    waits[1].wait()
    relax = relax_of(rate[...], flags[...])
    table[16:24, 0:CELLS] = jnp.broadcast_to(relax, (8, CELLS))
    weights = bands_of(jnp.broadcast_to(relax, (16, CELLS)), positive)
    towards = jnp.where(positive, 1, -1)
    distance = (lanes_of((CELLS, CELLS)) - rows_of((CELLS, CELLS))) * towards
    waits[2].wait()
    for u in range(2):
        b = banded(weights, u, distance)
        bh = b.astype(bf16)
        bl = (b - bh.astype(f32)).astype(bf16)
        rows = pl.ds(u * BLOCK, BLOCK)
        x = dist[rows, :]
        value = jnp.dot(x, bh, preferred_element_type=f32)
        value += jnp.dot(x, bl, preferred_element_type=f32)
        out[rows, :] = value

    for copy in waits[3:]:
        copy.wait()
    table[0:16, 0:128] = jnp.zeros((16, 128), f32)
    table[0:K, 0:K] = coupling_raw[...]
    c = table[0:16, 0:128]
    ch = c.astype(bf16).astype(f32)
    pieces = [ch, ch, c - ch]
    terms = pieces[0]
    for n in range(1, 3):
        terms = terms + pltpu.roll(pieces[n], 16 * n, 1)
    block[0:16, 128:256] = terms.astype(bf16)
    block[176:192, 128:256] = own6[...]
    shape = (16, K)
    chosen = jnp.where(lanes_of(shape) == rows_of(shape), jnp.broadcast_to(diff_raw[...], shape), 0.0)
    table[0:16, 128:256] = jnp.broadcast_to(jnp.sum(chosen, axis=1, keepdims=True), (16, 128))


UPDATE_ROWS = 256


def strips_of(n_space, sent):
    raw = []
    lane1 = lanes_of((16, 128))
    for n in range(4):
        which = ((lane1 + 128 - 32 * n) % 128 // 16 + 1) // 2
        tiles = []
        for t in range(4):
            tile = jnp.zeros((16, 128), f32)
            for k in range(5):
                if 4 * t + k < n_space:
                    tile = jnp.where(which == k, sent[4 * t + k], tile)
            amount = (STEP[t] - 32 * n) % 128
            tiles.append(pltpu.roll(tile, amount, 1) if amount else tile)
        raw.append(jnp.concatenate(tiles, axis=1))
    shape = (16, STRIPS)
    row = rows_of(shape)
    turned = jnp.concatenate([(lane1 + 128 - STEP[t]) % 128 + 128 * t for t in range(4)], axis=1)
    at = turned % 32
    valid = (turned < 32 * (n_space - 1)) & (at < 2 * SIDE)
    mask = jnp.where(valid, 1.0, 0.0)
    moments = jnp.where(row < K, mask, 0.0)
    closer = [tile_roll(x, 128 - 3) for x in raw]
    arrays = [jnp.where(at < SIDE, x, y) for x, y in zip(raw, closer)]
    r = mask * jnp.broadcast_to(arrays[3][K : K + 1], shape)
    s1, s2, s3, start = (moments * x for x in arrays)
    ups = [jnp.where((at >= SIDE - 3) & (at < SIDE), moments * x, 0.0) for x in closer[:3]]
    downs = [tile_roll(x, 128 - 16) for x in raw[:3]]
    downs = [jnp.where((at >= SIDE) & (at < SIDE + 3), moments * x, 0.0) for x in downs]
    zero = jnp.zeros(shape, f32)
    over_up = advance_three(1.0 - r, zero, ups, [], strip_up, strip_down)
    over_down = advance_three(1.0 - r, zero, [], downs, strip_up, strip_down)
    s = [x + jnp.where(at < SIDE, y, z) for x, y, z in zip((s1, s2, s3), over_down, over_up)]
    s = [mask * x for x in s]
    counted = jnp.where((at >= SIDE - RIM) & (at < SIDE + RIM), mask, 0.0)
    return s, start, r, mask, counted


def update_kernel(
    n_space,
    sent,
    fields,
    table,
    block,
    base,
    edges_in,
    out,
    macro,
    done,
    macro_part,
    products,
    sheets,
    edges,
    ends,
    sems,
):
    place = lax.axis_index("vel")
    slab = lax.axis_index("space")
    positive = place >= PEERS // 2
    (edge_copy,) = copies_of([(edges_in, edges)], sems.at[pl.ds(ROWS // UPDATE_ROWS + 1, 1)])

    def known(at):
        return table[at : at + 8, 0:128]

    (s1, s2, s3), strip_start, strip_r, strip_mask, counted = strips_of(n_space, sent)
    diffusion = jnp.concatenate([table[0:16, 128:256]] * 4, axis=1)
    strip_fields, plain, once, again = fields_of(
        s1, s2, s3, strip_start, strip_r, strip_mask, diffusion, block, strip_up, strip_down
    )
    operands = product_operands(plain, once, again, counted)
    gathered = sent[0, 8:16, :]
    for j in range(1, n_space):
        gathered = gathered + sent[j, 8:16, :]
    row8 = rows_of((8, 128))
    (top,) = early_products(operands, sheets, products)
    early = jnp.where(row8 == 0, gathered[6:7] + top[0:1], 0.0) * known(48)
    cpl = table[0:16, 0:128]
    lane16 = lanes_of((16, 128))
    row16 = rows_of((16, 128))
    size = jnp.sum(jnp.abs(cpl), axis=1, keepdims=True)
    middle = jnp.sum(jnp.where(lane16 == row16, cpl, 0.0), axis=1, keepdims=True)
    real = row16[:, 0:1] < K
    most = jnp.max(jnp.where(real, size + 4.0 * table[0:16, 128:129], 0.0), axis=0, keepdims=True)
    least = jnp.min(jnp.where(real, 2.0 * middle - size, 1e30), axis=0, keepdims=True)
    low_step, high_step = 1.0 / most, 1.0 / least

    def summed(weighted, which):
        picked = jnp.where(known(24) == which, weighted, 0.0)
        return jnp.sum(jnp.sum(picked, axis=0, keepdims=True), axis=1, keepdims=True)

    def clipped(x):
        return jnp.minimum(jnp.maximum(x, low_step), high_step)

    def weights_of(stage, weighted):
        rr, ra, aa, aaa = (summed(weighted, 4 * stage + n) for n in range(4))
        s1 = clipped(rr / ra)
        rr2 = rr - 2.0 * s1 * ra + s1 * s1 * aa
        ra2 = ra - 2.0 * s1 * aa + s1 * s1 * aaa
        s2 = clipped(rr2 / ra2)
        return s1 + s2, -s1 * s2

    li, ri = (known(n).astype(jnp.int32) for n in (32, 40))

    def choose(index, zero, one, two):
        return jnp.where(index == 0, zero, jnp.where(index == 1, one, two))

    a1, b1 = weights_of(0, early)
    a2, b2 = weights_of(1, early * choose(li, 1.0, a1, b1) * choose(ri, 1.0, a1, b1))

    def both(index):
        outer = (index >= 3).astype(jnp.int32) + (index >= 6).astype(jnp.int32)
        return choose(outer, 1.0, a2, b2) * choose(index - 3 * outer, 1.0, a1, b1)

    tops = late_products(operands, sheets, products)
    line_a = gathered[6:7] + tops[0][0:1]
    line_b = gathered[7:8] + tops[1][0:1]
    total = jnp.where(row8 == 0, line_a, jnp.where(row8 == 1, line_b, 0.0))
    total = total * known(48)
    a3, b3 = weights_of(2, total * both(li) * both(ri))

    def last_fields(at, r):
        start, shares, res, e = (at(n) for n in range(4))
        corr1 = a1 * res + b1 * e
        cur1 = shares + corr1
        res2 = at(4) + a1 * at(5) + b1 * at(6)
        e2 = at(7) + a1 * at(8) + b1 * at(9)
        corr2 = a2 * res2 + b2 * e2
        cur2 = res2 + cur1 + corr2

        def third(first):
            rows = [at(first + 3 * n) + a1 * at(first + 3 * n + 1) + b1 * at(first + 3 * n + 2) for n in range(3)]
            return rows[0] + a2 * rows[1] + b2 * rows[2]

        res3, e3 = third(10), third(19)
        corr3 = a3 * res3 + b3 * e3
        row = rows_of(r.shape)
        scaled = r * jnp.where(row < 5, 1.0, jnp.where(row < 10, 0.0, 1.0 / 3.0))
        f1 = scaled * start + corr1
        f2 = scaled * cur1 + corr2
        f3 = scaled * cur2 + corr3
        return f1, f2, f3, res3 + cur2 + corr3, r

    own = last_fields(lambda n: fields[n], jnp.broadcast_to(table[16:17, 0:CELLS], (16, CELLS)))
    strips = last_fields(lambda n: strip_fields[n], strip_r)
    lane1 = lanes_of((16, 128))
    has_left, has_right = jnp.where(slab > 0, 1, 0), jnp.where(slab < n_space - 1, 1, 0)
    near_left = (lane1 < RIM * has_left)
    near_right = (lane1 >= 128 - RIM * has_right)
    far_left = (lane1 >= 128 - 2 * has_left)
    far_right = (lane1 < 2 * has_right)
    wide = []
    for x, y in zip(own, strips):
        y = jnp.concatenate([y[:, 0:256], tile_roll(y[:, 256:512], 112)], axis=1)
        y = pltpu.roll(y, lax.rem(STRIPS + 32 - 32 * slab, STRIPS), 1)[:, 0:128]
        from_left = pltpu.roll(y, 128 - SIDE, 1)
        from_right = pltpu.roll(y, 96 - SIDE, 1)
        tiles = [
            jnp.where(near_left, from_left, x[:, 0:128]),
            jnp.where(near_right, from_right, x[:, 128:256]),
            jnp.where(far_left, from_left, jnp.where(far_right, from_right, 0.0)),
        ]
        wide.append(jnp.concatenate(tiles, axis=1))
    f1, f2, f3, cur3, r = wide
    mine = pltpu.roll(cur3[:, 0:CELLS], lax.rem(CELLS - 16 * place, CELLS), 1)
    macro_part[...] = mine[0:K, 0:16]
    macro_copy = pltpu.make_async_copy(macro_part, macro, sems.at[ROWS // UPDATE_ROWS])
    macro_copy.start()
    y = jnp.dot(
        block[176:192, 128:176], split3(jnp.concatenate([f1, f2, f3], axis=1)), preferred_element_type=f32
    )
    y1, y2, y3 = (y[:, n * WIDE : (n + 1) * WIDE] for n in range(3))
    a = speeds_of((16, WIDE))
    stay = 1.0 - r - a

    def moved(x):
        return stay * x + a * jnp.where(positive, shift_up(x), shift_down(x))

    h = (moved(moved(y1) + y2) + y3)[:, 0:CELLS]
    hh = h.astype(bf16).astype(f32)
    hm = (h - hh).astype(bf16).astype(f32)

    weights = bands_of(r, positive)
    towards = jnp.where(positive, 1, -1)
    at8 = rows_of((8, 128))
    at8 = jnp.where(positive, -1 - at8, at8 + CELLS)
    low = jnp.where(positive, 0, CELLS - 128)
    distance = (lanes_of((8, 128)) + low - at8) * towards
    weights = [jnp.where(positive, x[:, 0:128], x[:, 128:256]) for x in weights]
    ends[...] = jnp.zeros((16, ROWS), f32)
    edge_copy.wait()
    for n in range(3):
        for k in range(16):
            row = edges[16 * n + k : 16 * n + k + 1, :]
            ends[n : n + 1, 128 * k : 128 * k + 128] = row
            ends[8 + n : 9 + n, 128 * k : 128 * k + 128] = row

    sends = [macro_copy]
    for u in range(2):
        hu, mu = hh[8 * u : 8 * u + 8], hm[8 * u : 8 * u + 8]
        mixed = jnp.concatenate([hu, mu, hu, jnp.zeros((104, CELLS), f32)], axis=0).astype(bf16)
        b = banded(weights, u, distance)
        bh = b.astype(bf16).astype(f32)
        b = jnp.concatenate([bh, b - bh], axis=0).astype(bf16)
        for n in range(BLOCK // UPDATE_ROWS):
            part = u * (BLOCK // UPDATE_ROWS) + n
            rows = pl.ds(part * UPDATE_ROWS, UPDATE_ROWS)
            value = jnp.dot(block[pl.ds(n * UPDATE_ROWS, UPDATE_ROWS), 0:128], mixed, preferred_element_type=f32)
            near = lax.dot_general(ends[:, rows].astype(bf16), b, (((0,), (0,)), ((), ())), preferred_element_type=f32)
            value += base[rows, :]
            done[rows, 0:128] = (value[:, 0:128] + jnp.where(positive, near, 0.0)).astype(bf16)
            done[rows, 128:256] = (value[:, 128:256] + jnp.where(positive, 0.0, near)).astype(bf16)
            copy = pltpu.make_async_copy(done.at[rows, :], out.at[rows, :], sems.at[part])
            copy.start()
            sends.append(copy)
    for copy in sends:
        copy.wait()


def vmem():
    return pl.BlockSpec(memory_space=pltpu.VMEM)


def hbm():
    return pl.BlockSpec(memory_space=pltpu.HBM)


def shaped(shape, dtype=f32):
    return pltpu.VMEM(shape, dtype)


def stored(shape, dtype=f32):
    return pltpu.HBM(shape, dtype)


def placed_at(space, arrays):
    return [pltpu.with_memory_space_constraint(x, space) for x in arrays]


def near(*arrays):
    return placed_at(pltpu.VMEM, arrays)


def far(*arrays):
    return placed_at(pltpu.HBM, arrays)


def limit(mib):
    return pltpu.CompilerParams(vmem_limit_bytes=mib * 2**20)


def make_per_device(n_space):
    block, p3, own6 = grid_constants()
    pairs = pair_arrays()

    def per_device(velocity_dist, macro_state, collision_rate, wall_flags, diffusivity, coupling):
        rate = collision_rate.reshape(1, CELLS)
        flags = wall_flags.reshape(1, CELLS)
        packed, edges = pl.pallas_call(
            sums_kernel,
            out_shape=(shaped((PEERS, 40, 128)), shaped((48, 128))),
            in_specs=[hbm()] * 3,
            out_specs=(vmem(), vmem()),
            scratch_shapes=[
                pltpu.VMEM((ROWS, CELLS), bf16),
                pltpu.VMEM((16, BLOCK), bf16),
                pltpu.VMEM((K, 16), f32),
                pltpu.VMEM((16, 128), f32),
                pltpu.SemaphoreType.DMA((2 + CHUNKS,)),
            ],
            compiler_params=limit(8),
            name="sums",
        )(*far(velocity_dist, jnp.asarray(p3), macro_state))
        got = lax.all_to_all(packed, "vel", split_axis=0, concat_axis=0, tiled=True)
        rising = [(i, i + 1) for i in range(n_space - 1)]
        half = PEERS // 2
        downwind = [(i * PEERS + n, j * PEERS + n) for i, j in rising for n in range(half, PEERS)]
        downwind += [(j * PEERS + n, i * PEERS + n) for i, j in rising for n in range(half)]
        edges = lax.ppermute(edges, ("space", "vel"), downwind)
        base, known, constants = pl.pallas_call(
            stream_kernel,
            out_shape=(shaped((ROWS, CELLS)), shaped((56, WIDE)), shaped(block.shape, bf16)),
            in_specs=[hbm()] * 8,
            out_specs=(vmem(),) * 3,
            scratch_shapes=[
                pltpu.VMEM((ROWS, CELLS), bf16),
                pltpu.VMEM((16, 128), bf16),
                pltpu.VMEM((K, K), f32),
                pltpu.VMEM((1, K), f32),
                pltpu.VMEM((1, CELLS), f32),
                pltpu.VMEM((1, CELLS), jnp.int32),
                pltpu.SemaphoreType.DMA((8,)),
            ],
            compiler_params=limit(16),
            cost_estimate=pl.CostEstimate(flops=600_000_000, bytes_accessed=4_000_000, transcendentals=0),
            name="stream",
        )(
            *far(velocity_dist, *(jnp.asarray(x) for x in (block, pairs, own6))),
            *far(coupling, diffusivity.reshape(1, K), rate, flags),
        )
        got, base, edges = lax.optimization_barrier((got, base, edges))
        fields, sent = pl.pallas_call(
            lambda *refs: fields_kernel(n_space, *refs),
            out_shape=(shaped((N_FIELDS, 16, CELLS)), shaped((n_space, 16, 128))),
            in_specs=[vmem()] * 3,
            out_specs=(vmem(), vmem()),
            scratch_shapes=[pltpu.VMEM((384, 128), f32), pltpu.VMEM((SHEETS, 128), f32)],
            compiler_params=limit(12),
            name="fields",
        )(*near(got, known, constants))
        sent = lax.all_to_all(sent, "space", split_axis=0, concat_axis=0, tiled=True)
        return pl.pallas_call(
            lambda *refs: update_kernel(n_space, *refs),
            out_shape=(stored((ROWS, CELLS), bf16), stored((K, 16))),
            in_specs=[vmem()] * 5 + [hbm()],
            out_specs=(hbm(), hbm()),
            scratch_shapes=[
                pltpu.VMEM((ROWS, CELLS), bf16),
                pltpu.VMEM((K, 16), f32),
                pltpu.VMEM((384, 128), f32),
                pltpu.VMEM((SHEETS, 128), f32),
                pltpu.VMEM((48, 128), f32),
                pltpu.VMEM((16, ROWS), f32),
                pltpu.SemaphoreType.DMA((ROWS // UPDATE_ROWS + 2,)),
            ],
            compiler_params=limit(12),
            name="update",
        )(*near(sent, fields, known, constants, base), *far(edges))

    return per_device


def solution(mesh):
    placed = (P("vel", "space"), P(None, ("space", "vel")), P("space"), P("space"), P(), P())
    return jax.shard_map(
        make_per_device(mesh.shape["space"]),
        mesh=mesh,
        in_specs=placed,
        out_specs=(P("vel", "space"), P(None, ("space", "vel"))),
        check_vma=False,
    )
```

```python
import math

import jax
import jax.numpy as jnp
import numpy as np
from jax import lax
from jax.experimental import pallas as pl
from jax.experimental.pallas import tpu as pltpu
from jax.sharding import PartitionSpec as P

NV1 = 32
K = 13
time_step = 0.125
spacing = 8.0 / NV1
CELLS = 256
WIDE = 384
PEERS = 16
ROWS = 2048
BLOCK = 1024
bf16 = jnp.bfloat16
f32 = jnp.float32


def parts_of(x, number):
    rest = np.asarray(x, np.float64)
    out = []
    for _ in range(number):
        piece = rest.astype(np.float32).astype(bf16)
        out.append(piece)
        rest = rest - piece.astype(np.float64)
    return out


def grid_constants():
    v = (np.arange(NV1) + 0.5) * spacing - 4.0
    w = np.exp(-0.5 * v * v) * spacing / math.sqrt(2.0 * math.pi)
    vy, vz = np.repeat(v, NV1), np.tile(v, NV1)
    wyz = np.repeat(w, NV1) * np.tile(w, NV1)
    one = np.ones_like(vy)
    yz = vy * vy + vz * vz
    phi = np.stack([one, vy, vz, vy * vz, vy * vy, vz * vz, vy * yz, vz * yz])
    cmat = np.zeros((NV1, K, 8))
    for i, x in enumerate(v):
        c = cmat[i]
        c[0, 0] = 1.0
        c[1, 0] = x
        c[2, 1] = 1.0
        c[3, 2] = 1.0
        c[4, 0] = (x * x - 3.0) / math.sqrt(6.0)
        c[4, 4] = c[4, 5] = 1.0 / math.sqrt(6.0)
        c[5, 1] = x
        c[6, 2] = x
        c[7, 3] = 1.0
        c[8, 0] = 0.5 * x * x
        c[8, 4] = -0.5
        c[9, 0] = x * x / math.sqrt(12.0)
        c[9, 4] = 1.0 / math.sqrt(12.0)
        c[9, 5] = -2.0 / math.sqrt(12.0)
        c[10, 0] = x * (x * x - 5.0) / math.sqrt(10.0)
        c[10, 4] = c[10, 5] = x / math.sqrt(10.0)
        c[11, 1] = (x * x - 5.0) / math.sqrt(10.0)
        c[11, 6] = 1.0 / math.sqrt(10.0)
        c[12, 2] = (x * x - 5.0) / math.sqrt(10.0)
        c[12, 7] = 1.0 / math.sqrt(10.0)
    a = time_step * np.abs(v)
    plus = v > 0.0
    proj = phi * wyz
    groups = [np.ones(NV1)]
    for power in (1, 2, 3):
        groups += [a**power * plus, a**power * ~plus]
    big = np.zeros((7 * 16, 8 * NV1))
    for g, factor in enumerate(groups):
        for i in range(NV1):
            big[16 * g : 16 * g + K, 8 * i : 8 * i + 8] = factor[i] * w[i] * cmat[i]
    gram2 = proj @ phi.T
    shakhov = np.array([1.0] * 5 + [0.0] * 5 + [1.0 / 3.0] * 3)

    def between(factor):
        out = np.zeros((16, 16))
        for i in range(NV1):
            out[:K, :K] += factor[i] * w[i] * cmat[i] @ gram2 @ cmat[i].T
        return out

    c16 = np.zeros(16)
    c16[:K] = shakhov
    g, gp, gm, g2p, g2m = (between(groups[k]) for k in (0, 1, 2, 3, 4))
    mats = [g, gp, gm, g * c16, gp * c16, gm * c16, g2p, g2m, g2p * c16, g2m * c16]
    block = np.zeros((BLOCK + 224, 256), bf16)
    block[16:176, 128:176] = three_terms(np.concatenate(mats, axis=0))
    block[BLOCK:] = np.concatenate(parts_of(big, 2), axis=0)
    p3 = np.concatenate(parts_of(proj, 2), axis=0)
    ph, pm = parts_of(phi.T, 2)
    block[0:BLOCK, 0:24] = np.concatenate([ph, ph, pm], axis=1)
    own = np.zeros((PEERS, 16, 16))
    for j in range(PEERS):
        for u in range(2):
            own[j, 8 * u : 8 * u + 8, :K] = cmat[2 * j + u].T
    own = np.concatenate([three_terms(own), np.zeros((PEERS, 16, 80), bf16)], axis=2)
    return block, p3, own


def three_terms(x):
    h, m = parts_of(x, 2)
    return np.concatenate([h, h, m], axis=-1)


BASES = (1, 3, 9)


def pair_table():
    entries = []
    for stage, size in enumerate(BASES):
        for quantity in range(4):
            for i in range(size):
                for j in range(i, size):
                    entries.append((stage, quantity, i, j))
    return entries


PAIRS = pair_table()


def pair_arrays():
    kind = np.full((8, 128), -1, np.int32)
    left = np.zeros((8, 128), np.int32)
    right = np.zeros((8, 128), np.int32)
    twice = np.zeros((8, 128), np.int32)
    for n, (stage, quantity, i, j) in enumerate(PAIRS):
        at = (n // 128, n % 128)
        kind[at] = 4 * stage + quantity
        left[at], right[at] = i, j
        twice[at] = 1 if i == j else 2
    return np.concatenate([kind, left, right, twice], axis=0).astype(np.float32)


def lanes_of(shape):
    return lax.broadcasted_iota(jnp.int32, shape, len(shape) - 1)


def rows_of(shape):
    return lax.broadcasted_iota(jnp.int32, shape, 0)


def split3(f):
    h = f.astype(bf16)
    m = (f - h.astype(f32)).astype(bf16)
    return jnp.concatenate([h, m, h], axis=0)


def relax_of(rate, flags):
    return (time_step * rate) * (1.0 + flags.astype(f32))


def shift_up(x):
    return pltpu.roll(x, 1, 1)


def shift_down(x):
    return pltpu.roll(x, x.shape[1] - 1, 1)


def diff_up(x):
    return x - shift_up(x)


def diff_down(x):
    return x - shift_down(x)


def copies_of(pairs, sems):
    made = [pltpu.make_async_copy(x, y, sems.at[n]) for n, (x, y) in enumerate(pairs)]
    for copy in made:
        copy.start()
    return made


CHUNKS = 8


def chunks_of(source, target):
    rows = [pl.ds(n * (ROWS // CHUNKS), ROWS // CHUNKS) for n in range(CHUNKS)]
    return [(source.at[row, :], target.at[row, :]) for row in rows]


def sums_kernel(dist_in, p3_in, start_in, packed, edges, dist, p3, start, padded, whole, sems, sends):
    positive = lax.axis_index("vel") >= PEERS // 2
    halves = [pl.ds(u * BLOCK, BLOCK) for u in range(2)]
    pairs = [(p3_in, p3), (start_in, start)] + chunks_of(dist_in, dist)
    waits = copies_of(pairs, sems)
    waits[0].wait()
    waits[1].wait()
    padded[...] = jnp.zeros((16, 128), f32)
    padded[0:K, 0:16] = start[...]
    owned = padded[0:8, :] + pltpu.roll(padded[8:16, :], 16, 1)
    for j in range(PEERS):
        whole[j, 0:8, :] = owned
    e_lane = lanes_of((16, 128))
    e_row = rows_of((16, 128))
    cell = jnp.where(positive, 127 - e_row, e_row)
    pick = jnp.where((e_lane == cell) & (e_row < 3), 1.0, 0.0).astype(bf16)
    side = pl.multiple_of(jnp.where(positive, 128, 0), 128)
    going = []
    for u in range(2):
        for n in range(CHUNKS // 2):
            waits[2 + u * (CHUNKS // 2) + n].wait()
        y = jnp.dot(p3[...], dist[halves[u], :], preferred_element_type=f32)
        w = y[0:8] + y[8:16]
        for j in range(PEERS):
            whole[j, 8 + 16 * u : 16 + 16 * u, :] = w[:, 0:128]
            whole[j, 16 + 16 * u : 24 + 16 * u, :] = w[:, 128:256]
        rows = pl.ds(0, 24) if u == 0 else pl.ds(24, 16)
        going += copies_of([(whole.at[:, rows, :], packed.at[:, rows, :])], sends.at[pl.ds(u, 1)])
        near = dist[halves[u], pl.ds(side, 128)]
        e = lax.dot_general(pick, near, (((1,), (1,)), ((), ())), preferred_element_type=f32)
        for n in range(3):
            for k in range(8):
                at = 16 * n + 8 * u + k
                edges[at : at + 1, :] = e[n : n + 1, 128 * k : 128 * k + 128]
    for copy in going:
        copy.wait()


N_FIELDS = 28
RIM = 7
SIDE = 13
STRIPS = 512


def tiles_of(x):
    return [x[:, 128 * t : 128 * t + 128] for t in range(x.shape[1] // 128)]


def own_shifts():
    lane = lanes_of((16, 128))
    zero = jnp.zeros((16, 128), f32)

    def up(x):
        first, second = (pltpu.roll(t, 1, 1) for t in tiles_of(x))
        return jnp.concatenate([jnp.where(lane == 0, zero, first), jnp.where(lane == 0, first, second)], axis=1)

    def down(x):
        first, second = (pltpu.roll(t, 127, 1) for t in tiles_of(x))
        return jnp.concatenate([jnp.where(lane == 127, second, first), jnp.where(lane == 127, zero, second)], axis=1)

    return up, down


STEP = (0, 0, 16, 16)


def tile_roll(x, amount):
    return jnp.concatenate([pltpu.roll(t, amount, 1) for t in tiles_of(x)], axis=1)


def strip_up(x):
    return tile_roll(x, 1)


def strip_down(x):
    return tile_roll(x, 127)


def advance_three(keep, base, ups, downs, up, down):
    out = []
    for _ in range(3):
        base = keep * base
        if ups:
            base = base - (ups[0] - up(ups[0]))
        if downs:
            base = base - (downs[0] - down(downs[0]))
        ups = [keep * x - (y - up(y)) for x, y in zip(ups[:-1], ups[1:])]
        downs = [keep * x - (y - down(y)) for x, y in zip(downs[:-1], downs[1:])]
        out.append(base)
    return out


def fields_of(s1, s2, s3, start, r, mask, diffusion, block, up, down):
    width = r.shape[1]
    keep = 1.0 - r

    def up_diff(x):
        return x - up(x)

    def down_diff(x):
        return x - down(x)

    def times(first, last, inputs):
        stacked = split3(jnp.concatenate(inputs, axis=1) if len(inputs) > 1 else inputs[0])
        y = jnp.dot(block[16 * first : 16 * last, 128:176], stacked, preferred_element_type=f32)
        out = []
        for n in range(len(inputs)):
            cut = y[:, n * width : (n + 1) * width]
            out.append([cut[16 * g : 16 * g + 16] for g in range(last - first)])
        return out

    def applied(f, coupled):
        return mask * (coupled + diffusion * (2.0 * f - up(f) - down(f)))

    def streamed(g, gp, gm):
        return keep * g - up_diff(gp) - down_diff(gm)

    def streamed_twice(k1, gp, gm, g2p, g2m):
        return keep * k1 - up_diff(keep * gp - up_diff(g2p)) - down_diff(keep * gm - down_diff(g2m))

    ((gc, gcp, gcm, _, _, g2cp, g2cm),) = times(4, 11, [start])
    relaxed = r * gc
    shares = mask * (s1 + relaxed)
    res = mask * (shares - start)
    k1_start = streamed(relaxed, r * gcp, r * gcm)
    k2_start = streamed_twice(k1_start, r * gcp, r * gcm, r * g2cp, r * g2cm)

    def parts(f, ys):
        out = [applied(f, ys[0])]
        k1 = streamed(ys[1], ys[2], ys[3])
        rg = r * ys[4]
        held = rg - f
        out += [mask * (k1 + held), held]
        if len(ys) > 5:
            out.append(streamed_twice(k1, ys[2], ys[3], ys[7], ys[8]))
            out.append(streamed(rg, r * ys[5], r * ys[6]) + held)
        return out

    y_shares, y_res = times(0, 9, [shares, res])
    rg = r * y_shares[4]
    held_shares = rg - shares
    n_shares = streamed(rg, r * y_shares[5], r * y_shares[6]) + held_shares
    p0 = mask * (s2 + k1_start + held_shares)
    e, p1, _, k2_res, n_res = parts(res, y_res)

    y_e, y_p0, y_p1 = times(0, 9, [e, p0, p1])
    ee, p2, _, k2_e, n_e = parts(e, y_e)
    ap0, q3, held_p0 = parts(p0, y_p0[:5])
    ap1, q4, held_p1 = parts(p1, y_p1[:5])
    q0 = mask * (s3 + k2_start + n_shares + held_p0)
    q1 = mask * (k2_res + n_res + held_p1)

    y_p2, y_ap0, y_ap1, y_q0, y_q1, y_q3, y_q4 = times(0, 5, [p2, ap0, ap1, q0, q1, q3, q4])
    ap2, q5, held_p2 = parts(p2, y_p2)
    aap0, q6, _ = parts(ap0, y_ap0)
    aap1, q7, _ = parts(ap1, y_ap1)
    q2 = mask * (k2_e + n_e + held_p2)
    aq0, aq1, aq3, aq4 = (applied(f, y[0]) for f, y in ((q0, y_q0), (q1, y_q1), (q3, y_q3), (q4, y_q4)))

    (y_ap2,) = times(0, 5, [ap2])
    aap2, q8, _ = parts(ap2, y_ap2)
    first = [q2, q5, q6, q7, aq0, aq1, aq3, aq4]
    aq2, aq5, aq6, aq7, aaq0, aaq1, aaq3, aaq4 = (applied(f, y[0]) for f, y in zip(first, times(0, 1, first)))
    second = [q8, aq2, aq5, aq6, aq7]
    aq8, aaq2, aaq5, aaq6, aaq7 = (applied(f, y[0]) for f, y in zip(second, times(0, 1, second)))
    ((y_aq8,),) = times(0, 1, [aq8])
    aaq8 = applied(aq8, y_aq8)

    q = [q0, q1, q2, q3, q4, q5, q6, q7, q8]
    aq = [aq0, aq1, aq2, aq3, aq4, aq5, aq6, aq7, aq8]
    aaq = [aaq0, aaq1, aaq2, aaq3, aaq4, aaq5, aaq6, aaq7, aaq8]
    fields = [start, shares, res, e, p0, p1, p2, ap0, ap1, ap2] + q + aq
    plain = [[res], [p0, p1, p2], q]
    once = [[e], [ap0, ap1, ap2], aq]
    again = [[ee], [aap0, aap1, aap2], aaq]
    return fields, plain, once, again


EARLY = 4 * 1 + 4 * 6
LATE_FROM = EARLY // 8 * 8
EARLY_SHEETS = (EARLY + 7) // 8 * 64 + 8
SHEETS = EARLY_SHEETS + 8 * (len(PAIRS) - LATE_FROM) + 8


def product_operands(plain, once, again, counted):
    lefts = [[[counted * x for x in xs] for xs in xss] for xss in (plain, once)]
    rights = [plain, once, again]
    if counted.shape[1] == STRIPS:
        def folded(x):
            return x[:, 0:256] + x[:, 256:512]

        lefts = [[[folded(x) for x in xs] for xs in xss] for xss in lefts]
        rights = lefts + [[[folded(counted * x) for x in xs] for xs in again]]
    return lefts, rights


def inner_products(operands, entries, first, sheets, table):
    lefts, rights = operands
    start = first // 8 * 8
    stop = entries.stop
    zero = jnp.zeros((8, 128), f32)
    end = (stop + 7) // 8 * 8
    for n in range(start, end):
        if n not in entries:
            sheets[8 * (n - start) : 8 * (n - start) + 8, :] = zero
            continue
        stage, quantity, i, j = PAIRS[n]
        x, y = ((0, 0), (0, 1), (1, 1), (1, 2))[quantity]
        product = lefts[x][stage][i] * rights[y][stage][j]
        half = product[:, 0:128] + product[:, 128:256]
        sheets[8 * (n - start) : 8 * (n - start) + 8, :] = half[0:8] + half[8:16]
    lines = (end + 127) // 128
    if start:
        table[0:start, :] = jnp.zeros((start, 128), f32)
    if end < 128 * lines:
        table[end : 128 * lines, :] = jnp.zeros((128 * lines - end, 128), f32)
    for n in range(start, end, 8):
        rows = [sheets[pl.ds(8 * (n - start) + k, 8, stride=8), :] for k in range(8)]
        while len(rows) > 1:
            rows = [p + q for p, q in zip(rows[0::2], rows[1::2])]
        table[n : n + 8, :] = rows[0]
    ones = jnp.ones((8, 128), f32)
    return [
        lax.dot_general(
            ones,
            table[128 * n : 128 * n + 128, :],
            (((1,), (1,)), ((), ())),
            precision=lax.Precision.HIGHEST,
            preferred_element_type=f32,
        )
        for n in range(lines)
    ]


def early_products(operands, sheets, table):
    return inner_products(operands, range(EARLY), 0, sheets.at[0:EARLY_SHEETS, :], table.at[0:128, :])


def late_products(operands, sheets, table):
    return inner_products(operands, range(EARLY, len(PAIRS)), EARLY, sheets.at[EARLY_SHEETS:SHEETS, :], table.at[128:384, :])


def fields_kernel(n_space, got, known, block, fields, sent, table, sheets):
    slab = lax.axis_index("space")
    wide = (16, CELLS)
    w = [
        jnp.concatenate([got[:, 8 + 8 * t : 16 + 8 * t, :], got[:, 24 + 8 * t : 32 + 8 * t, :]], axis=1)
        for t in range(2)
    ]
    w = jnp.concatenate([x.reshape(PEERS * 16, 128) for x in w], axis=1)
    wh = w.astype(bf16)
    wm = (w - wh.astype(f32)).astype(bf16)
    y = jnp.dot(block[BLOCK : BLOCK + 224, :], wh, preferred_element_type=f32)
    z = jnp.dot(block[BLOCK : BLOCK + 112, :], wm, preferred_element_type=f32)
    mu = (y[112:224] + z) + y[0:112]
    mu = [mu[16 * g : 16 * g + 16] for g in range(7)]

    lane8 = lanes_of((8, 128))
    parts = [[jnp.zeros((8, 128), f32)] * 2 for _ in range(2)]
    for j in range(PEERS):
        tile = got[j, 0:8, :]
        here = lane8 // 16 == j % 8
        for half in range(2):
            amount = (16 * j - 16 * half) % 128
            moved = pltpu.roll(tile, amount, 1) if amount else tile
            parts[half][j // 8] = jnp.where(here, moved, parts[half][j // 8])
    start = jnp.concatenate([jnp.concatenate(x, axis=1) for x in parts], axis=0)

    r = jnp.broadcast_to(known[16:17, 0:CELLS], wide)
    diffusion = jnp.concatenate([known[0:16, 128:256]] * 2, axis=1)
    up, down = own_shifts()
    s1, s2, s3 = advance_three(1.0 - r, mu[0], [mu[1], mu[3], mu[5]], [mu[2], mu[4], mu[6]], up, down)
    out, plain, once, again = fields_of(s1, s2, s3, start, r, 1.0, diffusion, block, up, down)
    for n, f in enumerate(out):
        fields[n] = f
    lane = lanes_of(wide)
    low = jnp.where(slab > 0, RIM, 0)
    high = jnp.where(slab < n_space - 1, CELLS - RIM, CELLS)
    counted = jnp.where((lane >= low) & (lane < high), 1.0, 0.0)
    operands = product_operands(plain, once, again, counted)
    tops = early_products(operands, sheets, table) + late_products(operands, sheets, table)

    lane1 = lanes_of((16, 128))
    row1 = rows_of((16, 128))
    start_relax = jnp.where(rows_of(wide) == K, r, start)
    tile = jnp.zeros((16, 128), f32)
    for n, f in enumerate([s1, s2, s3, start_relax]):
        at = lane1 - 32 * n
        begin = pltpu.roll(f[:, 0:128], 32 * n, 1) if n else f[:, 0:128]
        tile = jnp.where((at >= 0) & (at < SIDE), begin, tile)
        end = pltpu.roll(f[:, 128:256], (32 * n + 16 + SIDE) % 128, 1)
        tile = jnp.where((at >= 16) & (at < 16 + SIDE), end, tile)
        if n < 3:
            begin = pltpu.roll(mu[2 + 2 * n][:, 0:128], 32 * n + SIDE, 1)
            tile = jnp.where((at >= SIDE) & (at < 16), begin, tile)
            end = pltpu.roll(mu[1 + 2 * n][:, 128:256], (32 * n + 32) % 128, 1)
            tile = jnp.where((at >= 16 + SIDE) & (at < 32), end, tile)
    tile = pltpu.roll(tile, lax.rem(32 * lax.rem(slab, 4) + 112, 128), 1)
    row_a = jnp.broadcast_to(tops[0][0:1] + tops[1][0:1], (16, 128))
    row_b = jnp.broadcast_to(tops[2][0:1], (16, 128))
    tile = jnp.where(row1 == 14, row_a, jnp.where(row1 == 15, row_b, tile))
    for j in range(n_space):
        sent[j] = tile


def speeds_of(shape):
    number = 2 * lax.axis_index("vel") + jnp.where(rows_of(shape) >= 8, 1, 0)
    return time_step * jnp.abs((number.astype(f32) + 0.5) * spacing - 4.0)


def bands_of(r, positive):
    a = speeds_of(r.shape)
    stay = 1.0 - r - a

    def before(x):
        return jnp.where(positive, shift_up(x), shift_down(x))

    once = before(stay)
    two = before(once)
    t0 = stay * stay * stay
    t1 = a * (stay * (stay + once) + once * once)
    t2 = a * a * (stay + once + two)
    return t0, t1, t2, a * a * a


def banded(weights, u, distance):
    value = jnp.zeros(distance.shape, f32)
    for n, x in enumerate(weights):
        row = jnp.broadcast_to(x[8 * u : 8 * u + 1, 0 : distance.shape[1]], distance.shape)
        value = jnp.where(distance == n, row, value)
    return value


def stream_kernel(
    dist_in,
    block_in,
    pairs_in,
    own_in,
    coupling_in,
    diff_in,
    rate_in,
    flags_in,
    out,
    table,
    block,
    dist,
    own6,
    coupling_raw,
    diff_raw,
    rate,
    flags,
    sems,
):
    vel = lax.axis_index("vel")
    positive = vel >= PEERS // 2
    moves = [(rate_in, rate), (flags_in, flags), (dist_in, dist)]
    moves += [(coupling_in, coupling_raw), (diff_in, diff_raw), (own_in.at[vel], own6)]
    moves += [(pairs_in, table.at[24:56, 0:128]), (block_in, block)]
    waits = copies_of(moves, sems)
    waits[0].wait()
    waits[1].wait()
    relax = relax_of(rate[...], flags[...])
    table[16:24, 0:CELLS] = jnp.broadcast_to(relax, (8, CELLS))
    weights = bands_of(jnp.broadcast_to(relax, (16, CELLS)), positive)
    towards = jnp.where(positive, 1, -1)
    distance = (lanes_of((CELLS, CELLS)) - rows_of((CELLS, CELLS))) * towards
    waits[2].wait()
    for u in range(2):
        b = banded(weights, u, distance)
        bh = b.astype(bf16)
        bl = (b - bh.astype(f32)).astype(bf16)
        rows = pl.ds(u * BLOCK, BLOCK)
        x = dist[rows, :]
        value = jnp.dot(x, bh, preferred_element_type=f32)
        value += jnp.dot(x, bl, preferred_element_type=f32)
        out[rows, :] = value

    for copy in waits[3:]:
        copy.wait()
    table[0:16, 0:128] = jnp.zeros((16, 128), f32)
    table[0:K, 0:K] = coupling_raw[...]
    c = table[0:16, 0:128]
    ch = c.astype(bf16).astype(f32)
    pieces = [ch, ch, c - ch]
    terms = pieces[0]
    for n in range(1, 3):
        terms = terms + pltpu.roll(pieces[n], 16 * n, 1)
    block[0:16, 128:256] = terms.astype(bf16)
    block[176:192, 128:256] = own6[...]
    shape = (16, K)
    chosen = jnp.where(lanes_of(shape) == rows_of(shape), jnp.broadcast_to(diff_raw[...], shape), 0.0)
    table[0:16, 128:256] = jnp.broadcast_to(jnp.sum(chosen, axis=1, keepdims=True), (16, 128))


UPDATE_ROWS = 256


def strips_of(n_space, sent):
    raw = []
    lane1 = lanes_of((16, 128))
    for n in range(4):
        which = ((lane1 + 128 - 32 * n) % 128 // 16 + 1) // 2
        tiles = []
        for t in range(4):
            tile = jnp.zeros((16, 128), f32)
            for k in range(5):
                if 4 * t + k < n_space:
                    tile = jnp.where(which == k, sent[4 * t + k], tile)
            amount = (STEP[t] - 32 * n) % 128
            tiles.append(pltpu.roll(tile, amount, 1) if amount else tile)
        raw.append(jnp.concatenate(tiles, axis=1))
    shape = (16, STRIPS)
    row = rows_of(shape)
    turned = jnp.concatenate([(lane1 + 128 - STEP[t]) % 128 + 128 * t for t in range(4)], axis=1)
    at = turned % 32
    valid = (turned < 32 * (n_space - 1)) & (at < 2 * SIDE)
    mask = jnp.where(valid, 1.0, 0.0)
    moments = jnp.where(row < K, mask, 0.0)
    closer = [tile_roll(x, 128 - 3) for x in raw]
    arrays = [jnp.where(at < SIDE, x, y) for x, y in zip(raw, closer)]
    r = mask * jnp.broadcast_to(arrays[3][K : K + 1], shape)
    s1, s2, s3, start = (moments * x for x in arrays)
    ups = [jnp.where((at >= SIDE - 3) & (at < SIDE), moments * x, 0.0) for x in closer[:3]]
    downs = [tile_roll(x, 128 - 16) for x in raw[:3]]
    downs = [jnp.where((at >= SIDE) & (at < SIDE + 3), moments * x, 0.0) for x in downs]
    zero = jnp.zeros(shape, f32)
    over_up = advance_three(1.0 - r, zero, ups, [], strip_up, strip_down)
    over_down = advance_three(1.0 - r, zero, [], downs, strip_up, strip_down)
    s = [x + jnp.where(at < SIDE, y, z) for x, y, z in zip((s1, s2, s3), over_down, over_up)]
    s = [mask * x for x in s]
    counted = jnp.where((at >= SIDE - RIM) & (at < SIDE + RIM), mask, 0.0)
    return s, start, r, mask, counted


def update_kernel(
    n_space,
    sent,
    fields,
    table,
    block,
    base,
    edges_in,
    out,
    macro,
    done,
    macro_part,
    products,
    sheets,
    edges,
    ends,
    sems,
):
    place = lax.axis_index("vel")
    slab = lax.axis_index("space")
    positive = place >= PEERS // 2
    (edge_copy,) = copies_of([(edges_in, edges)], sems.at[pl.ds(ROWS // UPDATE_ROWS + 1, 1)])

    def known(at):
        return table[at : at + 8, 0:128]

    (s1, s2, s3), strip_start, strip_r, strip_mask, counted = strips_of(n_space, sent)
    diffusion = jnp.concatenate([table[0:16, 128:256]] * 4, axis=1)
    strip_fields, plain, once, again = fields_of(
        s1, s2, s3, strip_start, strip_r, strip_mask, diffusion, block, strip_up, strip_down
    )
    operands = product_operands(plain, once, again, counted)
    gathered = sent[0, 8:16, :]
    for j in range(1, n_space):
        gathered = gathered + sent[j, 8:16, :]
    row8 = rows_of((8, 128))
    (top,) = early_products(operands, sheets, products)
    early = jnp.where(row8 == 0, gathered[6:7] + top[0:1], 0.0) * known(48)
    cpl = table[0:16, 0:128]
    lane16 = lanes_of((16, 128))
    row16 = rows_of((16, 128))
    size = jnp.sum(jnp.abs(cpl), axis=1, keepdims=True)
    middle = jnp.sum(jnp.where(lane16 == row16, cpl, 0.0), axis=1, keepdims=True)
    real = row16[:, 0:1] < K
    most = jnp.max(jnp.where(real, size + 4.0 * table[0:16, 128:129], 0.0), axis=0, keepdims=True)
    least = jnp.min(jnp.where(real, 2.0 * middle - size, 1e30), axis=0, keepdims=True)
    low_step, high_step = 1.0 / most, 1.0 / least

    def summed(weighted, which):
        picked = jnp.where(known(24) == which, weighted, 0.0)
        return jnp.sum(jnp.sum(picked, axis=0, keepdims=True), axis=1, keepdims=True)

    def clipped(x):
        return jnp.minimum(jnp.maximum(x, low_step), high_step)

    def weights_of(stage, weighted):
        rr, ra, aa, aaa = (summed(weighted, 4 * stage + n) for n in range(4))
        s1 = clipped(rr / ra)
        rr2 = rr - 2.0 * s1 * ra + s1 * s1 * aa
        ra2 = ra - 2.0 * s1 * aa + s1 * s1 * aaa
        s2 = clipped(rr2 / ra2)
        return s1 + s2, -s1 * s2

    li, ri = (known(n).astype(jnp.int32) for n in (32, 40))

    def choose(index, zero, one, two):
        return jnp.where(index == 0, zero, jnp.where(index == 1, one, two))

    a1, b1 = weights_of(0, early)
    a2, b2 = weights_of(1, early * choose(li, 1.0, a1, b1) * choose(ri, 1.0, a1, b1))

    def both(index):
        outer = (index >= 3).astype(jnp.int32) + (index >= 6).astype(jnp.int32)
        return choose(outer, 1.0, a2, b2) * choose(index - 3 * outer, 1.0, a1, b1)

    tops = late_products(operands, sheets, products)
    line_a = gathered[6:7] + tops[0][0:1]
    line_b = gathered[7:8] + tops[1][0:1]
    total = jnp.where(row8 == 0, line_a, jnp.where(row8 == 1, line_b, 0.0))
    total = total * known(48)
    a3, b3 = weights_of(2, total * both(li) * both(ri))

    def last_fields(at, r):
        start, shares, res, e = (at(n) for n in range(4))
        corr1 = a1 * res + b1 * e
        cur1 = shares + corr1
        res2 = at(4) + a1 * at(5) + b1 * at(6)
        e2 = at(7) + a1 * at(8) + b1 * at(9)
        corr2 = a2 * res2 + b2 * e2
        cur2 = res2 + cur1 + corr2

        def third(first):
            rows = [at(first + 3 * n) + a1 * at(first + 3 * n + 1) + b1 * at(first + 3 * n + 2) for n in range(3)]
            return rows[0] + a2 * rows[1] + b2 * rows[2]

        res3, e3 = third(10), third(19)
        corr3 = a3 * res3 + b3 * e3
        row = rows_of(r.shape)
        scaled = r * jnp.where(row < 5, 1.0, jnp.where(row < 10, 0.0, 1.0 / 3.0))
        f1 = scaled * start + corr1
        f2 = scaled * cur1 + corr2
        f3 = scaled * cur2 + corr3
        return f1, f2, f3, res3 + cur2 + corr3, r

    own = last_fields(lambda n: fields[n], jnp.broadcast_to(table[16:17, 0:CELLS], (16, CELLS)))
    strips = last_fields(lambda n: strip_fields[n], strip_r)
    lane1 = lanes_of((16, 128))
    has_left, has_right = jnp.where(slab > 0, 1, 0), jnp.where(slab < n_space - 1, 1, 0)
    near_left = (lane1 < RIM * has_left)
    near_right = (lane1 >= 128 - RIM * has_right)
    far_left = (lane1 >= 128 - 2 * has_left)
    far_right = (lane1 < 2 * has_right)
    wide = []
    for x, y in zip(own, strips):
        y = jnp.concatenate([y[:, 0:256], tile_roll(y[:, 256:512], 112)], axis=1)
        y = pltpu.roll(y, lax.rem(STRIPS + 32 - 32 * slab, STRIPS), 1)[:, 0:128]
        from_left = pltpu.roll(y, 128 - SIDE, 1)
        from_right = pltpu.roll(y, 96 - SIDE, 1)
        tiles = [
            jnp.where(near_left, from_left, x[:, 0:128]),
            jnp.where(near_right, from_right, x[:, 128:256]),
            jnp.where(far_left, from_left, jnp.where(far_right, from_right, 0.0)),
        ]
        wide.append(jnp.concatenate(tiles, axis=1))
    f1, f2, f3, cur3, r = wide
    mine = pltpu.roll(cur3[:, 0:CELLS], lax.rem(CELLS - 16 * place, CELLS), 1)
    macro_part[...] = mine[0:K, 0:16]
    macro_copy = pltpu.make_async_copy(macro_part, macro, sems.at[ROWS // UPDATE_ROWS])
    macro_copy.start()
    y = jnp.dot(
        block[176:192, 128:176], split3(jnp.concatenate([f1, f2, f3], axis=1)), preferred_element_type=f32
    )
    y1, y2, y3 = (y[:, n * WIDE : (n + 1) * WIDE] for n in range(3))
    a = speeds_of((16, WIDE))
    stay = 1.0 - r - a

    def moved(x):
        return stay * x + a * jnp.where(positive, shift_up(x), shift_down(x))

    h = (moved(moved(y1) + y2) + y3)[:, 0:CELLS]
    hh = h.astype(bf16).astype(f32)
    hm = (h - hh).astype(bf16).astype(f32)

    weights = bands_of(r, positive)
    towards = jnp.where(positive, 1, -1)
    at8 = rows_of((8, 128))
    at8 = jnp.where(positive, -1 - at8, at8 + CELLS)
    low = jnp.where(positive, 0, CELLS - 128)
    distance = (lanes_of((8, 128)) + low - at8) * towards
    weights = [jnp.where(positive, x[:, 0:128], x[:, 128:256]) for x in weights]
    ends[...] = jnp.zeros((16, ROWS), f32)
    edge_copy.wait()
    for n in range(3):
        for k in range(16):
            row = edges[16 * n + k : 16 * n + k + 1, :]
            ends[n : n + 1, 128 * k : 128 * k + 128] = row
            ends[8 + n : 9 + n, 128 * k : 128 * k + 128] = row

    sends = [macro_copy]
    for u in range(2):
        hu, mu = hh[8 * u : 8 * u + 8], hm[8 * u : 8 * u + 8]
        mixed = jnp.concatenate([hu, mu, hu, jnp.zeros((104, CELLS), f32)], axis=0).astype(bf16)
        b = banded(weights, u, distance)
        bh = b.astype(bf16).astype(f32)
        b = jnp.concatenate([bh, b - bh], axis=0).astype(bf16)
        for n in range(BLOCK // UPDATE_ROWS):
            part = u * (BLOCK // UPDATE_ROWS) + n
            rows = pl.ds(part * UPDATE_ROWS, UPDATE_ROWS)
            value = jnp.dot(block[pl.ds(n * UPDATE_ROWS, UPDATE_ROWS), 0:128], mixed, preferred_element_type=f32)
            near = lax.dot_general(ends[:, rows].astype(bf16), b, (((0,), (0,)), ((), ())), preferred_element_type=f32)
            value += base[rows, :]
            done[rows, 0:128] = (value[:, 0:128] + jnp.where(positive, near, 0.0)).astype(bf16)
            done[rows, 128:256] = (value[:, 128:256] + jnp.where(positive, 0.0, near)).astype(bf16)
            copy = pltpu.make_async_copy(done.at[rows, :], out.at[rows, :], sems.at[part])
            copy.start()
            sends.append(copy)
    for copy in sends:
        copy.wait()


def vmem():
    return pl.BlockSpec(memory_space=pltpu.VMEM)


def hbm():
    return pl.BlockSpec(memory_space=pltpu.HBM)


def shaped(shape, dtype=f32):
    return pltpu.VMEM(shape, dtype)


def stored(shape, dtype=f32):
    return pltpu.HBM(shape, dtype)


def placed_at(space, arrays):
    return [pltpu.with_memory_space_constraint(x, space) for x in arrays]


def near(*arrays):
    return placed_at(pltpu.VMEM, arrays)


def far(*arrays):
    return placed_at(pltpu.HBM, arrays)


def limit(mib):
    return pltpu.CompilerParams(vmem_limit_bytes=mib * 2**20)


def make_per_device(n_space):
    block, p3, own6 = grid_constants()
    pairs = pair_arrays()

    def per_device(velocity_dist, macro_state, collision_rate, wall_flags, diffusivity, coupling):
        rate = collision_rate.reshape(1, CELLS)
        flags = wall_flags.reshape(1, CELLS)
        packed, edges = pl.pallas_call(
            sums_kernel,
            out_shape=(stored((PEERS, 40, 128)), shaped((48, 128))),
            in_specs=[hbm()] * 3,
            out_specs=(hbm(), vmem()),
            scratch_shapes=[
                pltpu.VMEM((ROWS, CELLS), bf16),
                pltpu.VMEM((16, BLOCK), bf16),
                pltpu.VMEM((K, 16), f32),
                pltpu.VMEM((16, 128), f32),
                pltpu.VMEM((PEERS, 40, 128), f32),
                pltpu.SemaphoreType.DMA((2 + CHUNKS,)),
                pltpu.SemaphoreType.DMA((2,)),
            ],
            compiler_params=limit(8),
            name="sums",
        )(*far(velocity_dist, jnp.asarray(p3), macro_state))
        got = lax.all_to_all(packed, "vel", split_axis=0, concat_axis=0, tiled=True)
        rising = [(i, i + 1) for i in range(n_space - 1)]
        half = PEERS // 2
        downwind = [(i * PEERS + n, j * PEERS + n) for i, j in rising for n in range(half, PEERS)]
        downwind += [(j * PEERS + n, i * PEERS + n) for i, j in rising for n in range(half)]
        edges = lax.ppermute(edges, ("space", "vel"), downwind)
        base, known, constants = pl.pallas_call(
            stream_kernel,
            out_shape=(shaped((ROWS, CELLS)), shaped((56, WIDE)), shaped(block.shape, bf16)),
            in_specs=[hbm()] * 8,
            out_specs=(vmem(),) * 3,
            scratch_shapes=[
                pltpu.VMEM((ROWS, CELLS), bf16),
                pltpu.VMEM((16, 128), bf16),
                pltpu.VMEM((K, K), f32),
                pltpu.VMEM((1, K), f32),
                pltpu.VMEM((1, CELLS), f32),
                pltpu.VMEM((1, CELLS), jnp.int32),
                pltpu.SemaphoreType.DMA((8,)),
            ],
            compiler_params=limit(16),
            cost_estimate=pl.CostEstimate(flops=600_000_000, bytes_accessed=4_000_000, transcendentals=0),
            name="stream",
        )(
            *far(velocity_dist, *(jnp.asarray(x) for x in (block, pairs, own6))),
            *far(coupling, diffusivity.reshape(1, K), rate, flags),
        )
        got, base, edges = lax.optimization_barrier((got, base, edges))
        fields, sent = pl.pallas_call(
            lambda *refs: fields_kernel(n_space, *refs),
            out_shape=(shaped((N_FIELDS, 16, CELLS)), shaped((n_space, 16, 128))),
            in_specs=[vmem()] * 3,
            out_specs=(vmem(), vmem()),
            scratch_shapes=[pltpu.VMEM((384, 128), f32), pltpu.VMEM((SHEETS, 128), f32)],
            compiler_params=limit(12),
            name="fields",
        )(*near(got, known, constants))
        sent = lax.all_to_all(sent, "space", split_axis=0, concat_axis=0, tiled=True)
        return pl.pallas_call(
            lambda *refs: update_kernel(n_space, *refs),
            out_shape=(stored((ROWS, CELLS), bf16), stored((K, 16))),
            in_specs=[vmem()] * 5 + [hbm()],
            out_specs=(hbm(), hbm()),
            scratch_shapes=[
                pltpu.VMEM((ROWS, CELLS), bf16),
                pltpu.VMEM((K, 16), f32),
                pltpu.VMEM((384, 128), f32),
                pltpu.VMEM((SHEETS, 128), f32),
                pltpu.VMEM((48, 128), f32),
                pltpu.VMEM((16, ROWS), f32),
                pltpu.SemaphoreType.DMA((ROWS // UPDATE_ROWS + 2,)),
            ],
            compiler_params=limit(12),
            name="update",
        )(*near(sent, fields, known, constants, base), *far(edges))

    return per_device


def solution(mesh):
    placed = (P("vel", "space"), P(None, ("space", "vel")), P("space"), P("space"), P(), P())
    return jax.shard_map(
        make_per_device(mesh.shape["space"]),
        mesh=mesh,
        in_specs=placed,
        out_specs=(P("vel", "space"), P(None, ("space", "vel"))),
        check_vma=False,
    )
```

```python
import math

import jax
import jax.numpy as jnp
import numpy as np
from jax import lax
from jax.experimental import pallas as pl
from jax.experimental.pallas import tpu as pltpu
from jax.sharding import PartitionSpec as P

NV1 = 32
K = 13
time_step = 0.125
spacing = 8.0 / NV1
CELLS = 256
WIDE = 384
PEERS = 16
ROWS = 2048
BLOCK = 1024
bf16 = jnp.bfloat16
f32 = jnp.float32


def parts_of(x, number):
    rest = np.asarray(x, np.float64)
    out = []
    for _ in range(number):
        piece = rest.astype(np.float32).astype(bf16)
        out.append(piece)
        rest = rest - piece.astype(np.float64)
    return out


def grid_constants():
    v = (np.arange(NV1) + 0.5) * spacing - 4.0
    w = np.exp(-0.5 * v * v) * spacing / math.sqrt(2.0 * math.pi)
    vy, vz = np.repeat(v, NV1), np.tile(v, NV1)
    wyz = np.repeat(w, NV1) * np.tile(w, NV1)
    one = np.ones_like(vy)
    yz = vy * vy + vz * vz
    phi = np.stack([one, vy, vz, vy * vz, vy * vy, vz * vz, vy * yz, vz * yz])
    cmat = np.zeros((NV1, K, 8))
    for i, x in enumerate(v):
        c = cmat[i]
        c[0, 0] = 1.0
        c[1, 0] = x
        c[2, 1] = 1.0
        c[3, 2] = 1.0
        c[4, 0] = (x * x - 3.0) / math.sqrt(6.0)
        c[4, 4] = c[4, 5] = 1.0 / math.sqrt(6.0)
        c[5, 1] = x
        c[6, 2] = x
        c[7, 3] = 1.0
        c[8, 0] = 0.5 * x * x
        c[8, 4] = -0.5
        c[9, 0] = x * x / math.sqrt(12.0)
        c[9, 4] = 1.0 / math.sqrt(12.0)
        c[9, 5] = -2.0 / math.sqrt(12.0)
        c[10, 0] = x * (x * x - 5.0) / math.sqrt(10.0)
        c[10, 4] = c[10, 5] = x / math.sqrt(10.0)
        c[11, 1] = (x * x - 5.0) / math.sqrt(10.0)
        c[11, 6] = 1.0 / math.sqrt(10.0)
        c[12, 2] = (x * x - 5.0) / math.sqrt(10.0)
        c[12, 7] = 1.0 / math.sqrt(10.0)
    a = time_step * np.abs(v)
    plus = v > 0.0
    proj = phi * wyz
    groups = [np.ones(NV1)]
    for power in (1, 2, 3):
        groups += [a**power * plus, a**power * ~plus]
    big = np.zeros((7 * 16, 8 * NV1))
    for g, factor in enumerate(groups):
        for i in range(NV1):
            big[16 * g : 16 * g + K, 8 * i : 8 * i + 8] = factor[i] * w[i] * cmat[i]
    gram2 = proj @ phi.T
    shakhov = np.array([1.0] * 5 + [0.0] * 5 + [1.0 / 3.0] * 3)

    def between(factor):
        out = np.zeros((16, 16))
        for i in range(NV1):
            out[:K, :K] += factor[i] * w[i] * cmat[i] @ gram2 @ cmat[i].T
        return out

    c16 = np.zeros(16)
    c16[:K] = shakhov
    g, gp, gm, g2p, g2m = (between(groups[k]) for k in (0, 1, 2, 3, 4))
    mats = [g, gp, gm, g * c16, gp * c16, gm * c16, g2p, g2m, g2p * c16, g2m * c16]
    block = np.zeros((BLOCK + 224, 256), bf16)
    block[16:176, 128:176] = three_terms(np.concatenate(mats, axis=0))
    block[BLOCK:] = np.concatenate(parts_of(big, 2), axis=0)
    p3 = np.concatenate(parts_of(proj, 2), axis=0)
    ph, pm = parts_of(phi.T, 2)
    block[0:BLOCK, 0:24] = np.concatenate([ph, ph, pm], axis=1)
    own = np.zeros((PEERS, 16, 16))
    for j in range(PEERS):
        for u in range(2):
            own[j, 8 * u : 8 * u + 8, :K] = cmat[2 * j + u].T
    own = np.concatenate([three_terms(own), np.zeros((PEERS, 16, 80), bf16)], axis=2)
    return block, p3, own


def three_terms(x):
    h, m = parts_of(x, 2)
    return np.concatenate([h, h, m], axis=-1)


BASES = (1, 3, 9)


def pair_table():
    entries = []
    for stage, size in enumerate(BASES):
        for quantity in range(4):
            for i in range(size):
                for j in range(i, size):
                    entries.append((stage, quantity, i, j))
    return entries


PAIRS = pair_table()


def pair_arrays():
    kind = np.full((8, 128), -1, np.int32)
    left = np.zeros((8, 128), np.int32)
    right = np.zeros((8, 128), np.int32)
    twice = np.zeros((8, 128), np.int32)
    for n, (stage, quantity, i, j) in enumerate(PAIRS):
        at = (n // 128, n % 128)
        kind[at] = 4 * stage + quantity
        left[at], right[at] = i, j
        twice[at] = 1 if i == j else 2
    return np.concatenate([kind, left, right, twice], axis=0).astype(np.float32)


def lanes_of(shape):
    return lax.broadcasted_iota(jnp.int32, shape, len(shape) - 1)


def rows_of(shape):
    return lax.broadcasted_iota(jnp.int32, shape, 0)


def split3(f):
    h = f.astype(bf16)
    m = (f - h.astype(f32)).astype(bf16)
    return jnp.concatenate([h, m, h], axis=0)


def relax_of(rate, flags):
    return (time_step * rate) * (1.0 + flags.astype(f32))


def shift_up(x):
    return pltpu.roll(x, 1, 1)


def shift_down(x):
    return pltpu.roll(x, x.shape[1] - 1, 1)


def diff_up(x):
    return x - shift_up(x)


def diff_down(x):
    return x - shift_down(x)


def copies_of(pairs, sems):
    made = [pltpu.make_async_copy(x, y, sems.at[n]) for n, (x, y) in enumerate(pairs)]
    for copy in made:
        copy.start()
    return made


CHUNKS = 8


def chunks_of(source, target):
    rows = [pl.ds(n * (ROWS // CHUNKS), ROWS // CHUNKS) for n in range(CHUNKS)]
    return [(source.at[row, :], target.at[row, :]) for row in rows]


def sums_kernel(dist_in, p3_in, start_in, packed, edges, dist, p3, start, padded, whole, sems, sends):
    positive = lax.axis_index("vel") >= PEERS // 2
    halves = [pl.ds(u * BLOCK, BLOCK) for u in range(2)]
    pairs = [(p3_in, p3), (start_in, start)] + chunks_of(dist_in, dist)
    waits = copies_of(pairs, sems)
    waits[0].wait()
    waits[1].wait()
    padded[...] = jnp.zeros((16, 128), f32)
    padded[0:K, 0:16] = start[...]
    owned = padded[0:8, :] + pltpu.roll(padded[8:16, :], 16, 1)
    for j in range(PEERS):
        whole[j, 0:8, :] = owned
    e_lane = lanes_of((16, 128))
    e_row = rows_of((16, 128))
    cell = jnp.where(positive, 127 - e_row, e_row)
    pick = jnp.where((e_lane == cell) & (e_row < 3), 1.0, 0.0).astype(bf16)
    side = pl.multiple_of(jnp.where(positive, 128, 0), 128)
    going = []
    for u in range(2):
        for n in range(CHUNKS // 2):
            waits[2 + u * (CHUNKS // 2) + n].wait()
        y = jnp.dot(p3[...], dist[halves[u], :], preferred_element_type=f32)
        w = y[0:8] + y[8:16]
        for j in range(PEERS):
            whole[j, 8 + 16 * u : 16 + 16 * u, :] = w[:, 0:128]
            whole[j, 16 + 16 * u : 24 + 16 * u, :] = w[:, 128:256]
        rows = pl.ds(0, 24) if u == 0 else pl.ds(24, 16)
        going += copies_of([(whole.at[:, rows, :], packed.at[:, rows, :])], sends.at[pl.ds(u, 1)])
        near = dist[halves[u], pl.ds(side, 128)]
        e = lax.dot_general(pick, near, (((1,), (1,)), ((), ())), preferred_element_type=f32)
        for n in range(3):
            for k in range(8):
                at = 16 * n + 8 * u + k
                edges[at : at + 1, :] = e[n : n + 1, 128 * k : 128 * k + 128]
    for copy in going:
        copy.wait()


N_FIELDS = 28
RIM = 7
SIDE = 13
STRIPS = 512


def tiles_of(x):
    return [x[:, 128 * t : 128 * t + 128] for t in range(x.shape[1] // 128)]


def own_shifts():
    lane = lanes_of((16, 128))
    zero = jnp.zeros((16, 128), f32)

    def up(x):
        first, second = (pltpu.roll(t, 1, 1) for t in tiles_of(x))
        return jnp.concatenate([jnp.where(lane == 0, zero, first), jnp.where(lane == 0, first, second)], axis=1)

    def down(x):
        first, second = (pltpu.roll(t, 127, 1) for t in tiles_of(x))
        return jnp.concatenate([jnp.where(lane == 127, second, first), jnp.where(lane == 127, zero, second)], axis=1)

    return up, down


STEP = (0, 0, 16, 16)


def tile_roll(x, amount):
    return jnp.concatenate([pltpu.roll(t, amount, 1) for t in tiles_of(x)], axis=1)


def strip_up(x):
    return tile_roll(x, 1)


def strip_down(x):
    return tile_roll(x, 127)


def advance_three(keep, base, ups, downs, up, down):
    out = []
    for _ in range(3):
        base = keep * base
        if ups:
            base = base - (ups[0] - up(ups[0]))
        if downs:
            base = base - (downs[0] - down(downs[0]))
        ups = [keep * x - (y - up(y)) for x, y in zip(ups[:-1], ups[1:])]
        downs = [keep * x - (y - down(y)) for x, y in zip(downs[:-1], downs[1:])]
        out.append(base)
    return out


def fields_of(s1, s2, s3, start, r, mask, diffusion, block, up, down):
    width = r.shape[1]
    keep = 1.0 - r

    def up_diff(x):
        return x - up(x)

    def down_diff(x):
        return x - down(x)

    def times(first, last, inputs):
        stacked = split3(jnp.concatenate(inputs, axis=1) if len(inputs) > 1 else inputs[0])
        y = jnp.dot(block[16 * first : 16 * last, 128:176], stacked, preferred_element_type=f32)
        out = []
        for n in range(len(inputs)):
            cut = y[:, n * width : (n + 1) * width]
            out.append([cut[16 * g : 16 * g + 16] for g in range(last - first)])
        return out

    def applied(f, coupled):
        return mask * (coupled + diffusion * (2.0 * f - up(f) - down(f)))

    def streamed(g, gp, gm):
        return keep * g - up_diff(gp) - down_diff(gm)

    def streamed_twice(k1, gp, gm, g2p, g2m):
        return keep * k1 - up_diff(keep * gp - up_diff(g2p)) - down_diff(keep * gm - down_diff(g2m))

    ((gc, gcp, gcm, _, _, g2cp, g2cm),) = times(4, 11, [start])
    relaxed = r * gc
    shares = mask * (s1 + relaxed)
    res = mask * (shares - start)
    k1_start = streamed(relaxed, r * gcp, r * gcm)
    k2_start = streamed_twice(k1_start, r * gcp, r * gcm, r * g2cp, r * g2cm)

    def parts(f, ys):
        out = [applied(f, ys[0])]
        k1 = streamed(ys[1], ys[2], ys[3])
        rg = r * ys[4]
        held = rg - f
        out += [mask * (k1 + held), held]
        if len(ys) > 5:
            out.append(streamed_twice(k1, ys[2], ys[3], ys[7], ys[8]))
            out.append(streamed(rg, r * ys[5], r * ys[6]) + held)
        return out

    y_shares, y_res = times(0, 9, [shares, res])
    rg = r * y_shares[4]
    held_shares = rg - shares
    n_shares = streamed(rg, r * y_shares[5], r * y_shares[6]) + held_shares
    p0 = mask * (s2 + k1_start + held_shares)
    e, p1, _, k2_res, n_res = parts(res, y_res)

    y_e, y_p0, y_p1 = times(0, 9, [e, p0, p1])
    ee, p2, _, k2_e, n_e = parts(e, y_e)
    ap0, q3, held_p0 = parts(p0, y_p0[:5])
    ap1, q4, held_p1 = parts(p1, y_p1[:5])
    q0 = mask * (s3 + k2_start + n_shares + held_p0)
    q1 = mask * (k2_res + n_res + held_p1)

    y_p2, y_ap0, y_ap1, y_q0, y_q1, y_q3, y_q4 = times(0, 5, [p2, ap0, ap1, q0, q1, q3, q4])
    ap2, q5, held_p2 = parts(p2, y_p2)
    aap0, q6, _ = parts(ap0, y_ap0)
    aap1, q7, _ = parts(ap1, y_ap1)
    q2 = mask * (k2_e + n_e + held_p2)
    aq0, aq1, aq3, aq4 = (applied(f, y[0]) for f, y in ((q0, y_q0), (q1, y_q1), (q3, y_q3), (q4, y_q4)))

    (y_ap2,) = times(0, 5, [ap2])
    aap2, q8, _ = parts(ap2, y_ap2)
    first = [q2, q5, q6, q7, aq0, aq1, aq3, aq4]
    aq2, aq5, aq6, aq7, aaq0, aaq1, aaq3, aaq4 = (applied(f, y[0]) for f, y in zip(first, times(0, 1, first)))
    second = [q8, aq2, aq5, aq6, aq7]
    aq8, aaq2, aaq5, aaq6, aaq7 = (applied(f, y[0]) for f, y in zip(second, times(0, 1, second)))
    ((y_aq8,),) = times(0, 1, [aq8])
    aaq8 = applied(aq8, y_aq8)

    q = [q0, q1, q2, q3, q4, q5, q6, q7, q8]
    aq = [aq0, aq1, aq2, aq3, aq4, aq5, aq6, aq7, aq8]
    aaq = [aaq0, aaq1, aaq2, aaq3, aaq4, aaq5, aaq6, aaq7, aaq8]
    fields = [start, shares, res, e, p0, p1, p2, ap0, ap1, ap2] + q + aq
    plain = [[res], [p0, p1, p2], q]
    once = [[e], [ap0, ap1, ap2], aq]
    again = [[ee], [aap0, aap1, aap2], aaq]
    return fields, plain, once, again


EARLY = 4 * 1 + 4 * 6
LATE_FROM = EARLY // 8 * 8
EARLY_SHEETS = (EARLY + 7) // 8 * 64 + 8
SHEETS = EARLY_SHEETS + 8 * (len(PAIRS) - LATE_FROM) + 8


def product_operands(plain, once, again, counted):
    lefts = [[[counted * x for x in xs] for xs in xss] for xss in (plain, once)]
    rights = [plain, once, again]
    if counted.shape[1] == STRIPS:
        def folded(x):
            return x[:, 0:256] + x[:, 256:512]

        lefts = [[[folded(x) for x in xs] for xs in xss] for xss in lefts]
        rights = lefts + [[[folded(counted * x) for x in xs] for xs in again]]
    return lefts, rights


def inner_products(operands, entries, first, sheets, table):
    lefts, rights = operands
    start = first // 8 * 8
    stop = entries.stop
    zero = jnp.zeros((8, 128), f32)
    end = (stop + 7) // 8 * 8
    for n in range(start, end):
        if n not in entries:
            sheets[8 * (n - start) : 8 * (n - start) + 8, :] = zero
            continue
        stage, quantity, i, j = PAIRS[n]
        x, y = ((0, 0), (0, 1), (1, 1), (1, 2))[quantity]
        product = lefts[x][stage][i] * rights[y][stage][j]
        half = product[:, 0:128] + product[:, 128:256]
        sheets[8 * (n - start) : 8 * (n - start) + 8, :] = half[0:8] + half[8:16]
    lines = (end + 127) // 128
    if start:
        table[0:start, :] = jnp.zeros((start, 128), f32)
    if end < 128 * lines:
        table[end : 128 * lines, :] = jnp.zeros((128 * lines - end, 128), f32)
    for n in range(start, end, 8):
        rows = [sheets[pl.ds(8 * (n - start) + k, 8, stride=8), :] for k in range(8)]
        while len(rows) > 1:
            rows = [p + q for p, q in zip(rows[0::2], rows[1::2])]
        table[n : n + 8, :] = rows[0]
    ones = jnp.ones((8, 3 * 128), bf16)
    out = []
    for n in range(lines):
        x = table[128 * n : 128 * n + 128, :]
        h = x.astype(bf16)
        rest = x - h.astype(f32)
        m = rest.astype(bf16)
        low = (rest - m.astype(f32)).astype(bf16)
        x = jnp.concatenate([h, m, low], axis=1)
        out.append(lax.dot_general(ones, x, (((1,), (1,)), ((), ())), preferred_element_type=f32))
    return out


def early_products(operands, sheets, table):
    return inner_products(operands, range(EARLY), 0, sheets.at[0:EARLY_SHEETS, :], table.at[0:128, :])


def late_products(operands, sheets, table):
    return inner_products(operands, range(EARLY, len(PAIRS)), EARLY, sheets.at[EARLY_SHEETS:SHEETS, :], table.at[128:384, :])


def fields_kernel(n_space, got, known, block, fields, sent, table, sheets):
    slab = lax.axis_index("space")
    wide = (16, CELLS)
    w = [
        jnp.concatenate([got[:, 8 + 8 * t : 16 + 8 * t, :], got[:, 24 + 8 * t : 32 + 8 * t, :]], axis=1)
        for t in range(2)
    ]
    w = jnp.concatenate([x.reshape(PEERS * 16, 128) for x in w], axis=1)
    wh = w.astype(bf16)
    wm = (w - wh.astype(f32)).astype(bf16)
    y = jnp.dot(block[BLOCK : BLOCK + 224, :], wh, preferred_element_type=f32)
    z = jnp.dot(block[BLOCK : BLOCK + 112, :], wm, preferred_element_type=f32)
    mu = (y[112:224] + z) + y[0:112]
    mu = [mu[16 * g : 16 * g + 16] for g in range(7)]

    lane8 = lanes_of((8, 128))
    parts = [[jnp.zeros((8, 128), f32)] * 2 for _ in range(2)]
    for j in range(PEERS):
        tile = got[j, 0:8, :]
        here = lane8 // 16 == j % 8
        for half in range(2):
            amount = (16 * j - 16 * half) % 128
            moved = pltpu.roll(tile, amount, 1) if amount else tile
            parts[half][j // 8] = jnp.where(here, moved, parts[half][j // 8])
    start = jnp.concatenate([jnp.concatenate(x, axis=1) for x in parts], axis=0)

    r = jnp.broadcast_to(known[16:17, 0:CELLS], wide)
    diffusion = jnp.concatenate([known[0:16, 128:256]] * 2, axis=1)
    up, down = own_shifts()
    s1, s2, s3 = advance_three(1.0 - r, mu[0], [mu[1], mu[3], mu[5]], [mu[2], mu[4], mu[6]], up, down)
    out, plain, once, again = fields_of(s1, s2, s3, start, r, 1.0, diffusion, block, up, down)
    for n, f in enumerate(out):
        fields[n] = f
    lane = lanes_of(wide)
    low = jnp.where(slab > 0, RIM, 0)
    high = jnp.where(slab < n_space - 1, CELLS - RIM, CELLS)
    counted = jnp.where((lane >= low) & (lane < high), 1.0, 0.0)
    operands = product_operands(plain, once, again, counted)
    tops = early_products(operands, sheets, table) + late_products(operands, sheets, table)

    lane1 = lanes_of((16, 128))
    row1 = rows_of((16, 128))
    start_relax = jnp.where(rows_of(wide) == K, r, start)
    tile = jnp.zeros((16, 128), f32)
    for n, f in enumerate([s1, s2, s3, start_relax]):
        at = lane1 - 32 * n
        begin = pltpu.roll(f[:, 0:128], 32 * n, 1) if n else f[:, 0:128]
        tile = jnp.where((at >= 0) & (at < SIDE), begin, tile)
        end = pltpu.roll(f[:, 128:256], (32 * n + 16 + SIDE) % 128, 1)
        tile = jnp.where((at >= 16) & (at < 16 + SIDE), end, tile)
        if n < 3:
            begin = pltpu.roll(mu[2 + 2 * n][:, 0:128], 32 * n + SIDE, 1)
            tile = jnp.where((at >= SIDE) & (at < 16), begin, tile)
            end = pltpu.roll(mu[1 + 2 * n][:, 128:256], (32 * n + 32) % 128, 1)
            tile = jnp.where((at >= 16 + SIDE) & (at < 32), end, tile)
    tile = pltpu.roll(tile, lax.rem(32 * lax.rem(slab, 4) + 112, 128), 1)
    row_a = jnp.broadcast_to(tops[0][0:1] + tops[1][0:1], (16, 128))
    row_b = jnp.broadcast_to(tops[2][0:1], (16, 128))
    tile = jnp.where(row1 == 14, row_a, jnp.where(row1 == 15, row_b, tile))
    for j in range(n_space):
        sent[j] = tile


def speeds_of(shape):
    number = 2 * lax.axis_index("vel") + jnp.where(rows_of(shape) >= 8, 1, 0)
    return time_step * jnp.abs((number.astype(f32) + 0.5) * spacing - 4.0)


def bands_of(r, positive):
    a = speeds_of(r.shape)
    stay = 1.0 - r - a

    def before(x):
        return jnp.where(positive, shift_up(x), shift_down(x))

    once = before(stay)
    two = before(once)
    t0 = stay * stay * stay
    t1 = a * (stay * (stay + once) + once * once)
    t2 = a * a * (stay + once + two)
    return t0, t1, t2, a * a * a


def banded(weights, u, distance):
    value = jnp.zeros(distance.shape, f32)
    for n, x in enumerate(weights):
        row = jnp.broadcast_to(x[8 * u : 8 * u + 1, 0 : distance.shape[1]], distance.shape)
        value = jnp.where(distance == n, row, value)
    return value


def stream_kernel(
    dist_in,
    block_in,
    pairs_in,
    own_in,
    coupling_in,
    diff_in,
    rate_in,
    flags_in,
    out,
    table,
    block,
    dist,
    own6,
    coupling_raw,
    diff_raw,
    rate,
    flags,
    sems,
):
    vel = lax.axis_index("vel")
    positive = vel >= PEERS // 2
    moves = [(rate_in, rate), (flags_in, flags), (dist_in, dist)]
    moves += [(coupling_in, coupling_raw), (diff_in, diff_raw), (own_in.at[vel], own6)]
    moves += [(pairs_in, table.at[24:56, 0:128]), (block_in, block)]
    waits = copies_of(moves, sems)
    waits[0].wait()
    waits[1].wait()
    relax = relax_of(rate[...], flags[...])
    table[16:24, 0:CELLS] = jnp.broadcast_to(relax, (8, CELLS))
    weights = bands_of(jnp.broadcast_to(relax, (16, CELLS)), positive)
    towards = jnp.where(positive, 1, -1)
    distance = (lanes_of((CELLS, CELLS)) - rows_of((CELLS, CELLS))) * towards
    waits[2].wait()
    for u in range(2):
        b = banded(weights, u, distance)
        bh = b.astype(bf16)
        bl = (b - bh.astype(f32)).astype(bf16)
        rows = pl.ds(u * BLOCK, BLOCK)
        x = dist[rows, :]
        value = jnp.dot(x, bh, preferred_element_type=f32)
        value += jnp.dot(x, bl, preferred_element_type=f32)
        out[rows, :] = value

    for copy in waits[3:]:
        copy.wait()
    table[0:16, 0:128] = jnp.zeros((16, 128), f32)
    table[0:K, 0:K] = coupling_raw[...]
    c = table[0:16, 0:128]
    ch = c.astype(bf16).astype(f32)
    pieces = [ch, ch, c - ch]
    terms = pieces[0]
    for n in range(1, 3):
        terms = terms + pltpu.roll(pieces[n], 16 * n, 1)
    block[0:16, 128:256] = terms.astype(bf16)
    block[176:192, 128:256] = own6[...]
    shape = (16, K)
    chosen = jnp.where(lanes_of(shape) == rows_of(shape), jnp.broadcast_to(diff_raw[...], shape), 0.0)
    table[0:16, 128:256] = jnp.broadcast_to(jnp.sum(chosen, axis=1, keepdims=True), (16, 128))


UPDATE_ROWS = 256


def strips_of(n_space, sent):
    raw = []
    lane1 = lanes_of((16, 128))
    for n in range(4):
        which = ((lane1 + 128 - 32 * n) % 128 // 16 + 1) // 2
        tiles = []
        for t in range(4):
            tile = jnp.zeros((16, 128), f32)
            for k in range(5):
                if 4 * t + k < n_space:
                    tile = jnp.where(which == k, sent[4 * t + k], tile)
            amount = (STEP[t] - 32 * n) % 128
            tiles.append(pltpu.roll(tile, amount, 1) if amount else tile)
        raw.append(jnp.concatenate(tiles, axis=1))
    shape = (16, STRIPS)
    row = rows_of(shape)
    turned = jnp.concatenate([(lane1 + 128 - STEP[t]) % 128 + 128 * t for t in range(4)], axis=1)
    at = turned % 32
    valid = (turned < 32 * (n_space - 1)) & (at < 2 * SIDE)
    mask = jnp.where(valid, 1.0, 0.0)
    moments = jnp.where(row < K, mask, 0.0)
    closer = [tile_roll(x, 128 - 3) for x in raw]
    arrays = [jnp.where(at < SIDE, x, y) for x, y in zip(raw, closer)]
    r = mask * jnp.broadcast_to(arrays[3][K : K + 1], shape)
    s1, s2, s3, start = (moments * x for x in arrays)
    ups = [jnp.where((at >= SIDE - 3) & (at < SIDE), moments * x, 0.0) for x in closer[:3]]
    downs = [tile_roll(x, 128 - 16) for x in raw[:3]]
    downs = [jnp.where((at >= SIDE) & (at < SIDE + 3), moments * x, 0.0) for x in downs]
    zero = jnp.zeros(shape, f32)
    over_up = advance_three(1.0 - r, zero, ups, [], strip_up, strip_down)
    over_down = advance_three(1.0 - r, zero, [], downs, strip_up, strip_down)
    s = [x + jnp.where(at < SIDE, y, z) for x, y, z in zip((s1, s2, s3), over_down, over_up)]
    s = [mask * x for x in s]
    counted = jnp.where((at >= SIDE - RIM) & (at < SIDE + RIM), mask, 0.0)
    return s, start, r, mask, counted


def update_kernel(
    n_space,
    sent,
    fields,
    table,
    block,
    base,
    edges_in,
    out,
    macro,
    done,
    macro_part,
    products,
    sheets,
    edges,
    ends,
    sems,
):
    place = lax.axis_index("vel")
    slab = lax.axis_index("space")
    positive = place >= PEERS // 2
    (edge_copy,) = copies_of([(edges_in, edges)], sems.at[pl.ds(ROWS // UPDATE_ROWS + 1, 1)])

    def known(at):
        return table[at : at + 8, 0:128]

    (s1, s2, s3), strip_start, strip_r, strip_mask, counted = strips_of(n_space, sent)
    diffusion = jnp.concatenate([table[0:16, 128:256]] * 4, axis=1)
    strip_fields, plain, once, again = fields_of(
        s1, s2, s3, strip_start, strip_r, strip_mask, diffusion, block, strip_up, strip_down
    )
    operands = product_operands(plain, once, again, counted)
    gathered = sent[0, 8:16, :]
    for j in range(1, n_space):
        gathered = gathered + sent[j, 8:16, :]
    row8 = rows_of((8, 128))
    (top,) = early_products(operands, sheets, products)
    early = jnp.where(row8 == 0, gathered[6:7] + top[0:1], 0.0) * known(48)
    cpl = table[0:16, 0:128]
    lane16 = lanes_of((16, 128))
    row16 = rows_of((16, 128))
    size = jnp.sum(jnp.abs(cpl), axis=1, keepdims=True)
    middle = jnp.sum(jnp.where(lane16 == row16, cpl, 0.0), axis=1, keepdims=True)
    real = row16[:, 0:1] < K
    most = jnp.max(jnp.where(real, size + 4.0 * table[0:16, 128:129], 0.0), axis=0, keepdims=True)
    least = jnp.min(jnp.where(real, 2.0 * middle - size, 1e30), axis=0, keepdims=True)
    low_step, high_step = 1.0 / most, 1.0 / least

    def summed(weighted, which):
        picked = jnp.where(known(24) == which, weighted, 0.0)
        return jnp.sum(jnp.sum(picked, axis=0, keepdims=True), axis=1, keepdims=True)

    def clipped(x):
        return jnp.minimum(jnp.maximum(x, low_step), high_step)

    def weights_of(stage, weighted):
        rr, ra, aa, aaa = (summed(weighted, 4 * stage + n) for n in range(4))
        s1 = clipped(rr / ra)
        rr2 = rr - 2.0 * s1 * ra + s1 * s1 * aa
        ra2 = ra - 2.0 * s1 * aa + s1 * s1 * aaa
        s2 = clipped(rr2 / ra2)
        return s1 + s2, -s1 * s2

    li, ri = (known(n).astype(jnp.int32) for n in (32, 40))

    def choose(index, zero, one, two):
        return jnp.where(index == 0, zero, jnp.where(index == 1, one, two))

    a1, b1 = weights_of(0, early)
    a2, b2 = weights_of(1, early * choose(li, 1.0, a1, b1) * choose(ri, 1.0, a1, b1))

    def both(index):
        outer = (index >= 3).astype(jnp.int32) + (index >= 6).astype(jnp.int32)
        return choose(outer, 1.0, a2, b2) * choose(index - 3 * outer, 1.0, a1, b1)

    tops = late_products(operands, sheets, products)
    line_a = gathered[6:7] + tops[0][0:1]
    line_b = gathered[7:8] + tops[1][0:1]
    total = jnp.where(row8 == 0, line_a, jnp.where(row8 == 1, line_b, 0.0))
    total = total * known(48)
    a3, b3 = weights_of(2, total * both(li) * both(ri))

    def last_fields(at, r):
        start, shares, res, e = (at(n) for n in range(4))
        corr1 = a1 * res + b1 * e
        cur1 = shares + corr1
        res2 = at(4) + a1 * at(5) + b1 * at(6)
        e2 = at(7) + a1 * at(8) + b1 * at(9)
        corr2 = a2 * res2 + b2 * e2
        cur2 = res2 + cur1 + corr2

        def third(first):
            rows = [at(first + 3 * n) + a1 * at(first + 3 * n + 1) + b1 * at(first + 3 * n + 2) for n in range(3)]
            return rows[0] + a2 * rows[1] + b2 * rows[2]

        res3, e3 = third(10), third(19)
        corr3 = a3 * res3 + b3 * e3
        row = rows_of(r.shape)
        scaled = r * jnp.where(row < 5, 1.0, jnp.where(row < 10, 0.0, 1.0 / 3.0))
        f1 = scaled * start + corr1
        f2 = scaled * cur1 + corr2
        f3 = scaled * cur2 + corr3
        return f1, f2, f3, res3 + cur2 + corr3, r

    own = last_fields(lambda n: fields[n], jnp.broadcast_to(table[16:17, 0:CELLS], (16, CELLS)))
    strips = last_fields(lambda n: strip_fields[n], strip_r)
    lane1 = lanes_of((16, 128))
    has_left, has_right = jnp.where(slab > 0, 1, 0), jnp.where(slab < n_space - 1, 1, 0)
    near_left = (lane1 < RIM * has_left)
    near_right = (lane1 >= 128 - RIM * has_right)
    far_left = (lane1 >= 128 - 2 * has_left)
    far_right = (lane1 < 2 * has_right)
    wide = []
    for x, y in zip(own, strips):
        y = jnp.concatenate([y[:, 0:256], tile_roll(y[:, 256:512], 112)], axis=1)
        y = pltpu.roll(y, lax.rem(STRIPS + 32 - 32 * slab, STRIPS), 1)[:, 0:128]
        from_left = pltpu.roll(y, 128 - SIDE, 1)
        from_right = pltpu.roll(y, 96 - SIDE, 1)
        tiles = [
            jnp.where(near_left, from_left, x[:, 0:128]),
            jnp.where(near_right, from_right, x[:, 128:256]),
            jnp.where(far_left, from_left, jnp.where(far_right, from_right, 0.0)),
        ]
        wide.append(jnp.concatenate(tiles, axis=1))
    f1, f2, f3, cur3, r = wide
    mine = pltpu.roll(cur3[:, 0:CELLS], lax.rem(CELLS - 16 * place, CELLS), 1)
    macro_part[...] = mine[0:K, 0:16]
    macro_copy = pltpu.make_async_copy(macro_part, macro, sems.at[ROWS // UPDATE_ROWS])
    macro_copy.start()
    y = jnp.dot(
        block[176:192, 128:176], split3(jnp.concatenate([f1, f2, f3], axis=1)), preferred_element_type=f32
    )
    y1, y2, y3 = (y[:, n * WIDE : (n + 1) * WIDE] for n in range(3))
    a = speeds_of((16, WIDE))
    stay = 1.0 - r - a

    def moved(x):
        return stay * x + a * jnp.where(positive, shift_up(x), shift_down(x))

    h = (moved(moved(y1) + y2) + y3)[:, 0:CELLS]
    hh = h.astype(bf16).astype(f32)
    hm = (h - hh).astype(bf16).astype(f32)

    weights = bands_of(r, positive)
    towards = jnp.where(positive, 1, -1)
    at8 = rows_of((8, 128))
    at8 = jnp.where(positive, -1 - at8, at8 + CELLS)
    low = jnp.where(positive, 0, CELLS - 128)
    distance = (lanes_of((8, 128)) + low - at8) * towards
    weights = [jnp.where(positive, x[:, 0:128], x[:, 128:256]) for x in weights]
    ends[...] = jnp.zeros((16, ROWS), f32)
    edge_copy.wait()
    for n in range(3):
        for k in range(16):
            row = edges[16 * n + k : 16 * n + k + 1, :]
            ends[n : n + 1, 128 * k : 128 * k + 128] = row
            ends[8 + n : 9 + n, 128 * k : 128 * k + 128] = row

    sends = [macro_copy]
    for u in range(2):
        hu, mu = hh[8 * u : 8 * u + 8], hm[8 * u : 8 * u + 8]
        mixed = jnp.concatenate([hu, mu, hu, jnp.zeros((104, CELLS), f32)], axis=0).astype(bf16)
        b = banded(weights, u, distance)
        bh = b.astype(bf16).astype(f32)
        b = jnp.concatenate([bh, b - bh], axis=0).astype(bf16)
        for n in range(BLOCK // UPDATE_ROWS):
            part = u * (BLOCK // UPDATE_ROWS) + n
            rows = pl.ds(part * UPDATE_ROWS, UPDATE_ROWS)
            value = jnp.dot(block[pl.ds(n * UPDATE_ROWS, UPDATE_ROWS), 0:128], mixed, preferred_element_type=f32)
            near = lax.dot_general(ends[:, rows].astype(bf16), b, (((0,), (0,)), ((), ())), preferred_element_type=f32)
            value += base[rows, :]
            done[rows, 0:128] = (value[:, 0:128] + jnp.where(positive, near, 0.0)).astype(bf16)
            done[rows, 128:256] = (value[:, 128:256] + jnp.where(positive, 0.0, near)).astype(bf16)
            copy = pltpu.make_async_copy(done.at[rows, :], out.at[rows, :], sems.at[part])
            copy.start()
            sends.append(copy)
    for copy in sends:
        copy.wait()


def vmem():
    return pl.BlockSpec(memory_space=pltpu.VMEM)


def hbm():
    return pl.BlockSpec(memory_space=pltpu.HBM)


def shaped(shape, dtype=f32):
    return pltpu.VMEM(shape, dtype)


def stored(shape, dtype=f32):
    return pltpu.HBM(shape, dtype)


def placed_at(space, arrays):
    return [pltpu.with_memory_space_constraint(x, space) for x in arrays]


def near(*arrays):
    return placed_at(pltpu.VMEM, arrays)


def far(*arrays):
    return placed_at(pltpu.HBM, arrays)


def limit(mib):
    return pltpu.CompilerParams(vmem_limit_bytes=mib * 2**20)


def make_per_device(n_space):
    block, p3, own6 = grid_constants()
    pairs = pair_arrays()

    def per_device(velocity_dist, macro_state, collision_rate, wall_flags, diffusivity, coupling):
        rate = collision_rate.reshape(1, CELLS)
        flags = wall_flags.reshape(1, CELLS)
        packed, edges = pl.pallas_call(
            sums_kernel,
            out_shape=(stored((PEERS, 40, 128)), shaped((48, 128))),
            in_specs=[hbm()] * 3,
            out_specs=(hbm(), vmem()),
            scratch_shapes=[
                pltpu.VMEM((ROWS, CELLS), bf16),
                pltpu.VMEM((16, BLOCK), bf16),
                pltpu.VMEM((K, 16), f32),
                pltpu.VMEM((16, 128), f32),
                pltpu.VMEM((PEERS, 40, 128), f32),
                pltpu.SemaphoreType.DMA((2 + CHUNKS,)),
                pltpu.SemaphoreType.DMA((2,)),
            ],
            compiler_params=limit(8),
            name="sums",
        )(*far(velocity_dist, jnp.asarray(p3), macro_state))
        got = lax.all_to_all(packed, "vel", split_axis=0, concat_axis=0, tiled=True)
        rising = [(i, i + 1) for i in range(n_space - 1)]
        half = PEERS // 2
        downwind = [(i * PEERS + n, j * PEERS + n) for i, j in rising for n in range(half, PEERS)]
        downwind += [(j * PEERS + n, i * PEERS + n) for i, j in rising for n in range(half)]
        edges = lax.ppermute(edges, ("space", "vel"), downwind)
        base, known, constants = pl.pallas_call(
            stream_kernel,
            out_shape=(shaped((ROWS, CELLS)), shaped((56, WIDE)), shaped(block.shape, bf16)),
            in_specs=[hbm()] * 8,
            out_specs=(vmem(),) * 3,
            scratch_shapes=[
                pltpu.VMEM((ROWS, CELLS), bf16),
                pltpu.VMEM((16, 128), bf16),
                pltpu.VMEM((K, K), f32),
                pltpu.VMEM((1, K), f32),
                pltpu.VMEM((1, CELLS), f32),
                pltpu.VMEM((1, CELLS), jnp.int32),
                pltpu.SemaphoreType.DMA((8,)),
            ],
            compiler_params=limit(16),
            cost_estimate=pl.CostEstimate(flops=600_000_000, bytes_accessed=4_000_000, transcendentals=0),
            name="stream",
        )(
            *far(velocity_dist, *(jnp.asarray(x) for x in (block, pairs, own6))),
            *far(coupling, diffusivity.reshape(1, K), rate, flags),
        )
        got, base, edges = lax.optimization_barrier((got, base, edges))
        fields, sent = pl.pallas_call(
            lambda *refs: fields_kernel(n_space, *refs),
            out_shape=(shaped((N_FIELDS, 16, CELLS)), shaped((n_space, 16, 128))),
            in_specs=[vmem()] * 3,
            out_specs=(vmem(), vmem()),
            scratch_shapes=[pltpu.VMEM((384, 128), f32), pltpu.VMEM((SHEETS, 128), f32)],
            compiler_params=limit(12),
            name="fields",
        )(*near(got, known, constants))
        sent = lax.all_to_all(sent, "space", split_axis=0, concat_axis=0, tiled=True)
        return pl.pallas_call(
            lambda *refs: update_kernel(n_space, *refs),
            out_shape=(stored((ROWS, CELLS), bf16), stored((K, 16))),
            in_specs=[vmem()] * 5 + [hbm()],
            out_specs=(hbm(), hbm()),
            scratch_shapes=[
                pltpu.VMEM((ROWS, CELLS), bf16),
                pltpu.VMEM((K, 16), f32),
                pltpu.VMEM((384, 128), f32),
                pltpu.VMEM((SHEETS, 128), f32),
                pltpu.VMEM((48, 128), f32),
                pltpu.VMEM((16, ROWS), f32),
                pltpu.SemaphoreType.DMA((ROWS // UPDATE_ROWS + 2,)),
            ],
            compiler_params=limit(12),
            name="update",
        )(*near(sent, fields, known, constants, base), *far(edges))

    return per_device


def solution(mesh):
    placed = (P("vel", "space"), P(None, ("space", "vel")), P("space"), P("space"), P(), P())
    return jax.shard_map(
        make_per_device(mesh.shape["space"]),
        mesh=mesh,
        in_specs=placed,
        out_specs=(P("vel", "space"), P(None, ("space", "vel"))),
        check_vma=False,
    )
```
